32 devices in a mesh: dp: 2 (over core), row: 4 (over y, x), col: 4 (over z).
Axes of the slice: x: 2, y: 2, z: 4, core: 2. Of those that a mesh axis runs over, the one named last changes fastest.
Arguments:
- tokens: bfloat16 [768, 8192], P('row', ('dp', 'col')), may hold values from -6 to 6
- prefix: int32 [8], P(('dp', 'row')), may hold values from 102 to 512, as said below
- ln1_gain: float32 [768], replicated, may hold values from 0.5 to 1.5
- ln1_bias: float32 [768], replicated, may hold values from -3 to 3
- w_qkv: bfloat16 [3, 768, 768], P(None, 'row', 'col'), may hold values from -0.21875 to 0.21875
- qv_bias: float32 [2, 768], replicated, may hold values from -3 to 3
- w_out: bfloat16 [768, 768], P('col', 'row'), may hold values from -0.875 to 0.875
- out_bias: float32 [768], replicated, may hold values from -3 to 3
- ln2_gain: float32 [768], replicated, may hold values from 0.5 to 1.5
- ln2_bias: float32 [768], replicated, may hold values from -3 to 3
- w_fc: bfloat16 [768, 3072], P('row', 'col'), may hold values from -0.21875 to 0.21875
- fc_bias: float32 [3072], replicated, may hold values from -3 to 3
- w_proj: bfloat16 [768, 3072], P('row', 'col'), may hold values from -0.109375 to 0.109375
- proj_bias: float32 [768], replicated, may hold values from -3 to 3
- cotangent: bfloat16 [768, 8192], P('row', ('dp', 'col')), may hold values from -6 to 6
Outputs:
- output: bfloat16 [768, 8192], P('row', ('dp', 'col'))
- input_grad: float32 [768, 8192], P('row', ('dp', 'col'))
- ln1_gain_grad: float32 [768], replicated
- ln1_bias_grad: float32 [768], replicated
- w_qkv_grad: float32 [3, 768, 768], P(None, 'row', 'col')
- qv_bias_grad: float32 [2, 768], replicated
- w_out_grad: float32 [768, 768], P('col', 'row')
- out_bias_grad: float32 [768], replicated
- ln2_gain_grad: float32 [768], replicated
- ln2_bias_grad: float32 [768], replicated
- w_fc_grad: float32 [768, 3072], P('row', 'col')
- fc_bias_grad: float32 [3072], replicated
- w_proj_grad: float32 [768, 3072], P('row', 'col')
- proj_bias_grad: float32 [768], replicated
The draws below stay inside these ranges and needn't reach their ends.
Inputs may be any that keep to these rules, and one draw needn't show every extreme that they name: `prefix`: in every draw some sequence has exactly 102 and some other exactly 512.
All inputs are finite; a program needn't handle non-finite values.
Results may differ from the reference program's by a relative error of at most 0.012.
Values may be sent and summed in bfloat16 or wider, within the bound.
A program may use at most 256 MiB of HBM per device.

```python
import math
import jax
import jax.numpy as jnp
from jax import lax

D = 768
HEADS = 12
FF = 3072
HEAD_DIM = 64
LEN = 1024
SEQS = 8
TOKENS = 8192


def draw_prefix(key, part):
    first_key = jax.random.fold_in(key, 11)
    second_key = jax.random.fold_in(key, 12)
    third_key = jax.random.fold_in(key, 13)
    lowest = LEN // 10
    highest = LEN // 2
    lengths = jax.random.randint(first_key, (SEQS,), lowest, highest + 1, dtype=jnp.int32)
    top_place = jax.random.randint(second_key, (), 0, SEQS, dtype=jnp.int32)
    step_place = jax.random.randint(third_key, (), 1, SEQS, dtype=jnp.int32)
    bottom_place = (top_place + step_place) % SEQS
    lengths = lengths.at[top_place].set(highest)
    return lengths.at[bottom_place].set(lowest)


def steps_of(stream_key, shape, pieces, low, top_value):
    factor_of = 1.0
    for position, blocks in pieces:
        heights = jax.random.uniform(jax.random.fold_in(jax.random.fold_in(stream_key, 6), position), (blocks,), jnp.float32, low / len(pieces), top_value / len(pieces))
        factor_of = factor_of * jnp.repeat(jnp.exp(heights), shape[position] // blocks).reshape((-1,) + (1,) * (len(shape) - 1 - position))
    return factor_of


def gaussian(stream_key, shape, scale, limit, split=(), held_as=jnp.bfloat16):
    drawn = jax.random.normal(stream_key, shape, jnp.float32) * scale
    if len(split) > 0:
        drawn = steps_of(stream_key, shape, split, -0.22, 0.18) * drawn
    return jnp.clip(drawn, min=-limit, max=limit).astype(held_as)


def setup_inputs(seed: int = 0) -> dict:
    streams_of = jax.random.split(jax.random.key(seed), 16)
    tokens = gaussian(streams_of[0], (D, TOKENS), 1.0, 6.0, ((0, 4), (1, 8)))
    prefix = draw_prefix(jax.random.fold_in(streams_of[15], 71), 0)
    ln1_gain = jnp.clip(1.0 + 0.1 * jax.random.normal(streams_of[2], (D,), jnp.float32), 0.5, 1.5)
    ln1_bias = gaussian(streams_of[3], (D,), 0.5, 3.0, (), jnp.float32)
    w_qkv = gaussian(streams_of[4], (3, D, D), D ** -0.5, 0.21875, ((1, 4), (2, 4)))
    qv_bias = gaussian(streams_of[5], (2, D), 0.5, 3.0, (), jnp.float32)
    w_out = gaussian(streams_of[6], (D, D), (D // 16) ** -0.5, 0.875, ((0, 4), (1, 4)))
    out_bias = gaussian(streams_of[7], (D,), 0.5, 3.0, (), jnp.float32)
    ln2_gain = jnp.clip(1.0 + 0.1 * jax.random.normal(streams_of[8], (D,), jnp.float32), 0.5, 1.5)
    ln2_bias = gaussian(streams_of[9], (D,), 0.5, 3.0, (), jnp.float32)
    w_fc = gaussian(streams_of[10], (D, FF), D ** -0.5, 0.21875, ((0, 4), (1, 4)))
    fc_bias = gaussian(streams_of[11], (FF,), 0.5, 3.0, (), jnp.float32)
    w_proj = gaussian(streams_of[12], (D, FF), FF ** -0.5, 0.109375, ((0, 4), (1, 4)))
    proj_bias = gaussian(streams_of[13], (D,), 0.5, 3.0, (), jnp.float32)
    cotangent = gaussian(streams_of[14], (D, TOKENS), 1.0, 6.0, ((0, 4), (1, 8)))
    return dict(tokens=tokens, prefix=prefix, ln1_gain=ln1_gain, ln1_bias=ln1_bias, w_qkv=w_qkv, qv_bias=qv_bias, w_out=w_out, out_bias=out_bias, ln2_gain=ln2_gain, ln2_bias=ln2_bias, w_fc=w_fc, fc_bias=fc_bias, w_proj=w_proj, proj_bias=proj_bias, cotangent=cotangent)


@jax.custom_vjp
def low(v):
    return lax.optimization_barrier(v.astype(jnp.bfloat16)).astype(jnp.float32)

@jax.custom_vjp
def low_back(v):
    return v

def low_keep(v):
    return (low(v), None)

def low_pass(kept, grad):
    return (grad,)

def back_keep(v):
    return (v, None)

def back_low(kept, grad):
    return (low(grad),)
low.defvjp(low_keep, low_pass)
low_back.defvjp(back_keep, back_low)
epsilon = 1e-05
highest = lax.Precision.HIGHEST
masked_score = -1e+30

def layer_norm(values, norm_gain, norm_offset):
    center = lax.optimization_barrier(jnp.mean(values, axis=-1, keepdims=True))
    square = lax.optimization_barrier(jnp.mean(values * values, axis=-1, keepdims=True))
    inverse = lax.rsqrt(square - center * center + epsilon)
    return (values - center) * inverse * norm_gain + norm_offset

def attend(packed):
    block_rows, limit_value = packed
    queries = block_rows[:, 0].reshape(LEN, HEADS, HEAD_DIM)
    keys_block = block_rows[:, 1].reshape(LEN, HEADS, HEAD_DIM)
    values_block = block_rows[:, 2].reshape(LEN, HEADS, HEAD_DIM)
    scores = jnp.einsum('qhe,khe->hqk', queries, keys_block, precision=highest) * HEAD_DIM ** (-0.5)
    scores = low_back(scores)
    places = jnp.arange(LEN, dtype=jnp.int32)
    visible = (places[None, :] <= places[:, None]) | (places[None, :] < limit_value)
    scores = jnp.where(visible[None], scores, masked_score)
    largest = lax.optimization_barrier(jnp.max(scores, axis=-1, keepdims=True))
    weights = jnp.exp(scores - largest)
    probs = low(weights / lax.optimization_barrier(jnp.sum(weights, axis=-1, keepdims=True)))
    mixed = jnp.einsum('hqk,khe->qhe', probs, values_block, precision=highest)
    return mixed.reshape(LEN, D)

def block_forward(tokens_block, limits, ln1_gain, ln1_bias, w_qkv, qv_bias, w_out, out_bias, ln2_gain, ln2_bias, w_fc, fc_bias, w_proj, proj_bias):
    first_normed = low(layer_norm(tokens_block, ln1_gain, ln1_bias))
    joined = jnp.einsum('td,sde->tse', first_normed, w_qkv, precision=highest)
    bias_rows = jnp.stack([qv_bias[0], jnp.zeros_like(qv_bias[0]), qv_bias[1]])
    qkv = low(low_back(joined + bias_rows))
    sequences = qkv.reshape(-1, LEN, 3, D)
    mixed = lax.map(jax.checkpoint(attend), (sequences, limits))
    attn = low(low_back(mixed.reshape(-1, D)))
    branch = low_back(jnp.dot(attn, w_out, precision=highest) + out_bias)
    middle = tokens_block + branch
    second_normed = low(layer_norm(middle, ln2_gain, ln2_bias))
    hidden = low_back(jnp.dot(second_normed, w_fc, precision=highest) + fc_bias)
    active = low(jax.nn.gelu(hidden, approximate=True))
    return middle + jnp.einsum('tf,df->td', active, w_proj, precision=highest) + proj_bias

def reference(tokens, prefix, ln1_gain, ln1_bias, w_qkv, qv_bias, w_out, out_bias, ln2_gain, ln2_bias, w_fc, fc_bias, w_proj, proj_bias, cotangent):
    params = tuple((member.astype(jnp.float32) for member in (ln1_gain, ln1_bias, w_qkv, qv_bias, w_out, out_bias, ln2_gain, ln2_bias, w_fc, fc_bias, w_proj, proj_bias)))
    per_step = math.gcd(SEQS, max(1, 4096 // LEN))
    count_steps = SEQS // per_step
    token_groups = tokens.astype(jnp.float32).T.reshape(count_steps, per_step * LEN, D)
    limit_groups = prefix.reshape(count_steps, per_step)
    grad_groups = cotangent.astype(jnp.float32).T.reshape(count_steps, per_step * LEN, D)

    def advance(running, batch_group):
        tokens_block, limits, grad_block = batch_group

        def forward_only(tokens_in, *weights_in):
            return block_forward(tokens_in, limits, *weights_in)
        result, pullback = jax.vjp(forward_only, tokens_block, *params)
        gradients = pullback(grad_block)
        running = tuple((earlier + latest for earlier, latest in zip(running, gradients[1:])))
        return (running, (result.astype(jnp.bfloat16), gradients[0]))
    zeroed = tuple((jnp.zeros_like(member) for member in params))
    totals, (outputs, input_grads) = lax.scan(advance, zeroed, (token_groups, limit_groups, grad_groups))
    return (outputs.reshape(TOKENS, D).T, input_grads.reshape(TOKENS, D).T, totals[0], totals[1], totals[2], totals[3], totals[4], totals[5], totals[6], totals[7], totals[8], totals[9], totals[10], totals[11])
```

```python
import functools

import jax
import jax.numpy as jnp
from jax import lax
from jax.experimental import pallas as pl
from jax.experimental.pallas import tpu as pltpu
from jax.sharding import PartitionSpec as P

D = 768
FF = 3072
HEAD_DIM = 64
LEN = 1024


epsilon = 1e-05
masked_score = -1e30


def feature_totals(values):
    return lax.psum(values, "row")


def column_rows(values):
    return lax.all_gather(values, "col", axis=0, tiled=True)


def row_rows(values):
    return lax.all_gather(values, "row", axis=0, tiled=True)


def summed_over_row(term_fn, row_count):
    return lax.psum_scatter(
        term_fn(jnp.int32(0), row_count * lax.axis_size("row")),
        "row",
        scatter_dimension=0,
        tiled=True,
    )


def summed_over_col(term_fn, row_count):
    return lax.psum_scatter(
        term_fn(jnp.int32(0), row_count * lax.axis_size("col")),
        "col",
        scatter_dimension=0,
        tiled=True,
    )


def take_portion(complete, position, portion_size, along):
    return lax.dynamic_slice_in_dim(complete, position * portion_size, portion_size, along)


def place_portion(portion, position, full_size, along):
    zeroed_shape = portion.shape[:along] + (full_size,) + portion.shape[along + 1 :]
    zeroed = jnp.zeros(zeroed_shape, jnp.float32)
    return lax.dynamic_update_slice_in_dim(zeroed, portion, position * portion.shape[along], along)


def gelu_tanh(values):
    return jax.nn.gelu(values, approximate=True)


def norm_forward(values, norm_gain, norm_offset, totals_fn):
    plain_sum, square_sum = totals_fn((jnp.sum(values, axis=1), jnp.sum(values * values, axis=1)))
    center = (plain_sum / D)[:, None]
    inverse = lax.rsqrt(square_sum[:, None] / D - center * center + epsilon)
    unit_rows = (values - center) * inverse
    return (unit_rows * norm_gain + norm_offset, unit_rows, inverse)


def norm_backward(grad_rows, unit_rows, inverse, norm_gain, totals_fn):
    scaled = grad_rows * norm_gain
    plain_sum, cross_sum = totals_fn((jnp.sum(scaled, axis=1), jnp.sum(scaled * unit_rows, axis=1)))
    return inverse * (scaled - (plain_sum / D)[:, None] - unit_rows * (cross_sum / D)[:, None])


def split_heads(flat_rows):
    return flat_rows.reshape(LEN, flat_rows.shape[1] // HEAD_DIM, HEAD_DIM)


def scores_of(queries, keys_block, limit_value):
    raw_scores = jnp.einsum("qhe,khe->hqk", queries, keys_block, preferred_element_type=jnp.float32)
    raw_scores = raw_scores * HEAD_DIM ** (-0.5)
    places = jnp.arange(LEN, dtype=jnp.int32)
    visible = (places[None, :] <= places[:, None]) | (places[None, :] < limit_value)
    return jnp.where(visible[None], raw_scores, masked_score)


def attend_forward(packed):
    block_rows, limit_value = packed
    queries = split_heads(block_rows[:, 0])
    keys_block = split_heads(block_rows[:, 1])
    values_block = split_heads(block_rows[:, 2])
    scores = scores_of(queries, keys_block, limit_value)
    largest = jnp.max(scores, axis=-1, keepdims=True)
    weights = jnp.exp(scores - largest)
    row_totals = jnp.sum(weights, axis=-1, keepdims=True)
    probs = (weights / row_totals).astype(jnp.bfloat16)
    mixed = jnp.einsum("hqk,khe->qhe", probs, values_block, preferred_element_type=jnp.float32)
    return (mixed.reshape(LEN, -1).astype(jnp.bfloat16), (largest + jnp.log(row_totals))[..., 0])


def attend_backward(packed):
    block_rows, limit_value, log_total, out_grad = packed
    queries = split_heads(block_rows[:, 0])
    keys_block = split_heads(block_rows[:, 1])
    values_block = split_heads(block_rows[:, 2])
    scores = scores_of(queries, keys_block, limit_value)
    probs = jnp.exp(scores - log_total[..., None])
    probs_low = probs.astype(jnp.bfloat16)
    grad_heads = split_heads(out_grad)
    weight_grad = jnp.einsum(
        "qhe,khe->hqk", grad_heads, values_block, preferred_element_type=jnp.float32
    )
    row_inner = jnp.sum(probs * weight_grad, axis=-1, keepdims=True)
    score_grad = (probs * (weight_grad - row_inner)).astype(jnp.bfloat16)
    query_grad = jnp.einsum(
        "hqk,khe->qhe", score_grad, keys_block, preferred_element_type=jnp.float32
    )
    key_grad = jnp.einsum("hqk,qhe->khe", score_grad, queries, preferred_element_type=jnp.float32)
    value_grad = jnp.einsum(
        "hqk,qhe->khe", probs_low, grad_heads, preferred_element_type=jnp.float32
    )
    score_factor = HEAD_DIM ** (-0.5)
    stacked = jnp.stack(
        [
            (query_grad * score_factor).reshape(LEN, -1),
            (key_grad * score_factor).reshape(LEN, -1),
            value_grad.reshape(LEN, -1),
        ],
        axis=1,
    )
    return stacked.astype(jnp.bfloat16)


def general_device(
    tokens,
    prefix,
    ln1_gain,
    ln1_bias,
    w_qkv,
    qv_bias,
    w_out,
    out_bias,
    ln2_gain,
    ln2_bias,
    w_fc,
    fc_bias,
    w_proj,
    proj_bias,
    cotangent,
):
    row_place = lax.axis_index("row")
    col_place = lax.axis_index("col")
    row_devices = lax.axis_size("row")
    col_devices = lax.axis_size("col")
    width_row, local_rows = tokens.shape
    width_col = w_qkv.shape[2]
    hidden_col = w_fc.shape[1]
    seq_rows = local_rows * col_devices // row_devices
    seq_count = seq_rows // LEN
    residual = tokens.T.astype(jnp.float32)
    cotangent_local = cotangent.T
    first_gain = take_portion(ln1_gain, row_place, width_row, 0)
    first_normed, first_unit, first_inverse = norm_forward(
        residual, first_gain, take_portion(ln1_bias, row_place, width_row, 0), feature_totals
    )
    first_gathered = column_rows(first_normed.astype(jnp.bfloat16))

    def qkv_term(first_row, row_count):
        return jnp.einsum("td,sde->tse", first_gathered, w_qkv, preferred_element_type=jnp.float32)

    bias_col = take_portion(qv_bias, col_place, width_col, 1)
    bias_rows = jnp.stack([bias_col[0], jnp.zeros_like(bias_col[0]), bias_col[1]])
    qkv_sum = summed_over_row(qkv_term, seq_rows)
    qkv = (qkv_sum + bias_rows).astype(jnp.bfloat16)
    blocks = qkv.reshape(seq_count, LEN, 3, width_col)
    attn_blocks, log_totals = lax.map(attend_forward, (blocks, prefix))
    attn = attn_blocks.reshape(seq_rows, width_col)
    attn_gathered = row_rows(attn)

    def out_term(first_row, row_count):
        return jnp.dot(attn_gathered, w_out, preferred_element_type=jnp.float32)

    middle = (
        residual
        + summed_over_col(out_term, local_rows)
        + take_portion(out_bias, row_place, width_row, 0)
    )
    grad_output = cotangent_local.astype(jnp.float32)
    second_gain = take_portion(ln2_gain, row_place, width_row, 0)
    second_normed, second_unit, second_inverse = norm_forward(
        middle, second_gain, take_portion(ln2_bias, row_place, width_row, 0), feature_totals
    )
    second_gathered = column_rows(second_normed.astype(jnp.bfloat16))

    def up_term(first_row, row_count):
        return jnp.dot(second_gathered, w_fc, preferred_element_type=jnp.float32)

    hidden = summed_over_row(up_term, seq_rows) + take_portion(fc_bias, col_place, hidden_col, 0)
    active, gelu_pull = jax.vjp(gelu_tanh, hidden)
    active_gathered = row_rows(active.astype(jnp.bfloat16))

    def down_term(first_row, row_count):
        return jnp.einsum("tf,df->td", active_gathered, w_proj, preferred_element_type=jnp.float32)

    final_rows = (
        middle
        + summed_over_col(down_term, local_rows)
        + take_portion(proj_bias, row_place, width_row, 0)
    )
    output = final_rows.astype(jnp.bfloat16)
    grad_gathered = column_rows(cotangent_local)
    w_proj_grad = jnp.einsum(
        "tf,td->df", active_gathered, grad_gathered, preferred_element_type=jnp.float32
    )

    def active_term(first_row, row_count):
        return jnp.einsum("td,df->tf", grad_gathered, w_proj, preferred_element_type=jnp.float32)

    hidden_grad = gelu_pull(summed_over_row(active_term, seq_rows))[0].astype(jnp.bfloat16)
    hidden_gathered = row_rows(hidden_grad)
    w_fc_grad = jnp.einsum(
        "td,tf->df", second_gathered, hidden_gathered, preferred_element_type=jnp.float32
    )

    def second_term(first_row, row_count):
        return jnp.einsum("tf,df->td", hidden_gathered, w_fc, preferred_element_type=jnp.float32)

    second_grad = summed_over_col(second_term, local_rows)
    middle_grad = grad_output + norm_backward(
        second_grad, second_unit, second_inverse, second_gain, feature_totals
    )
    ln2_gain_part = place_portion(jnp.sum(second_grad * second_unit, axis=0), row_place, D, 0)
    ln2_bias_part = place_portion(jnp.sum(second_grad, axis=0), row_place, D, 0)
    fc_bias_part = place_portion(jnp.sum(hidden_grad.astype(jnp.float32), axis=0), col_place, FF, 0)
    proj_bias_part = place_portion(jnp.sum(grad_output, axis=0), row_place, D, 0)
    branch_grad = middle_grad.astype(jnp.bfloat16)
    branch_gathered = column_rows(branch_grad)
    w_out_grad = jnp.einsum(
        "te,td->ed", attn_gathered, branch_gathered, preferred_element_type=jnp.float32
    )

    def attn_term(first_row, row_count):
        return jnp.einsum("td,ed->te", branch_gathered, w_out, preferred_element_type=jnp.float32)

    attn_grad = summed_over_row(attn_term, seq_rows).astype(jnp.bfloat16)
    qkv_grad = lax.map(
        attend_backward, (blocks, prefix, log_totals, attn_grad.reshape(seq_count, LEN, width_col))
    )
    qkv_grad = qkv_grad.reshape(seq_rows, 3, width_col)
    qkv_gathered = row_rows(qkv_grad)
    w_qkv_grad = jnp.einsum(
        "td,tse->sde", first_gathered, qkv_gathered, preferred_element_type=jnp.float32
    )

    def first_term(first_row, row_count):
        return jnp.einsum("tse,sde->td", qkv_gathered, w_qkv, preferred_element_type=jnp.float32)

    first_grad = summed_over_col(first_term, local_rows)
    input_grad = middle_grad + norm_backward(
        first_grad, first_unit, first_inverse, first_gain, feature_totals
    )
    qkv_totals = jnp.sum(qkv_grad.astype(jnp.float32), axis=0)
    qv_part = place_portion(jnp.stack([qkv_totals[0], qkv_totals[2]]), col_place, D, 1)
    out_bias_part = place_portion(jnp.sum(branch_grad.astype(jnp.float32), axis=0), row_place, D, 0)
    ln1_gain_part = place_portion(jnp.sum(first_grad * first_unit, axis=0), row_place, D, 0)
    ln1_bias_part = place_portion(jnp.sum(first_grad, axis=0), row_place, D, 0)
    vectors = lax.psum(
        (
            ln1_gain_part,
            ln1_bias_part,
            qv_part,
            out_bias_part,
            ln2_gain_part,
            ln2_bias_part,
            fc_bias_part,
            proj_bias_part,
        ),
        ("dp", "row", "col"),
    )
    matrices = (
        lax.psum(w_qkv_grad.astype(jnp.bfloat16), "dp").astype(jnp.float32),
        lax.psum(w_out_grad.astype(jnp.bfloat16), "dp").astype(jnp.float32),
        lax.psum(w_fc_grad.astype(jnp.bfloat16), "dp").astype(jnp.float32),
        lax.psum(w_proj_grad.astype(jnp.bfloat16), "dp").astype(jnp.float32),
    )
    return (
        output.T,
        input_grad.T,
        vectors[0],
        vectors[1],
        matrices[0],
        vectors[2],
        matrices[1],
        vectors[3],
        vectors[4],
        vectors[5],
        matrices[2],
        vectors[6],
        matrices[3],
        vectors[7],
    )


MESH = pl.DeviceIdType.MESH
WIDTH = 192
HALF = 96
QUARTER = 256
PACK = 576 + 768 + 768
VMEM_LIMIT = 60 * 1024 * 1024
ANY = pl.BlockSpec(memory_space=pl.ANY)


class Links:
    def __init__(self, send_sems, recv_sems, local_sems):
        self.d, self.r, self.c = (lax.axis_index(n) for n in ("dp", "row", "col"))
        self.send_sems, self.recv_sems, self.local_sems = send_sems, recv_sems, local_sems
        self.remotes = 0
        self.locals = 0

    def across(self, k):
        if k == 1:
            return self.r + 1 - 2 * lax.rem(self.r, 2)
        return lax.rem(self.r + 2, 4) if k == 2 else 3 - self.r

    def plane(self, k):
        return (self.d, self.across(k), self.c)

    def height(self, k):
        return lax.rem(self.c + k, 4)

    def column(self, k):
        return (self.d, self.r, self.height(k))

    def partner(self):
        return (1 - self.d, self.r, self.c)

    def half(self, mine=True):
        place = self.d if mine else 1 - self.d
        return pl.ds(pl.multiple_of(place * HALF, 16), HALF)

    def meet(self, *devices):
        barrier = pltpu.get_barrier_semaphore()
        for device in devices:
            pl.semaphore_signal(barrier, 1, device_id=device, device_id_type=MESH)
        pl.semaphore_wait(barrier, len(devices))

    def send(self, source, target, device):
        place = self.remotes
        self.remotes += 1
        copy = pltpu.make_async_remote_copy(
            src_ref=source,
            dst_ref=target,
            send_sem=self.send_sems.at[place],
            recv_sem=self.recv_sems.at[place],
            device_id=device,
            device_id_type=MESH,
        )
        copy.start()
        return copy

    def local(self, source, target):
        place = self.locals
        self.locals += 1
        copy = pltpu.make_async_copy(source, target, self.local_sems.at[place])
        copy.start()
        return copy


def semaphores(remotes, locals_count):
    return [
        pltpu.SemaphoreType.DMA((remotes,)),
        pltpu.SemaphoreType.DMA((remotes,)),
        pltpu.SemaphoreType.DMA((locals_count,)),
    ]


def remote_call(kernel, collective, out_shapes, scratch, remotes, locals_count, args, cost_bytes=0):
    return pl.pallas_call(
        kernel,
        out_shape=out_shapes,
        in_specs=[ANY] * len(args),
        out_specs=[ANY] * len(out_shapes),
        scratch_shapes=list(scratch) + semaphores(remotes, locals_count),
        compiler_params=pltpu.CompilerParams(
            collective_id=collective, has_side_effects=True, vmem_limit_bytes=VMEM_LIMIT
        ),
        name=f"links_{collective}",
    )(*args)


def shape(dims, dtype=jnp.bfloat16):
    return jax.ShapeDtypeStruct(dims, dtype)


class PlaneGather:
    def __init__(self, links, source, target):
        self.links, self.target = links, target
        rows = source.shape[0] // 2
        self.low, self.high = pl.ds(0, rows), pl.ds(rows, rows)
        place = links.r
        self.x_low = links.send(source.at[self.low], target.at[place, self.low], links.plane(1))
        self.y_high = links.send(source.at[self.high], target.at[place, self.high], links.plane(2))
        self.x_high = links.send(source.at[self.high], target.at[place, self.high], links.plane(1))
        self.y_low = links.send(source.at[self.low], target.at[place, self.low], links.plane(2))

    def relay(self):
        links = self.links
        self.x_low.wait_recv()
        block = self.target.at[links.across(1), self.low]
        self.on_y = links.send(block, block, links.plane(2))
        self.y_high.wait_recv()
        block = self.target.at[links.across(2), self.high]
        self.on_x = links.send(block, block, links.plane(1))

    def finish(self):
        self.x_high.wait_recv()
        self.y_low.wait_recv()
        for copy in (self.x_low, self.y_high, self.x_high, self.y_low):
            copy.wait_send()
        self.on_y.wait()
        self.on_x.wait()


def gather_kernel(
    tok, cot, pre, wq, wf, wp, wo,
    all_tok, all_cot, all_pre, all_q, all_f, all_p, all_o,
    tok_here, cot_here, pre_here, zq, zf, zp, zo,
    send_sems, recv_sems, local_sems,
):
    links = Links(send_sems, recv_sems, local_sems)
    r, c = links.r, links.c
    mine = links.half()
    links.meet(
        links.partner(), *(links.plane(k) for k in (1, 2, 3)), *(links.column(k) for k in (1, 2, 3))
    )
    staged = [
        links.local(tok, tok_here),
        links.local(wq.at[mine], zq.at[c]),
        links.local(pre, pre_here),
        links.local(cot, cot_here),
        links.local(wf.at[mine], zf.at[c]),
        links.local(wp.at[mine], zp.at[c]),
        links.local(wo.at[mine], zo.at[c]),
    ]
    for copy in staged:
        copy.wait()
    kept = [
        links.local(tok_here, all_tok.at[r]),
        links.local(cot_here, all_cot.at[r]),
        links.local(pre_here, all_pre.at[r]),
    ]
    tokens = PlaneGather(links, tok_here, all_tok)

    def up(stage):
        return [links.send(stage.at[c], stage.at[c], links.column(k)) for k in (1, 2, 3)]

    up_q = up(zq)
    prefixes = [links.send(pre_here, all_pre.at[r], links.plane(k)) for k in (1, 2, 3)]
    tokens.relay()
    for copy in up_q:
        copy.wait()
    up_f, up_p, up_o = up(zf), up(zp), up(zo)

    def exchange(stage, target):
        kept.append(links.local(stage.at[r], target.at[r, mine]))
        return [
            links.send(stage.at[links.across(k)], target.at[r, mine], links.plane(k))
            for k in (3, 1, 2)
        ]

    def share(copies, target):
        for copy in copies:
            copy.wait()
        kept[-1].wait()
        kept.pop()
        block = target.at[:, mine]
        return links.send(block, block, links.partner())

    cross_q = exchange(zq, all_q)
    tokens.finish()
    share_q = share(cross_q, all_q)
    grads = PlaneGather(links, cot_here, all_cot)
    for copy in up_f:
        copy.wait()
    cross_f = exchange(zf, all_f)
    grads.relay()
    share_f = share(cross_f, all_f)
    for copy in up_p:
        copy.wait()
    cross_p = exchange(zp, all_p)
    grads.finish()
    share_p = share(cross_p, all_p)
    for copy in up_o:
        copy.wait()
    kept.append(links.local(zo, all_o.at[r, :, mine]))
    cross_o = [links.send(zo, all_o.at[r, :, mine], links.plane(k)) for k in (3, 1, 2)]
    for copy in cross_o:
        copy.wait()
    kept.pop().wait()
    block = all_o.at[:, :, mine]
    share_o = links.send(block, block, links.partner())
    for copy in (share_q, share_f, share_p, share_o, *prefixes, *kept):
        copy.wait()


def gather_inputs(tok, cot, pre, wq, wf, wp, wo):
    return remote_call(
        gather_kernel,
        0,
        [
            shape((4, WIDTH, LEN)),
            shape((4, WIDTH, LEN)),
            shape((4, 8, 128), jnp.int32),
            shape((4, WIDTH, 576)),
            shape((4, WIDTH, 768)),
            shape((4, WIDTH, 768)),
            shape((4, 4, WIDTH, WIDTH)),
        ],
        [
            pltpu.VMEM((WIDTH, LEN), jnp.bfloat16),
            pltpu.VMEM((WIDTH, LEN), jnp.bfloat16),
            pltpu.VMEM((8, 128), jnp.int32),
            pltpu.VMEM((4, HALF, 576), jnp.bfloat16),
            pltpu.VMEM((4, HALF, 768), jnp.bfloat16),
            pltpu.VMEM((4, HALF, 768), jnp.bfloat16),
            pltpu.VMEM((4, HALF, WIDTH), jnp.bfloat16),
        ],
        48,
        16,
        (tok, cot, pre, wq, wf, wp, wo),
    )


def plane_gather_kernel(block, target, here, send_sems, recv_sems, local_sems):
    links = Links(send_sems, recv_sems, local_sems)
    staged = links.local(block, here)
    links.meet(*(links.plane(k) for k in (1, 2, 3)))
    staged.wait()
    kept = links.local(here, target.at[links.r])
    gather = PlaneGather(links, here, target)
    gather.relay()
    gather.finish()
    kept.wait()


def plane_gather(block, collective):
    return remote_call(
        plane_gather_kernel,
        collective,
        [shape((4,) + block.shape)],
        [pltpu.VMEM(block.shape, jnp.bfloat16)],
        6,
        2,
        (block,),
    )[0]


def token_scatter_kernel(parts, received, send_sems, recv_sems, local_sems):
    links = Links(send_sems, recv_sems, local_sems)
    links.meet(*(links.plane(k) for k in (1, 2, 3)))
    copies = [
        links.send(
            parts.at[:, pl.ds(pl.multiple_of(links.across(k) * QUARTER, QUARTER), QUARTER)],
            received.at[k - 1],
            links.plane(k),
        )
        for k in (3, 1, 2)
    ]
    for copy in copies:
        copy.wait()


def token_scatter(parts, collective):
    return remote_call(
        token_scatter_kernel, collective, [shape((3, D, QUARTER))], [], 3, 1, (parts,)
    )[0]


def exchange_kernel(first, second, all_first, all_second, here, send_sems, recv_sems, local_sems):
    links = Links(send_sems, recv_sems, local_sems)
    r = links.r
    staged = [links.local(first.at[r], here.at[0]), links.local(second.at[r], here.at[1])]
    links.meet(*(links.plane(k) for k in (1, 2, 3)))
    copies = [
        links.send(first.at[links.across(k)], all_first.at[r], links.plane(k)) for k in (3, 1, 2)
    ]
    copies += [
        links.send(second.at[links.across(k)], all_second.at[r], links.plane(k)) for k in (3, 1, 2)
    ]
    for copy in staged:
        copy.wait()
    copies += [links.local(here.at[0], all_first.at[r]), links.local(here.at[1], all_second.at[r])]
    for copy in copies:
        copy.wait()


def exchange_heads(first, second, collective):
    return remote_call(
        exchange_kernel,
        collective,
        [shape((4, WIDTH, QUARTER))] * 2,
        [pltpu.VMEM((2, WIDTH, QUARTER), jnp.bfloat16)],
        6,
        4,
        (first, second),
    )


def add_rows(target, terms, rows):
    def step(i, carry):
        place = pl.ds(pl.multiple_of(i * 16, 16), 16)
        total = terms[0][place, :].astype(jnp.float32)
        for term in terms[1:]:
            total = total + term[place, :].astype(jnp.float32)
        target[place, :] = total.astype(target.dtype)
        return carry

    lax.fori_loop(0, rows // 16, step, 0)


def reduce_kernel(
    first_parts, out_parts, packed, square, vector, stats,
    got_first, got_out, all_packed, all_square, all_vector, all_stats,
    own, own_o, near, near_o, sums, sums_o, cross, cross_o, plane_o, high, high_o, final, final_o,
    vec, vec_in, stat, stat_in,
    send_sems, recv_sems, local_sems,
):
    links = Links(send_sems, recv_sems, local_sems)
    r, c = links.r, links.c
    mine, other = links.half(), links.half(False)
    staged = [
        links.local(packed.at[:, mine], own),
        links.local(square.at[:, :, mine], own_o),
        links.local(vector, vec.at[0]),
        links.local(stats, stat),
    ]
    links.meet(
        links.partner(), *(links.plane(k) for k in (1, 2, 3)), *(links.column(k) for k in (1, 2, 3))
    )
    to_near = links.send(packed.at[:, other], near, links.partner())
    to_near_o = links.send(square.at[:, :, other], near_o, links.partner())
    firsts = [
        links.send(first_parts.at[links.across(k)], got_first.at[k - 1], links.plane(k))
        for k in (3, 1, 2)
    ]
    for copy in staged:
        copy.wait()
    stat_sends = [links.send(stat, stat_in.at[k - 1], links.plane(k)) for k in (1, 2, 3)]
    vec_near = links.send(vec.at[0], vec_in.at[0], links.partner())
    to_near.wait()
    for b in range(4):
        add_rows(sums.at[b], [own.at[b], near.at[b]], HALF)
    to_near_o.wait()
    for b in range(4):
        for e in range(4):
            add_rows(sums_o.at[b, e], [own_o.at[b, e], near_o.at[b, e]], HALF)
    for copy in firsts:
        copy.wait()
    crossing = [
        links.send(sums.at[links.across(k)], cross.at[r], links.plane(k)) for k in (3, 1, 2)
    ]
    crossing.append(links.local(sums.at[r], cross.at[r]))
    crossing_o = [
        links.send(sums_o.at[links.across(k)], cross_o.at[k - 1], links.plane(k)) for k in (3, 1, 2)
    ]
    vec_near.wait()
    vec[1] = vec[0] + vec_in[0]
    vec_plane = [links.send(vec.at[1], vec_in.at[k], links.plane(k)) for k in (1, 2, 3)]
    for copy in crossing:
        copy.wait()
    rising = [
        links.send(cross.at[links.height(k)], high.at[k - 1], links.column(k)) for k in (2, 1, 3)
    ]
    outs = [
        links.send(out_parts.at[links.across(k)], got_out.at[k - 1], links.plane(k))
        for k in (3, 1, 2)
    ]
    for copy in crossing_o:
        copy.wait()
    for e in range(4):
        add_rows(
            plane_o.at[e],
            [sums_o.at[r, e], cross_o.at[0, e], cross_o.at[1, e], cross_o.at[2, e]],
            HALF,
        )
    rising_o = [
        links.send(plane_o.at[links.height(k)], high_o.at[k - 1], links.column(k)) for k in (2, 1, 3)
    ]
    for copy in vec_plane:
        copy.wait()
    vec[2] = vec[1] + vec_in[1] + vec_in[2] + vec_in[3]
    vec_high = [links.send(vec.at[2], vec_in.at[3 + k], links.column(k)) for k in (1, 2, 3)]
    for copy in stat_sends:
        copy.wait()
    stat[...] = stat[...] + stat_in[0] + stat_in[1] + stat_in[2]
    for copy in rising:
        copy.wait()
    add_rows(final, [cross.at[c], high.at[0], high.at[1], high.at[2]], HALF)
    last = [
        links.send(final, all_packed.at[mine], links.partner()),
        links.local(final, all_packed.at[mine]),
        links.local(stat, all_stats),
    ]
    for copy in rising_o:
        copy.wait()
    add_rows(final_o, [plane_o.at[c], high_o.at[0], high_o.at[1], high_o.at[2]], HALF)
    last.append(links.send(final_o, all_square.at[mine], links.partner()))
    last.append(links.local(final_o, all_square.at[mine]))
    for copy in vec_high:
        copy.wait()
    vec[3] = vec[2] + vec_in[4] + vec_in[5] + vec_in[6]
    last.append(links.local(vec.at[3], all_vector))
    for copy in outs + last:
        copy.wait()


def reduce_outputs(first_parts, out_parts, packed, square, vector, stats):
    low, wide = jnp.bfloat16, jnp.float32
    return remote_call(
        reduce_kernel,
        5,
        [
            shape((3, WIDTH, LEN)),
            shape((3, WIDTH, LEN)),
            shape((WIDTH, PACK), wide),
            shape((WIDTH, WIDTH), wide),
            shape(vector.shape, wide),
            shape(stats.shape, wide),
        ],
        [
            pltpu.VMEM((4, HALF, PACK), low),
            pltpu.VMEM((4, 4, HALF, WIDTH), low),
            pltpu.VMEM((4, HALF, PACK), low),
            pltpu.VMEM((4, 4, HALF, WIDTH), low),
            pltpu.VMEM((4, HALF, PACK), low),
            pltpu.VMEM((4, 4, HALF, WIDTH), low),
            pltpu.VMEM((4, HALF, PACK), low),
            pltpu.VMEM((3, 4, HALF, WIDTH), low),
            pltpu.VMEM((4, HALF, WIDTH), low),
            pltpu.VMEM((3, HALF, PACK), low),
            pltpu.VMEM((3, HALF, WIDTH), low),
            pltpu.VMEM((HALF, PACK), wide),
            pltpu.VMEM((HALF, WIDTH), wide),
            pltpu.VMEM((4,) + vector.shape, wide),
            pltpu.VMEM((7,) + vector.shape, wide),
            pltpu.VMEM(stats.shape, wide),
            pltpu.VMEM((3,) + stats.shape, wide),
        ],
        48,
        16,
        (first_parts, out_parts, packed, square, vector, stats),
    )


def norm_columns(values, norm_gain, norm_offset):
    center = jnp.mean(values, axis=0, keepdims=True)
    square = jnp.mean(values * values, axis=0, keepdims=True)
    inverse = lax.rsqrt(square - center * center + epsilon)
    unit = (values - center) * inverse
    normed = (unit * norm_gain[:, None] + norm_offset[:, None]).astype(jnp.bfloat16)
    return normed, unit, inverse


def product(pattern, left, right):
    return jnp.einsum(pattern, left, right, preferred_element_type=jnp.float32)


def masked_scores(keys_block, queries, limit_value):
    raw = product("hek,heq->hkq", keys_block, queries) * HEAD_DIM ** (-0.5)
    places = jnp.arange(LEN, dtype=jnp.int32)
    visible = (places[:, None] <= places[None, :]) | (places[:, None] < limit_value)
    return jnp.where(visible[None], raw, masked_score)


def heads_forward(qkv, limit_value):
    queries, keys_block, values_block = qkv.reshape(3, 3, HEAD_DIM, LEN)
    scores = masked_scores(keys_block, queries, limit_value)
    largest = jnp.max(scores, axis=1, keepdims=True)
    weights = jnp.exp(scores - largest)
    totals = jnp.sum(weights, axis=1, keepdims=True)
    probs = (weights / totals).astype(jnp.bfloat16)
    mixed = product("hek,hkq->heq", values_block, probs)
    return mixed.reshape(WIDTH, LEN).astype(jnp.bfloat16), largest + jnp.log(totals)


def heads_backward(qkv, limit_value, log_total, out_grad):
    queries, keys_block, values_block = qkv.reshape(3, 3, HEAD_DIM, LEN)
    grads = out_grad.reshape(3, HEAD_DIM, LEN)
    probs = jnp.exp(masked_scores(keys_block, queries, limit_value) - log_total)
    weight_grad = product("hek,heq->hkq", values_block, grads)
    inner = jnp.sum(probs * weight_grad, axis=1, keepdims=True)
    score_grad = (probs * (weight_grad - inner)).astype(jnp.bfloat16)
    factor = HEAD_DIM ** (-0.5)
    query_grad = product("hek,hkq->heq", keys_block, score_grad) * factor
    key_grad = product("heq,hkq->hek", queries, score_grad) * factor
    value_grad = product("heq,hkq->hek", grads, probs.astype(jnp.bfloat16))
    stacked = jnp.concatenate([query_grad, key_grad, value_grad], axis=0)
    return stacked.reshape(3 * WIDTH, LEN).astype(jnp.bfloat16)


def plane_device(
    tokens, prefix, ln1_gain, ln1_bias, w_qkv, qv_bias, w_out, out_bias,
    ln2_gain, ln2_bias, w_fc, fc_bias, w_proj, proj_bias, cotangent,
):
    r, c = lax.axis_index("row"), lax.axis_index("col")
    low = jnp.bfloat16
    own_q = w_qkv.transpose(1, 0, 2).reshape(WIDTH, 3 * WIDTH)
    all_tok, all_cot, all_pre, all_q, all_f, all_p, all_o = gather_inputs(
        tokens, cotangent, jnp.broadcast_to(prefix[:, None], (8, 128)), own_q, w_fc, w_proj, w_out
    )
    limit_value = lax.dynamic_index_in_dim(all_pre[:, 0, 0], c, 0, keepdims=False)
    grads = all_cot.reshape(D, LEN)
    wq, wf, wp = all_q.reshape(D, 3 * WIDTH), all_f.reshape(D, D), all_p.reshape(D, D)
    wo = all_o.transpose(1, 2, 0, 3).reshape(D, D)
    residual = all_tok.reshape(D, LEN).astype(jnp.float32)
    first_normed, first_unit, first_inverse = norm_columns(residual, ln1_gain, ln1_bias)
    bias = take_portion(qv_bias, r, WIDTH, 1)
    bias = jnp.concatenate([bias[0], jnp.zeros_like(bias[0]), bias[1]])
    qkv = (product("de,dt->et", wq, first_normed) + bias[:, None]).astype(low)
    attn, log_total = heads_forward(qkv, limit_value)
    all_attn = plane_gather(attn, 1).reshape(D, LEN)
    middle = residual + product("ed,et->dt", wo, all_attn) + out_bias[:, None]
    second_normed, second_unit, second_inverse = norm_columns(middle, ln2_gain, ln2_bias)
    hidden = product("df,dt->ft", wf, second_normed) + take_portion(fc_bias, r, D, 0)[:, None]
    active, gelu_pull = jax.vjp(gelu_tanh, hidden)
    active = active.astype(low)
    out_parts = product("df,ft->dt", wp, active).astype(low).reshape(4, WIDTH, LEN)
    hidden_grad = gelu_pull(product("df,dt->ft", wp, grads))[0].astype(low)
    second_parts = product("df,ft->dt", wf, hidden_grad).astype(low)
    w_proj_grad = product("dt,ft->df", grads, active).astype(low)
    w_fc_grad = product("dt,ft->df", second_normed, hidden_grad).astype(low)
    came = token_scatter(second_parts, 2)

    def here(array):
        return take_portion(array, r, QUARTER, 1)

    second_grad = here(second_parts).astype(jnp.float32) + came[0] + came[1] + came[2]
    scaled = second_grad * ln2_gain[:, None]
    unit = here(second_unit)
    plain_mean = jnp.mean(scaled, axis=0, keepdims=True)
    cross_mean = jnp.mean(scaled * unit, axis=0, keepdims=True)
    middle_grad = here(grads).astype(jnp.float32) + here(second_inverse) * (
        scaled - plain_mean - unit * cross_mean
    )
    branch_grad = middle_grad.astype(low)
    attn_parts = product("ed,dt->et", wo, branch_grad).astype(low)
    w_out_grad = product("et,dt->ed", here(all_attn), branch_grad).astype(low)
    attn_grad, branch_rows = exchange_heads(
        attn_parts.reshape(4, WIDTH, QUARTER), branch_grad.reshape(4, WIDTH, QUARTER), 3
    )
    attn_grad = attn_grad.transpose(1, 0, 2).reshape(WIDTH, LEN)
    branch_rows = branch_rows.transpose(1, 0, 2).reshape(WIDTH, LEN).astype(jnp.float32)
    qkv_grad = heads_backward(qkv, limit_value, log_total, attn_grad)
    w_qkv_grad = product("dt,et->de", first_normed, qkv_grad).astype(low)
    first_part = product("de,et->dt", wq, qkv_grad)
    weighted = first_part * first_unit
    stats = jnp.stack(
        [jnp.sum(first_part * ln1_gain[:, None], axis=0), jnp.sum(weighted * ln1_gain[:, None], axis=0)]
    )
    stats = jnp.concatenate([stats, jnp.zeros((6, LEN), jnp.float32)])
    bias_grads = jnp.sum(qkv_grad.astype(jnp.float32), axis=1).reshape(3, WIDTH)
    vector = jnp.concatenate(
        [
            jnp.sum(weighted, axis=1),
            jnp.sum(first_part, axis=1),
            place_portion(bias_grads[0], r, D, 0),
            place_portion(bias_grads[2], r, D, 0),
            jnp.sum(branch_grad.astype(jnp.float32), axis=1),
            jnp.sum(second_grad * unit, axis=1),
            jnp.sum(second_grad, axis=1),
            jnp.sum(here(grads).astype(jnp.float32), axis=1),
            place_portion(jnp.sum(hidden_grad.astype(jnp.float32), axis=1), r, FF, 0),
        ]
    ).reshape(72, 128)
    packed = jnp.concatenate([w_qkv_grad, w_fc_grad, w_proj_grad], axis=1).reshape(4, WIDTH, PACK)
    square = w_out_grad.reshape(4, WIDTH, 4, WIDTH).transpose(2, 0, 1, 3)
    first_parts = first_part.astype(low).reshape(4, WIDTH, LEN)
    got_first, got_out, packed, square, vector, stats = reduce_outputs(
        first_parts, out_parts, packed, square, vector, stats
    )

    def block(array):
        return lax.dynamic_index_in_dim(array, r, 0, keepdims=False).astype(jnp.float32)

    def rows(array):
        return take_portion(array, r, WIDTH, 0)

    output = rows(middle) + rows(proj_bias)[:, None]
    output = output + block(out_parts) + got_out[0] + got_out[1] + got_out[2]
    first_grad = block(first_parts) + got_first[0] + got_first[1] + got_first[2]
    input_grad = branch_rows + first_inverse * (
        first_grad * rows(ln1_gain)[:, None] - stats[0:1] / D - rows(first_unit) * (stats[1:2] / D)
    )
    vector = vector.reshape(72 * 128)
    single = vector[: 8 * D].reshape(8, D)
    w_qkv_total = packed[:, :576].reshape(WIDTH, 3, WIDTH).transpose(1, 0, 2)
    return (
        output.astype(low),
        input_grad,
        single[0],
        single[1],
        w_qkv_total,
        single[2:4],
        square,
        single[4],
        single[5],
        single[6],
        packed[:, 576:1344],
        vector[8 * D :],
        packed[:, 1344:],
        single[7],
    )


def solution(mesh):
    on_device = plane_device if dict(mesh.shape) == {"dp": 2, "row": 4, "col": 4} else general_device
    placed = (
        P("row", ("dp", "col")),
        P(("dp", "row")),
        P(),
        P(),
        P(None, "row", "col"),
        P(),
        P("col", "row"),
        P(),
        P(),
        P(),
        P("row", "col"),
        P(),
        P("row", "col"),
        P(),
        P("row", ("dp", "col")),
    )
    return jax.shard_map(
        on_device,
        mesh=mesh,
        in_specs=placed,
        out_specs=(
            P("row", ("dp", "col")),
            P("row", ("dp", "col")),
            P(),
            P(),
            P(None, "row", "col"),
            P(),
            P("col", "row"),
            P(),
            P(),
            P(),
            P("row", "col"),
            P(),
            P("row", "col"),
            P(),
        ),
        check_vma=False,
    )
```

```python
import functools

import jax
import jax.numpy as jnp
from jax import lax
from jax.experimental import pallas as pl
from jax.experimental.pallas import tpu as pltpu
from jax.sharding import PartitionSpec as P

D = 768
FF = 3072
HEAD_DIM = 64
LEN = 1024


epsilon = 1e-05
masked_score = -1e30


def feature_totals(values):
    return lax.psum(values, "row")


def column_rows(values):
    return lax.all_gather(values, "col", axis=0, tiled=True)


def row_rows(values):
    return lax.all_gather(values, "row", axis=0, tiled=True)


def summed_over_row(term_fn, row_count):
    return lax.psum_scatter(
        term_fn(jnp.int32(0), row_count * lax.axis_size("row")),
        "row",
        scatter_dimension=0,
        tiled=True,
    )


def summed_over_col(term_fn, row_count):
    return lax.psum_scatter(
        term_fn(jnp.int32(0), row_count * lax.axis_size("col")),
        "col",
        scatter_dimension=0,
        tiled=True,
    )


def take_portion(complete, position, portion_size, along):
    return lax.dynamic_slice_in_dim(complete, position * portion_size, portion_size, along)


def place_portion(portion, position, full_size, along):
    zeroed_shape = portion.shape[:along] + (full_size,) + portion.shape[along + 1 :]
    zeroed = jnp.zeros(zeroed_shape, jnp.float32)
    return lax.dynamic_update_slice_in_dim(zeroed, portion, position * portion.shape[along], along)


def gelu_tanh(values):
    return jax.nn.gelu(values, approximate=True)


def norm_forward(values, norm_gain, norm_offset, totals_fn):
    plain_sum, square_sum = totals_fn((jnp.sum(values, axis=1), jnp.sum(values * values, axis=1)))
    center = (plain_sum / D)[:, None]
    inverse = lax.rsqrt(square_sum[:, None] / D - center * center + epsilon)
    unit_rows = (values - center) * inverse
    return (unit_rows * norm_gain + norm_offset, unit_rows, inverse)


def norm_backward(grad_rows, unit_rows, inverse, norm_gain, totals_fn):
    scaled = grad_rows * norm_gain
    plain_sum, cross_sum = totals_fn((jnp.sum(scaled, axis=1), jnp.sum(scaled * unit_rows, axis=1)))
    return inverse * (scaled - (plain_sum / D)[:, None] - unit_rows * (cross_sum / D)[:, None])


def split_heads(flat_rows):
    return flat_rows.reshape(LEN, flat_rows.shape[1] // HEAD_DIM, HEAD_DIM)


def scores_of(queries, keys_block, limit_value):
    raw_scores = jnp.einsum("qhe,khe->hqk", queries, keys_block, preferred_element_type=jnp.float32)
    raw_scores = raw_scores * HEAD_DIM ** (-0.5)
    places = jnp.arange(LEN, dtype=jnp.int32)
    visible = (places[None, :] <= places[:, None]) | (places[None, :] < limit_value)
    return jnp.where(visible[None], raw_scores, masked_score)


def attend_forward(packed):
    block_rows, limit_value = packed
    queries = split_heads(block_rows[:, 0])
    keys_block = split_heads(block_rows[:, 1])
    values_block = split_heads(block_rows[:, 2])
    scores = scores_of(queries, keys_block, limit_value)
    largest = jnp.max(scores, axis=-1, keepdims=True)
    weights = jnp.exp(scores - largest)
    row_totals = jnp.sum(weights, axis=-1, keepdims=True)
    probs = (weights / row_totals).astype(jnp.bfloat16)
    mixed = jnp.einsum("hqk,khe->qhe", probs, values_block, preferred_element_type=jnp.float32)
    return (mixed.reshape(LEN, -1).astype(jnp.bfloat16), (largest + jnp.log(row_totals))[..., 0])


def attend_backward(packed):
    block_rows, limit_value, log_total, out_grad = packed
    queries = split_heads(block_rows[:, 0])
    keys_block = split_heads(block_rows[:, 1])
    values_block = split_heads(block_rows[:, 2])
    scores = scores_of(queries, keys_block, limit_value)
    probs = jnp.exp(scores - log_total[..., None])
    probs_low = probs.astype(jnp.bfloat16)
    grad_heads = split_heads(out_grad)
    weight_grad = jnp.einsum(
        "qhe,khe->hqk", grad_heads, values_block, preferred_element_type=jnp.float32
    )
    row_inner = jnp.sum(probs * weight_grad, axis=-1, keepdims=True)
    score_grad = (probs * (weight_grad - row_inner)).astype(jnp.bfloat16)
    query_grad = jnp.einsum(
        "hqk,khe->qhe", score_grad, keys_block, preferred_element_type=jnp.float32
    )
    key_grad = jnp.einsum("hqk,qhe->khe", score_grad, queries, preferred_element_type=jnp.float32)
    value_grad = jnp.einsum(
        "hqk,qhe->khe", probs_low, grad_heads, preferred_element_type=jnp.float32
    )
    score_factor = HEAD_DIM ** (-0.5)
    stacked = jnp.stack(
        [
            (query_grad * score_factor).reshape(LEN, -1),
            (key_grad * score_factor).reshape(LEN, -1),
            value_grad.reshape(LEN, -1),
        ],
        axis=1,
    )
    return stacked.astype(jnp.bfloat16)


def general_device(
    tokens,
    prefix,
    ln1_gain,
    ln1_bias,
    w_qkv,
    qv_bias,
    w_out,
    out_bias,
    ln2_gain,
    ln2_bias,
    w_fc,
    fc_bias,
    w_proj,
    proj_bias,
    cotangent,
):
    row_place = lax.axis_index("row")
    col_place = lax.axis_index("col")
    row_devices = lax.axis_size("row")
    col_devices = lax.axis_size("col")
    width_row, local_rows = tokens.shape
    width_col = w_qkv.shape[2]
    hidden_col = w_fc.shape[1]
    seq_rows = local_rows * col_devices // row_devices
    seq_count = seq_rows // LEN
    residual = tokens.T.astype(jnp.float32)
    cotangent_local = cotangent.T
    first_gain = take_portion(ln1_gain, row_place, width_row, 0)
    first_normed, first_unit, first_inverse = norm_forward(
        residual, first_gain, take_portion(ln1_bias, row_place, width_row, 0), feature_totals
    )
    first_gathered = column_rows(first_normed.astype(jnp.bfloat16))

    def qkv_term(first_row, row_count):
        return jnp.einsum("td,sde->tse", first_gathered, w_qkv, preferred_element_type=jnp.float32)

    bias_col = take_portion(qv_bias, col_place, width_col, 1)
    bias_rows = jnp.stack([bias_col[0], jnp.zeros_like(bias_col[0]), bias_col[1]])
    qkv_sum = summed_over_row(qkv_term, seq_rows)
    qkv = (qkv_sum + bias_rows).astype(jnp.bfloat16)
    blocks = qkv.reshape(seq_count, LEN, 3, width_col)
    attn_blocks, log_totals = lax.map(attend_forward, (blocks, prefix))
    attn = attn_blocks.reshape(seq_rows, width_col)
    attn_gathered = row_rows(attn)

    def out_term(first_row, row_count):
        return jnp.dot(attn_gathered, w_out, preferred_element_type=jnp.float32)

    middle = (
        residual
        + summed_over_col(out_term, local_rows)
        + take_portion(out_bias, row_place, width_row, 0)
    )
    grad_output = cotangent_local.astype(jnp.float32)
    second_gain = take_portion(ln2_gain, row_place, width_row, 0)
    second_normed, second_unit, second_inverse = norm_forward(
        middle, second_gain, take_portion(ln2_bias, row_place, width_row, 0), feature_totals
    )
    second_gathered = column_rows(second_normed.astype(jnp.bfloat16))

    def up_term(first_row, row_count):
        return jnp.dot(second_gathered, w_fc, preferred_element_type=jnp.float32)

    hidden = summed_over_row(up_term, seq_rows) + take_portion(fc_bias, col_place, hidden_col, 0)
    active, gelu_pull = jax.vjp(gelu_tanh, hidden)
    active_gathered = row_rows(active.astype(jnp.bfloat16))

    def down_term(first_row, row_count):
        return jnp.einsum("tf,df->td", active_gathered, w_proj, preferred_element_type=jnp.float32)

    final_rows = (
        middle
        + summed_over_col(down_term, local_rows)
        + take_portion(proj_bias, row_place, width_row, 0)
    )
    output = final_rows.astype(jnp.bfloat16)
    grad_gathered = column_rows(cotangent_local)
    w_proj_grad = jnp.einsum(
        "tf,td->df", active_gathered, grad_gathered, preferred_element_type=jnp.float32
    )

    def active_term(first_row, row_count):
        return jnp.einsum("td,df->tf", grad_gathered, w_proj, preferred_element_type=jnp.float32)

    hidden_grad = gelu_pull(summed_over_row(active_term, seq_rows))[0].astype(jnp.bfloat16)
    hidden_gathered = row_rows(hidden_grad)
    w_fc_grad = jnp.einsum(
        "td,tf->df", second_gathered, hidden_gathered, preferred_element_type=jnp.float32
    )

    def second_term(first_row, row_count):
        return jnp.einsum("tf,df->td", hidden_gathered, w_fc, preferred_element_type=jnp.float32)

    second_grad = summed_over_col(second_term, local_rows)
    middle_grad = grad_output + norm_backward(
        second_grad, second_unit, second_inverse, second_gain, feature_totals
    )
    ln2_gain_part = place_portion(jnp.sum(second_grad * second_unit, axis=0), row_place, D, 0)
    ln2_bias_part = place_portion(jnp.sum(second_grad, axis=0), row_place, D, 0)
    fc_bias_part = place_portion(jnp.sum(hidden_grad.astype(jnp.float32), axis=0), col_place, FF, 0)
    proj_bias_part = place_portion(jnp.sum(grad_output, axis=0), row_place, D, 0)
    branch_grad = middle_grad.astype(jnp.bfloat16)
    branch_gathered = column_rows(branch_grad)
    w_out_grad = jnp.einsum(
        "te,td->ed", attn_gathered, branch_gathered, preferred_element_type=jnp.float32
    )

    def attn_term(first_row, row_count):
        return jnp.einsum("td,ed->te", branch_gathered, w_out, preferred_element_type=jnp.float32)

    attn_grad = summed_over_row(attn_term, seq_rows).astype(jnp.bfloat16)
    qkv_grad = lax.map(
        attend_backward, (blocks, prefix, log_totals, attn_grad.reshape(seq_count, LEN, width_col))
    )
    qkv_grad = qkv_grad.reshape(seq_rows, 3, width_col)
    qkv_gathered = row_rows(qkv_grad)
    w_qkv_grad = jnp.einsum(
        "td,tse->sde", first_gathered, qkv_gathered, preferred_element_type=jnp.float32
    )

    def first_term(first_row, row_count):
        return jnp.einsum("tse,sde->td", qkv_gathered, w_qkv, preferred_element_type=jnp.float32)

    first_grad = summed_over_col(first_term, local_rows)
    input_grad = middle_grad + norm_backward(
        first_grad, first_unit, first_inverse, first_gain, feature_totals
    )
    qkv_totals = jnp.sum(qkv_grad.astype(jnp.float32), axis=0)
    qv_part = place_portion(jnp.stack([qkv_totals[0], qkv_totals[2]]), col_place, D, 1)
    out_bias_part = place_portion(jnp.sum(branch_grad.astype(jnp.float32), axis=0), row_place, D, 0)
    ln1_gain_part = place_portion(jnp.sum(first_grad * first_unit, axis=0), row_place, D, 0)
    ln1_bias_part = place_portion(jnp.sum(first_grad, axis=0), row_place, D, 0)
    vectors = lax.psum(
        (
            ln1_gain_part,
            ln1_bias_part,
            qv_part,
            out_bias_part,
            ln2_gain_part,
            ln2_bias_part,
            fc_bias_part,
            proj_bias_part,
        ),
        ("dp", "row", "col"),
    )
    matrices = (
        lax.psum(w_qkv_grad.astype(jnp.bfloat16), "dp").astype(jnp.float32),
        lax.psum(w_out_grad.astype(jnp.bfloat16), "dp").astype(jnp.float32),
        lax.psum(w_fc_grad.astype(jnp.bfloat16), "dp").astype(jnp.float32),
        lax.psum(w_proj_grad.astype(jnp.bfloat16), "dp").astype(jnp.float32),
    )
    return (
        output.T,
        input_grad.T,
        vectors[0],
        vectors[1],
        matrices[0],
        vectors[2],
        matrices[1],
        vectors[3],
        vectors[4],
        vectors[5],
        matrices[2],
        vectors[6],
        matrices[3],
        vectors[7],
    )


MESH = pl.DeviceIdType.MESH
WIDTH = 192
HALF = 96
QUARTER = 256
LANES = 128
WQ = 3 * WIDTH
VMEM_LIMIT = 67043328
REMOTES = 112
LOCALS = 40
FACTOR = HEAD_DIM ** (-0.5)
ANY = pl.BlockSpec(memory_space=pl.ANY)
GAIN1, BIAS1, OUT_BIAS, GAIN2, BIAS2, FC_BIAS, QKV_BIAS, PROJ_BIAS = range(8)
V_GAIN1, V_BIAS1, V_QUERY, V_VALUE, V_OUT, V_GAIN2, V_BIAS2, V_PROJ, V_FC = range(9)
CENTER, INVERSE = range(2)


def dot(left, right, left_axis, right_axis):
    return lax.dot_general(
        left, right, (((left_axis,), (right_axis,)), ((), ())), preferred_element_type=jnp.float32
    )


def low(value):
    return value.astype(jnp.bfloat16)


def wide(value):
    return value.astype(jnp.float32)


def aligned(start, size):
    return pl.ds(pl.multiple_of(start, size), size)


def merged(value):
    return value.reshape((value.shape[0] * value.shape[1],) + value.shape[2:])


def each(count, body):
    def step(i, carry):
        body(i)
        return carry

    lax.fori_loop(0, count, step, 0)


class Links:
    def __init__(self, send_sems, recv_sems, local_sems):
        self.d, self.r, self.c = (lax.axis_index(n) for n in ("dp", "row", "col"))
        self.send_sems, self.recv_sems, self.local_sems = send_sems, recv_sems, local_sems
        self.remotes = 0
        self.locals = 0

    def across(self, k):
        if k == 0:
            return self.r
        if k == 1:
            return self.r + 1 - 2 * lax.rem(self.r, 2)
        return lax.rem(self.r + 2, 4) if k == 2 else 3 - self.r

    def plane(self, k):
        return (self.d, self.across(k), self.c)

    def height(self, k):
        return lax.rem(self.c + k, 4)

    def column(self, k):
        return (self.d, self.r, self.height(k))

    def partner(self):
        return (1 - self.d, self.r, self.c)

    def half(self, mine=True):
        place = self.d if mine else 1 - self.d
        return pl.ds(pl.multiple_of(place * HALF, 16), HALF)

    def meet(self, *devices):
        barrier = pltpu.get_barrier_semaphore()
        for device in devices:
            pl.semaphore_signal(barrier, 1, device_id=device, device_id_type=MESH)
        pl.semaphore_wait(barrier, len(devices))

    def send(self, source, target, device):
        place = self.remotes
        self.remotes += 1
        copy = pltpu.make_async_remote_copy(
            src_ref=source,
            dst_ref=target,
            send_sem=self.send_sems.at[place],
            recv_sem=self.recv_sems.at[place],
            device_id=device,
            device_id_type=MESH,
        )
        copy.start()
        return copy

    def local(self, source, target):
        place = self.locals
        self.locals += 1
        copy = pltpu.make_async_copy(source, target, self.local_sems.at[place])
        copy.start()
        return copy


class PlaneGather:
    def __init__(self, links, target):
        self.links, self.target = links, target
        rows = target.shape[1] // 2
        self.low, self.high = pl.ds(0, rows), pl.ds(rows, rows)
        first, second = target.at[links.r, self.low], target.at[links.r, self.high]
        self.x_low = links.send(first, first, links.plane(1))
        self.y_high = links.send(second, second, links.plane(2))
        self.x_high = links.send(second, second, links.plane(1))
        self.y_low = links.send(first, first, links.plane(2))

    def relay(self):
        links = self.links
        self.x_low.wait_recv()
        block = self.target.at[links.across(1), self.low]
        self.on_y = links.send(block, block, links.plane(2))
        self.y_high.wait_recv()
        block = self.target.at[links.across(2), self.high]
        self.on_x = links.send(block, block, links.plane(1))

    def finish(self):
        self.x_high.wait_recv()
        self.y_low.wait_recv()
        for copy in (self.x_low, self.y_high, self.x_high, self.y_low):
            copy.wait_send()
        self.on_y.wait()
        self.on_x.wait()


class WeightGather:
    def __init__(self, links, stage, target):
        self.links, self.stage, self.target = links, stage, target
        block = stage.at[links.c]
        self.rising = [links.send(block, block, links.column(k)) for k in (2, 1, 3)]

    def cross(self):
        links, mine = self.links, self.links.half()
        for copy in self.rising:
            copy.wait()
        self.crossing = [
            links.send(self.stage.at[links.across(k)], self.target.at[links.r, mine], links.plane(k))
            for k in (3, 1, 2)
        ]
        self.crossing.append(links.local(self.stage.at[links.r], self.target.at[links.r, mine]))

    def share(self):
        for copy in self.crossing:
            copy.wait()
        block = self.target.at[:, self.links.half()]
        self.shared = self.links.send(block, block, self.links.partner())

    def finish(self):
        self.shared.wait()


class SquareGather(WeightGather):
    def cross(self):
        links, mine = self.links, self.links.half()
        for copy in self.rising:
            copy.wait()
        block = self.target.at[links.r, :, mine]
        self.crossing = [links.send(self.stage, block, links.plane(k)) for k in (3, 1, 2)]
        self.crossing.append(links.local(self.stage, block))

    def share(self):
        for copy in self.crossing:
            copy.wait()
        block = self.target.at[:, :, self.links.half()]
        self.shared = self.links.send(block, block, self.links.partner())


def add_rows(target, terms):
    def step(i):
        place = aligned(i * 16, 16)
        total = wide(terms[0][place, :])
        for term in terms[1:]:
            total = total + wide(term[place, :])
        target[place, :] = total.astype(target.dtype)

    each(target.shape[0] // 16, step)


class WeightReduce:
    def __init__(self, links, grad, near, sums, cross, high, final, result):
        self.links, self.grad, self.near, self.sums = links, grad, near, sums
        self.crossed, self.high, self.final, self.result = cross, high, final, result
        self.to_near = links.send(grad.at[:, links.half(False)], near, links.partner())

    def cross(self):
        links, mine = self.links, self.links.half()
        self.to_near.wait()
        for b in range(4):
            add_rows(self.sums.at[b], [self.grad.at[b, mine], self.near.at[b]])
        self.crossing = [
            links.send(self.sums.at[links.across(k)], self.crossed.at[links.r], links.plane(k))
            for k in (3, 1, 2)
        ]
        self.crossing.append(links.local(self.sums.at[links.r], self.crossed.at[links.r]))

    def rise(self):
        links = self.links
        for copy in self.crossing:
            copy.wait()
        self.rising = [
            links.send(self.crossed.at[links.height(k)], self.high.at[k - 1], links.column(k))
            for k in (2, 1, 3)
        ]

    def total(self):
        links, mine = self.links, self.links.half()
        for copy in self.rising:
            copy.wait()
        high = self.high
        add_rows(self.final, [self.crossed.at[links.c], high.at[0], high.at[1], high.at[2]])
        self.last = [
            links.send(self.final, self.result.at[mine], links.partner()),
            links.local(self.final, self.result.at[mine]),
        ]

    def finish(self):
        for copy in self.last:
            copy.wait()


class SquareReduce(WeightReduce):
    def __init__(self, links, grad, near, sums, came, cross, high, final, result):
        self.came = came
        self.links, self.grad, self.near, self.sums = links, grad, near, sums
        self.crossed, self.high, self.final, self.result = cross, high, final, result
        self.to_near = links.send(grad.at[:, :, links.half(False)], near, links.partner())

    def cross(self):
        links, mine = self.links, self.links.half()
        self.to_near.wait()

        def add(i):
            b, e = lax.div(i, 4), lax.rem(i, 4)
            add_rows(self.sums.at[b, e], [self.grad.at[b, e, mine], self.near.at[b, e]])

        each(16, add)
        self.crossing = [
            links.send(self.sums.at[links.across(k)], self.came.at[k - 1], links.plane(k))
            for k in (3, 1, 2)
        ]

    def rise(self):
        for copy in self.crossing:
            copy.wait()

        def add(e):
            terms = [self.sums.at[self.links.r, e]] + [self.came.at[k, e] for k in range(3)]
            add_rows(self.crossed.at[e], terms)

        each(4, add)
        self.crossing = []
        WeightReduce.rise(self)


def normalize(source_of, target, stats, gain, offset):
    def step(j):
        lanes = aligned(j * LANES, LANES)
        values = source_of(lanes)
        center = jnp.sum(values, axis=0, keepdims=True) / D
        square = jnp.sum(values * values, axis=0, keepdims=True) / D
        inverse = lax.rsqrt(square - center * center + epsilon)
        stats[CENTER : CENTER + 1, lanes] = center
        stats[INVERSE : INVERSE + 1, lanes] = inverse
        target[:, lanes] = low((values - center) * inverse * gain[...] + offset[...])

    each(LEN // LANES, step)


def key_span(block):
    return max(512, (block + 1) * QUARTER), block * QUARTER


def visible(block, first, last, limit_value):
    shape = (last - first, QUARTER)
    keys = lax.broadcasted_iota(jnp.int32, shape, 0) + first
    queries = lax.broadcasted_iota(jnp.int32, shape, 1) + block * QUARTER
    return (keys <= queries) | (keys < limit_value)


def masked(value, block, limit_value, fill):
    last, first = key_span(block)
    tail = jnp.where(visible(block, first, last, limit_value), value[first:], fill)
    return jnp.concatenate([value[:first], tail], axis=0) if first else tail


def head_rows(h, part):
    return pl.ds(pl.multiple_of(h * HEAD_DIM + part * WIDTH, HEAD_DIM), HEAD_DIM)


def attend(qkv, limit_value, attn_of, log_total):
    def head(h):
        for block in range(4):
            last, _ = key_span(block)
            lanes = slice(block * QUARTER, (block + 1) * QUARTER)
            queries = qkv[head_rows(h, 0), lanes] * jnp.bfloat16(FACTOR)
            scores = dot(qkv[head_rows(h, 1), :last], queries, 0, 0)
            scores = masked(scores, block, limit_value, masked_score)
            largest = jnp.max(scores, axis=0, keepdims=True)
            weights = jnp.exp(scores - largest)
            total = jnp.sum(weights, axis=0, keepdims=True)
            mixed = dot(qkv[head_rows(h, 2), :last], low(weights), 1, 0)
            attn_of(head_rows(h, 0), lanes, low(mixed * (1.0 / total)))
            log_total[pl.ds(h, 1), lanes] = largest + jnp.log(total)

    each(3, head)


def attend_back(qkv, limit_value, attn_of, log_total, out_grad, qkv_grad, key_sum, value_sum):
    def head(h):
        for block in (3, 2, 1, 0):
            last, _ = key_span(block)
            lanes = slice(block * QUARTER, (block + 1) * QUARTER)
            queries = qkv[head_rows(h, 0), lanes] * jnp.bfloat16(FACTOR)
            grads = out_grad[head_rows(h, 0), lanes]
            inner = jnp.sum(
                wide(attn_of(head_rows(h, 0), lanes)) * wide(grads), axis=0, keepdims=True
            )
            scores = dot(qkv[head_rows(h, 1), :last], queries, 0, 0)
            probs = jnp.exp(scores - log_total[pl.ds(h, 1), lanes])
            probs = masked(probs, block, limit_value, 0.0)
            weight_grad = dot(qkv[head_rows(h, 2), :last], grads, 0, 0)
            score_grad = low(probs * (weight_grad - inner))
            query_grad = dot(qkv[head_rows(h, 1), :last], score_grad, 1, 0) * FACTOR
            qkv_grad[head_rows(h, 0), lanes] = low(query_grad)
            key_grad = dot(queries, score_grad, 1, 1)
            value_grad = dot(grads, low(probs), 1, 1)
            if block == 3:
                key_sum[...] = key_grad
                value_sum[...] = value_grad
            else:
                key_sum[:, :last] += key_grad
                value_sum[:, :last] += value_grad
        qkv_grad[head_rows(h, 1), :] = low(key_sum[...])
        qkv_grad[head_rows(h, 2), :] = low(value_sum[...])

    each(3, head)


def gelu_parts(u):
    slope = (2.0 / 3.141592653589793) ** 0.5
    square = u * u
    bent = jnp.tanh(slope * u * (1.0 + 0.044715 * square))
    shared = 0.5 * (1.0 + bent)
    derivative = shared + 0.5 * u * (1.0 - bent * bent) * (slope * (1.0 + 3.0 * 0.044715 * square))
    return u * shared, derivative


def block_kernel(
    tok, cot, pre, wq_in, wf_in, wp_in, wo_in, cols_in,
    out_hbm, grad_hbm, wq_hbm, wf_hbm, wp_hbm, wo_hbm, vec_hbm,
    xt, gt, wqa, wfa, wpa, woa, zq, zf, zp, zo, pres, cols, colb,
    fn, qkv, at, lse, st1, st2, mid, sn, act, slope, op, hg, sp,
    came2, came_out, came1, br, ap, dout, brf, dqkv, ksum, vsum,
    gf, gp, gq, near_f, near_p, near_q, sum_f, sum_p, sum_q, cross_f, cross_p, cross_q,
    high_f, high_p, high_q, fin_f, fin_p, fin_q,
    sq, near_o, sum_o, came_o, cross_o, high_o, fin_o,
    fgp, vcol, vec, vec_in, stat, stat_in, out_v, grad_v,
    send_sems, recv_sems, local_sems,
):
    links = Links(send_sems, recv_sems, local_sems)
    r, c = links.r, links.c
    mine = links.half()
    own = aligned(r * QUARTER, QUARTER)
    staged = [
        links.local(tok, xt.at[r]),
        links.local(wq_in.at[mine], zq.at[c]),
        links.local(pre, pres.at[r]),
        links.local(cols_in, cols),
        links.local(wo_in.at[mine], zo.at[c]),
        links.local(wf_in.at[mine], zf.at[c]),
        links.local(wp_in.at[mine], zp.at[c]),
        links.local(cot, gt.at[r]),
    ]
    links.meet(
        links.partner(), *(links.plane(k) for k in (1, 2, 3)), *(links.column(k) for k in (1, 2, 3))
    )
    for copy in staged:
        copy.wait()

    tokens = PlaneGather(links, xt)
    get_q = WeightGather(links, zq, wqa)
    prefixes = [links.send(pres.at[r], pres.at[r], links.plane(k)) for k in (1, 2, 3)]
    for j in range(7):
        colb[j] = jnp.broadcast_to(cols[:, j : j + 1], (D, LANES))
    tokens.relay()
    get_q.cross()
    get_o = SquareGather(links, zo, woa)
    get_f = WeightGather(links, zf, wfa)
    get_p = WeightGather(links, zp, wpa)
    tokens.finish()
    normalize(
        lambda lanes: wide(merged(xt[:, :, lanes])), fn, st1, colb.at[GAIN1], colb.at[BIAS1]
    )
    get_q.share()
    get_o.cross()
    get_f.cross()
    for copy in prefixes:
        copy.wait()
    get_q.finish()

    def project(b):
        lanes = aligned(b * QUARTER, QUARTER)
        bias = colb[QKV_BIAS, :WQ]
        value = dot(merged(wqa[...]), fn[:, lanes], 0, 0)
        qkv[:, lanes] = low(value + jnp.concatenate([bias, bias], axis=1))

    each(4, project)
    limit_value = pres[c][0:1, 0:1]

    def put_attn(rows, lanes, value):
        at[r, rows, lanes] = value

    def get_attn(rows, lanes):
        return at[r, rows, lanes]

    attend(qkv, limit_value, put_attn, lse)
    attns = PlaneGather(links, at)
    get_o.share()
    get_f.share()
    attns.relay()
    grads = PlaneGather(links, gt)
    get_p.cross()
    get_o.finish()
    attns.finish()

    def join(i):
        b, lanes = lax.div(i, 4), aligned(lax.rem(i, 4) * QUARTER, QUARTER)
        rows = aligned(b * WIDTH, WIDTH)
        bias = colb[OUT_BIAS, rows]
        value = dot(merged(woa[b]), merged(at[:, :, lanes]), 0, 0)
        mid[rows, lanes] = wide(xt[b, :, lanes]) + (value + jnp.concatenate([bias, bias], axis=1))

    each(16, join)
    normalize(lambda lanes: mid[:, lanes], sn, st2, colb.at[GAIN2], colb.at[BIAS2])
    grads.relay()
    get_f.finish()

    def up(b):
        lanes = aligned(b * QUARTER, QUARTER)
        bias = colb[FC_BIAS]
        value = dot(merged(wfa[...]), sn[:, lanes], 0, 0) + jnp.concatenate([bias, bias], axis=1)
        value, derivative = gelu_parts(value)
        act[:, lanes] = low(value)
        slope[:, lanes] = derivative

    each(4, up)
    get_p.share()
    grads.finish()
    get_p.finish()

    returns = []
    for k in (3, 1, 2, 0):
        lanes = aligned(links.across(k) * QUARTER, QUARTER)
        value = dot(merged(wpa[...]), merged(gt[:, :, lanes]), 0, 0)
        hg[:, lanes] = low(value * slope[:, lanes])
        sp[:, lanes] = low(dot(merged(wfa[...]), hg[:, lanes], 1, 0))
        if k:
            returns.append(links.send(sp.at[:, lanes], came2.at[k - 1], links.plane(k)))

    def weight_grads(b):
        gp[b] = low(dot(gt[b], act[...], 1, 1))
        gf[b] = low(dot(sn[aligned(b * WIDTH, WIDTH), :], hg[...], 1, 1))

    each(4, weight_grads)
    put_f = WeightReduce(links, gf, near_f, sum_f, cross_f, high_f, fin_f, wf_hbm)
    put_p = WeightReduce(links, gp, near_p, sum_p, cross_p, high_p, fin_p, wp_hbm)

    def down(b):
        lanes = aligned(b * QUARTER, QUARTER)
        value = low(dot(merged(wpa[...]), act[:, lanes], 1, 0))
        op[:, :, lanes] = value.reshape(4, WIDTH, QUARTER)

    each(4, down)

    lane = lax.broadcasted_iota(jnp.int32, (D, LANES), 1)
    total = jnp.zeros((D, 1), jnp.float32)
    for b in range(4):
        lanes = slice(b * QUARTER, (b + 1) * QUARTER)
        total = total + jnp.sum(wide(hg[:, lanes]), axis=1, keepdims=True)
    vcol[...] = jnp.where(lane == V_FC + r, total, 0.0)
    for copy in returns:
        copy.wait()

    def back(j):
        lanes = aligned(r * QUARTER + j * LANES, LANES)
        part = aligned(j * LANES, LANES)
        given = wide(sp[:, lanes]) + wide(came2[0, :, part])
        given = given + wide(came2[1, :, part]) + wide(came2[2, :, part])
        inverse = st2[INVERSE : INVERSE + 1, lanes]
        unit = (mid[:, lanes] - st2[CENTER : CENTER + 1, lanes]) * inverse
        scaled = given * colb[GAIN2]
        plain = jnp.sum(scaled, axis=0, keepdims=True) / D
        cross = jnp.sum(scaled * unit, axis=0, keepdims=True) / D
        above = wide(merged(gt[:, :, lanes]))
        branch = low(above + inverse * (scaled - plain - unit * cross))
        br[:, :, part] = branch.reshape(4, WIDTH, LANES)
        value = jnp.where(lane == V_GAIN2, jnp.sum(given * unit, axis=1, keepdims=True), 0.0)
        value = jnp.where(lane == V_BIAS2, jnp.sum(given, axis=1, keepdims=True), value)
        value = jnp.where(lane == V_OUT, jnp.sum(wide(branch), axis=1, keepdims=True), value)
        value = jnp.where(lane == V_PROJ, jnp.sum(above, axis=1, keepdims=True), value)
        vcol[...] = vcol[...] + value

    each(2, back)
    value = dot(merged(woa[0]), br[0], 1, 0)
    for b in range(1, 4):
        value = value + dot(merged(woa[b]), br[b], 1, 0)
    ap[...] = low(value).reshape(4, WIDTH, QUARTER)
    turns = [
        links.send(ap.at[links.across(k)], dout.at[:, own], links.plane(k)) for k in (3, 1, 2)
    ]
    turns.append(links.local(ap.at[r], dout.at[:, own]))
    swaps = [
        links.send(br.at[links.across(k)], brf.at[:, own], links.plane(k)) for k in (3, 1, 2)
    ]
    swaps.append(links.local(br.at[r], brf.at[:, own]))

    def square_grads(b):
        value = low(dot(merged(at[:, :, own]), br[b], 1, 1))
        sq[b] = value.reshape(4, WIDTH, WIDTH)

    each(4, square_grads)
    put_o = SquareReduce(links, sq, near_o, sum_o, came_o, cross_o, high_o, fin_o, wo_hbm)
    for copy in turns:
        copy.wait()
    put_f.cross()
    put_p.cross()
    attend_back(qkv, limit_value, get_attn, lse, dout, dqkv, ksum, vsum)

    stat[...] = jnp.zeros_like(stat)
    firsts = []
    for k in (3, 1, 2, 0):
        b = links.across(k)
        rows = aligned(b * WIDTH, WIDTH)

        def first_part(j, b=b, rows=rows):
            lanes = aligned(j * QUARTER, QUARTER)
            value = dot(wqa[b], dqkv[:, lanes], 1, 0)
            fgp[b, :, lanes] = low(value)
            for i in range(2):
                half = aligned(j * QUARTER + i * LANES, LANES)
                piece = value[:, i * LANES : (i + 1) * LANES]
                unit = wide(xt[b, :, half]) - st1[CENTER : CENTER + 1, half]
                unit = unit * st1[INVERSE : INVERSE + 1, half]
                weighted = piece * unit
                gain = colb[GAIN1, rows]
                stat[0:1, half] += jnp.sum(piece * gain, axis=0, keepdims=True)
                stat[1:2, half] += jnp.sum(weighted * gain, axis=0, keepdims=True)
                spot = lane[:WIDTH]
                add = jnp.where(spot == V_GAIN1, jnp.sum(weighted, axis=1, keepdims=True), 0.0)
                add = jnp.where(spot == V_BIAS1, jnp.sum(piece, axis=1, keepdims=True), add)
                vcol[rows, :] = vcol[rows, :] + add

        each(4, first_part)
        if k:
            firsts.append(links.send(fgp.at[b], came1.at[k - 1], links.plane(k)))
    stat_sends = [links.send(stat, stat_in.at[k - 1], links.plane(k)) for k in (1, 2, 3)]

    def query_grads(b):
        gq[b] = low(dot(fn[aligned(b * WIDTH, WIDTH), :], dqkv[...], 1, 1))

    each(4, query_grads)
    put_q = WeightReduce(links, gq, near_q, sum_q, cross_q, high_q, fin_q, wq_hbm)
    put_f.rise()
    put_p.rise()
    rows = aligned(r * WIDTH, WIDTH)
    spot = lane[:WIDTH]
    query = jnp.zeros((WIDTH, 1), jnp.float32)
    value = jnp.zeros((WIDTH, 1), jnp.float32)
    for b in range(4):
        lanes = slice(b * QUARTER, (b + 1) * QUARTER)
        query = query + jnp.sum(wide(dqkv[:WIDTH, lanes]), axis=1, keepdims=True)
        value = value + jnp.sum(wide(dqkv[2 * WIDTH :, lanes]), axis=1, keepdims=True)
    add = jnp.where(spot == V_QUERY, query, jnp.where(spot == V_VALUE, value, 0.0))
    vcol[rows, :] = vcol[rows, :] + add
    vec[0] = vcol[...].T[:16]
    vec_near = links.send(vec.at[0], vec_in.at[0], links.partner())
    put_o.cross()
    put_q.cross()
    outs = [
        links.send(op.at[links.across(k)], came_out.at[k - 1], links.plane(k)) for k in (3, 1, 2)
    ]
    vec_near.wait()
    vec[1] = vec[0] + vec_in[0]
    vec_plane = [links.send(vec.at[1], vec_in.at[k], links.plane(k)) for k in (1, 2, 3)]
    put_o.rise()
    put_q.rise()
    for copy in vec_plane:
        copy.wait()
    vec[2] = vec[1] + vec_in[1] + vec_in[2] + vec_in[3]
    vec_high = [links.send(vec.at[2], vec_in.at[3 + k], links.column(k)) for k in (1, 2, 3)]
    put_f.total()
    put_p.total()
    for copy in swaps + firsts + stat_sends:
        copy.wait()
    stat[...] = stat[...] + stat_in[0] + stat_in[1] + stat_in[2]

    def last_grad(j):
        lanes = aligned(j * LANES, LANES)
        given = wide(fgp[r, :, lanes]) + wide(came1[0, :, lanes])
        given = given + wide(came1[1, :, lanes]) + wide(came1[2, :, lanes])
        inverse = st1[INVERSE : INVERSE + 1, lanes]
        unit = (wide(xt[r, :, lanes]) - st1[CENTER : CENTER + 1, lanes]) * inverse
        value = given * colb[GAIN1, rows] - stat[0:1, lanes] / D - unit * (stat[1:2, lanes] / D)
        grad_v[:, lanes] = wide(brf[:, lanes]) + inverse * value

    each(LEN // LANES, last_grad)
    ends = [links.local(grad_v, grad_hbm)]
    for copy in outs:
        copy.wait()

    def last_out(j):
        lanes = aligned(j * LANES, LANES)
        value = mid[rows, lanes] + cols[rows, PROJ_BIAS : PROJ_BIAS + 1] + wide(op[r, :, lanes])
        for k in range(3):
            value = value + wide(came_out[k, :, lanes])
        out_v[:, lanes] = low(value)

    each(LEN // LANES, last_out)
    ends.append(links.local(out_v, out_hbm))
    for copy in vec_high:
        copy.wait()
    vec[3] = vec[2] + vec_in[4] + vec_in[5] + vec_in[6]
    ends.append(links.local(vec.at[3], vec_hbm))
    put_o.total()
    put_q.total()
    for copy in ends:
        copy.wait()
    for put in (put_f, put_p, put_o, put_q):
        put.finish()


def run_block(*arguments):
    narrow, full = jnp.bfloat16, jnp.float32
    vmem = pltpu.VMEM
    sequence, tall = (4, WIDTH, LEN), (D, LEN)

    def reduce_buffers(kind):
        return [vmem(kind + (HALF, width), narrow) for width in (D, D, WQ)]

    scratch = [
        vmem(sequence, narrow), vmem(sequence, narrow),
        vmem((4, WIDTH, WQ), narrow), vmem((4, WIDTH, D), narrow), vmem((4, WIDTH, D), narrow),
        vmem((4, 4, WIDTH, WIDTH), narrow),
        vmem((4, HALF, WQ), narrow), vmem((4, HALF, D), narrow), vmem((4, HALF, D), narrow),
        vmem((4, HALF, WIDTH), narrow),
        vmem((4, 8, LANES), jnp.int32), vmem((D, 8), full), vmem((7, D, LANES), full),
        vmem(tall, narrow), vmem((WQ, LEN), narrow), vmem(sequence, narrow),
        vmem((8, LEN), full), vmem((8, LEN), full), vmem((8, LEN), full),
        vmem(tall, full), vmem(tall, narrow), vmem(tall, narrow), vmem(tall, full),
        vmem(sequence, narrow), vmem(tall, narrow), vmem(tall, narrow),
        vmem((3, D, QUARTER), narrow), vmem((3, WIDTH, LEN), narrow), vmem((3, WIDTH, LEN), narrow),
        vmem((4, WIDTH, QUARTER), narrow), vmem((4, WIDTH, QUARTER), narrow),
        vmem((WIDTH, LEN), narrow), vmem((WIDTH, LEN), narrow), vmem((WQ, LEN), narrow),
        vmem((HEAD_DIM, LEN), full), vmem((HEAD_DIM, LEN), full),
        vmem((4, WIDTH, D), narrow), vmem((4, WIDTH, D), narrow), vmem((4, WIDTH, WQ), narrow),
        *reduce_buffers((4,)), *reduce_buffers((4,)), *reduce_buffers((4,)), *reduce_buffers((3,)),
        vmem((HALF, D), full), vmem((HALF, D), full), vmem((HALF, WQ), full),
        vmem((4, 4, WIDTH, WIDTH), narrow), vmem((4, 4, HALF, WIDTH), narrow),
        vmem((4, 4, HALF, WIDTH), narrow), vmem((3, 4, HALF, WIDTH), narrow),
        vmem((4, HALF, WIDTH), narrow), vmem((3, HALF, WIDTH), narrow), vmem((HALF, WIDTH), full),
        vmem(sequence, narrow), vmem((D, LANES), full),
        vmem((4, 16, D), full), vmem((7, 16, D), full), vmem((8, LEN), full), vmem((3, 8, LEN), full),
        vmem((WIDTH, LEN), narrow), vmem((WIDTH, LEN), full),
        pltpu.SemaphoreType.DMA((REMOTES,)), pltpu.SemaphoreType.DMA((REMOTES,)),
        pltpu.SemaphoreType.DMA((LOCALS,)),
    ]
    results = [
        ((WIDTH, LEN), narrow), ((WIDTH, LEN), full), ((WIDTH, WQ), full), ((WIDTH, D), full),
        ((WIDTH, D), full), ((WIDTH, WIDTH), full), ((16, D), full),
    ]
    return pl.pallas_call(
        block_kernel,
        out_shape=[jax.ShapeDtypeStruct(*result) for result in results],
        in_specs=[ANY] * len(arguments),
        out_specs=[ANY] * len(results),
        scratch_shapes=scratch,
        compiler_params=pltpu.CompilerParams(
            collective_id=0, has_side_effects=True, vmem_limit_bytes=VMEM_LIMIT
        ),
        name="block",
    )(*arguments)


def plane_device(
    tokens, prefix, ln1_gain, ln1_bias, w_qkv, qv_bias, w_out, out_bias,
    ln2_gain, ln2_bias, w_fc, fc_bias, w_proj, proj_bias, cotangent,
):
    r = lax.axis_index("row")
    bias = take_portion(qv_bias, r, WIDTH, 1)
    nothing = jnp.zeros((WIDTH,), jnp.float32)
    bias = jnp.concatenate([bias[0], nothing, bias[1], nothing])
    columns = jnp.stack(
        [
            ln1_gain, ln1_bias, out_bias, ln2_gain, ln2_bias,
            take_portion(fc_bias, r, D, 0), bias, proj_bias,
        ],
        axis=1,
    )
    output, input_grad, w_qkv_grad, w_fc_grad, w_proj_grad, w_out_grad, vector = run_block(
        tokens,
        cotangent,
        jnp.broadcast_to(prefix[:, None], (8, LANES)),
        w_qkv.transpose(1, 0, 2).reshape(WIDTH, WQ),
        w_fc,
        w_proj,
        w_out,
        columns,
    )
    return (
        output,
        input_grad,
        vector[V_GAIN1],
        vector[V_BIAS1],
        w_qkv_grad.reshape(WIDTH, 3, WIDTH).transpose(1, 0, 2),
        vector[V_QUERY : V_VALUE + 1],
        w_out_grad,
        vector[V_OUT],
        vector[V_GAIN2],
        vector[V_BIAS2],
        w_fc_grad,
        vector[V_FC : V_FC + 4].reshape(FF),
        w_proj_grad,
        vector[V_PROJ],
    )


def solution(mesh):
    on_device = plane_device if dict(mesh.shape) == {"dp": 2, "row": 4, "col": 4} else general_device
    placed = (
        P("row", ("dp", "col")),
        P(("dp", "row")),
        P(),
        P(),
        P(None, "row", "col"),
        P(),
        P("col", "row"),
        P(),
        P(),
        P(),
        P("row", "col"),
        P(),
        P("row", "col"),
        P(),
        P("row", ("dp", "col")),
    )
    return jax.shard_map(
        on_device,
        mesh=mesh,
        in_specs=placed,
        out_specs=(
            P("row", ("dp", "col")),
            P("row", ("dp", "col")),
            P(),
            P(),
            P(None, "row", "col"),
            P(),
            P("col", "row"),
            P(),
            P(),
            P(),
            P("row", "col"),
            P(),
            P("row", "col"),
            P(),
        ),
        check_vma=False,
    )
```

```python
import functools

import jax
import jax.numpy as jnp
from jax import lax
from jax.experimental import pallas as pl
from jax.experimental.pallas import tpu as pltpu
from jax.sharding import PartitionSpec as P

D = 768
FF = 3072
HEAD_DIM = 64
LEN = 1024


epsilon = 1e-05
masked_score = -1e30


def feature_totals(values):
    return lax.psum(values, "row")


def column_rows(values):
    return lax.all_gather(values, "col", axis=0, tiled=True)


def row_rows(values):
    return lax.all_gather(values, "row", axis=0, tiled=True)


def summed_over_row(term_fn, row_count):
    return lax.psum_scatter(
        term_fn(jnp.int32(0), row_count * lax.axis_size("row")),
        "row",
        scatter_dimension=0,
        tiled=True,
    )


def summed_over_col(term_fn, row_count):
    return lax.psum_scatter(
        term_fn(jnp.int32(0), row_count * lax.axis_size("col")),
        "col",
        scatter_dimension=0,
        tiled=True,
    )


def take_portion(complete, position, portion_size, along):
    return lax.dynamic_slice_in_dim(complete, position * portion_size, portion_size, along)


def place_portion(portion, position, full_size, along):
    zeroed_shape = portion.shape[:along] + (full_size,) + portion.shape[along + 1 :]
    zeroed = jnp.zeros(zeroed_shape, jnp.float32)
    return lax.dynamic_update_slice_in_dim(zeroed, portion, position * portion.shape[along], along)


def gelu_tanh(values):
    return jax.nn.gelu(values, approximate=True)


def norm_forward(values, norm_gain, norm_offset, totals_fn):
    plain_sum, square_sum = totals_fn((jnp.sum(values, axis=1), jnp.sum(values * values, axis=1)))
    center = (plain_sum / D)[:, None]
    inverse = lax.rsqrt(square_sum[:, None] / D - center * center + epsilon)
    unit_rows = (values - center) * inverse
    return (unit_rows * norm_gain + norm_offset, unit_rows, inverse)


def norm_backward(grad_rows, unit_rows, inverse, norm_gain, totals_fn):
    scaled = grad_rows * norm_gain
    plain_sum, cross_sum = totals_fn((jnp.sum(scaled, axis=1), jnp.sum(scaled * unit_rows, axis=1)))
    return inverse * (scaled - (plain_sum / D)[:, None] - unit_rows * (cross_sum / D)[:, None])


def split_heads(flat_rows):
    return flat_rows.reshape(LEN, flat_rows.shape[1] // HEAD_DIM, HEAD_DIM)


def scores_of(queries, keys_block, limit_value):
    raw_scores = jnp.einsum("qhe,khe->hqk", queries, keys_block, preferred_element_type=jnp.float32)
    raw_scores = raw_scores * HEAD_DIM ** (-0.5)
    places = jnp.arange(LEN, dtype=jnp.int32)
    visible = (places[None, :] <= places[:, None]) | (places[None, :] < limit_value)
    return jnp.where(visible[None], raw_scores, masked_score)


def attend_forward(packed):
    block_rows, limit_value = packed
    queries = split_heads(block_rows[:, 0])
    keys_block = split_heads(block_rows[:, 1])
    values_block = split_heads(block_rows[:, 2])
    scores = scores_of(queries, keys_block, limit_value)
    largest = jnp.max(scores, axis=-1, keepdims=True)
    weights = jnp.exp(scores - largest)
    row_totals = jnp.sum(weights, axis=-1, keepdims=True)
    probs = (weights / row_totals).astype(jnp.bfloat16)
    mixed = jnp.einsum("hqk,khe->qhe", probs, values_block, preferred_element_type=jnp.float32)
    return (mixed.reshape(LEN, -1).astype(jnp.bfloat16), (largest + jnp.log(row_totals))[..., 0])


def attend_backward(packed):
    block_rows, limit_value, log_total, out_grad = packed
    queries = split_heads(block_rows[:, 0])
    keys_block = split_heads(block_rows[:, 1])
    values_block = split_heads(block_rows[:, 2])
    scores = scores_of(queries, keys_block, limit_value)
    probs = jnp.exp(scores - log_total[..., None])
    probs_low = probs.astype(jnp.bfloat16)
    grad_heads = split_heads(out_grad)
    weight_grad = jnp.einsum(
        "qhe,khe->hqk", grad_heads, values_block, preferred_element_type=jnp.float32
    )
    row_inner = jnp.sum(probs * weight_grad, axis=-1, keepdims=True)
    score_grad = (probs * (weight_grad - row_inner)).astype(jnp.bfloat16)
    query_grad = jnp.einsum(
        "hqk,khe->qhe", score_grad, keys_block, preferred_element_type=jnp.float32
    )
    key_grad = jnp.einsum("hqk,qhe->khe", score_grad, queries, preferred_element_type=jnp.float32)
    value_grad = jnp.einsum(
        "hqk,qhe->khe", probs_low, grad_heads, preferred_element_type=jnp.float32
    )
    score_factor = HEAD_DIM ** (-0.5)
    stacked = jnp.stack(
        [
            (query_grad * score_factor).reshape(LEN, -1),
            (key_grad * score_factor).reshape(LEN, -1),
            value_grad.reshape(LEN, -1),
        ],
        axis=1,
    )
    return stacked.astype(jnp.bfloat16)


def general_device(
    tokens,
    prefix,
    ln1_gain,
    ln1_bias,
    w_qkv,
    qv_bias,
    w_out,
    out_bias,
    ln2_gain,
    ln2_bias,
    w_fc,
    fc_bias,
    w_proj,
    proj_bias,
    cotangent,
):
    row_place = lax.axis_index("row")
    col_place = lax.axis_index("col")
    row_devices = lax.axis_size("row")
    col_devices = lax.axis_size("col")
    width_row, local_rows = tokens.shape
    width_col = w_qkv.shape[2]
    hidden_col = w_fc.shape[1]
    seq_rows = local_rows * col_devices // row_devices
    seq_count = seq_rows // LEN
    residual = tokens.T.astype(jnp.float32)
    cotangent_local = cotangent.T
    first_gain = take_portion(ln1_gain, row_place, width_row, 0)
    first_normed, first_unit, first_inverse = norm_forward(
        residual, first_gain, take_portion(ln1_bias, row_place, width_row, 0), feature_totals
    )
    first_gathered = column_rows(first_normed.astype(jnp.bfloat16))

    def qkv_term(first_row, row_count):
        return jnp.einsum("td,sde->tse", first_gathered, w_qkv, preferred_element_type=jnp.float32)

    bias_col = take_portion(qv_bias, col_place, width_col, 1)
    bias_rows = jnp.stack([bias_col[0], jnp.zeros_like(bias_col[0]), bias_col[1]])
    qkv_sum = summed_over_row(qkv_term, seq_rows)
    qkv = (qkv_sum + bias_rows).astype(jnp.bfloat16)
    blocks = qkv.reshape(seq_count, LEN, 3, width_col)
    attn_blocks, log_totals = lax.map(attend_forward, (blocks, prefix))
    attn = attn_blocks.reshape(seq_rows, width_col)
    attn_gathered = row_rows(attn)

    def out_term(first_row, row_count):
        return jnp.dot(attn_gathered, w_out, preferred_element_type=jnp.float32)

    middle = (
        residual
        + summed_over_col(out_term, local_rows)
        + take_portion(out_bias, row_place, width_row, 0)
    )
    grad_output = cotangent_local.astype(jnp.float32)
    second_gain = take_portion(ln2_gain, row_place, width_row, 0)
    second_normed, second_unit, second_inverse = norm_forward(
        middle, second_gain, take_portion(ln2_bias, row_place, width_row, 0), feature_totals
    )
    second_gathered = column_rows(second_normed.astype(jnp.bfloat16))

    def up_term(first_row, row_count):
        return jnp.dot(second_gathered, w_fc, preferred_element_type=jnp.float32)

    hidden = summed_over_row(up_term, seq_rows) + take_portion(fc_bias, col_place, hidden_col, 0)
    active, gelu_pull = jax.vjp(gelu_tanh, hidden)
    active_gathered = row_rows(active.astype(jnp.bfloat16))

    def down_term(first_row, row_count):
        return jnp.einsum("tf,df->td", active_gathered, w_proj, preferred_element_type=jnp.float32)

    final_rows = (
        middle
        + summed_over_col(down_term, local_rows)
        + take_portion(proj_bias, row_place, width_row, 0)
    )
    output = final_rows.astype(jnp.bfloat16)
    grad_gathered = column_rows(cotangent_local)
    w_proj_grad = jnp.einsum(
        "tf,td->df", active_gathered, grad_gathered, preferred_element_type=jnp.float32
    )

    def active_term(first_row, row_count):
        return jnp.einsum("td,df->tf", grad_gathered, w_proj, preferred_element_type=jnp.float32)

    hidden_grad = gelu_pull(summed_over_row(active_term, seq_rows))[0].astype(jnp.bfloat16)
    hidden_gathered = row_rows(hidden_grad)
    w_fc_grad = jnp.einsum(
        "td,tf->df", second_gathered, hidden_gathered, preferred_element_type=jnp.float32
    )

    def second_term(first_row, row_count):
        return jnp.einsum("tf,df->td", hidden_gathered, w_fc, preferred_element_type=jnp.float32)

    second_grad = summed_over_col(second_term, local_rows)
    middle_grad = grad_output + norm_backward(
        second_grad, second_unit, second_inverse, second_gain, feature_totals
    )
    ln2_gain_part = place_portion(jnp.sum(second_grad * second_unit, axis=0), row_place, D, 0)
    ln2_bias_part = place_portion(jnp.sum(second_grad, axis=0), row_place, D, 0)
    fc_bias_part = place_portion(jnp.sum(hidden_grad.astype(jnp.float32), axis=0), col_place, FF, 0)
    proj_bias_part = place_portion(jnp.sum(grad_output, axis=0), row_place, D, 0)
    branch_grad = middle_grad.astype(jnp.bfloat16)
    branch_gathered = column_rows(branch_grad)
    w_out_grad = jnp.einsum(
        "te,td->ed", attn_gathered, branch_gathered, preferred_element_type=jnp.float32
    )

    def attn_term(first_row, row_count):
        return jnp.einsum("td,ed->te", branch_gathered, w_out, preferred_element_type=jnp.float32)

    attn_grad = summed_over_row(attn_term, seq_rows).astype(jnp.bfloat16)
    qkv_grad = lax.map(
        attend_backward, (blocks, prefix, log_totals, attn_grad.reshape(seq_count, LEN, width_col))
    )
    qkv_grad = qkv_grad.reshape(seq_rows, 3, width_col)
    qkv_gathered = row_rows(qkv_grad)
    w_qkv_grad = jnp.einsum(
        "td,tse->sde", first_gathered, qkv_gathered, preferred_element_type=jnp.float32
    )

    def first_term(first_row, row_count):
        return jnp.einsum("tse,sde->td", qkv_gathered, w_qkv, preferred_element_type=jnp.float32)

    first_grad = summed_over_col(first_term, local_rows)
    input_grad = middle_grad + norm_backward(
        first_grad, first_unit, first_inverse, first_gain, feature_totals
    )
    qkv_totals = jnp.sum(qkv_grad.astype(jnp.float32), axis=0)
    qv_part = place_portion(jnp.stack([qkv_totals[0], qkv_totals[2]]), col_place, D, 1)
    out_bias_part = place_portion(jnp.sum(branch_grad.astype(jnp.float32), axis=0), row_place, D, 0)
    ln1_gain_part = place_portion(jnp.sum(first_grad * first_unit, axis=0), row_place, D, 0)
    ln1_bias_part = place_portion(jnp.sum(first_grad, axis=0), row_place, D, 0)
    vectors = lax.psum(
        (
            ln1_gain_part,
            ln1_bias_part,
            qv_part,
            out_bias_part,
            ln2_gain_part,
            ln2_bias_part,
            fc_bias_part,
            proj_bias_part,
        ),
        ("dp", "row", "col"),
    )
    matrices = (
        lax.psum(w_qkv_grad.astype(jnp.bfloat16), "dp").astype(jnp.float32),
        lax.psum(w_out_grad.astype(jnp.bfloat16), "dp").astype(jnp.float32),
        lax.psum(w_fc_grad.astype(jnp.bfloat16), "dp").astype(jnp.float32),
        lax.psum(w_proj_grad.astype(jnp.bfloat16), "dp").astype(jnp.float32),
    )
    return (
        output.T,
        input_grad.T,
        vectors[0],
        vectors[1],
        matrices[0],
        vectors[2],
        matrices[1],
        vectors[3],
        vectors[4],
        vectors[5],
        matrices[2],
        vectors[6],
        matrices[3],
        vectors[7],
    )


MESH = pl.DeviceIdType.MESH
WIDTH = 192
HALF = 96
QUARTER = 256
LANES = 128
WQ = 3 * WIDTH
VMEM_LIMIT = 67043328
REMOTES = 144
LOCALS = 40
FACTOR = HEAD_DIM ** (-0.5)
ANY = pl.BlockSpec(memory_space=pl.ANY)
GAIN1, BIAS1, OUT_BIAS, GAIN2, BIAS2, FC_BIAS, QKV_BIAS, PROJ_BIAS = range(8)
V_GAIN1, V_BIAS1, V_QUERY, V_VALUE, V_OUT, V_GAIN2, V_BIAS2, V_PROJ, V_FC = range(9)
CENTER, INVERSE = range(2)


def dot(left, right, left_axis, right_axis):
    return lax.dot_general(
        left, right, (((left_axis,), (right_axis,)), ((), ())), preferred_element_type=jnp.float32
    )


def low(value):
    return value.astype(jnp.bfloat16)


def wide(value):
    return value.astype(jnp.float32)


def aligned(start, size):
    return pl.ds(pl.multiple_of(start, size), size)


def merged(value):
    return value.reshape((value.shape[0] * value.shape[1],) + value.shape[2:])


def each(count, body):
    def step(i, carry):
        body(i)
        return carry

    lax.fori_loop(0, count, step, 0)


class Links:
    def __init__(self, send_sems, recv_sems, local_sems):
        self.d, self.r, self.c = (lax.axis_index(n) for n in ("dp", "row", "col"))
        self.send_sems, self.recv_sems, self.local_sems = send_sems, recv_sems, local_sems
        self.remotes = 0
        self.locals = 0

    def across(self, k):
        if k == 0:
            return self.r
        if k == 1:
            return self.r + 1 - 2 * lax.rem(self.r, 2)
        return lax.rem(self.r + 2, 4) if k == 2 else 3 - self.r

    def plane(self, k):
        return (self.d, self.across(k), self.c)

    def height(self, k):
        return lax.rem(self.c + k, 4)

    def column(self, k):
        return (self.d, self.r, self.height(k))

    def partner(self):
        return (1 - self.d, self.r, self.c)

    def half(self, mine=True):
        place = self.d if mine else 1 - self.d
        return pl.ds(pl.multiple_of(place * HALF, 16), HALF)

    def crossing(self, row, place):
        place = place + self.d * (3 - 2 * place)
        low_bit = lax.rem(lax.rem(row, 2) + lax.rem(place, 2), 2)
        return low_bit + 2 * lax.rem(lax.div(row, 2) + lax.div(place, 2), 2)

    def meet(self, *devices):
        barrier = pltpu.get_barrier_semaphore()
        for device in devices:
            pl.semaphore_signal(barrier, 1, device_id=device, device_id_type=MESH)
        pl.semaphore_wait(barrier, len(devices))

    def send(self, source, target, device):
        place = self.remotes
        self.remotes += 1
        copy = pltpu.make_async_remote_copy(
            src_ref=source,
            dst_ref=target,
            send_sem=self.send_sems.at[place],
            recv_sem=self.recv_sems.at[place],
            device_id=device,
            device_id_type=MESH,
        )
        copy.start()
        return copy

    def local(self, source, target):
        place = self.locals
        self.locals += 1
        copy = pltpu.make_async_copy(source, target, self.local_sems.at[place])
        copy.start()
        return copy


class Ticket:
    def __init__(self, links, device):
        self.place = links.remotes
        links.remotes += 1
        self.links, self.device = links, device

    def __call__(self, source, target):
        return pltpu.make_async_remote_copy(
            src_ref=source,
            dst_ref=target,
            send_sem=self.links.send_sems.at[self.place],
            recv_sem=self.links.recv_sems.at[self.place],
            device_id=self.device,
            device_id_type=MESH,
        )


class Move:
    def __init__(self, links, stays, source, target, device):
        self.stays = stays
        self.ticket = Ticket(links, device)
        self.source, self.target = source, target
        place = links.locals
        links.locals += 1
        self.local_sem = links.local_sems.at[place]

        @pl.when(jnp.logical_not(stays))
        def _():
            self.ticket(source, target).start()

        @pl.when(stays)
        def _():
            pltpu.make_async_copy(source, target, self.local_sem).start()

    def wait(self):
        @pl.when(jnp.logical_not(self.stays))
        def _():
            self.ticket(self.source, self.target).wait()

        @pl.when(self.stays)
        def _():
            pltpu.make_async_copy(self.source, self.target, self.local_sem).wait()


class PlaneGather:
    def __init__(self, links, target):
        self.links, self.target = links, target
        rows = target.shape[1] // 2
        self.low, self.high = pl.ds(0, rows), pl.ds(rows, rows)
        first, second = target.at[links.r, self.low], target.at[links.r, self.high]
        self.x_low = links.send(first, first, links.plane(1))
        self.y_high = links.send(second, second, links.plane(2))
        self.x_high = links.send(second, second, links.plane(1))
        self.y_low = links.send(first, first, links.plane(2))

    def relay(self):
        links = self.links
        self.x_low.wait_recv()
        block = self.target.at[links.across(1), self.low]
        self.on_y = links.send(block, block, links.plane(2))
        self.y_high.wait_recv()
        block = self.target.at[links.across(2), self.high]
        self.on_x = links.send(block, block, links.plane(1))

    def finish(self):
        self.x_high.wait_recv()
        self.y_low.wait_recv()
        for copy in (self.x_low, self.y_high, self.x_high, self.y_low):
            copy.wait_send()
        self.on_y.wait()
        self.on_x.wait()


class PlaneReduce:
    def __init__(self, links, part_of, rows, over_x, over_y, relayed):
        self.links, self.part_of = links, part_of
        self.halves = (pl.ds(0, rows // 2), pl.ds(rows // 2, rows // 2))
        self.over_x, self.over_y, self.relayed = over_x, over_y, relayed
        self.copies = {}

    def part(self, k, half):
        return self.part_of(self.links.across(k)).at[self.halves[half]]

    def give(self, k):
        links = self.links
        if k == 3:
            self.copies["x3"] = links.send(self.part(3, 0), self.over_x.at[1], links.plane(1))
            self.copies["y3"] = links.send(self.part(3, 1), self.over_y.at[1], links.plane(2))
        elif k == 1:
            self.copies["x1"] = links.send(self.part(1, 0), self.over_x.at[0], links.plane(1))
        elif k == 2:
            self.copies["y2"] = links.send(self.part(2, 1), self.over_y.at[0], links.plane(2))

    def relay(self):
        links = self.links
        self.copies["x3"].wait_recv()
        add_rows(self.over_x.at[1], [self.over_x.at[1], self.part(2, 0)])
        self.copies["xy"] = links.send(self.over_x.at[1], self.relayed.at[0], links.plane(2))
        self.copies["y3"].wait_recv()
        add_rows(self.over_y.at[1], [self.over_y.at[1], self.part(1, 1)])
        self.copies["yx"] = links.send(self.over_y.at[1], self.relayed.at[1], links.plane(1))

    def finish(self):
        for name in ("x3", "y3"):
            self.copies[name].wait_send()
        for name in ("x1", "y2", "xy", "yx"):
            self.copies[name].wait()

    def total(self, lanes):
        parts = []
        for half, over in ((0, self.over_x), (1, self.over_y)):
            value = wide(self.part(0, half)[:, lanes]) + wide(over[0, :, lanes])
            parts.append(value + wide(self.relayed[half, :, lanes]))
        return jnp.concatenate(parts, axis=0)


class Line:
    def __init__(self, links, block_of):
        self.links, self.block_of = links, block_of
        c = links.c
        self.up = [Ticket(links, (links.d, links.r, lax.rem(c + 1, 4))) for _ in range(3)]
        self.down = [Ticket(links, (links.d, links.r, lax.rem(c + 3, 4))) for _ in range(3)]

    def copy(self, ticket, place):
        return ticket(self.block_of(place), self.block_of(place))

    def step(self, t):
        c = self.links.c
        if t > 0:

            @pl.when(c >= t)
            def _():
                self.copy(self.up[t - 1], c - t).wait_recv()

            @pl.when(c <= 3 - t)
            def _():
                self.copy(self.down[t - 1], c + t).wait_recv()

        if t < 3:

            @pl.when(jnp.logical_and(c >= t, c < 3))
            def _():
                self.copy(self.up[t], c - t).start()

            @pl.when(jnp.logical_and(c <= 3 - t, c > 0))
            def _():
                self.copy(self.down[t], c + t).start()

    def finish(self):
        c = self.links.c
        for t in range(3):

            @pl.when(jnp.logical_and(c >= t, c < 3))
            def _(t=t):
                self.copy(self.up[t], c - t).wait_send()

            @pl.when(jnp.logical_and(c <= 3 - t, c > 0))
            def _(t=t):
                self.copy(self.down[t], c + t).wait_send()


class WeightGather:
    def __init__(self, links, stage, moved, target):
        self.links, self.moved, self.target = links, moved, target
        r, c = links.r, links.c
        self.mine = links.half()
        self.goal = links.crossing(r, c)
        self.turn = Move(links, self.goal == c, stage, moved, (links.d, r, self.goal))

    def hop(self):
        links = self.links
        self.turn.wait()
        block = self.target.at[links.r, self.mine]
        device = (links.d, self.goal, links.c)
        self.turn = Move(links, self.goal == links.r, self.moved, block, device)

    def block_of(self, place):
        return self.target.at[self.links.crossing(self.links.r, place), self.mine]

    def line(self, t):
        if t == 0:
            self.turn.wait()
            self.way = Line(self.links, self.block_of)
        self.way.step(t)

    def share(self):
        self.way.finish()
        block = self.target.at[:, self.mine]
        self.shared = self.links.send(block, block, self.links.partner())

    def finish(self):
        self.shared.wait()


class SquareGather(WeightGather):
    def __init__(self, links, target):
        self.links, self.target = links, target
        self.mine = links.half()
        self.plane = PlaneGather(links, target.at[:, links.c, self.mine])

    def block_of(self, place):
        return self.target.at[:, place, self.mine]

    def line(self, t):
        if t == 0:
            self.plane.finish()
            self.way = Line(self.links, self.block_of)
        self.way.step(t)

    def share(self):
        self.way.finish()
        block = self.target.at[:, :, self.mine]
        self.shared = self.links.send(block, block, self.links.partner())


def add_rows(target, terms):
    def step(i):
        place = aligned(i * 16, 16)
        total = wide(terms[0][place, :])
        for term in terms[1:]:
            total = total + wide(term[place, :])
        target[place, :] = total.astype(target.dtype)

    each(target.shape[0] // 16, step)


def add_blocks(target, terms):
    if len(target.shape) == 2:
        add_rows(target, terms)
    else:
        each(target.shape[0], lambda i: add_blocks(target.at[i], [term.at[i] for term in terms]))


class LineReduce:
    def __init__(self, links, block_of, up, down):
        self.links, self.block_of, self.up, self.down = links, block_of, up, down
        c = links.c
        self.rise = [Ticket(links, (links.d, links.r, lax.rem(c + 1, 4))) for _ in range(3)]
        self.fall = [Ticket(links, (links.d, links.r, lax.rem(c + 3, 4))) for _ in range(3)]

    def step(self, i):
        c = self.links.c
        goal = 3 - i
        slot = self.up.at[goal - 1]
        self.pass_on(self.rise[goal - 1], slot, goal, c == 0, jnp.logical_and(c > 0, c < goal))
        goal = i
        slot = self.down.at[goal]
        self.pass_on(self.fall[goal], slot, goal, c == 3, jnp.logical_and(c < 3, c > goal))

    def pass_on(self, ticket, slot, goal, begins, adds):
        @pl.when(begins)
        def _():
            ticket(self.block_of(goal), slot).start()

        @pl.when(adds)
        def _():
            ticket(slot, slot).wait_recv()
            add_blocks(slot, [slot, self.block_of(goal)])
            ticket(slot, slot).start()

    def total(self, target):
        c = self.links.c
        for goal in range(4):

            @pl.when(c == goal)
            def _(goal=goal):
                terms = [self.block_of(goal)]
                if goal > 0:
                    slot = self.up.at[goal - 1]
                    self.rise[goal - 1](slot, slot).wait_recv()
                    terms.append(slot)
                if goal < 3:
                    slot = self.down.at[goal]
                    self.fall[goal](slot, slot).wait_recv()
                    terms.append(slot)
                add_blocks(target, terms)

        for i in range(3):
            rising, falling = self.up.at[i], self.down.at[i]

            @pl.when(c < i + 1)
            def _(i=i, slot=rising):
                self.rise[i](slot, slot).wait_send()

            @pl.when(c > i)
            def _(i=i, slot=falling):
                self.fall[i](slot, slot).wait_send()


class WeightReduce:
    def __init__(self, links, grad, near, sums, up, down, fin, moved, arrived, result):
        self.links, self.grad, self.near, self.sums = links, grad, near, sums
        self.up, self.down, self.fin = up, down, fin
        self.moved, self.arrived, self.result = moved, arrived, result
        self.to_near = links.send(grad.at[:, links.half(False)], near, links.partner())

    def block_of(self, place):
        return self.sums.at[self.links.crossing(self.links.r, place)]

    def add_near(self):
        mine = self.links.half()
        self.to_near.wait()
        each(4, lambda b: add_rows(self.sums.at[b], [self.grad.at[b, mine], self.near.at[b]]))
        self.way = LineReduce(self.links, self.block_of, self.up, self.down)

    def line(self, i):
        self.way.step(i)

    def hop(self):
        links = self.links
        self.way.total(self.fin)
        self.goal = links.crossing(links.r, links.c)
        device = (links.d, self.goal, links.c)
        self.turn = Move(links, self.goal == links.r, self.fin, self.moved, device)

    def back(self):
        links = self.links
        self.turn.wait()
        device = (links.d, links.r, self.goal)
        self.turn = Move(links, self.goal == links.c, self.moved, self.arrived, device)

    def share(self):
        self.turn.wait()
        self.give(self.arrived)

    def give(self, total):
        links, mine = self.links, self.links.half()
        self.last = [
            links.send(total, self.result.at[mine], links.partner()),
            links.local(total, self.result.at[mine]),
        ]

    def finish(self):
        for copy in self.last:
            copy.wait()


class SquareReduce(WeightReduce):
    def __init__(self, links, grad, near, sums, up, down, fin, came, arrived, result):
        self.links, self.grad, self.near, self.sums = links, grad, near, sums
        self.up, self.down, self.fin = up, down, fin
        self.came, self.arrived, self.result = came, arrived, result
        self.to_near = links.send(grad.at[:, :, links.half(False)], near, links.partner())

    def block_of(self, place):
        return self.sums.at[:, place]

    def add_near(self):
        mine = self.links.half()
        self.to_near.wait()
        add_blocks(self.sums, [self.grad.at[:, :, mine], self.near])
        self.way = LineReduce(self.links, self.block_of, self.up, self.down)

    def hop(self):
        links = self.links
        self.way.total(self.fin)
        self.crossing = [
            links.send(self.fin.at[links.across(k)], self.came.at[k - 1], links.plane(k))
            for k in (3, 1, 2)
        ]

    def back(self):
        for copy in self.crossing:
            copy.wait()
        came = self.came
        add_rows(self.arrived, [self.fin.at[self.links.r], came.at[0], came.at[1], came.at[2]])

    def share(self):
        self.give(self.arrived)


def normalize(source_of, target, stats, gain, offset):
    def step(j):
        lanes = aligned(j * LANES, LANES)
        values = source_of(lanes)
        center = jnp.sum(values, axis=0, keepdims=True) / D
        square = jnp.sum(values * values, axis=0, keepdims=True) / D
        inverse = lax.rsqrt(square - center * center + epsilon)
        stats[CENTER : CENTER + 1, lanes] = center
        stats[INVERSE : INVERSE + 1, lanes] = inverse
        target[:, lanes] = low((values - center) * inverse * gain[...] + offset[...])

    each(LEN // LANES, step)


def key_span(block):
    return max(512, (block + 1) * QUARTER), block * QUARTER


def visible(block, first, last, limit_value):
    shape = (last - first, QUARTER)
    keys = lax.broadcasted_iota(jnp.int32, shape, 0) + first
    queries = lax.broadcasted_iota(jnp.int32, shape, 1) + block * QUARTER
    return (keys <= queries) | (keys < limit_value)


def masked(value, block, limit_value, fill):
    last, first = key_span(block)
    tail = jnp.where(visible(block, first, last, limit_value), value[first:], fill)
    return jnp.concatenate([value[:first], tail], axis=0) if first else tail


def head_rows(h, part):
    return pl.ds(h * HEAD_DIM + part * WIDTH, HEAD_DIM)


def attend(qkv, limit_value, attn_of, log_total, between):
    def head(h):
        between[h]()
        for block in range(4):
            last, _ = key_span(block)
            lanes = slice(block * QUARTER, (block + 1) * QUARTER)
            queries = qkv[head_rows(h, 0), lanes] * jnp.bfloat16(FACTOR)
            scores = dot(qkv[head_rows(h, 1), :last], queries, 0, 0)
            scores = masked(scores, block, limit_value, masked_score)
            largest = jnp.max(scores, axis=0, keepdims=True)
            weights = jnp.exp(scores - largest)
            total = jnp.sum(weights, axis=0, keepdims=True)
            mixed = dot(qkv[head_rows(h, 2), :last], low(weights), 1, 0)
            attn_of(head_rows(h, 0), lanes, low(mixed * (1.0 / total)))
            log_total[pl.ds(h, 1), lanes] = largest + jnp.log(total)

    for h in range(3):
        head(h)


def attend_back(
    qkv, limit_value, attn_of, log_total, out_grad, qkv_grad, key_sum, value_sum, between
):
    def head(h):
        between[h]()
        for block in (3, 2, 1, 0):
            last, _ = key_span(block)
            lanes = slice(block * QUARTER, (block + 1) * QUARTER)
            queries = qkv[head_rows(h, 0), lanes] * jnp.bfloat16(FACTOR)
            grads = out_grad[head_rows(h, 0), lanes]
            inner = jnp.sum(
                wide(attn_of(head_rows(h, 0), lanes)) * wide(grads), axis=0, keepdims=True
            )
            scores = dot(qkv[head_rows(h, 1), :last], queries, 0, 0)
            probs = jnp.exp(scores - log_total[pl.ds(h, 1), lanes])
            probs = masked(probs, block, limit_value, 0.0)
            weight_grad = dot(qkv[head_rows(h, 2), :last], grads, 0, 0)
            score_grad = low(probs * (weight_grad - inner))
            query_grad = dot(qkv[head_rows(h, 1), :last], score_grad, 1, 0) * FACTOR
            qkv_grad[head_rows(h, 0), lanes] = low(query_grad)
            key_grad = dot(queries, score_grad, 1, 1)
            value_grad = dot(grads, low(probs), 1, 1)
            if block == 3:
                key_sum[...] = key_grad
                value_sum[...] = value_grad
            else:
                key_sum[:, :last] += key_grad
                value_sum[:, :last] += value_grad
        qkv_grad[head_rows(h, 1), :] = low(key_sum[...])
        qkv_grad[head_rows(h, 2), :] = low(value_sum[...])

    for h in range(3):
        head(h)


def gelu_parts(u):
    slope = (2.0 / 3.141592653589793) ** 0.5
    square = u * u
    bent = jnp.tanh(slope * u * (1.0 + 0.044715 * square))
    shared = 0.5 * (1.0 + bent)
    derivative = shared + 0.5 * u * (1.0 - bent * bent) * (slope * (1.0 + 3.0 * 0.044715 * square))
    return u * shared, derivative


def in_turn(*actions):
    def run():
        for action in actions:
            action()

    return run


def block_kernel(
    tok, cot, pre, wq_in, wf_in, wp_in, wo_in, cols_in,
    out_hbm, grad_hbm, wq_hbm, wf_hbm, wp_hbm, wo_hbm, vec_hbm,
    xt, gt, wqa, wfa, wpa, woa, zq, zf, zp, mq, mf, mp, pres, cols, colb,
    fn, qkv, at, lse, st1, st2, mid, sn, act, slope, op, hg, sp,
    x2, y2, z2, x_out, y_out, z_out, x1, y1, z1, br, ap, dout, brf, dqkv, ksum, vsum,
    gf, gp, gq, near_f, near_p, near_q, sum_f, sum_p, sum_q, up_f, up_p, up_q, dn_f, dn_p, dn_q,
    fin_f, fin_p, fin_q, hop_f, hop_p, hop_q, got_f, got_p, got_q,
    sq, near_o, sum_o, up_o, dn_o, fin_o, hop_o, got_o,
    fgp, vcol, vec, vec_in, stat, stat_in, out_v, grad_v,
    send_sems, recv_sems, local_sems,
):
    links = Links(send_sems, recv_sems, local_sems)
    r, c = links.r, links.c
    mine = links.half()
    own = aligned(r * QUARTER, QUARTER)
    staged = [
        links.local(tok, xt.at[r]),
        links.local(wq_in.at[mine], zq),
        links.local(pre, pres.at[r]),
        links.local(cols_in, cols),
        links.local(wo_in.at[mine], woa.at[r, c, mine]),
        links.local(wf_in.at[mine], zf),
        links.local(wp_in.at[mine], zp),
        links.local(cot, gt.at[r]),
    ]
    links.meet(
        links.partner(), *(links.plane(k) for k in (1, 2, 3)), *(links.column(k) for k in (1, 2, 3))
    )
    for copy in staged:
        copy.wait()

    get_q = WeightGather(links, zq, mq, wqa)
    tokens = PlaneGather(links, xt)
    prefixes = [links.send(pres.at[r], pres.at[r], links.plane(k)) for k in (1, 2, 3)]
    get_o = SquareGather(links, woa)
    for j in range(7):
        colb[j] = jnp.broadcast_to(cols[:, j : j + 1], (D, LANES))
    get_q.hop()
    get_o.plane.relay()
    get_q.line(0)
    tokens.relay()
    get_q.line(1)
    get_q.line(2)
    get_o.line(0)
    get_q.line(3)
    get_q.share()
    tokens.finish()
    grads = PlaneGather(links, gt)
    normalize(
        lambda lanes: wide(merged(xt[:, :, lanes])), fn, st1, colb.at[GAIN1], colb.at[BIAS1]
    )
    for copy in prefixes:
        copy.wait()
    get_o.line(1)
    get_f = WeightGather(links, zf, mf, wfa)
    get_q.finish()

    def project(b):
        lanes = aligned(b * QUARTER, QUARTER)
        bias = colb[QKV_BIAS, :WQ]
        value = dot(merged(wqa[...]), fn[:, lanes], 0, 0)
        qkv[:, lanes] = low(value + jnp.concatenate([bias, bias], axis=1))

    each(4, project)
    limit_value = pres[c][0:1, 0:1]

    def put_attn(rows, lanes, value):
        at[r, rows, lanes] = value

    def get_attn(rows, lanes):
        return at[r, rows, lanes]

    attend(
        qkv,
        limit_value,
        put_attn,
        lse,
        [
            in_turn(lambda: get_o.line(2), get_f.hop),
            in_turn(lambda: get_o.line(3), lambda: get_f.line(0), grads.relay),
            lambda: get_f.line(1),
        ],
    )
    attns = PlaneGather(links, at)
    get_p = WeightGather(links, zp, mp, wpa)
    get_o.share()
    get_f.line(2)
    get_p.hop()
    get_f.line(3)
    get_f.share()
    get_p.line(0)
    attns.relay()
    get_o.finish()
    grads.finish()
    get_p.line(1)
    attns.finish()

    def join(i):
        b, lanes = lax.div(i, 4), aligned(lax.rem(i, 4) * QUARTER, QUARTER)
        rows = aligned(b * WIDTH, WIDTH)
        bias = colb[OUT_BIAS, rows]
        value = dot(merged(woa[b]), merged(at[:, :, lanes]), 0, 0)
        mid[rows, lanes] = wide(xt[b, :, lanes]) + (value + jnp.concatenate([bias, bias], axis=1))

    each(16, join)
    get_p.line(2)
    normalize(lambda lanes: mid[:, lanes], sn, st2, colb.at[GAIN2], colb.at[BIAS2])
    get_p.line(3)
    get_p.share()
    get_f.finish()

    def up(b):
        lanes = aligned(b * QUARTER, QUARTER)
        bias = colb[FC_BIAS]
        value = dot(merged(wfa[...]), sn[:, lanes], 0, 0) + jnp.concatenate([bias, bias], axis=1)
        value, derivative = gelu_parts(value)
        act[:, lanes] = low(value)
        slope[:, lanes] = derivative

    each(4, up)
    get_p.finish()

    seconds = PlaneReduce(
        links, lambda place: sp.at[:, aligned(place * QUARTER, QUARTER)], D, x2, y2, z2
    )
    for k in (3, 1, 2, 0):
        lanes = aligned(links.across(k) * QUARTER, QUARTER)
        value = dot(merged(wpa[...]), merged(gt[:, :, lanes]), 0, 0)
        hg[:, lanes] = low(value * slope[:, lanes])
        sp[:, lanes] = low(dot(merged(wfa[...]), hg[:, lanes], 1, 0))
        seconds.give(k)

    def proj_grads(b):
        gp[b] = low(dot(gt[b], act[...], 1, 1))

    def fc_grads(b):
        gf[b] = low(dot(sn[aligned(b * WIDTH, WIDTH), :], hg[...], 1, 1))

    each(4, proj_grads)
    put_p = WeightReduce(links, gp, near_p, sum_p, up_p, dn_p, fin_p, hop_p, got_p, wp_hbm)
    seconds.relay()
    each(4, fc_grads)
    put_f = WeightReduce(links, gf, near_f, sum_f, up_f, dn_f, fin_f, hop_f, got_f, wf_hbm)
    put_p.add_near()
    put_p.line(0)

    def down(b):
        lanes = aligned(b * QUARTER, QUARTER)
        value = low(dot(merged(wpa[...]), act[:, lanes], 1, 0))
        op[:, :, lanes] = value.reshape(4, WIDTH, QUARTER)

    each(4, down)
    outs = PlaneReduce(links, lambda place: op.at[place], WIDTH, x_out, y_out, z_out)

    lane = lax.broadcasted_iota(jnp.int32, (D, LANES), 1)
    total = jnp.zeros((D, 1), jnp.float32)
    for b in range(4):
        lanes = slice(b * QUARTER, (b + 1) * QUARTER)
        total = total + jnp.sum(wide(hg[:, lanes]), axis=1, keepdims=True)
    vcol[...] = jnp.where(lane == V_FC + r, total, 0.0)
    put_p.line(1)
    put_f.add_near()
    put_p.line(2)
    put_f.line(0)
    seconds.finish()

    def back(j):
        lanes = aligned(r * QUARTER + j * LANES, LANES)
        part = aligned(j * LANES, LANES)
        given = seconds.total(part)
        inverse = st2[INVERSE : INVERSE + 1, lanes]
        unit = (mid[:, lanes] - st2[CENTER : CENTER + 1, lanes]) * inverse
        scaled = given * colb[GAIN2]
        plain = jnp.sum(scaled, axis=0, keepdims=True) / D
        cross = jnp.sum(scaled * unit, axis=0, keepdims=True) / D
        above = wide(merged(gt[:, :, lanes]))
        branch = low(above + inverse * (scaled - plain - unit * cross))
        br[:, :, part] = branch.reshape(4, WIDTH, LANES)
        value = jnp.where(lane == V_GAIN2, jnp.sum(given * unit, axis=1, keepdims=True), 0.0)
        value = jnp.where(lane == V_BIAS2, jnp.sum(given, axis=1, keepdims=True), value)
        value = jnp.where(lane == V_OUT, jnp.sum(wide(branch), axis=1, keepdims=True), value)
        value = jnp.where(lane == V_PROJ, jnp.sum(above, axis=1, keepdims=True), value)
        vcol[...] = vcol[...] + value

    for j in range(2):
        back(j)
    value = dot(merged(woa[0]), br[0], 1, 0)
    for b in range(1, 4):
        value = value + dot(merged(woa[b]), br[b], 1, 0)
    ap[...] = low(value).reshape(4, WIDTH, QUARTER)
    turns = [
        links.send(ap.at[links.across(k)], dout.at[:, own], links.plane(k)) for k in (3, 1, 2)
    ]
    turns.append(links.local(ap.at[r], dout.at[:, own]))
    swaps = [
        links.send(br.at[links.across(k)], brf.at[:, own], links.plane(k)) for k in (3, 1, 2)
    ]
    swaps.append(links.local(br.at[r], brf.at[:, own]))

    def square_grads(b):
        value = low(dot(merged(at[:, :, own]), br[b], 1, 1))
        sq[b] = value.reshape(4, WIDTH, WIDTH)

    each(4, square_grads)
    put_o = SquareReduce(links, sq, near_o, sum_o, up_o, dn_o, fin_o, hop_o, got_o, wo_hbm)
    put_p.hop()
    put_f.line(1)
    put_f.line(2)
    put_o.add_near()
    for copy in turns:
        copy.wait()
    for k in (3, 1, 2):
        outs.give(k)
    attend_back(
        qkv, limit_value, get_attn, lse, dout, dqkv, ksum, vsum,
        [
            in_turn(put_p.back, lambda: put_o.line(0)),
            in_turn(put_f.hop, lambda: put_o.line(1)),
            in_turn(outs.relay, put_p.share, lambda: put_o.line(2)),
        ],
    )

    def query_grads(b):
        gq[b] = low(dot(fn[aligned(b * WIDTH, WIDTH), :], dqkv[...], 1, 1))

    each(4, query_grads)
    put_q = WeightReduce(links, gq, near_q, sum_q, up_q, dn_q, fin_q, hop_q, got_q, wq_hbm)

    stat[...] = jnp.zeros_like(stat)
    firsts = PlaneReduce(links, lambda place: fgp.at[place], WIDTH, x1, y1, z1)
    for k in (3, 1, 2, 0):
        b = links.across(k)
        rows = aligned(b * WIDTH, WIDTH)

        def first_part(j, b=b, rows=rows):
            lanes = aligned(j * QUARTER, QUARTER)
            value = dot(wqa[b], dqkv[:, lanes], 1, 0)
            fgp[b, :, lanes] = low(value)
            for i in range(2):
                half = aligned(j * QUARTER + i * LANES, LANES)
                piece = value[:, i * LANES : (i + 1) * LANES]
                unit = wide(xt[b, :, half]) - st1[CENTER : CENTER + 1, half]
                unit = unit * st1[INVERSE : INVERSE + 1, half]
                weighted = piece * unit
                gain = colb[GAIN1, rows]
                stat[0:1, half] += jnp.sum(piece * gain, axis=0, keepdims=True)
                stat[1:2, half] += jnp.sum(weighted * gain, axis=0, keepdims=True)
                spot = lane[:WIDTH]
                add = jnp.where(spot == V_GAIN1, jnp.sum(weighted, axis=1, keepdims=True), 0.0)
                add = jnp.where(spot == V_BIAS1, jnp.sum(piece, axis=1, keepdims=True), add)
                vcol[rows, :] = vcol[rows, :] + add

        each(4, first_part)
        firsts.give(k)
        if k == 3:
            put_q.add_near()
            put_q.line(0)
        elif k == 2:
            put_q.line(1)
    stat_sends = [links.send(stat, stat_in.at[k - 1], links.plane(k)) for k in (1, 2, 3)]
    put_q.line(2)
    firsts.relay()
    put_f.back()
    put_o.hop()
    rows = aligned(r * WIDTH, WIDTH)
    spot = lane[:WIDTH]
    query = jnp.zeros((WIDTH, 1), jnp.float32)
    value = jnp.zeros((WIDTH, 1), jnp.float32)
    for b in range(4):
        lanes = slice(b * QUARTER, (b + 1) * QUARTER)
        query = query + jnp.sum(wide(dqkv[:WIDTH, lanes]), axis=1, keepdims=True)
        value = value + jnp.sum(wide(dqkv[2 * WIDTH :, lanes]), axis=1, keepdims=True)
    add = jnp.where(spot == V_QUERY, query, jnp.where(spot == V_VALUE, value, 0.0))
    vcol[rows, :] = vcol[rows, :] + add
    vec[0] = vcol[...].T[:16]
    vec_near = links.send(vec.at[0], vec_in.at[0], links.partner())
    put_q.hop()
    vec_near.wait()
    vec[1] = vec[0] + vec_in[0]
    vec_plane = [links.send(vec.at[1], vec_in.at[k], links.plane(k)) for k in (1, 2, 3)]
    put_f.share()
    put_o.back()
    put_q.back()
    put_o.share()
    for copy in vec_plane:
        copy.wait()
    vec[2] = vec[1] + vec_in[1] + vec_in[2] + vec_in[3]
    vec_high = [links.send(vec.at[2], vec_in.at[3 + k], links.column(k)) for k in (1, 2, 3)]
    outs.finish()

    def last_out(j):
        lanes = aligned(j * LANES, LANES)
        value = mid[rows, lanes] + cols[rows, PROJ_BIAS : PROJ_BIAS + 1] + outs.total(lanes)
        out_v[:, lanes] = low(value)

    each(LEN // LANES, last_out)
    ends = [links.local(out_v, out_hbm)]
    for copy in swaps + stat_sends:
        copy.wait()
    firsts.finish()
    stat[...] = stat[...] + stat_in[0] + stat_in[1] + stat_in[2]

    def last_grad(j):
        lanes = aligned(j * LANES, LANES)
        inverse = st1[INVERSE : INVERSE + 1, lanes]
        unit = (wide(xt[r, :, lanes]) - st1[CENTER : CENTER + 1, lanes]) * inverse
        value = firsts.total(lanes) * colb[GAIN1, rows] - stat[0:1, lanes] / D
        grad_v[:, lanes] = wide(brf[:, lanes]) + inverse * (value - unit * (stat[1:2, lanes] / D))

    each(LEN // LANES, last_grad)
    ends.append(links.local(grad_v, grad_hbm))
    put_q.share()
    for copy in vec_high:
        copy.wait()
    vec[3] = vec[2] + vec_in[4] + vec_in[5] + vec_in[6]
    ends.append(links.local(vec.at[3], vec_hbm))
    for copy in ends:
        copy.wait()
    for put in (put_f, put_p, put_o, put_q):
        put.finish()


def run_block(*arguments):
    narrow, full = jnp.bfloat16, jnp.float32
    vmem = pltpu.VMEM
    sequence, tall = (4, WIDTH, LEN), (D, LEN)

    def thirds(lead=()):
        return [vmem(lead + (HALF, width), narrow) for width in (D, D, WQ)]

    def plane_sums(rows, lanes):
        return [vmem((2, rows // 2, lanes), narrow) for _ in range(3)]

    scratch = [
        vmem(sequence, narrow), vmem(sequence, narrow),
        vmem((4, WIDTH, WQ), narrow), vmem((4, WIDTH, D), narrow), vmem((4, WIDTH, D), narrow),
        vmem((4, 4, WIDTH, WIDTH), narrow),
        vmem((HALF, WQ), narrow), vmem((HALF, D), narrow), vmem((HALF, D), narrow),
        vmem((HALF, WQ), narrow), vmem((HALF, D), narrow), vmem((HALF, D), narrow),
        vmem((4, 8, LANES), jnp.int32), vmem((D, 8), full), vmem((7, D, LANES), full),
        vmem(tall, narrow), vmem((WQ, LEN), narrow), vmem(sequence, narrow),
        vmem((8, LEN), full), vmem((8, LEN), full), vmem((8, LEN), full),
        vmem(tall, full), vmem(tall, narrow), vmem(tall, narrow), vmem(tall, full),
        vmem(sequence, narrow), vmem(tall, narrow), vmem(tall, narrow),
        *plane_sums(D, QUARTER), *plane_sums(WIDTH, LEN), *plane_sums(WIDTH, LEN),
        vmem((4, WIDTH, QUARTER), narrow), vmem((4, WIDTH, QUARTER), narrow),
        vmem((WIDTH, LEN), narrow), vmem((WIDTH, LEN), narrow), vmem((WQ, LEN), narrow),
        vmem((HEAD_DIM, LEN), full), vmem((HEAD_DIM, LEN), full),
        vmem((4, WIDTH, D), narrow), vmem((4, WIDTH, D), narrow), vmem((4, WIDTH, WQ), narrow),
        *thirds((4,)), *thirds((4,)), *thirds((3,)), *thirds((3,)), *thirds(), *thirds(), *thirds(),
        vmem((4, 4, WIDTH, WIDTH), narrow), vmem((4, 4, HALF, WIDTH), narrow),
        vmem((4, 4, HALF, WIDTH), narrow), vmem((3, 4, HALF, WIDTH), narrow),
        vmem((3, 4, HALF, WIDTH), narrow), vmem((4, HALF, WIDTH), narrow),
        vmem((3, HALF, WIDTH), narrow), vmem((HALF, WIDTH), narrow),
        vmem(sequence, narrow), vmem((D, LANES), full),
        vmem((4, 16, D), full), vmem((7, 16, D), full), vmem((8, LEN), full), vmem((3, 8, LEN), full),
        vmem((WIDTH, LEN), narrow), vmem((WIDTH, LEN), full),
        pltpu.SemaphoreType.DMA((REMOTES,)), pltpu.SemaphoreType.DMA((REMOTES,)),
        pltpu.SemaphoreType.DMA((LOCALS,)),
    ]
    results = [
        ((WIDTH, LEN), narrow), ((WIDTH, LEN), full), ((WIDTH, WQ), narrow), ((WIDTH, D), narrow),
        ((WIDTH, D), narrow), ((WIDTH, WIDTH), narrow), ((16, D), full),
    ]
    return pl.pallas_call(
        block_kernel,
        out_shape=[jax.ShapeDtypeStruct(*result) for result in results],
        in_specs=[ANY] * len(arguments),
        out_specs=[ANY] * len(results),
        scratch_shapes=scratch,
        compiler_params=pltpu.CompilerParams(
            collective_id=0, has_side_effects=True, vmem_limit_bytes=VMEM_LIMIT
        ),
        name="block",
    )(*arguments)


def plane_device(
    tokens, prefix, ln1_gain, ln1_bias, w_qkv, qv_bias, w_out, out_bias,
    ln2_gain, ln2_bias, w_fc, fc_bias, w_proj, proj_bias, cotangent,
):
    r = lax.axis_index("row")
    bias = take_portion(qv_bias, r, WIDTH, 1)
    nothing = jnp.zeros((WIDTH,), jnp.float32)
    bias = jnp.concatenate([bias[0], nothing, bias[1], nothing])
    columns = jnp.stack(
        [
            ln1_gain, ln1_bias, out_bias, ln2_gain, ln2_bias,
            take_portion(fc_bias, r, D, 0), bias, proj_bias,
        ],
        axis=1,
    )
    output, input_grad, w_qkv_grad, w_fc_grad, w_proj_grad, w_out_grad, vector = run_block(
        tokens,
        cotangent,
        jnp.broadcast_to(prefix[:, None], (8, LANES)),
        w_qkv.transpose(1, 0, 2).reshape(WIDTH, WQ),
        w_fc,
        w_proj,
        w_out,
        columns,
    )
    return (
        output,
        input_grad,
        vector[V_GAIN1],
        vector[V_BIAS1],
        wide(w_qkv_grad.reshape(WIDTH, 3, WIDTH).transpose(1, 0, 2)),
        vector[V_QUERY : V_VALUE + 1],
        wide(w_out_grad),
        vector[V_OUT],
        vector[V_GAIN2],
        vector[V_BIAS2],
        wide(w_fc_grad),
        vector[V_FC : V_FC + 4].reshape(FF),
        wide(w_proj_grad),
        vector[V_PROJ],
    )


def solution(mesh):
    on_device = plane_device if dict(mesh.shape) == {"dp": 2, "row": 4, "col": 4} else general_device
    placed = (
        P("row", ("dp", "col")),
        P(("dp", "row")),
        P(),
        P(),
        P(None, "row", "col"),
        P(),
        P("col", "row"),
        P(),
        P(),
        P(),
        P("row", "col"),
        P(),
        P("row", "col"),
        P(),
        P("row", ("dp", "col")),
    )
    return jax.shard_map(
        on_device,
        mesh=mesh,
        in_specs=placed,
        out_specs=(
            P("row", ("dp", "col")),
            P("row", ("dp", "col")),
            P(),
            P(),
            P(None, "row", "col"),
            P(),
            P("col", "row"),
            P(),
            P(),
            P(),
            P("row", "col"),
            P(),
            P("row", "col"),
            P(),
        ),
        check_vma=False,
    )
```

```python
import functools

import jax
import jax.numpy as jnp
from jax import lax
from jax.experimental import pallas as pl
from jax.experimental.pallas import tpu as pltpu
from jax.sharding import PartitionSpec as P

D = 768
FF = 3072
HEAD_DIM = 64
LEN = 1024


epsilon = 1e-05
masked_score = -1e30


def feature_totals(values):
    return lax.psum(values, "row")


def column_rows(values):
    return lax.all_gather(values, "col", axis=0, tiled=True)


def row_rows(values):
    return lax.all_gather(values, "row", axis=0, tiled=True)


def summed_over_row(term_fn, row_count):
    return lax.psum_scatter(
        term_fn(jnp.int32(0), row_count * lax.axis_size("row")),
        "row",
        scatter_dimension=0,
        tiled=True,
    )


def summed_over_col(term_fn, row_count):
    return lax.psum_scatter(
        term_fn(jnp.int32(0), row_count * lax.axis_size("col")),
        "col",
        scatter_dimension=0,
        tiled=True,
    )


def take_portion(complete, position, portion_size, along):
    return lax.dynamic_slice_in_dim(complete, position * portion_size, portion_size, along)


def place_portion(portion, position, full_size, along):
    zeroed_shape = portion.shape[:along] + (full_size,) + portion.shape[along + 1 :]
    zeroed = jnp.zeros(zeroed_shape, jnp.float32)
    return lax.dynamic_update_slice_in_dim(zeroed, portion, position * portion.shape[along], along)


def gelu_tanh(values):
    return jax.nn.gelu(values, approximate=True)


def norm_forward(values, norm_gain, norm_offset, totals_fn):
    plain_sum, square_sum = totals_fn((jnp.sum(values, axis=1), jnp.sum(values * values, axis=1)))
    center = (plain_sum / D)[:, None]
    inverse = lax.rsqrt(square_sum[:, None] / D - center * center + epsilon)
    unit_rows = (values - center) * inverse
    return (unit_rows * norm_gain + norm_offset, unit_rows, inverse)


def norm_backward(grad_rows, unit_rows, inverse, norm_gain, totals_fn):
    scaled = grad_rows * norm_gain
    plain_sum, cross_sum = totals_fn((jnp.sum(scaled, axis=1), jnp.sum(scaled * unit_rows, axis=1)))
    return inverse * (scaled - (plain_sum / D)[:, None] - unit_rows * (cross_sum / D)[:, None])


def split_heads(flat_rows):
    return flat_rows.reshape(LEN, flat_rows.shape[1] // HEAD_DIM, HEAD_DIM)


def scores_of(queries, keys_block, limit_value):
    raw_scores = jnp.einsum("qhe,khe->hqk", queries, keys_block, preferred_element_type=jnp.float32)
    raw_scores = raw_scores * HEAD_DIM ** (-0.5)
    places = jnp.arange(LEN, dtype=jnp.int32)
    visible = (places[None, :] <= places[:, None]) | (places[None, :] < limit_value)
    return jnp.where(visible[None], raw_scores, masked_score)


def attend_forward(packed):
    block_rows, limit_value = packed
    queries = split_heads(block_rows[:, 0])
    keys_block = split_heads(block_rows[:, 1])
    values_block = split_heads(block_rows[:, 2])
    scores = scores_of(queries, keys_block, limit_value)
    largest = jnp.max(scores, axis=-1, keepdims=True)
    weights = jnp.exp(scores - largest)
    row_totals = jnp.sum(weights, axis=-1, keepdims=True)
    probs = (weights / row_totals).astype(jnp.bfloat16)
    mixed = jnp.einsum("hqk,khe->qhe", probs, values_block, preferred_element_type=jnp.float32)
    return (mixed.reshape(LEN, -1).astype(jnp.bfloat16), (largest + jnp.log(row_totals))[..., 0])


def attend_backward(packed):
    block_rows, limit_value, log_total, out_grad = packed
    queries = split_heads(block_rows[:, 0])
    keys_block = split_heads(block_rows[:, 1])
    values_block = split_heads(block_rows[:, 2])
    scores = scores_of(queries, keys_block, limit_value)
    probs = jnp.exp(scores - log_total[..., None])
    probs_low = probs.astype(jnp.bfloat16)
    grad_heads = split_heads(out_grad)
    weight_grad = jnp.einsum(
        "qhe,khe->hqk", grad_heads, values_block, preferred_element_type=jnp.float32
    )
    row_inner = jnp.sum(probs * weight_grad, axis=-1, keepdims=True)
    score_grad = (probs * (weight_grad - row_inner)).astype(jnp.bfloat16)
    query_grad = jnp.einsum(
        "hqk,khe->qhe", score_grad, keys_block, preferred_element_type=jnp.float32
    )
    key_grad = jnp.einsum("hqk,qhe->khe", score_grad, queries, preferred_element_type=jnp.float32)
    value_grad = jnp.einsum(
        "hqk,qhe->khe", probs_low, grad_heads, preferred_element_type=jnp.float32
    )
    score_factor = HEAD_DIM ** (-0.5)
    stacked = jnp.stack(
        [
            (query_grad * score_factor).reshape(LEN, -1),
            (key_grad * score_factor).reshape(LEN, -1),
            value_grad.reshape(LEN, -1),
        ],
        axis=1,
    )
    return stacked.astype(jnp.bfloat16)


def general_device(
    tokens,
    prefix,
    ln1_gain,
    ln1_bias,
    w_qkv,
    qv_bias,
    w_out,
    out_bias,
    ln2_gain,
    ln2_bias,
    w_fc,
    fc_bias,
    w_proj,
    proj_bias,
    cotangent,
):
    row_place = lax.axis_index("row")
    col_place = lax.axis_index("col")
    row_devices = lax.axis_size("row")
    col_devices = lax.axis_size("col")
    width_row, local_rows = tokens.shape
    width_col = w_qkv.shape[2]
    hidden_col = w_fc.shape[1]
    seq_rows = local_rows * col_devices // row_devices
    seq_count = seq_rows // LEN
    residual = tokens.T.astype(jnp.float32)
    cotangent_local = cotangent.T
    first_gain = take_portion(ln1_gain, row_place, width_row, 0)
    first_normed, first_unit, first_inverse = norm_forward(
        residual, first_gain, take_portion(ln1_bias, row_place, width_row, 0), feature_totals
    )
    first_gathered = column_rows(first_normed.astype(jnp.bfloat16))

    def qkv_term(first_row, row_count):
        return jnp.einsum("td,sde->tse", first_gathered, w_qkv, preferred_element_type=jnp.float32)

    bias_col = take_portion(qv_bias, col_place, width_col, 1)
    bias_rows = jnp.stack([bias_col[0], jnp.zeros_like(bias_col[0]), bias_col[1]])
    qkv_sum = summed_over_row(qkv_term, seq_rows)
    qkv = (qkv_sum + bias_rows).astype(jnp.bfloat16)
    blocks = qkv.reshape(seq_count, LEN, 3, width_col)
    attn_blocks, log_totals = lax.map(attend_forward, (blocks, prefix))
    attn = attn_blocks.reshape(seq_rows, width_col)
    attn_gathered = row_rows(attn)

    def out_term(first_row, row_count):
        return jnp.dot(attn_gathered, w_out, preferred_element_type=jnp.float32)

    middle = (
        residual
        + summed_over_col(out_term, local_rows)
        + take_portion(out_bias, row_place, width_row, 0)
    )
    grad_output = cotangent_local.astype(jnp.float32)
    second_gain = take_portion(ln2_gain, row_place, width_row, 0)
    second_normed, second_unit, second_inverse = norm_forward(
        middle, second_gain, take_portion(ln2_bias, row_place, width_row, 0), feature_totals
    )
    second_gathered = column_rows(second_normed.astype(jnp.bfloat16))

    def up_term(first_row, row_count):
        return jnp.dot(second_gathered, w_fc, preferred_element_type=jnp.float32)

    hidden = summed_over_row(up_term, seq_rows) + take_portion(fc_bias, col_place, hidden_col, 0)
    active, gelu_pull = jax.vjp(gelu_tanh, hidden)
    active_gathered = row_rows(active.astype(jnp.bfloat16))

    def down_term(first_row, row_count):
        return jnp.einsum("tf,df->td", active_gathered, w_proj, preferred_element_type=jnp.float32)

    final_rows = (
        middle
        + summed_over_col(down_term, local_rows)
        + take_portion(proj_bias, row_place, width_row, 0)
    )
    output = final_rows.astype(jnp.bfloat16)
    grad_gathered = column_rows(cotangent_local)
    w_proj_grad = jnp.einsum(
        "tf,td->df", active_gathered, grad_gathered, preferred_element_type=jnp.float32
    )

    def active_term(first_row, row_count):
        return jnp.einsum("td,df->tf", grad_gathered, w_proj, preferred_element_type=jnp.float32)

    hidden_grad = gelu_pull(summed_over_row(active_term, seq_rows))[0].astype(jnp.bfloat16)
    hidden_gathered = row_rows(hidden_grad)
    w_fc_grad = jnp.einsum(
        "td,tf->df", second_gathered, hidden_gathered, preferred_element_type=jnp.float32
    )

    def second_term(first_row, row_count):
        return jnp.einsum("tf,df->td", hidden_gathered, w_fc, preferred_element_type=jnp.float32)

    second_grad = summed_over_col(second_term, local_rows)
    middle_grad = grad_output + norm_backward(
        second_grad, second_unit, second_inverse, second_gain, feature_totals
    )
    ln2_gain_part = place_portion(jnp.sum(second_grad * second_unit, axis=0), row_place, D, 0)
    ln2_bias_part = place_portion(jnp.sum(second_grad, axis=0), row_place, D, 0)
    fc_bias_part = place_portion(jnp.sum(hidden_grad.astype(jnp.float32), axis=0), col_place, FF, 0)
    proj_bias_part = place_portion(jnp.sum(grad_output, axis=0), row_place, D, 0)
    branch_grad = middle_grad.astype(jnp.bfloat16)
    branch_gathered = column_rows(branch_grad)
    w_out_grad = jnp.einsum(
        "te,td->ed", attn_gathered, branch_gathered, preferred_element_type=jnp.float32
    )

    def attn_term(first_row, row_count):
        return jnp.einsum("td,ed->te", branch_gathered, w_out, preferred_element_type=jnp.float32)

    attn_grad = summed_over_row(attn_term, seq_rows).astype(jnp.bfloat16)
    qkv_grad = lax.map(
        attend_backward, (blocks, prefix, log_totals, attn_grad.reshape(seq_count, LEN, width_col))
    )
    qkv_grad = qkv_grad.reshape(seq_rows, 3, width_col)
    qkv_gathered = row_rows(qkv_grad)
    w_qkv_grad = jnp.einsum(
        "td,tse->sde", first_gathered, qkv_gathered, preferred_element_type=jnp.float32
    )

    def first_term(first_row, row_count):
        return jnp.einsum("tse,sde->td", qkv_gathered, w_qkv, preferred_element_type=jnp.float32)

    first_grad = summed_over_col(first_term, local_rows)
    input_grad = middle_grad + norm_backward(
        first_grad, first_unit, first_inverse, first_gain, feature_totals
    )
    qkv_totals = jnp.sum(qkv_grad.astype(jnp.float32), axis=0)
    qv_part = place_portion(jnp.stack([qkv_totals[0], qkv_totals[2]]), col_place, D, 1)
    out_bias_part = place_portion(jnp.sum(branch_grad.astype(jnp.float32), axis=0), row_place, D, 0)
    ln1_gain_part = place_portion(jnp.sum(first_grad * first_unit, axis=0), row_place, D, 0)
    ln1_bias_part = place_portion(jnp.sum(first_grad, axis=0), row_place, D, 0)
    vectors = lax.psum(
        (
            ln1_gain_part,
            ln1_bias_part,
            qv_part,
            out_bias_part,
            ln2_gain_part,
            ln2_bias_part,
            fc_bias_part,
            proj_bias_part,
        ),
        ("dp", "row", "col"),
    )
    matrices = (
        lax.psum(w_qkv_grad.astype(jnp.bfloat16), "dp").astype(jnp.float32),
        lax.psum(w_out_grad.astype(jnp.bfloat16), "dp").astype(jnp.float32),
        lax.psum(w_fc_grad.astype(jnp.bfloat16), "dp").astype(jnp.float32),
        lax.psum(w_proj_grad.astype(jnp.bfloat16), "dp").astype(jnp.float32),
    )
    return (
        output.T,
        input_grad.T,
        vectors[0],
        vectors[1],
        matrices[0],
        vectors[2],
        matrices[1],
        vectors[3],
        vectors[4],
        vectors[5],
        matrices[2],
        vectors[6],
        matrices[3],
        vectors[7],
    )


MESH = pl.DeviceIdType.MESH
WIDTH = 192
HALF = 96
QUARTER = 256
LANES = 128
WQ = 3 * WIDTH
VMEM_LIMIT = 67043328
REMOTES = 208
LOCALS = 48
FACTOR = HEAD_DIM ** (-0.5)
ANY = pl.BlockSpec(memory_space=pl.ANY)
GAIN1, BIAS1, OUT_BIAS, GAIN2, BIAS2, FC_BIAS, QKV_BIAS, PROJ_BIAS = range(8)
V_GAIN1, V_BIAS1, V_QUERY, V_VALUE, V_OUT, V_GAIN2, V_BIAS2, V_PROJ, V_FC = range(9)
CENTER, INVERSE = range(2)


def dot(left, right, left_axis, right_axis):
    return lax.dot_general(
        left, right, (((left_axis,), (right_axis,)), ((), ())), preferred_element_type=jnp.float32
    )


def low(value):
    return value.astype(jnp.bfloat16)


def wide(value):
    return value.astype(jnp.float32)


def aligned(start, size):
    return pl.ds(pl.multiple_of(start, size), size)


def merged(value):
    return value.reshape((value.shape[0] * value.shape[1],) + value.shape[2:])


def each(count, body):
    def step(i, carry):
        body(i)
        return carry

    lax.fori_loop(0, count, step, 0)


class Links:
    def __init__(self, send_sems, recv_sems, local_sems):
        self.d, self.r, self.c = (lax.axis_index(n) for n in ("dp", "row", "col"))
        self.send_sems, self.recv_sems, self.local_sems = send_sems, recv_sems, local_sems
        self.remotes = 0
        self.locals = 0

    def across(self, k):
        if k == 0:
            return self.r
        if k == 1:
            return self.r + 1 - 2 * lax.rem(self.r, 2)
        return lax.rem(self.r + 2, 4) if k == 2 else 3 - self.r

    def plane(self, k):
        return (self.d, self.across(k), self.c)

    def height(self, k):
        return lax.rem(self.c + k, 4)

    def column(self, k):
        return (self.d, self.r, self.height(k))

    def partner(self):
        return (1 - self.d, self.r, self.c)

    def half(self, mine=True):
        place = self.d if mine else 1 - self.d
        return pl.ds(pl.multiple_of(place * HALF, 16), HALF)

    def crossing(self, row, place):
        place = place + self.d * (3 - 2 * place)
        low_bit = lax.rem(lax.rem(row, 2) + lax.rem(place, 2), 2)
        return low_bit + 2 * lax.rem(lax.div(row, 2) + lax.div(place, 2), 2)

    def meet(self, *devices):
        barrier = pltpu.get_barrier_semaphore()
        for device in devices:
            pl.semaphore_signal(barrier, 1, device_id=device, device_id_type=MESH)
        pl.semaphore_wait(barrier, len(devices))

    def send(self, source, target, device):
        place = self.remotes
        self.remotes += 1
        copy = pltpu.make_async_remote_copy(
            src_ref=source,
            dst_ref=target,
            send_sem=self.send_sems.at[place],
            recv_sem=self.recv_sems.at[place],
            device_id=device,
            device_id_type=MESH,
        )
        copy.start()
        return copy

    def local(self, source, target):
        place = self.locals
        self.locals += 1
        copy = pltpu.make_async_copy(source, target, self.local_sems.at[place])
        copy.start()
        return copy


class Ticket:
    def __init__(self, links, device):
        self.place = links.remotes
        links.remotes += 1
        self.links, self.device = links, device

    def __call__(self, source, target):
        return pltpu.make_async_remote_copy(
            src_ref=source,
            dst_ref=target,
            send_sem=self.links.send_sems.at[self.place],
            recv_sem=self.links.recv_sems.at[self.place],
            device_id=self.device,
            device_id_type=MESH,
        )


class Move:
    def __init__(self, links, stays, source, target, device):
        self.stays = stays
        self.ticket = Ticket(links, device)
        self.source, self.target = source, target
        place = links.locals
        links.locals += 1
        self.local_sem = links.local_sems.at[place]

        @pl.when(jnp.logical_not(stays))
        def _():
            self.ticket(source, target).start()

        @pl.when(stays)
        def _():
            pltpu.make_async_copy(source, target, self.local_sem).start()

    def wait(self):
        @pl.when(jnp.logical_not(self.stays))
        def _():
            self.ticket(self.source, self.target).wait()

        @pl.when(self.stays)
        def _():
            pltpu.make_async_copy(self.source, self.target, self.local_sem).wait()


class PlaneGather:
    def __init__(self, links, target):
        self.links, self.target = links, target
        rows = target.shape[1] // 2
        self.low, self.high = pl.ds(0, rows), pl.ds(rows, rows)
        first, second = target.at[links.r, self.low], target.at[links.r, self.high]
        self.x_low = links.send(first, first, links.plane(1))
        self.y_high = links.send(second, second, links.plane(2))
        self.x_high = links.send(second, second, links.plane(1))
        self.y_low = links.send(first, first, links.plane(2))

    def relay(self):
        links = self.links
        self.x_low.wait_recv()
        block = self.target.at[links.across(1), self.low]
        self.on_y = links.send(block, block, links.plane(2))
        self.y_high.wait_recv()
        block = self.target.at[links.across(2), self.high]
        self.on_x = links.send(block, block, links.plane(1))

    def finish(self):
        self.x_high.wait_recv()
        self.y_low.wait_recv()
        for copy in (self.x_low, self.y_high, self.x_high, self.y_low):
            copy.wait_send()
        self.on_y.wait()
        self.on_x.wait()


class PlaneReduce:
    def __init__(self, links, part_of, rows, over_x, over_y, relayed):
        self.links, self.part_of = links, part_of
        self.halves = (pl.ds(0, rows // 2), pl.ds(rows // 2, rows // 2))
        self.over_x, self.over_y, self.relayed = over_x, over_y, relayed
        self.copies = {}

    def part(self, k, half):
        return self.part_of(self.links.across(k)).at[self.halves[half]]

    def give(self, k):
        links = self.links
        if k == 3:
            self.copies["x3"] = links.send(self.part(3, 0), self.over_x.at[1], links.plane(1))
            self.copies["y3"] = links.send(self.part(3, 1), self.over_y.at[1], links.plane(2))
        elif k == 1:
            self.copies["x1"] = links.send(self.part(1, 0), self.over_x.at[0], links.plane(1))
        elif k == 2:
            self.copies["y2"] = links.send(self.part(2, 1), self.over_y.at[0], links.plane(2))

    def relay(self):
        links = self.links
        self.copies["x3"].wait_recv()
        add_rows(self.over_x.at[1], [self.over_x.at[1], self.part(2, 0)])
        self.copies["xy"] = links.send(self.over_x.at[1], self.relayed.at[0], links.plane(2))
        self.copies["y3"].wait_recv()
        add_rows(self.over_y.at[1], [self.over_y.at[1], self.part(1, 1)])
        self.copies["yx"] = links.send(self.over_y.at[1], self.relayed.at[1], links.plane(1))

    def finish(self):
        for name in ("x3", "y3"):
            self.copies[name].wait_send()
        for name in ("x1", "y2", "xy", "yx"):
            self.copies[name].wait()

    def total(self, lanes):
        parts = []
        for half, over in ((0, self.over_x), (1, self.over_y)):
            value = wide(self.part(0, half)[:, lanes]) + wide(over[0, :, lanes])
            parts.append(value + wide(self.relayed[half, :, lanes]))
        return jnp.concatenate(parts, axis=0)


class Line:
    def __init__(self, links, block_of):
        self.links, self.block_of = links, block_of
        c = links.c
        self.up = [Ticket(links, (links.d, links.r, lax.rem(c + 1, 4))) for _ in range(3)]
        self.down = [Ticket(links, (links.d, links.r, lax.rem(c + 3, 4))) for _ in range(3)]

    def copy(self, ticket, place):
        return ticket(self.block_of(place), self.block_of(place))

    def step(self, t):
        c = self.links.c
        if t > 0:

            @pl.when(c >= t)
            def _():
                self.copy(self.up[t - 1], c - t).wait_recv()

            @pl.when(c <= 3 - t)
            def _():
                self.copy(self.down[t - 1], c + t).wait_recv()

        if t < 3:

            @pl.when(jnp.logical_and(c >= t, c < 3))
            def _():
                self.copy(self.up[t], c - t).start()

            @pl.when(jnp.logical_and(c <= 3 - t, c > 0))
            def _():
                self.copy(self.down[t], c + t).start()

    def finish(self):
        c = self.links.c
        for t in range(3):

            @pl.when(jnp.logical_and(c >= t, c < 3))
            def _(t=t):
                self.copy(self.up[t], c - t).wait_send()

            @pl.when(jnp.logical_and(c <= 3 - t, c > 0))
            def _(t=t):
                self.copy(self.down[t], c + t).wait_send()


class WeightGather:
    def __init__(self, links, stage, moved, target, pieces=1):
        self.links, self.moved, self.target = links, moved, target
        r, c = links.r, links.c
        self.mine = links.half()
        self.goal = links.crossing(r, c)
        size = HALF // pieces
        self.local_rows = [pl.ds(i * size, size) for i in range(pieces)]
        start = links.d * HALF
        self.rows = [pl.ds(pl.multiple_of(start + i * size, 16), size) for i in range(pieces)]
        device = (links.d, r, self.goal)
        self.turns = [
            Move(links, self.goal == c, stage.at[rows], moved.at[rows], device)
            for rows in self.local_rows
        ]

    def hop(self):
        links = self.links
        device = (links.d, self.goal, links.c)
        for i, rows in enumerate(self.local_rows):
            self.turns[i].wait()
            block = self.target.at[links.r, self.rows[i]]
            self.turns[i] = Move(links, self.goal == links.r, self.moved.at[rows], block, device)

    def begin(self):
        links = self.links

        def block_of(rows):
            return lambda place: self.target.at[links.crossing(links.r, place), rows]

        self.ways = []
        for turn, rows in zip(self.turns, self.rows):
            turn.wait()
            self.ways.append(Line(links, block_of(rows)))
            self.ways[-1].step(0)

    def line(self, t):
        if t == 0:
            self.begin()
        else:
            for way in self.ways:
                way.step(t)

    def share(self):
        for way in self.ways:
            way.finish()
        block = self.target.at[:, self.mine]
        self.shared = self.links.send(block, block, self.links.partner())

    def finish(self):
        self.shared.wait()


class SquareGather(WeightGather):
    def __init__(self, links, target):
        self.links, self.target = links, target
        self.mine = links.half()
        self.plane = PlaneGather(links, target.at[:, links.c, self.mine])

    def begin(self):
        self.plane.finish()
        self.ways = [Line(self.links, lambda place: self.target.at[:, place, self.mine])]
        self.ways[0].step(0)

    def share(self):
        self.ways[0].finish()
        block = self.target.at[:, :, self.mine]
        self.shared = self.links.send(block, block, self.links.partner())


def add_rows(target, terms):
    def step(i):
        place = aligned(i * 16, 16)
        total = wide(terms[0][place, :])
        for term in terms[1:]:
            total = total + wide(term[place, :])
        target[place, :] = total.astype(target.dtype)

    each(target.shape[0] // 16, step)


def add_blocks(target, terms):
    if len(target.shape) == 2:
        add_rows(target, terms)
    else:
        each(target.shape[0], lambda i: add_blocks(target.at[i], [term.at[i] for term in terms]))


class LineReduce:
    def __init__(self, links, block_of, up, down):
        self.links, self.block_of, self.up, self.down = links, block_of, up, down
        c = links.c
        self.rise = [Ticket(links, (links.d, links.r, lax.rem(c + 1, 4))) for _ in range(3)]
        self.fall = [Ticket(links, (links.d, links.r, lax.rem(c + 3, 4))) for _ in range(3)]

    def step(self, t):
        c = self.links.c
        for i in range(t + 1):
            goal = 3 - t + i
            self.pass_on(c == i, self.rise[goal - 1], self.up.at[goal - 1], goal, i > 0)
            goal = t - i
            self.pass_on(c == 3 - i, self.fall[goal], self.down.at[goal], goal, i > 0)

    def pass_on(self, here, ticket, slot, goal, adds):
        @pl.when(here)
        def _():
            if adds:
                ticket(slot, slot).wait_recv()
                add_blocks(slot, [slot, self.block_of(goal)])
                ticket(slot, slot).start()
            else:
                ticket(self.block_of(goal), slot).start()

    def total(self, target):
        c = self.links.c
        for goal in range(4):

            @pl.when(c == goal)
            def _(goal=goal):
                terms = [self.block_of(goal)]
                if goal > 0:
                    slot = self.up.at[goal - 1]
                    self.rise[goal - 1](slot, slot).wait_recv()
                    terms.append(slot)
                if goal < 3:
                    slot = self.down.at[goal]
                    self.fall[goal](slot, slot).wait_recv()
                    terms.append(slot)
                add_blocks(target, terms)

        for i in range(3):
            rising, falling = self.up.at[i], self.down.at[i]

            @pl.when(c < i + 1)
            def _(i=i, slot=rising):
                self.rise[i](slot, slot).wait_send()

            @pl.when(c > i)
            def _(i=i, slot=falling):
                self.fall[i](slot, slot).wait_send()


class WeightReduce:
    def __init__(self, links, grad, near, sums, up, down, fin, moved, arrived, result, pieces=1):
        self.links, self.grad, self.near, self.sums = links, grad, near, sums
        self.up, self.down, self.fin = up, down, fin
        self.moved, self.arrived, self.result = moved, arrived, result
        size = HALF // pieces
        self.rows = [pl.ds(i * size, size) for i in range(pieces)]
        self.to_near = [self.send_near(i * size, size) for i in range(pieces)]

    def send_near(self, first, size):
        links = self.links
        other = pl.ds(pl.multiple_of((1 - links.d) * HALF + first, 16), size)
        rows = pl.ds(first, size)
        return links.send(self.grad.at[:, other], self.near.at[:, rows], links.partner())

    def add_near(self):
        links = self.links

        def block_of(rows):
            return lambda place: self.sums.at[links.crossing(links.r, place), rows]

        self.ways = []
        for copy, rows in zip(self.to_near, self.rows):
            copy.wait()
            first = links.d * HALF + rows.start
            mine = pl.ds(pl.multiple_of(first, 16), rows.size)
            each(
                4,
                lambda b, rows=rows, mine=mine: add_rows(
                    self.sums.at[b, rows], [self.grad.at[b, mine], self.near.at[b, rows]]
                ),
            )
            up, down = self.up.at[:, rows], self.down.at[:, rows]
            self.ways.append(LineReduce(links, block_of(rows), up, down))

    def line(self, i):
        for way in self.ways:
            way.step(i)

    def hop(self):
        links = self.links
        self.goal = links.crossing(links.r, links.c)
        device = (links.d, self.goal, links.c)
        self.turns = []
        for way, rows in zip(self.ways, self.rows):
            way.total(self.fin.at[rows])
            stays = self.goal == links.r
            self.turns.append(Move(links, stays, self.fin.at[rows], self.moved.at[rows], device))

    def back(self):
        links = self.links
        device = (links.d, links.r, self.goal)
        for i, rows in enumerate(self.rows):
            self.turns[i].wait()
            stays = self.goal == links.c
            self.turns[i] = Move(links, stays, self.moved.at[rows], self.arrived.at[rows], device)

    def share(self):
        for turn in self.turns:
            turn.wait()
        self.give(self.arrived)

    def give(self, total):
        links, mine = self.links, self.links.half()
        self.last = [
            links.send(total, self.result.at[mine], links.partner()),
            links.local(total, self.result.at[mine]),
        ]

    def finish(self):
        for copy in self.last:
            copy.wait()


class SquareReduce(WeightReduce):
    def __init__(self, links, grad, near, sums, up, down, fin, came, arrived, result):
        self.links, self.grad, self.near, self.sums = links, grad, near, sums
        self.up, self.down, self.fin = up, down, fin
        self.came, self.arrived, self.result = came, arrived, result
        self.to_near = links.send(grad.at[:, :, links.half(False)], near, links.partner())

    def add_near(self):
        mine = self.links.half()
        self.to_near.wait()
        add_blocks(self.sums, [self.grad.at[:, :, mine], self.near])
        self.ways = [
            LineReduce(self.links, lambda place: self.sums.at[:, place], self.up, self.down)
        ]

    def hop(self):
        links = self.links
        self.ways[0].total(self.fin)
        self.crossing = [
            links.send(self.fin.at[links.across(k)], self.came.at[k - 1], links.plane(k))
            for k in (3, 1, 2)
        ]

    def back(self):
        for copy in self.crossing:
            copy.wait()
        came = self.came
        add_rows(self.arrived, [self.fin.at[self.links.r], came.at[0], came.at[1], came.at[2]])

    def share(self):
        self.give(self.arrived)


def normalize(source_of, target, stats, gain, offset):
    def step(j):
        lanes = aligned(j * LANES, LANES)
        values = source_of(lanes)
        center = jnp.sum(values, axis=0, keepdims=True) / D
        square = jnp.sum(values * values, axis=0, keepdims=True) / D
        inverse = lax.rsqrt(square - center * center + epsilon)
        stats[CENTER : CENTER + 1, lanes] = center
        stats[INVERSE : INVERSE + 1, lanes] = inverse
        target[:, lanes] = low((values - center) * inverse * gain[...] + offset[...])

    each(LEN // LANES, step)


def key_span(block):
    return max(512, (block + 1) * QUARTER), block * QUARTER


def visible(block, first, last, limit_value):
    shape = (last - first, QUARTER)
    keys = lax.broadcasted_iota(jnp.int32, shape, 0) + first
    queries = lax.broadcasted_iota(jnp.int32, shape, 1) + block * QUARTER
    return (keys <= queries) | (keys < limit_value)


def masked(value, block, limit_value, fill):
    last, first = key_span(block)
    tail = jnp.where(visible(block, first, last, limit_value), value[first:], fill)
    return jnp.concatenate([value[:first], tail], axis=0) if first else tail


def head_rows(h, part):
    return pl.ds(h * HEAD_DIM + part * WIDTH, HEAD_DIM)


def attend(qkv, limit_value, attn_of, log_total, between):
    def head(h):
        between[h]()
        for block in range(4):
            last, _ = key_span(block)
            lanes = slice(block * QUARTER, (block + 1) * QUARTER)
            queries = qkv[head_rows(h, 0), lanes] * jnp.bfloat16(FACTOR)
            scores = dot(qkv[head_rows(h, 1), :last], queries, 0, 0)
            scores = masked(scores, block, limit_value, masked_score)
            largest = jnp.max(scores, axis=0, keepdims=True)
            weights = jnp.exp(scores - largest)
            total = jnp.sum(weights, axis=0, keepdims=True)
            mixed = dot(qkv[head_rows(h, 2), :last], low(weights), 1, 0)
            attn_of(head_rows(h, 0), lanes, low(mixed * (1.0 / total)))
            log_total[pl.ds(h, 1), lanes] = largest + jnp.log(total)

    for h in range(3):
        head(h)


def attend_back(
    qkv, limit_value, attn_of, log_total, out_grad, qkv_grad, key_sum, value_sum, between
):
    def head(h):
        between[h]()
        for block in (3, 2, 1, 0):
            last, _ = key_span(block)
            lanes = slice(block * QUARTER, (block + 1) * QUARTER)
            queries = qkv[head_rows(h, 0), lanes] * jnp.bfloat16(FACTOR)
            grads = out_grad[head_rows(h, 0), lanes]
            inner = jnp.sum(
                wide(attn_of(head_rows(h, 0), lanes)) * wide(grads), axis=0, keepdims=True
            )
            scores = dot(qkv[head_rows(h, 1), :last], queries, 0, 0)
            probs = jnp.exp(scores - log_total[pl.ds(h, 1), lanes])
            probs = masked(probs, block, limit_value, 0.0)
            weight_grad = dot(qkv[head_rows(h, 2), :last], grads, 0, 0)
            score_grad = low(probs * (weight_grad - inner))
            query_grad = dot(qkv[head_rows(h, 1), :last], score_grad, 1, 0) * FACTOR
            qkv_grad[head_rows(h, 0), lanes] = low(query_grad)
            key_grad = dot(queries, score_grad, 1, 1)
            value_grad = dot(grads, low(probs), 1, 1)
            if block == 3:
                key_sum[...] = key_grad
                value_sum[...] = value_grad
            else:
                key_sum[:, :last] += key_grad
                value_sum[:, :last] += value_grad
        qkv_grad[head_rows(h, 1), :] = low(key_sum[...])
        qkv_grad[head_rows(h, 2), :] = low(value_sum[...])

    for h in range(3):
        head(h)


def gelu_parts(u):
    slope = (2.0 / 3.141592653589793) ** 0.5
    square = u * u
    bent = jnp.tanh(slope * u * (1.0 + 0.044715 * square))
    shared = 0.5 * (1.0 + bent)
    derivative = shared + 0.5 * u * (1.0 - bent * bent) * (slope * (1.0 + 3.0 * 0.044715 * square))
    return u * shared, derivative


def in_turn(*actions):
    def run():
        for action in actions:
            action()

    return run


def block_kernel(
    tok, cot, pre, wq_in, wf_in, wp_in, wo_in, cols_in,
    out_hbm, grad_hbm, wq_hbm, wf_hbm, wp_hbm, wo_hbm, vec_hbm,
    xt, gt, wqa, wfa, wpa, woa, zq, zf, zp, mq, mf, mp, pres, cols, colb,
    fn, qkv, at, lse, st1, st2, mid, sn, act, slope, op, hg, sp,
    x2, y2, z2, x_out, y_out, z_out, x1, y1, z1, br, ap, dout, brf, dqkv, ksum, vsum,
    gf, gp, gq, near_f, near_p, near_q, sum_f, sum_p, sum_q, up_f, up_p, up_q, dn_f, dn_p, dn_q,
    fin_f, fin_p, fin_q, hop_f, hop_p, hop_q, got_f, got_p, got_q,
    sq, near_o, sum_o, up_o, dn_o, fin_o, hop_o, got_o,
    fgp, vcol, vec, vec_in, stat, stat_in, out_v, grad_v,
    send_sems, recv_sems, local_sems,
):
    links = Links(send_sems, recv_sems, local_sems)
    r, c = links.r, links.c
    mine = links.half()
    own = aligned(r * QUARTER, QUARTER)
    first = [links.local(wq_in.at[mine], zq), links.local(tok, xt.at[r])]
    first += [links.local(pre, pres.at[r]), links.local(wo_in.at[mine], woa.at[r, c, mine])]
    then = [links.local(wf_in.at[mine], zf), links.local(wp_in.at[mine], zp)]
    then += [links.local(cols_in, cols), links.local(cot, gt.at[r])]
    links.meet(
        links.partner(), *(links.plane(k) for k in (1, 2, 3)), *(links.column(k) for k in (1, 2, 3))
    )
    for copy in first:
        copy.wait()

    get_q = WeightGather(links, zq, mq, wqa, 3)
    tokens = PlaneGather(links, xt)
    prefixes = [links.send(pres.at[r], pres.at[r], links.plane(k)) for k in (1, 2, 3)]
    get_o = SquareGather(links, woa)
    for copy in then:
        copy.wait()
    for j in range(7):
        colb[j] = jnp.broadcast_to(cols[:, j : j + 1], (D, LANES))
    get_q.hop()
    get_f = WeightGather(links, zf, mf, wfa)
    get_p = WeightGather(links, zp, mp, wpa)
    get_o.plane.relay()
    get_q.line(0)
    tokens.relay()
    get_q.line(1)
    get_q.line(2)
    get_o.line(0)
    get_q.line(3)
    get_q.share()
    tokens.finish()
    grads = PlaneGather(links, gt)
    normalize(
        lambda lanes: wide(merged(xt[:, :, lanes])), fn, st1, colb.at[GAIN1], colb.at[BIAS1]
    )
    for copy in prefixes:
        copy.wait()
    get_f.hop()
    get_p.hop()
    get_o.line(1)
    get_q.finish()

    def project(b):
        lanes = aligned(b * QUARTER, QUARTER)
        bias = colb[QKV_BIAS, :WQ]
        value = dot(merged(wqa[...]), fn[:, lanes], 0, 0)
        qkv[:, lanes] = low(value + jnp.concatenate([bias, bias], axis=1))

    each(4, project)
    limit_value = pres[c][0:1, 0:1]

    def put_attn(rows, lanes, value):
        at[r, rows, lanes] = value

    def get_attn(rows, lanes):
        return at[r, rows, lanes]

    attns = []

    def gather_head(h):
        attns.append(PlaneGather(links, at.at[:, h * HEAD_DIM : (h + 1) * HEAD_DIM]))

    attend(
        qkv,
        limit_value,
        put_attn,
        lse,
        [
            in_turn(lambda: get_o.line(2), lambda: get_f.line(0)),
            in_turn(lambda: gather_head(0), lambda: get_o.line(3), lambda: get_f.line(1)),
            in_turn(
                lambda: gather_head(1), get_o.share, grads.relay, lambda: attns[0].relay(),
                lambda: get_f.line(2), lambda: get_p.line(0),
            ),
        ],
    )
    gather_head(2)
    attns[1].relay()
    get_f.line(3)
    get_f.share()
    get_p.line(1)
    attns[2].relay()
    get_p.line(2)
    get_o.finish()
    grads.finish()
    for attn in attns:
        attn.finish()

    def join(i):
        b, lanes = lax.div(i, 4), aligned(lax.rem(i, 4) * QUARTER, QUARTER)
        rows = aligned(b * WIDTH, WIDTH)
        bias = colb[OUT_BIAS, rows]
        value = dot(merged(woa[b]), merged(at[:, :, lanes]), 0, 0)
        mid[rows, lanes] = wide(xt[b, :, lanes]) + (value + jnp.concatenate([bias, bias], axis=1))

    each(16, join)
    get_p.line(3)
    get_p.share()
    normalize(lambda lanes: mid[:, lanes], sn, st2, colb.at[GAIN2], colb.at[BIAS2])
    get_f.finish()

    def up(b):
        lanes = aligned(b * QUARTER, QUARTER)
        bias = colb[FC_BIAS]
        value = dot(merged(wfa[...]), sn[:, lanes], 0, 0) + jnp.concatenate([bias, bias], axis=1)
        value, derivative = gelu_parts(value)
        act[:, lanes] = low(value)
        slope[:, lanes] = derivative

    each(4, up)
    get_p.finish()

    seconds = PlaneReduce(
        links, lambda place: sp.at[:, aligned(place * QUARTER, QUARTER)], D, x2, y2, z2
    )
    for k in (3, 1, 2, 0):
        lanes = aligned(links.across(k) * QUARTER, QUARTER)
        value = dot(merged(wpa[...]), merged(gt[:, :, lanes]), 0, 0)
        hg[:, lanes] = low(value * slope[:, lanes])
        sp[:, lanes] = low(dot(merged(wfa[...]), hg[:, lanes], 1, 0))
        seconds.give(k)

    def proj_grads(b):
        gp[b] = low(dot(gt[b], act[...], 1, 1))

    def fc_grads(b):
        gf[b] = low(dot(sn[aligned(b * WIDTH, WIDTH), :], hg[...], 1, 1))

    each(4, proj_grads)
    put_p = WeightReduce(links, gp, near_p, sum_p, up_p, dn_p, fin_p, hop_p, got_p, wp_hbm)
    each(4, fc_grads)
    put_f = WeightReduce(links, gf, near_f, sum_f, up_f, dn_f, fin_f, hop_f, got_f, wf_hbm)
    seconds.relay()
    put_p.add_near()
    put_p.line(0)

    def down(b):
        lanes = aligned(b * QUARTER, QUARTER)
        value = low(dot(merged(wpa[...]), act[:, lanes], 1, 0))
        op[:, :, lanes] = value.reshape(4, WIDTH, QUARTER)

    each(4, down)
    outs = PlaneReduce(links, lambda place: op.at[place], WIDTH, x_out, y_out, z_out)

    lane = lax.broadcasted_iota(jnp.int32, (D, LANES), 1)
    total = jnp.zeros((D, 1), jnp.float32)
    for b in range(4):
        lanes = slice(b * QUARTER, (b + 1) * QUARTER)
        total = total + jnp.sum(wide(hg[:, lanes]), axis=1, keepdims=True)
    vcol[...] = jnp.where(lane == V_FC + r, total, 0.0)
    put_f.add_near()
    put_p.line(1)
    put_f.line(0)
    seconds.finish()

    def back(j):
        lanes = aligned(r * QUARTER + j * LANES, LANES)
        part = aligned(j * LANES, LANES)
        given = seconds.total(part)
        inverse = st2[INVERSE : INVERSE + 1, lanes]
        unit = (mid[:, lanes] - st2[CENTER : CENTER + 1, lanes]) * inverse
        scaled = given * colb[GAIN2]
        plain = jnp.sum(scaled, axis=0, keepdims=True) / D
        cross = jnp.sum(scaled * unit, axis=0, keepdims=True) / D
        above = wide(merged(gt[:, :, lanes]))
        branch = low(above + inverse * (scaled - plain - unit * cross))
        br[:, :, part] = branch.reshape(4, WIDTH, LANES)
        value = jnp.where(lane == V_GAIN2, jnp.sum(given * unit, axis=1, keepdims=True), 0.0)
        value = jnp.where(lane == V_BIAS2, jnp.sum(given, axis=1, keepdims=True), value)
        value = jnp.where(lane == V_OUT, jnp.sum(wide(branch), axis=1, keepdims=True), value)
        value = jnp.where(lane == V_PROJ, jnp.sum(above, axis=1, keepdims=True), value)
        vcol[...] = vcol[...] + value

    for j in range(2):
        back(j)
    value = dot(merged(woa[0]), br[0], 1, 0)
    for b in range(1, 4):
        value = value + dot(merged(woa[b]), br[b], 1, 0)
    ap[...] = low(value).reshape(4, WIDTH, QUARTER)
    turns = [
        links.send(ap.at[links.across(k)], dout.at[:, own], links.plane(k)) for k in (3, 1, 2)
    ]
    turns.append(links.local(ap.at[r], dout.at[:, own]))
    swaps = [
        links.send(br.at[links.across(k)], brf.at[:, own], links.plane(k)) for k in (3, 1, 2)
    ]
    swaps.append(links.local(br.at[r], brf.at[:, own]))

    def square_grads(b):
        value = low(dot(merged(at[:, :, own]), br[b], 1, 1))
        sq[b] = value.reshape(4, WIDTH, WIDTH)

    each(4, square_grads)
    put_o = SquareReduce(links, sq, near_o, sum_o, up_o, dn_o, fin_o, hop_o, got_o, wo_hbm)
    put_p.line(2)
    put_f.line(1)
    put_o.add_near()
    for copy in turns:
        copy.wait()
    for k in (3, 1, 2):
        outs.give(k)
    attend_back(
        qkv, limit_value, get_attn, lse, dout, dqkv, ksum, vsum,
        [
            in_turn(put_p.hop, lambda: put_f.line(2)),
            in_turn(put_p.back, put_f.hop, lambda: put_o.line(0)),
            in_turn(outs.relay, put_p.share, put_f.back, lambda: put_o.line(1)),
        ],
    )

    def query_grads(b):
        gq[b] = low(dot(fn[aligned(b * WIDTH, WIDTH), :], dqkv[...], 1, 1))

    each(4, query_grads)
    put_q = WeightReduce(links, gq, near_q, sum_q, up_q, dn_q, fin_q, hop_q, got_q, wq_hbm, 3)

    stat[...] = jnp.zeros_like(stat)
    firsts = PlaneReduce(links, lambda place: fgp.at[place], WIDTH, x1, y1, z1)
    for k in (3, 1, 2, 0):
        b = links.across(k)
        rows = aligned(b * WIDTH, WIDTH)

        def first_part(j, b=b, rows=rows):
            lanes = aligned(j * QUARTER, QUARTER)
            value = dot(wqa[b], dqkv[:, lanes], 1, 0)
            fgp[b, :, lanes] = low(value)
            for i in range(2):
                half = aligned(j * QUARTER + i * LANES, LANES)
                piece = value[:, i * LANES : (i + 1) * LANES]
                unit = wide(xt[b, :, half]) - st1[CENTER : CENTER + 1, half]
                unit = unit * st1[INVERSE : INVERSE + 1, half]
                weighted = piece * unit
                gain = colb[GAIN1, rows]
                stat[0:1, half] += jnp.sum(piece * gain, axis=0, keepdims=True)
                stat[1:2, half] += jnp.sum(weighted * gain, axis=0, keepdims=True)
                spot = lane[:WIDTH]
                add = jnp.where(spot == V_GAIN1, jnp.sum(weighted, axis=1, keepdims=True), 0.0)
                add = jnp.where(spot == V_BIAS1, jnp.sum(piece, axis=1, keepdims=True), add)
                vcol[rows, :] = vcol[rows, :] + add

        each(4, first_part)
        firsts.give(k)
        if k == 3:
            put_q.add_near()
            put_q.line(0)
        elif k == 1:
            put_o.line(2)
            put_q.line(1)
        elif k == 2:
            put_f.share()
            put_q.line(2)
            firsts.relay()
    stat_sends = [links.send(stat, stat_in.at[k - 1], links.plane(k)) for k in (1, 2, 3)]
    put_o.hop()
    rows = aligned(r * WIDTH, WIDTH)
    spot = lane[:WIDTH]
    query = jnp.zeros((WIDTH, 1), jnp.float32)
    value = jnp.zeros((WIDTH, 1), jnp.float32)
    for b in range(4):
        lanes = slice(b * QUARTER, (b + 1) * QUARTER)
        query = query + jnp.sum(wide(dqkv[:WIDTH, lanes]), axis=1, keepdims=True)
        value = value + jnp.sum(wide(dqkv[2 * WIDTH :, lanes]), axis=1, keepdims=True)
    add = jnp.where(spot == V_QUERY, query, jnp.where(spot == V_VALUE, value, 0.0))
    vcol[rows, :] = vcol[rows, :] + add
    vec[0] = vcol[...].T[:16]
    vec_near = links.send(vec.at[0], vec_in.at[0], links.partner())
    put_q.hop()
    vec_near.wait()
    vec[1] = vec[0] + vec_in[0]
    vec_plane = [links.send(vec.at[1], vec_in.at[k], links.plane(k)) for k in (1, 2, 3)]
    put_o.back()
    put_o.share()
    put_q.back()
    for copy in vec_plane:
        copy.wait()
    vec[2] = vec[1] + vec_in[1] + vec_in[2] + vec_in[3]
    vec_high = [links.send(vec.at[2], vec_in.at[3 + k], links.column(k)) for k in (1, 2, 3)]
    outs.finish()

    def last_out(j):
        lanes = aligned(j * LANES, LANES)
        value = mid[rows, lanes] + cols[rows, PROJ_BIAS : PROJ_BIAS + 1] + outs.total(lanes)
        out_v[:, lanes] = low(value)

    each(LEN // LANES, last_out)
    ends = [links.local(out_v, out_hbm)]
    for copy in swaps + stat_sends:
        copy.wait()
    firsts.finish()
    stat[...] = stat[...] + stat_in[0] + stat_in[1] + stat_in[2]

    def last_grad(j):
        lanes = aligned(j * LANES, LANES)
        inverse = st1[INVERSE : INVERSE + 1, lanes]
        unit = (wide(xt[r, :, lanes]) - st1[CENTER : CENTER + 1, lanes]) * inverse
        value = firsts.total(lanes) * colb[GAIN1, rows] - stat[0:1, lanes] / D
        grad_v[:, lanes] = wide(brf[:, lanes]) + inverse * (value - unit * (stat[1:2, lanes] / D))

    each(LEN // LANES, last_grad)
    ends.append(links.local(grad_v, grad_hbm))
    put_q.share()
    for copy in vec_high:
        copy.wait()
    vec[3] = vec[2] + vec_in[4] + vec_in[5] + vec_in[6]
    ends.append(links.local(vec.at[3], vec_hbm))
    for copy in ends:
        copy.wait()
    for put in (put_f, put_p, put_o, put_q):
        put.finish()


def run_block(*arguments):
    narrow, full = jnp.bfloat16, jnp.float32
    vmem = pltpu.VMEM
    sequence, tall = (4, WIDTH, LEN), (D, LEN)

    def thirds(lead=()):
        return [vmem(lead + (HALF, width), narrow) for width in (D, D, WQ)]

    def plane_sums(rows, lanes):
        return [vmem((2, rows // 2, lanes), narrow) for _ in range(3)]

    scratch = [
        vmem(sequence, narrow), vmem(sequence, narrow),
        vmem((4, WIDTH, WQ), narrow), vmem((4, WIDTH, D), narrow), vmem((4, WIDTH, D), narrow),
        vmem((4, 4, WIDTH, WIDTH), narrow),
        vmem((HALF, WQ), narrow), vmem((HALF, D), narrow), vmem((HALF, D), narrow),
        vmem((HALF, WQ), narrow), vmem((HALF, D), narrow), vmem((HALF, D), narrow),
        vmem((4, 8, LANES), jnp.int32), vmem((D, 8), full), vmem((7, D, LANES), full),
        vmem(tall, narrow), vmem((WQ, LEN), narrow), vmem(sequence, narrow),
        vmem((8, LEN), full), vmem((8, LEN), full), vmem((8, LEN), full),
        vmem(tall, full), vmem(tall, narrow), vmem(tall, narrow), vmem(tall, full),
        vmem(sequence, narrow), vmem(tall, narrow), vmem(tall, narrow),
        *plane_sums(D, QUARTER), *plane_sums(WIDTH, LEN), *plane_sums(WIDTH, LEN),
        vmem((4, WIDTH, QUARTER), narrow), vmem((4, WIDTH, QUARTER), narrow),
        vmem((WIDTH, LEN), narrow), vmem((WIDTH, LEN), narrow), vmem((WQ, LEN), narrow),
        vmem((HEAD_DIM, LEN), full), vmem((HEAD_DIM, LEN), full),
        vmem((4, WIDTH, D), narrow), vmem((4, WIDTH, D), narrow), vmem((4, WIDTH, WQ), narrow),
        *thirds((4,)), *thirds((4,)), *thirds((3,)), *thirds((3,)), *thirds(), *thirds(), *thirds(),
        vmem((4, 4, WIDTH, WIDTH), narrow), vmem((4, 4, HALF, WIDTH), narrow),
        vmem((4, 4, HALF, WIDTH), narrow), vmem((3, 4, HALF, WIDTH), narrow),
        vmem((3, 4, HALF, WIDTH), narrow), vmem((4, HALF, WIDTH), narrow),
        vmem((3, HALF, WIDTH), narrow), vmem((HALF, WIDTH), narrow),
        vmem(sequence, narrow), vmem((D, LANES), full),
        vmem((4, 16, D), full), vmem((7, 16, D), full), vmem((8, LEN), full), vmem((3, 8, LEN), full),
        vmem((WIDTH, LEN), narrow), vmem((WIDTH, LEN), full),
        pltpu.SemaphoreType.DMA((REMOTES,)), pltpu.SemaphoreType.DMA((REMOTES,)),
        pltpu.SemaphoreType.DMA((LOCALS,)),
    ]
    results = [
        ((WIDTH, LEN), narrow), ((WIDTH, LEN), full), ((WIDTH, WQ), narrow), ((WIDTH, D), narrow),
        ((WIDTH, D), narrow), ((WIDTH, WIDTH), narrow), ((16, D), full),
    ]
    return pl.pallas_call(
        block_kernel,
        out_shape=[jax.ShapeDtypeStruct(*result) for result in results],
        in_specs=[ANY] * len(arguments),
        out_specs=[ANY] * len(results),
        scratch_shapes=scratch,
        compiler_params=pltpu.CompilerParams(
            collective_id=0, has_side_effects=True, vmem_limit_bytes=VMEM_LIMIT
        ),
        name="block",
    )(*arguments)


def plane_device(
    tokens, prefix, ln1_gain, ln1_bias, w_qkv, qv_bias, w_out, out_bias,
    ln2_gain, ln2_bias, w_fc, fc_bias, w_proj, proj_bias, cotangent,
):
    r = lax.axis_index("row")
    bias = take_portion(qv_bias, r, WIDTH, 1)
    nothing = jnp.zeros((WIDTH,), jnp.float32)
    bias = jnp.concatenate([bias[0], nothing, bias[1], nothing])
    columns = jnp.stack(
        [
            ln1_gain, ln1_bias, out_bias, ln2_gain, ln2_bias,
            take_portion(fc_bias, r, D, 0), bias, proj_bias,
        ],
        axis=1,
    )
    output, input_grad, w_qkv_grad, w_fc_grad, w_proj_grad, w_out_grad, vector = run_block(
        tokens,
        cotangent,
        jnp.broadcast_to(prefix[:, None], (8, LANES)),
        w_qkv.transpose(1, 0, 2).reshape(WIDTH, WQ),
        w_fc,
        w_proj,
        w_out,
        columns,
    )
    return (
        output,
        input_grad,
        vector[V_GAIN1],
        vector[V_BIAS1],
        wide(w_qkv_grad.reshape(WIDTH, 3, WIDTH).transpose(1, 0, 2)),
        vector[V_QUERY : V_VALUE + 1],
        wide(w_out_grad),
        vector[V_OUT],
        vector[V_GAIN2],
        vector[V_BIAS2],
        wide(w_fc_grad),
        vector[V_FC : V_FC + 4].reshape(FF),
        wide(w_proj_grad),
        vector[V_PROJ],
    )


def solution(mesh):
    on_device = plane_device if dict(mesh.shape) == {"dp": 2, "row": 4, "col": 4} else general_device
    placed = (
        P("row", ("dp", "col")),
        P(("dp", "row")),
        P(),
        P(),
        P(None, "row", "col"),
        P(),
        P("col", "row"),
        P(),
        P(),
        P(),
        P("row", "col"),
        P(),
        P("row", "col"),
        P(),
        P("row", ("dp", "col")),
    )
    return jax.shard_map(
        on_device,
        mesh=mesh,
        in_specs=placed,
        out_specs=(
            P("row", ("dp", "col")),
            P("row", ("dp", "col")),
            P(),
            P(),
            P(None, "row", "col"),
            P(),
            P("col", "row"),
            P(),
            P(),
            P(),
            P("row", "col"),
            P(),
            P("row", "col"),
            P(),
        ),
        check_vma=False,
    )
```

```python
import functools

import jax
import jax.numpy as jnp
from jax import lax
from jax.experimental import pallas as pl
from jax.experimental.pallas import tpu as pltpu
from jax.sharding import PartitionSpec as P

D = 768
FF = 3072
HEAD_DIM = 64
LEN = 1024


epsilon = 1e-05
masked_score = -1e30


def feature_totals(values):
    return lax.psum(values, "row")


def column_rows(values):
    return lax.all_gather(values, "col", axis=0, tiled=True)


def row_rows(values):
    return lax.all_gather(values, "row", axis=0, tiled=True)


def summed_over_row(term_fn, row_count):
    return lax.psum_scatter(
        term_fn(jnp.int32(0), row_count * lax.axis_size("row")),
        "row",
        scatter_dimension=0,
        tiled=True,
    )


def summed_over_col(term_fn, row_count):
    return lax.psum_scatter(
        term_fn(jnp.int32(0), row_count * lax.axis_size("col")),
        "col",
        scatter_dimension=0,
        tiled=True,
    )


def take_portion(complete, position, portion_size, along):
    return lax.dynamic_slice_in_dim(complete, position * portion_size, portion_size, along)


def place_portion(portion, position, full_size, along):
    zeroed_shape = portion.shape[:along] + (full_size,) + portion.shape[along + 1 :]
    zeroed = jnp.zeros(zeroed_shape, jnp.float32)
    return lax.dynamic_update_slice_in_dim(zeroed, portion, position * portion.shape[along], along)


def gelu_tanh(values):
    return jax.nn.gelu(values, approximate=True)


def norm_forward(values, norm_gain, norm_offset, totals_fn):
    plain_sum, square_sum = totals_fn((jnp.sum(values, axis=1), jnp.sum(values * values, axis=1)))
    center = (plain_sum / D)[:, None]
    inverse = lax.rsqrt(square_sum[:, None] / D - center * center + epsilon)
    unit_rows = (values - center) * inverse
    return (unit_rows * norm_gain + norm_offset, unit_rows, inverse)


def norm_backward(grad_rows, unit_rows, inverse, norm_gain, totals_fn):
    scaled = grad_rows * norm_gain
    plain_sum, cross_sum = totals_fn((jnp.sum(scaled, axis=1), jnp.sum(scaled * unit_rows, axis=1)))
    return inverse * (scaled - (plain_sum / D)[:, None] - unit_rows * (cross_sum / D)[:, None])


def split_heads(flat_rows):
    return flat_rows.reshape(LEN, flat_rows.shape[1] // HEAD_DIM, HEAD_DIM)


def scores_of(queries, keys_block, limit_value):
    raw_scores = jnp.einsum("qhe,khe->hqk", queries, keys_block, preferred_element_type=jnp.float32)
    raw_scores = raw_scores * HEAD_DIM ** (-0.5)
    places = jnp.arange(LEN, dtype=jnp.int32)
    visible = (places[None, :] <= places[:, None]) | (places[None, :] < limit_value)
    return jnp.where(visible[None], raw_scores, masked_score)


def attend_forward(packed):
    block_rows, limit_value = packed
    queries = split_heads(block_rows[:, 0])
    keys_block = split_heads(block_rows[:, 1])
    values_block = split_heads(block_rows[:, 2])
    scores = scores_of(queries, keys_block, limit_value)
    largest = jnp.max(scores, axis=-1, keepdims=True)
    weights = jnp.exp(scores - largest)
    row_totals = jnp.sum(weights, axis=-1, keepdims=True)
    probs = (weights / row_totals).astype(jnp.bfloat16)
    mixed = jnp.einsum("hqk,khe->qhe", probs, values_block, preferred_element_type=jnp.float32)
    return (mixed.reshape(LEN, -1).astype(jnp.bfloat16), (largest + jnp.log(row_totals))[..., 0])


def attend_backward(packed):
    block_rows, limit_value, log_total, out_grad = packed
    queries = split_heads(block_rows[:, 0])
    keys_block = split_heads(block_rows[:, 1])
    values_block = split_heads(block_rows[:, 2])
    scores = scores_of(queries, keys_block, limit_value)
    probs = jnp.exp(scores - log_total[..., None])
    probs_low = probs.astype(jnp.bfloat16)
    grad_heads = split_heads(out_grad)
    weight_grad = jnp.einsum(
        "qhe,khe->hqk", grad_heads, values_block, preferred_element_type=jnp.float32
    )
    row_inner = jnp.sum(probs * weight_grad, axis=-1, keepdims=True)
    score_grad = (probs * (weight_grad - row_inner)).astype(jnp.bfloat16)
    query_grad = jnp.einsum(
        "hqk,khe->qhe", score_grad, keys_block, preferred_element_type=jnp.float32
    )
    key_grad = jnp.einsum("hqk,qhe->khe", score_grad, queries, preferred_element_type=jnp.float32)
    value_grad = jnp.einsum(
        "hqk,qhe->khe", probs_low, grad_heads, preferred_element_type=jnp.float32
    )
    score_factor = HEAD_DIM ** (-0.5)
    stacked = jnp.stack(
        [
            (query_grad * score_factor).reshape(LEN, -1),
            (key_grad * score_factor).reshape(LEN, -1),
            value_grad.reshape(LEN, -1),
        ],
        axis=1,
    )
    return stacked.astype(jnp.bfloat16)


def general_device(
    tokens,
    prefix,
    ln1_gain,
    ln1_bias,
    w_qkv,
    qv_bias,
    w_out,
    out_bias,
    ln2_gain,
    ln2_bias,
    w_fc,
    fc_bias,
    w_proj,
    proj_bias,
    cotangent,
):
    row_place = lax.axis_index("row")
    col_place = lax.axis_index("col")
    row_devices = lax.axis_size("row")
    col_devices = lax.axis_size("col")
    width_row, local_rows = tokens.shape
    width_col = w_qkv.shape[2]
    hidden_col = w_fc.shape[1]
    seq_rows = local_rows * col_devices // row_devices
    seq_count = seq_rows // LEN
    residual = tokens.T.astype(jnp.float32)
    cotangent_local = cotangent.T
    first_gain = take_portion(ln1_gain, row_place, width_row, 0)
    first_normed, first_unit, first_inverse = norm_forward(
        residual, first_gain, take_portion(ln1_bias, row_place, width_row, 0), feature_totals
    )
    first_gathered = column_rows(first_normed.astype(jnp.bfloat16))

    def qkv_term(first_row, row_count):
        return jnp.einsum("td,sde->tse", first_gathered, w_qkv, preferred_element_type=jnp.float32)

    bias_col = take_portion(qv_bias, col_place, width_col, 1)
    bias_rows = jnp.stack([bias_col[0], jnp.zeros_like(bias_col[0]), bias_col[1]])
    qkv_sum = summed_over_row(qkv_term, seq_rows)
    qkv = (qkv_sum + bias_rows).astype(jnp.bfloat16)
    blocks = qkv.reshape(seq_count, LEN, 3, width_col)
    attn_blocks, log_totals = lax.map(attend_forward, (blocks, prefix))
    attn = attn_blocks.reshape(seq_rows, width_col)
    attn_gathered = row_rows(attn)

    def out_term(first_row, row_count):
        return jnp.dot(attn_gathered, w_out, preferred_element_type=jnp.float32)

    middle = (
        residual
        + summed_over_col(out_term, local_rows)
        + take_portion(out_bias, row_place, width_row, 0)
    )
    grad_output = cotangent_local.astype(jnp.float32)
    second_gain = take_portion(ln2_gain, row_place, width_row, 0)
    second_normed, second_unit, second_inverse = norm_forward(
        middle, second_gain, take_portion(ln2_bias, row_place, width_row, 0), feature_totals
    )
    second_gathered = column_rows(second_normed.astype(jnp.bfloat16))

    def up_term(first_row, row_count):
        return jnp.dot(second_gathered, w_fc, preferred_element_type=jnp.float32)

    hidden = summed_over_row(up_term, seq_rows) + take_portion(fc_bias, col_place, hidden_col, 0)
    active, gelu_pull = jax.vjp(gelu_tanh, hidden)
    active_gathered = row_rows(active.astype(jnp.bfloat16))

    def down_term(first_row, row_count):
        return jnp.einsum("tf,df->td", active_gathered, w_proj, preferred_element_type=jnp.float32)

    final_rows = (
        middle
        + summed_over_col(down_term, local_rows)
        + take_portion(proj_bias, row_place, width_row, 0)
    )
    output = final_rows.astype(jnp.bfloat16)
    grad_gathered = column_rows(cotangent_local)
    w_proj_grad = jnp.einsum(
        "tf,td->df", active_gathered, grad_gathered, preferred_element_type=jnp.float32
    )

    def active_term(first_row, row_count):
        return jnp.einsum("td,df->tf", grad_gathered, w_proj, preferred_element_type=jnp.float32)

    hidden_grad = gelu_pull(summed_over_row(active_term, seq_rows))[0].astype(jnp.bfloat16)
    hidden_gathered = row_rows(hidden_grad)
    w_fc_grad = jnp.einsum(
        "td,tf->df", second_gathered, hidden_gathered, preferred_element_type=jnp.float32
    )

    def second_term(first_row, row_count):
        return jnp.einsum("tf,df->td", hidden_gathered, w_fc, preferred_element_type=jnp.float32)

    second_grad = summed_over_col(second_term, local_rows)
    middle_grad = grad_output + norm_backward(
        second_grad, second_unit, second_inverse, second_gain, feature_totals
    )
    ln2_gain_part = place_portion(jnp.sum(second_grad * second_unit, axis=0), row_place, D, 0)
    ln2_bias_part = place_portion(jnp.sum(second_grad, axis=0), row_place, D, 0)
    fc_bias_part = place_portion(jnp.sum(hidden_grad.astype(jnp.float32), axis=0), col_place, FF, 0)
    proj_bias_part = place_portion(jnp.sum(grad_output, axis=0), row_place, D, 0)
    branch_grad = middle_grad.astype(jnp.bfloat16)
    branch_gathered = column_rows(branch_grad)
    w_out_grad = jnp.einsum(
        "te,td->ed", attn_gathered, branch_gathered, preferred_element_type=jnp.float32
    )

    def attn_term(first_row, row_count):
        return jnp.einsum("td,ed->te", branch_gathered, w_out, preferred_element_type=jnp.float32)

    attn_grad = summed_over_row(attn_term, seq_rows).astype(jnp.bfloat16)
    qkv_grad = lax.map(
        attend_backward, (blocks, prefix, log_totals, attn_grad.reshape(seq_count, LEN, width_col))
    )
    qkv_grad = qkv_grad.reshape(seq_rows, 3, width_col)
    qkv_gathered = row_rows(qkv_grad)
    w_qkv_grad = jnp.einsum(
        "td,tse->sde", first_gathered, qkv_gathered, preferred_element_type=jnp.float32
    )

    def first_term(first_row, row_count):
        return jnp.einsum("tse,sde->td", qkv_gathered, w_qkv, preferred_element_type=jnp.float32)

    first_grad = summed_over_col(first_term, local_rows)
    input_grad = middle_grad + norm_backward(
        first_grad, first_unit, first_inverse, first_gain, feature_totals
    )
    qkv_totals = jnp.sum(qkv_grad.astype(jnp.float32), axis=0)
    qv_part = place_portion(jnp.stack([qkv_totals[0], qkv_totals[2]]), col_place, D, 1)
    out_bias_part = place_portion(jnp.sum(branch_grad.astype(jnp.float32), axis=0), row_place, D, 0)
    ln1_gain_part = place_portion(jnp.sum(first_grad * first_unit, axis=0), row_place, D, 0)
    ln1_bias_part = place_portion(jnp.sum(first_grad, axis=0), row_place, D, 0)
    vectors = lax.psum(
        (
            ln1_gain_part,
            ln1_bias_part,
            qv_part,
            out_bias_part,
            ln2_gain_part,
            ln2_bias_part,
            fc_bias_part,
            proj_bias_part,
        ),
        ("dp", "row", "col"),
    )
    matrices = (
        lax.psum(w_qkv_grad.astype(jnp.bfloat16), "dp").astype(jnp.float32),
        lax.psum(w_out_grad.astype(jnp.bfloat16), "dp").astype(jnp.float32),
        lax.psum(w_fc_grad.astype(jnp.bfloat16), "dp").astype(jnp.float32),
        lax.psum(w_proj_grad.astype(jnp.bfloat16), "dp").astype(jnp.float32),
    )
    return (
        output.T,
        input_grad.T,
        vectors[0],
        vectors[1],
        matrices[0],
        vectors[2],
        matrices[1],
        vectors[3],
        vectors[4],
        vectors[5],
        matrices[2],
        vectors[6],
        matrices[3],
        vectors[7],
    )


MESH = pl.DeviceIdType.MESH
WIDTH = 192
HALF = 96
QUARTER = 256
LANES = 128
WQ = 3 * WIDTH
VMEM_LIMIT = 67043328
REMOTES = 208
LOCALS = 64
FACTOR = HEAD_DIM ** (-0.5)
ANY = pl.BlockSpec(memory_space=pl.ANY)
GAIN1, BIAS1, OUT_BIAS, GAIN2, BIAS2, PROJ_BIAS, Q_BIAS, V_BIAS, FC_BIAS = range(9)
V_GAIN1, V_BIAS1, V_QUERY, V_VALUE, V_OUT, V_GAIN2, V_BIAS2, V_PROJ, V_FC = range(9)
CENTER, INVERSE = range(2)


def dot(left, right, left_axis, right_axis):
    return lax.dot_general(
        left, right, (((left_axis,), (right_axis,)), ((), ())), preferred_element_type=jnp.float32
    )


def low(value):
    return value.astype(jnp.bfloat16)


def wide(value):
    return value.astype(jnp.float32)


def aligned(start, size):
    return pl.ds(pl.multiple_of(start, size), size)


def merged(value):
    return value.reshape((value.shape[0] * value.shape[1],) + value.shape[2:])


def each(count, body):
    def step(i, carry):
        body(i)
        return carry

    lax.fori_loop(0, count, step, 0)


class Links:
    def __init__(self, send_sems, recv_sems, local_sems):
        self.d, self.r, self.c = (lax.axis_index(n) for n in ("dp", "row", "col"))
        self.send_sems, self.recv_sems, self.local_sems = send_sems, recv_sems, local_sems
        self.remotes = 0
        self.locals = 0

    def across(self, k):
        if k == 0:
            return self.r
        if k == 1:
            return self.r + 1 - 2 * lax.rem(self.r, 2)
        return lax.rem(self.r + 2, 4) if k == 2 else 3 - self.r

    def plane(self, k):
        return (self.d, self.across(k), self.c)

    def height(self, k):
        return lax.rem(self.c + k, 4)

    def column(self, k):
        return (self.d, self.r, self.height(k))

    def partner(self):
        return (1 - self.d, self.r, self.c)

    def half(self, mine=True):
        place = self.d if mine else 1 - self.d
        return pl.ds(pl.multiple_of(place * HALF, 16), HALF)

    def crossing(self, row, place):
        place = place + self.d * (3 - 2 * place)
        low_bit = lax.rem(lax.rem(row, 2) + lax.rem(place, 2), 2)
        return low_bit + 2 * lax.rem(lax.div(row, 2) + lax.div(place, 2), 2)

    def greet(self):
        devices = [self.partner(), *(self.plane(k) for k in (1, 2, 3))]
        devices += [self.column(k) for k in (1, 2, 3)]
        barrier = pltpu.get_barrier_semaphore()
        for device in devices:
            pl.semaphore_signal(barrier, 1, device_id=device, device_id_type=MESH)
        self.greeted = len(devices)

    def meet(self):
        pl.semaphore_wait(pltpu.get_barrier_semaphore(), self.greeted)

    def send(self, source, target, device):
        place = self.remotes
        self.remotes += 1
        copy = pltpu.make_async_remote_copy(
            src_ref=source,
            dst_ref=target,
            send_sem=self.send_sems.at[place],
            recv_sem=self.recv_sems.at[place],
            device_id=device,
            device_id_type=MESH,
        )
        copy.start()
        return copy

    def local(self, source, target):
        place = self.locals
        self.locals += 1
        copy = pltpu.make_async_copy(source, target, self.local_sems.at[place])
        copy.start()
        return copy


class Ticket:
    def __init__(self, links, device):
        self.place = links.remotes
        links.remotes += 1
        self.links, self.device = links, device

    def __call__(self, source, target):
        return pltpu.make_async_remote_copy(
            src_ref=source,
            dst_ref=target,
            send_sem=self.links.send_sems.at[self.place],
            recv_sem=self.links.recv_sems.at[self.place],
            device_id=self.device,
            device_id_type=MESH,
        )


class Move:
    def __init__(self, links, stays, source, target, device):
        self.stays = stays
        self.ticket = Ticket(links, device)
        self.source, self.target = source, target
        place = links.locals
        links.locals += 1
        self.local_sem = links.local_sems.at[place]

        @pl.when(jnp.logical_not(stays))
        def _():
            self.ticket(source, target).start()

        @pl.when(stays)
        def _():
            pltpu.make_async_copy(source, target, self.local_sem).start()

    def wait(self):
        @pl.when(jnp.logical_not(self.stays))
        def _():
            self.ticket(self.source, self.target).wait()

        @pl.when(self.stays)
        def _():
            pltpu.make_async_copy(self.source, self.target, self.local_sem).wait()


class PlaneGather:
    def __init__(self, links, target, in_parts=False):
        self.links, self.target = links, target
        rows = target.shape[1] // 2
        self.low, self.high = pl.ds(0, rows), pl.ds(rows, rows)
        first, second = target.at[links.r, self.low], target.at[links.r, self.high]
        self.x_low = links.send(first, first, links.plane(1))
        self.y_high = links.send(second, second, links.plane(2))
        if not in_parts:
            self.rest()

    def rest(self):
        links, target = self.links, self.target
        first, second = target.at[links.r, self.low], target.at[links.r, self.high]
        self.x_high = links.send(second, second, links.plane(1))
        self.y_low = links.send(first, first, links.plane(2))

    def relay(self):
        links = self.links
        self.x_low.wait_recv()
        block = self.target.at[links.across(1), self.low]
        self.on_y = links.send(block, block, links.plane(2))
        self.y_high.wait_recv()
        block = self.target.at[links.across(2), self.high]
        self.on_x = links.send(block, block, links.plane(1))

    def finish(self):
        self.x_high.wait_recv()
        self.y_low.wait_recv()
        for copy in (self.x_low, self.y_high, self.x_high, self.y_low):
            copy.wait_send()
        self.on_y.wait()
        self.on_x.wait()


class PlaneReduce:
    def __init__(self, links, part_of, rows, over_x, over_y, relayed):
        self.links, self.part_of = links, part_of
        self.halves = (pl.ds(0, rows // 2), pl.ds(rows // 2, rows // 2))
        self.over_x, self.over_y, self.relayed = over_x, over_y, relayed
        self.copies = {}

    def part(self, k, half):
        return self.part_of(self.links.across(k)).at[self.halves[half]]

    def give(self, k):
        links = self.links
        if k == 3:
            self.copies["x3"] = links.send(self.part(3, 0), self.over_x.at[1], links.plane(1))
            self.copies["y3"] = links.send(self.part(3, 1), self.over_y.at[1], links.plane(2))
        elif k == 1:
            self.copies["x1"] = links.send(self.part(1, 0), self.over_x.at[0], links.plane(1))
        elif k == 2:
            self.copies["y2"] = links.send(self.part(2, 1), self.over_y.at[0], links.plane(2))

    def relay(self):
        links = self.links
        self.copies["x3"].wait_recv()
        add_rows(self.over_x.at[1], [self.over_x.at[1], self.part(2, 0)])
        self.copies["xy"] = links.send(self.over_x.at[1], self.relayed.at[0], links.plane(2))
        self.copies["y3"].wait_recv()
        add_rows(self.over_y.at[1], [self.over_y.at[1], self.part(1, 1)])
        self.copies["yx"] = links.send(self.over_y.at[1], self.relayed.at[1], links.plane(1))

    def finish(self):
        for name in ("x3", "y3"):
            self.copies[name].wait_send()
        for name in ("x1", "y2", "xy", "yx"):
            self.copies[name].wait()

    def total(self, lanes):
        parts = []
        for half, over in ((0, self.over_x), (1, self.over_y)):
            value = wide(self.part(0, half)[:, lanes]) + wide(over[0, :, lanes])
            parts.append(value + wide(self.relayed[half, :, lanes]))
        return jnp.concatenate(parts, axis=0)


class Line:
    def __init__(self, links, block_of):
        self.links, self.block_of = links, block_of
        c = links.c
        self.up = [Ticket(links, (links.d, links.r, lax.rem(c + 1, 4))) for _ in range(3)]
        self.down = [Ticket(links, (links.d, links.r, lax.rem(c + 3, 4))) for _ in range(3)]

    def copy(self, ticket, place):
        return ticket(self.block_of(place), self.block_of(place))

    def step(self, t):
        c = self.links.c
        if t > 0:

            @pl.when(c >= t)
            def _():
                self.copy(self.up[t - 1], c - t).wait_recv()

            @pl.when(c <= 3 - t)
            def _():
                self.copy(self.down[t - 1], c + t).wait_recv()

        if t < 3:

            @pl.when(jnp.logical_and(c >= t, c < 3))
            def _():
                self.copy(self.up[t], c - t).start()

            @pl.when(jnp.logical_and(c <= 3 - t, c > 0))
            def _():
                self.copy(self.down[t], c + t).start()

    def finish(self):
        c = self.links.c
        for t in range(3):

            @pl.when(jnp.logical_and(c >= t, c < 3))
            def _(t=t):
                self.copy(self.up[t], c - t).wait_send()

            @pl.when(jnp.logical_and(c <= 3 - t, c > 0))
            def _(t=t):
                self.copy(self.down[t], c + t).wait_send()


class WeightGather:
    def __init__(self, links, stage, moved, target, pieces=1):
        self.links, self.moved, self.target = links, moved, target
        r, c = links.r, links.c
        self.mine = links.half()
        self.goal = links.crossing(r, c)
        size = HALF // pieces
        self.local_rows = [pl.ds(i * size, size) for i in range(pieces)]
        start = links.d * HALF
        self.rows = [pl.ds(pl.multiple_of(start + i * size, 16), size) for i in range(pieces)]
        device = (links.d, r, self.goal)
        self.turns = [
            Move(links, self.goal == c, stage.at[rows], moved.at[rows], device)
            for rows in self.local_rows
        ]

    def hop(self):
        links = self.links
        device = (links.d, self.goal, links.c)
        for i, rows in enumerate(self.local_rows):
            self.turns[i].wait()
            block = self.target.at[links.r, self.rows[i]]
            self.turns[i] = Move(links, self.goal == links.r, self.moved.at[rows], block, device)

    def begin(self):
        links = self.links

        def block_of(rows):
            return lambda place: self.target.at[links.crossing(links.r, place), rows]

        self.ways = []
        for turn, rows in zip(self.turns, self.rows):
            turn.wait()
            self.ways.append(Line(links, block_of(rows)))
            self.ways[-1].step(0)

    def line(self, t):
        if t == 0:
            self.begin()
        else:
            for way in self.ways:
                way.step(t)

    def share(self):
        for way in self.ways:
            way.finish()
        block = self.target.at[:, self.mine]
        self.shared = self.links.send(block, block, self.links.partner())

    def finish(self):
        self.shared.wait()


class SquareGather(WeightGather):
    def __init__(self, links, target):
        self.links, self.target = links, target
        self.mine = links.half()
        self.plane = PlaneGather(links, target.at[:, links.c, self.mine])

    def begin(self):
        self.plane.finish()
        self.ways = [Line(self.links, lambda place: self.target.at[:, place, self.mine])]
        self.ways[0].step(0)

    def share(self):
        self.ways[0].finish()
        block = self.target.at[:, :, self.mine]
        self.shared = self.links.send(block, block, self.links.partner())


def add_rows(target, terms):
    def step(i):
        place = aligned(i * 16, 16)
        total = wide(terms[0][place, :])
        for term in terms[1:]:
            total = total + wide(term[place, :])
        target[place, :] = total.astype(target.dtype)

    each(target.shape[0] // 16, step)


def add_blocks(target, terms):
    if len(target.shape) == 2:
        add_rows(target, terms)
    else:
        each(target.shape[0], lambda i: add_blocks(target.at[i], [term.at[i] for term in terms]))


class LineReduce:
    def __init__(self, links, block_of, up, down):
        self.links, self.block_of, self.up, self.down = links, block_of, up, down
        c = links.c
        self.rise = [Ticket(links, (links.d, links.r, lax.rem(c + 1, 4))) for _ in range(3)]
        self.fall = [Ticket(links, (links.d, links.r, lax.rem(c + 3, 4))) for _ in range(3)]

    def step(self, t):
        c = self.links.c
        for i in range(t + 1):
            goal = 3 - t + i
            self.pass_on(c == i, self.rise[goal - 1], self.up.at[goal - 1], goal, i > 0)
            goal = t - i
            self.pass_on(c == 3 - i, self.fall[goal], self.down.at[goal], goal, i > 0)

    def pass_on(self, here, ticket, slot, goal, adds):
        @pl.when(here)
        def _():
            if adds:
                ticket(slot, slot).wait_recv()
                add_blocks(slot, [slot, self.block_of(goal)])
                ticket(slot, slot).start()
            else:
                ticket(self.block_of(goal), slot).start()

    def total(self, target):
        c = self.links.c
        for goal in range(4):

            @pl.when(c == goal)
            def _(goal=goal):
                terms = [self.block_of(goal)]
                if goal > 0:
                    slot = self.up.at[goal - 1]
                    self.rise[goal - 1](slot, slot).wait_recv()
                    terms.append(slot)
                if goal < 3:
                    slot = self.down.at[goal]
                    self.fall[goal](slot, slot).wait_recv()
                    terms.append(slot)
                add_blocks(target, terms)

        for i in range(3):
            rising, falling = self.up.at[i], self.down.at[i]

            @pl.when(c < i + 1)
            def _(i=i, slot=rising):
                self.rise[i](slot, slot).wait_send()

            @pl.when(c > i)
            def _(i=i, slot=falling):
                self.fall[i](slot, slot).wait_send()


class WeightReduce:
    def __init__(self, links, grad, near, sums, up, down, fin, moved, arrived, result, pieces=1):
        self.links, self.grad, self.near, self.sums = links, grad, near, sums
        self.up, self.down, self.fin = up, down, fin
        self.moved, self.arrived, self.result = moved, arrived, result
        size = HALF // pieces
        self.rows = [pl.ds(i * size, size) for i in range(pieces)]
        self.to_near = [self.send_near(i * size, size) for i in range(pieces)]

    def send_near(self, first, size):
        links = self.links
        other = pl.ds(pl.multiple_of((1 - links.d) * HALF + first, 16), size)
        rows = pl.ds(first, size)
        return links.send(self.grad.at[:, other], self.near.at[:, rows], links.partner())

    def add_near(self):
        links = self.links

        def block_of(rows):
            return lambda place: self.sums.at[links.crossing(links.r, place), rows]

        self.ways = []
        for copy, rows in zip(self.to_near, self.rows):
            copy.wait()
            first = links.d * HALF + rows.start
            mine = pl.ds(pl.multiple_of(first, 16), rows.size)
            each(
                4,
                lambda b, rows=rows, mine=mine: add_rows(
                    self.sums.at[b, rows], [self.grad.at[b, mine], self.near.at[b, rows]]
                ),
            )
            up, down = self.up.at[:, rows], self.down.at[:, rows]
            self.ways.append(LineReduce(links, block_of(rows), up, down))

    def line(self, i):
        for way in self.ways:
            way.step(i)

    def hop(self):
        links = self.links
        self.goal = links.crossing(links.r, links.c)
        device = (links.d, self.goal, links.c)
        self.turns = []
        for way, rows in zip(self.ways, self.rows):
            way.total(self.fin.at[rows])
            stays = self.goal == links.r
            self.turns.append(Move(links, stays, self.fin.at[rows], self.moved.at[rows], device))

    def back(self):
        links = self.links
        device = (links.d, links.r, self.goal)
        for i, rows in enumerate(self.rows):
            self.turns[i].wait()
            stays = self.goal == links.c
            self.turns[i] = Move(links, stays, self.moved.at[rows], self.arrived.at[rows], device)

    def share(self):
        for turn in self.turns:
            turn.wait()
        self.give(self.arrived)

    def give(self, total):
        links, mine = self.links, self.links.half()
        self.last = [
            links.send(total, self.result.at[mine], links.partner()),
            links.local(total, self.result.at[mine]),
        ]

    def finish(self):
        for copy in self.last:
            copy.wait()


class SquareReduce(WeightReduce):
    def __init__(self, links, grad, near, sums, up, down, fin, came, arrived, result):
        self.links, self.grad, self.near, self.sums = links, grad, near, sums
        self.up, self.down, self.fin = up, down, fin
        self.came, self.arrived, self.result = came, arrived, result
        self.to_near = links.send(grad.at[:, :, links.half(False)], near, links.partner())

    def add_near(self):
        mine = self.links.half()
        self.to_near.wait()
        add_blocks(self.sums, [self.grad.at[:, :, mine], self.near])
        self.ways = [
            LineReduce(self.links, lambda place: self.sums.at[:, place], self.up, self.down)
        ]

    def hop(self):
        links = self.links
        self.ways[0].total(self.fin)
        self.crossing = [
            links.send(self.fin.at[links.across(k)], self.came.at[k - 1], links.plane(k))
            for k in (3, 1, 2)
        ]

    def back(self):
        for copy in self.crossing:
            copy.wait()
        came = self.came
        add_rows(self.arrived, [self.fin.at[self.links.r], came.at[0], came.at[1], came.at[2]])

    def share(self):
        self.give(self.arrived)


def normalize(source_of, target, stats, gain, offset):
    def step(j):
        lanes = aligned(j * LANES, LANES)
        values = source_of(lanes)
        center = jnp.sum(values, axis=0, keepdims=True) / D
        square = jnp.sum(values * values, axis=0, keepdims=True) / D
        inverse = lax.rsqrt(square - center * center + epsilon)
        stats[CENTER : CENTER + 1, lanes] = center
        stats[INVERSE : INVERSE + 1, lanes] = inverse
        target[:, lanes] = low((values - center) * inverse * gain[...] + offset[...])

    each(LEN // LANES, step)


def key_span(block):
    return max(512, (block + 1) * QUARTER), block * QUARTER


def visible(block, first, last, limit_value):
    shape = (last - first, QUARTER)
    keys = lax.broadcasted_iota(jnp.int32, shape, 0) + first
    queries = lax.broadcasted_iota(jnp.int32, shape, 1) + block * QUARTER
    return (keys <= queries) | (keys < limit_value)


def masked(value, block, limit_value, fill):
    last, first = key_span(block)
    tail = jnp.where(visible(block, first, last, limit_value), value[first:], fill)
    return jnp.concatenate([value[:first], tail], axis=0) if first else tail


def head_rows(h, part):
    return pl.ds(h * HEAD_DIM + part * WIDTH, HEAD_DIM)


def attend(qkv, limit_value, attn_of, log_total, between):
    def head(h):
        for block in range(4):
            for action in between.get(h * 4 + block, ()):
                action()
            last, _ = key_span(block)
            lanes = slice(block * QUARTER, (block + 1) * QUARTER)
            queries = qkv[head_rows(h, 0), lanes] * jnp.bfloat16(FACTOR)
            scores = dot(qkv[head_rows(h, 1), :last], queries, 0, 0)
            scores = masked(scores, block, limit_value, masked_score)
            largest = jnp.max(scores, axis=0, keepdims=True)
            weights = jnp.exp(scores - largest)
            total = jnp.sum(weights, axis=0, keepdims=True)
            mixed = dot(qkv[head_rows(h, 2), :last], low(weights), 1, 0)
            attn_of(head_rows(h, 0), lanes, low(mixed * (1.0 / total)))
            log_total[pl.ds(h, 1), lanes] = largest + jnp.log(total)

    for h in range(3):
        head(h)


def attend_back(
    qkv, limit_value, attn_of, log_total, out_grad, qkv_grad, key_sum, value_sum, between
):
    def head(h):
        for block in (3, 2, 1, 0):
            for action in between.get(h * 4 + 3 - block, ()):
                action()
            last, _ = key_span(block)
            lanes = slice(block * QUARTER, (block + 1) * QUARTER)
            queries = qkv[head_rows(h, 0), lanes] * jnp.bfloat16(FACTOR)
            grads = out_grad[head_rows(h, 0), lanes]
            inner = jnp.sum(
                wide(attn_of(head_rows(h, 0), lanes)) * wide(grads), axis=0, keepdims=True
            )
            scores = dot(qkv[head_rows(h, 1), :last], queries, 0, 0)
            probs = jnp.exp(scores - log_total[pl.ds(h, 1), lanes])
            probs = masked(probs, block, limit_value, 0.0)
            weight_grad = dot(qkv[head_rows(h, 2), :last], grads, 0, 0)
            score_grad = low(probs * (weight_grad - inner))
            query_grad = dot(qkv[head_rows(h, 1), :last], score_grad, 1, 0) * FACTOR
            qkv_grad[head_rows(h, 0), lanes] = low(query_grad)
            key_grad = dot(queries, score_grad, 1, 1)
            value_grad = dot(grads, low(probs), 1, 1)
            if block == 3:
                key_sum[...] = key_grad
                value_sum[...] = value_grad
            else:
                key_sum[:, :last] += key_grad
                value_sum[:, :last] += value_grad
        qkv_grad[head_rows(h, 1), :] = low(key_sum[...])
        qkv_grad[head_rows(h, 2), :] = low(value_sum[...])

    for h in range(3):
        head(h)


def gelu_parts(u):
    slope = (2.0 / 3.141592653589793) ** 0.5
    square = u * u
    bent = jnp.tanh(slope * u * (1.0 + 0.044715 * square))
    shared = 0.5 * (1.0 + bent)
    derivative = shared + 0.5 * u * (1.0 - bent * bent) * (slope * (1.0 + 3.0 * 0.044715 * square))
    return u * shared, derivative


def block_kernel(
    limit, tok, gain1_in, bias1_in, wq_in, qv_in, wo_in, out_in, gain2_in, bias2_in,
    wf_in, fc_in, wp_in, proj_in, cot,
    out_hbm, grad_hbm, wq_hbm, wf_hbm, wp_hbm, wo_hbm, vec_hbm,
    rows1, qv, fc, wq_here, xt, gt, wqa, wfa, wpa, woa, zq, zf, zp, mq, mf, mp, pres, colb,
    fn, qkv, at, lse, st1, st2, mid, sn, act, slope, op, hg, sp,
    x2, y2, z2, x_out, y_out, z_out, x1, y1, z1, br, ap, dout, brf, dqkv, ksum, vsum,
    gf, gp, gq, near_f, near_p, near_q, sum_f, sum_p, sum_q, up_f, up_p, up_q, dn_f, dn_p, dn_q,
    fin_f, fin_p, fin_q, hop_f, hop_p, hop_q, got_f, got_p, got_q,
    sq, near_o, sum_o, up_o, dn_o, fin_o, hop_o, got_o,
    fgp, vcol, vec, vec_in, stat, stat_in, out_v, grad_v,
    send_sems, recv_sems, local_sems,
):
    links = Links(send_sems, recv_sems, local_sems)
    r, c = links.r, links.c
    mine = links.half()
    own = aligned(r * QUARTER, QUARTER)
    links.greet()
    singles = (gain1_in, bias1_in, out_in, gain2_in, bias2_in, proj_in)
    first = [links.local(wq_in.at[:, mine], wq_here), links.local(tok, xt.at[r])]
    first += [links.local(source, rows1.at[i]) for i, source in enumerate(singles)]
    first += [links.local(qv_in, qv), links.local(fc_in, fc)]
    then = [links.local(wf_in.at[mine], zf), links.local(wp_in.at[mine], zp)]
    then += [links.local(wo_in.at[mine], woa.at[r, c, mine]), links.local(cot, gt.at[r])]
    for copy in first:
        copy.wait()
    zq[...] = jnp.concatenate([wq_here[i] for i in range(3)], axis=1)
    pres[r] = jnp.full((8, LANES), limit[0], jnp.int32)

    def column(kind, place, values):
        spread = jnp.broadcast_to(values[None, :], (LANES, LANES))
        colb[kind, pl.ds(place * LANES, LANES)] = spread.T

    for place in range(D // LANES):
        part = pl.ds(place * LANES, LANES)
        for kind in range(len(singles)):
            column(kind, place, rows1[kind, part])
        column(Q_BIAS, place, qv[0, part])
        column(V_BIAS, place, qv[1, part])
        column(FC_BIAS, place, fc[pl.ds(pl.multiple_of(r * D + place * LANES, LANES), LANES)])
    links.meet()

    get_q = WeightGather(links, zq, mq, wqa, 3)
    tokens = PlaneGather(links, xt, in_parts=True)
    for copy in then:
        copy.wait()
    get_q.hop()
    tokens.rest()
    get_f = WeightGather(links, zf, mf, wfa)
    prefixes = [links.send(pres.at[r], pres.at[r], links.plane(k)) for k in (1, 2, 3)]
    get_q.line(0)
    tokens.relay()
    get_o = SquareGather(links, woa)
    get_q.line(1)
    get_p = WeightGather(links, zp, mp, wpa)
    get_o.plane.relay()
    get_q.line(2)
    get_o.line(0)
    get_q.line(3)
    get_q.share()
    tokens.finish()
    grads = PlaneGather(links, gt)
    get_f.hop()
    get_p.hop()
    normalize(
        lambda lanes: wide(merged(xt[:, :, lanes])), fn, st1, colb.at[GAIN1], colb.at[BIAS1]
    )
    for copy in prefixes:
        copy.wait()
    get_q.finish()
    head_bias = aligned(r * WIDTH, WIDTH)

    def project(b):
        lanes = aligned(b * QUARTER, QUARTER)
        nothing = jnp.zeros((WIDTH, LANES), jnp.float32)
        bias = [colb[Q_BIAS, head_bias], nothing, colb[V_BIAS, head_bias]]
        bias = jnp.concatenate(bias, axis=0)
        value = dot(merged(wqa[...]), fn[:, lanes], 0, 0)
        qkv[:, lanes] = low(value + jnp.concatenate([bias, bias], axis=1))

    each(4, project)
    limit_value = pres[c][0:1, 0:1]

    def put_attn(rows, lanes, value):
        at[r, rows, lanes] = value

    def get_attn(rows, lanes):
        return at[r, rows, lanes]

    attns = []

    def gather_head(h):
        attns.append(PlaneGather(links, at.at[:, h * HEAD_DIM : (h + 1) * HEAD_DIM]))

    attend(
        qkv,
        limit_value,
        put_attn,
        lse,
        {
            0: [lambda: get_o.line(1)],
            3: [lambda: get_f.line(0)],
            4: [lambda: gather_head(0), grads.relay],
            7: [lambda: get_o.line(2)],
            8: [lambda: gather_head(1), lambda: attns[0].relay()],
            10: [lambda: get_f.line(1)],
        },
    )
    gather_head(2)
    attns[1].relay()
    get_o.line(3)
    get_o.share()
    get_f.line(2)
    get_p.line(0)
    attns[2].relay()
    get_f.line(3)
    get_f.share()
    get_p.line(1)
    get_o.finish()
    for attn in attns:
        attn.finish()

    def join(i):
        b, lanes = lax.div(i, 4), aligned(lax.rem(i, 4) * QUARTER, QUARTER)
        rows = aligned(b * WIDTH, WIDTH)
        bias = colb[OUT_BIAS, rows]
        value = dot(merged(woa[b]), merged(at[:, :, lanes]), 0, 0)
        mid[rows, lanes] = wide(xt[b, :, lanes]) + (value + jnp.concatenate([bias, bias], axis=1))

    each(16, join)
    get_p.line(2)
    normalize(lambda lanes: mid[:, lanes], sn, st2, colb.at[GAIN2], colb.at[BIAS2])
    get_f.finish()

    def up(b):
        lanes = aligned(b * QUARTER, QUARTER)
        bias = colb[FC_BIAS]
        value = dot(merged(wfa[...]), sn[:, lanes], 0, 0) + jnp.concatenate([bias, bias], axis=1)
        value, derivative = gelu_parts(value)
        act[:, lanes] = low(value)
        slope[:, lanes] = derivative

    each(2, up)
    get_p.line(3)
    get_p.share()
    each(2, lambda b: up(b + 2))
    grads.finish()

    def proj_grads(b):
        gp[b] = low(dot(gt[b], act[...], 1, 1))

    each(4, proj_grads)
    put_p = WeightReduce(links, gp, near_p, sum_p, up_p, dn_p, fin_p, hop_p, got_p, wp_hbm)
    get_p.finish()

    seconds = PlaneReduce(
        links, lambda place: sp.at[:, aligned(place * QUARTER, QUARTER)], D, x2, y2, z2
    )
    for k in (3, 1, 2, 0):
        lanes = aligned(links.across(k) * QUARTER, QUARTER)
        value = dot(merged(wpa[...]), merged(gt[:, :, lanes]), 0, 0)
        hg[:, lanes] = low(value * slope[:, lanes])
        sp[:, lanes] = low(dot(merged(wfa[...]), hg[:, lanes], 1, 0))
        seconds.give(k)
        if k == 3:
            put_p.add_near()
            put_p.line(0)

    def fc_grads(b):
        gf[b] = low(dot(sn[aligned(b * WIDTH, WIDTH), :], hg[...], 1, 1))

    each(4, fc_grads)
    put_f = WeightReduce(links, gf, near_f, sum_f, up_f, dn_f, fin_f, hop_f, got_f, wf_hbm)
    seconds.relay()
    put_p.line(1)

    def down(b):
        lanes = aligned(b * QUARTER, QUARTER)
        value = low(dot(merged(wpa[...]), act[:, lanes], 1, 0))
        op[:, :, lanes] = value.reshape(4, WIDTH, QUARTER)

    each(4, down)
    outs = PlaneReduce(links, lambda place: op.at[place], WIDTH, x_out, y_out, z_out)
    put_f.add_near()
    put_f.line(0)
    lane = lax.broadcasted_iota(jnp.int32, (D, LANES), 1)
    total = jnp.zeros((D, 1), jnp.float32)
    for b in range(4):
        lanes = slice(b * QUARTER, (b + 1) * QUARTER)
        total = total + jnp.sum(wide(hg[:, lanes]), axis=1, keepdims=True)
    vcol[...] = jnp.where(lane == V_FC + r, total, 0.0)
    put_p.line(2)
    seconds.finish()

    def back(j):
        lanes = aligned(r * QUARTER + j * LANES, LANES)
        part = aligned(j * LANES, LANES)
        given = seconds.total(part)
        inverse = st2[INVERSE : INVERSE + 1, lanes]
        unit = (mid[:, lanes] - st2[CENTER : CENTER + 1, lanes]) * inverse
        scaled = given * colb[GAIN2]
        plain = jnp.sum(scaled, axis=0, keepdims=True) / D
        cross = jnp.sum(scaled * unit, axis=0, keepdims=True) / D
        above = wide(merged(gt[:, :, lanes]))
        branch = low(above + inverse * (scaled - plain - unit * cross))
        br[:, :, part] = branch.reshape(4, WIDTH, LANES)
        value = jnp.where(lane == V_GAIN2, jnp.sum(given * unit, axis=1, keepdims=True), 0.0)
        value = jnp.where(lane == V_BIAS2, jnp.sum(given, axis=1, keepdims=True), value)
        value = jnp.where(lane == V_OUT, jnp.sum(wide(branch), axis=1, keepdims=True), value)
        value = jnp.where(lane == V_PROJ, jnp.sum(above, axis=1, keepdims=True), value)
        vcol[...] = vcol[...] + value

    for j in range(2):
        back(j)
    value = dot(merged(woa[0]), br[0], 1, 0)
    for b in range(1, 4):
        value = value + dot(merged(woa[b]), br[b], 1, 0)
    ap[...] = low(value).reshape(4, WIDTH, QUARTER)
    turns = [
        links.send(ap.at[links.across(k)], dout.at[:, own], links.plane(k)) for k in (3, 1, 2)
    ]
    turns.append(links.local(ap.at[r], dout.at[:, own]))
    swaps = [
        links.send(br.at[links.across(k)], brf.at[:, own], links.plane(k)) for k in (3, 1, 2)
    ]
    swaps.append(links.local(br.at[r], brf.at[:, own]))

    def square_grads(b):
        value = low(dot(merged(at[:, :, own]), br[b], 1, 1))
        sq[b] = value.reshape(4, WIDTH, WIDTH)

    each(4, square_grads)
    put_o = SquareReduce(links, sq, near_o, sum_o, up_o, dn_o, fin_o, hop_o, got_o, wo_hbm)
    put_f.line(1)
    put_o.add_near()
    put_p.hop()
    for copy in turns:
        copy.wait()
    for k in (3, 1, 2):
        outs.give(k)
    attend_back(
        qkv, limit_value, get_attn, lse, dout, dqkv, ksum, vsum,
        {
            1: [lambda: put_o.line(0)],
            2: [lambda: put_f.line(2)],
            4: [put_p.back],
            5: [outs.relay],
            7: [lambda: put_o.line(1)],
            9: [put_f.hop, put_p.share],
            11: [lambda: put_o.line(2)],
        },
    )

    def query_grads(b):
        gq[b] = low(dot(fn[aligned(b * WIDTH, WIDTH), :], dqkv[...], 1, 1))

    each(4, query_grads)
    put_q = WeightReduce(links, gq, near_q, sum_q, up_q, dn_q, fin_q, hop_q, got_q, wq_hbm, 3)

    stat[...] = jnp.zeros_like(stat)
    firsts = PlaneReduce(links, lambda place: fgp.at[place], WIDTH, x1, y1, z1)
    for k in (3, 1, 2, 0):
        b = links.across(k)
        rows = aligned(b * WIDTH, WIDTH)

        def first_part(j, b=b, rows=rows):
            lanes = aligned(j * QUARTER, QUARTER)
            value = dot(wqa[b], dqkv[:, lanes], 1, 0)
            fgp[b, :, lanes] = low(value)
            for i in range(2):
                half = aligned(j * QUARTER + i * LANES, LANES)
                piece = value[:, i * LANES : (i + 1) * LANES]
                unit = wide(xt[b, :, half]) - st1[CENTER : CENTER + 1, half]
                unit = unit * st1[INVERSE : INVERSE + 1, half]
                weighted = piece * unit
                gain = colb[GAIN1, rows]
                stat[0:1, half] += jnp.sum(piece * gain, axis=0, keepdims=True)
                stat[1:2, half] += jnp.sum(weighted * gain, axis=0, keepdims=True)
                spot = lane[:WIDTH]
                add = jnp.where(spot == V_GAIN1, jnp.sum(weighted, axis=1, keepdims=True), 0.0)
                add = jnp.where(spot == V_BIAS1, jnp.sum(piece, axis=1, keepdims=True), add)
                vcol[rows, :] = vcol[rows, :] + add

        each(4, first_part)
        firsts.give(k)
        if k == 3:
            put_q.add_near()
            put_q.line(0)
        elif k == 1:
            put_f.back()
        elif k == 2:
            put_q.line(1)
            firsts.relay()
    stat_sends = [links.send(stat, stat_in.at[k - 1], links.plane(k)) for k in (1, 2, 3)]
    put_q.line(2)
    put_o.hop()
    rows = aligned(r * WIDTH, WIDTH)
    spot = lane[:WIDTH]
    query = jnp.zeros((WIDTH, 1), jnp.float32)
    value = jnp.zeros((WIDTH, 1), jnp.float32)
    for b in range(4):
        lanes = slice(b * QUARTER, (b + 1) * QUARTER)
        query = query + jnp.sum(wide(dqkv[:WIDTH, lanes]), axis=1, keepdims=True)
        value = value + jnp.sum(wide(dqkv[2 * WIDTH :, lanes]), axis=1, keepdims=True)
    add = jnp.where(spot == V_QUERY, query, jnp.where(spot == V_VALUE, value, 0.0))
    vcol[rows, :] = vcol[rows, :] + add
    vec[0] = vcol[...].T[:16]
    vec_near = links.send(vec.at[0], vec_in.at[0], links.partner())
    put_f.share()
    put_q.hop()
    vec_near.wait()
    vec[1] = vec[0] + vec_in[0]
    vec_plane = [links.send(vec.at[1], vec_in.at[k], links.plane(k)) for k in (1, 2, 3)]
    put_o.back()
    put_o.share()
    put_q.back()
    for copy in vec_plane:
        copy.wait()
    vec[2] = vec[1] + vec_in[1] + vec_in[2] + vec_in[3]
    vec_high = [links.send(vec.at[2], vec_in.at[3 + k], links.column(k)) for k in (1, 2, 3)]
    outs.finish()

    def last_out(j):
        lanes = aligned(j * LANES, LANES)
        value = mid[rows, lanes] + colb[PROJ_BIAS, rows] + outs.total(lanes)
        out_v[:, lanes] = low(value)

    each(LEN // LANES, last_out)
    ends = [links.local(out_v, out_hbm)]
    for copy in swaps + stat_sends:
        copy.wait()
    firsts.finish()
    stat[...] = stat[...] + stat_in[0] + stat_in[1] + stat_in[2]

    def last_grad(j):
        lanes = aligned(j * LANES, LANES)
        inverse = st1[INVERSE : INVERSE + 1, lanes]
        unit = (wide(xt[r, :, lanes]) - st1[CENTER : CENTER + 1, lanes]) * inverse
        value = firsts.total(lanes) * colb[GAIN1, rows] - stat[0:1, lanes] / D
        grad_v[:, lanes] = wide(brf[:, lanes]) + inverse * (value - unit * (stat[1:2, lanes] / D))

    each(LEN // LANES, last_grad)
    ends.append(links.local(grad_v, grad_hbm))
    put_q.share()
    for copy in vec_high:
        copy.wait()
    vec[3] = vec[2] + vec_in[4] + vec_in[5] + vec_in[6]
    ends.append(links.local(vec.at[3], vec_hbm))
    for copy in ends:
        copy.wait()
    for put in (put_f, put_p, put_o, put_q):
        put.finish()


def run_block(*arguments):
    narrow, full = jnp.bfloat16, jnp.float32
    vmem = pltpu.VMEM
    sequence, tall = (4, WIDTH, LEN), (D, LEN)

    def thirds(lead=()):
        return [vmem(lead + (HALF, width), narrow) for width in (D, D, WQ)]

    def plane_sums(rows, lanes):
        return [vmem((2, rows // 2, lanes), narrow) for _ in range(3)]

    scratch = [
        vmem((6, D), full), vmem((2, D), full), vmem((FF,), full), vmem((3, HALF, WIDTH), narrow),
        vmem(sequence, narrow), vmem(sequence, narrow),
        vmem((4, WIDTH, WQ), narrow), vmem((4, WIDTH, D), narrow), vmem((4, WIDTH, D), narrow),
        vmem((4, 4, WIDTH, WIDTH), narrow),
        vmem((HALF, WQ), narrow), vmem((HALF, D), narrow), vmem((HALF, D), narrow),
        vmem((HALF, WQ), narrow), vmem((HALF, D), narrow), vmem((HALF, D), narrow),
        vmem((4, 8, LANES), jnp.int32), vmem((9, D, LANES), full),
        vmem(tall, narrow), vmem((WQ, LEN), narrow), vmem(sequence, narrow),
        vmem((8, LEN), full), vmem((8, LEN), full), vmem((8, LEN), full),
        vmem(tall, full), vmem(tall, narrow), vmem(tall, narrow), vmem(tall, full),
        vmem(sequence, narrow), vmem(tall, narrow), vmem(tall, narrow),
        *plane_sums(D, QUARTER), *plane_sums(WIDTH, LEN), *plane_sums(WIDTH, LEN),
        vmem((4, WIDTH, QUARTER), narrow), vmem((4, WIDTH, QUARTER), narrow),
        vmem((WIDTH, LEN), narrow), vmem((WIDTH, LEN), narrow), vmem((WQ, LEN), narrow),
        vmem((HEAD_DIM, LEN), full), vmem((HEAD_DIM, LEN), full),
        vmem((4, WIDTH, D), narrow), vmem((4, WIDTH, D), narrow), vmem((4, WIDTH, WQ), narrow),
        *thirds((4,)), *thirds((4,)), *thirds((3,)), *thirds((3,)), *thirds(), *thirds(), *thirds(),
        vmem((4, 4, WIDTH, WIDTH), narrow), vmem((4, 4, HALF, WIDTH), narrow),
        vmem((4, 4, HALF, WIDTH), narrow), vmem((3, 4, HALF, WIDTH), narrow),
        vmem((3, 4, HALF, WIDTH), narrow), vmem((4, HALF, WIDTH), narrow),
        vmem((3, HALF, WIDTH), narrow), vmem((HALF, WIDTH), narrow),
        vmem(sequence, narrow), vmem((D, LANES), full),
        vmem((4, 16, D), full), vmem((7, 16, D), full), vmem((8, LEN), full), vmem((3, 8, LEN), full),
        vmem((WIDTH, LEN), narrow), vmem((WIDTH, LEN), full),
        pltpu.SemaphoreType.DMA((REMOTES,)), pltpu.SemaphoreType.DMA((REMOTES,)),
        pltpu.SemaphoreType.DMA((LOCALS,)),
    ]
    results = [
        ((WIDTH, LEN), narrow), ((WIDTH, LEN), full), ((WIDTH, WQ), narrow), ((WIDTH, D), narrow),
        ((WIDTH, D), narrow), ((WIDTH, WIDTH), narrow), ((16, D), full),
    ]
    return pl.pallas_call(
        block_kernel,
        out_shape=[jax.ShapeDtypeStruct(*result) for result in results],
        in_specs=[pl.BlockSpec(memory_space=pltpu.SMEM)] + [ANY] * (len(arguments) - 1),
        out_specs=[ANY] * len(results),
        scratch_shapes=scratch,
        compiler_params=pltpu.CompilerParams(
            collective_id=0, has_side_effects=True, vmem_limit_bytes=VMEM_LIMIT
        ),
        name="block",
    )(*arguments)


def finish_kernel(
    out, grad, wq, wf, wp, wo, vec,
    out_done, grad_done, gain1, bias1, wq_done, qv, wo_done, out_bias, gain2, bias2,
    wf_done, fc, wp_done, proj,
):
    out_done[...] = out[...]
    grad_done[...] = grad[...]
    for i in range(3):
        wq_done[i] = wide(wq[:, i * WIDTH : (i + 1) * WIDTH])
    wo_done[...] = wide(wo[...])
    wf_done[...] = wide(wf[...])
    wp_done[...] = wide(wp[...])
    singles = ((gain1, V_GAIN1), (bias1, V_BIAS1), (out_bias, V_OUT), (gain2, V_GAIN2))
    for target, row in singles + ((bias2, V_BIAS2), (proj, V_PROJ)):
        target[...] = vec[row]
    qv[...] = vec[V_QUERY : V_VALUE + 1]
    for i in range(4):
        fc[pl.ds(i * D, D)] = vec[V_FC + i]


def plane_device(
    tokens, prefix, ln1_gain, ln1_bias, w_qkv, qv_bias, w_out, out_bias,
    ln2_gain, ln2_bias, w_fc, fc_bias, w_proj, proj_bias, cotangent,
):
    pieces = run_block(
        prefix, tokens, ln1_gain, ln1_bias, w_qkv, qv_bias, w_out, out_bias,
        ln2_gain, ln2_bias, w_fc, fc_bias, w_proj, proj_bias, cotangent,
    )
    wide_results = [
        (WIDTH, LEN), (D,), (D,), (3, WIDTH, WIDTH), (2, D), (WIDTH, WIDTH), (D,), (D,), (D,),
        (WIDTH, D), (FF,), (WIDTH, D), (D,),
    ]
    results = [jax.ShapeDtypeStruct((WIDTH, LEN), jnp.bfloat16)]
    results += [jax.ShapeDtypeStruct(dims, jnp.float32) for dims in wide_results]
    return pl.pallas_call(
        finish_kernel,
        out_shape=results,
        in_specs=[pl.BlockSpec(memory_space=pltpu.VMEM)] * len(pieces),
        out_specs=[pl.BlockSpec(memory_space=pltpu.VMEM)] * len(results),
        name="results",
    )(*pieces)


def solution(mesh):
    on_device = plane_device if dict(mesh.shape) == {"dp": 2, "row": 4, "col": 4} else general_device
    placed = (
        P("row", ("dp", "col")),
        P(("dp", "row")),
        P(),
        P(),
        P(None, "row", "col"),
        P(),
        P("col", "row"),
        P(),
        P(),
        P(),
        P("row", "col"),
        P(),
        P("row", "col"),
        P(),
        P("row", ("dp", "col")),
    )
    return jax.shard_map(
        on_device,
        mesh=mesh,
        in_specs=placed,
        out_specs=(
            P("row", ("dp", "col")),
            P("row", ("dp", "col")),
            P(),
            P(),
            P(None, "row", "col"),
            P(),
            P("col", "row"),
            P(),
            P(),
            P(),
            P("row", "col"),
            P(),
            P("row", "col"),
            P(),
        ),
        check_vma=False,
    )
```

```python
import functools

import jax
import jax.numpy as jnp
from jax import lax
from jax.experimental import pallas as pl
from jax.experimental.pallas import tpu as pltpu
from jax.sharding import PartitionSpec as P

D = 768
FF = 3072
HEAD_DIM = 64
LEN = 1024


epsilon = 1e-05
masked_score = -1e30


def feature_totals(values):
    return lax.psum(values, "row")


def column_rows(values):
    return lax.all_gather(values, "col", axis=0, tiled=True)


def row_rows(values):
    return lax.all_gather(values, "row", axis=0, tiled=True)


def summed_over_row(term_fn, row_count):
    return lax.psum_scatter(
        term_fn(jnp.int32(0), row_count * lax.axis_size("row")),
        "row",
        scatter_dimension=0,
        tiled=True,
    )


def summed_over_col(term_fn, row_count):
    return lax.psum_scatter(
        term_fn(jnp.int32(0), row_count * lax.axis_size("col")),
        "col",
        scatter_dimension=0,
        tiled=True,
    )


def take_portion(complete, position, portion_size, along):
    return lax.dynamic_slice_in_dim(complete, position * portion_size, portion_size, along)


def place_portion(portion, position, full_size, along):
    zeroed_shape = portion.shape[:along] + (full_size,) + portion.shape[along + 1 :]
    zeroed = jnp.zeros(zeroed_shape, jnp.float32)
    return lax.dynamic_update_slice_in_dim(zeroed, portion, position * portion.shape[along], along)


def gelu_tanh(values):
    return jax.nn.gelu(values, approximate=True)


def norm_forward(values, norm_gain, norm_offset, totals_fn):
    plain_sum, square_sum = totals_fn((jnp.sum(values, axis=1), jnp.sum(values * values, axis=1)))
    center = (plain_sum / D)[:, None]
    inverse = lax.rsqrt(square_sum[:, None] / D - center * center + epsilon)
    unit_rows = (values - center) * inverse
    return (unit_rows * norm_gain + norm_offset, unit_rows, inverse)


def norm_backward(grad_rows, unit_rows, inverse, norm_gain, totals_fn):
    scaled = grad_rows * norm_gain
    plain_sum, cross_sum = totals_fn((jnp.sum(scaled, axis=1), jnp.sum(scaled * unit_rows, axis=1)))
    return inverse * (scaled - (plain_sum / D)[:, None] - unit_rows * (cross_sum / D)[:, None])


def split_heads(flat_rows):
    return flat_rows.reshape(LEN, flat_rows.shape[1] // HEAD_DIM, HEAD_DIM)


def scores_of(queries, keys_block, limit_value):
    raw_scores = jnp.einsum("qhe,khe->hqk", queries, keys_block, preferred_element_type=jnp.float32)
    raw_scores = raw_scores * HEAD_DIM ** (-0.5)
    places = jnp.arange(LEN, dtype=jnp.int32)
    visible = (places[None, :] <= places[:, None]) | (places[None, :] < limit_value)
    return jnp.where(visible[None], raw_scores, masked_score)


def attend_forward(packed):
    block_rows, limit_value = packed
    queries = split_heads(block_rows[:, 0])
    keys_block = split_heads(block_rows[:, 1])
    values_block = split_heads(block_rows[:, 2])
    scores = scores_of(queries, keys_block, limit_value)
    largest = jnp.max(scores, axis=-1, keepdims=True)
    weights = jnp.exp(scores - largest)
    row_totals = jnp.sum(weights, axis=-1, keepdims=True)
    probs = (weights / row_totals).astype(jnp.bfloat16)
    mixed = jnp.einsum("hqk,khe->qhe", probs, values_block, preferred_element_type=jnp.float32)
    return (mixed.reshape(LEN, -1).astype(jnp.bfloat16), (largest + jnp.log(row_totals))[..., 0])


def attend_backward(packed):
    block_rows, limit_value, log_total, out_grad = packed
    queries = split_heads(block_rows[:, 0])
    keys_block = split_heads(block_rows[:, 1])
    values_block = split_heads(block_rows[:, 2])
    scores = scores_of(queries, keys_block, limit_value)
    probs = jnp.exp(scores - log_total[..., None])
    probs_low = probs.astype(jnp.bfloat16)
    grad_heads = split_heads(out_grad)
    weight_grad = jnp.einsum(
        "qhe,khe->hqk", grad_heads, values_block, preferred_element_type=jnp.float32
    )
    row_inner = jnp.sum(probs * weight_grad, axis=-1, keepdims=True)
    score_grad = (probs * (weight_grad - row_inner)).astype(jnp.bfloat16)
    query_grad = jnp.einsum(
        "hqk,khe->qhe", score_grad, keys_block, preferred_element_type=jnp.float32
    )
    key_grad = jnp.einsum("hqk,qhe->khe", score_grad, queries, preferred_element_type=jnp.float32)
    value_grad = jnp.einsum(
        "hqk,qhe->khe", probs_low, grad_heads, preferred_element_type=jnp.float32
    )
    score_factor = HEAD_DIM ** (-0.5)
    stacked = jnp.stack(
        [
            (query_grad * score_factor).reshape(LEN, -1),
            (key_grad * score_factor).reshape(LEN, -1),
            value_grad.reshape(LEN, -1),
        ],
        axis=1,
    )
    return stacked.astype(jnp.bfloat16)


def general_device(
    tokens,
    prefix,
    ln1_gain,
    ln1_bias,
    w_qkv,
    qv_bias,
    w_out,
    out_bias,
    ln2_gain,
    ln2_bias,
    w_fc,
    fc_bias,
    w_proj,
    proj_bias,
    cotangent,
):
    row_place = lax.axis_index("row")
    col_place = lax.axis_index("col")
    row_devices = lax.axis_size("row")
    col_devices = lax.axis_size("col")
    width_row, local_rows = tokens.shape
    width_col = w_qkv.shape[2]
    hidden_col = w_fc.shape[1]
    seq_rows = local_rows * col_devices // row_devices
    seq_count = seq_rows // LEN
    residual = tokens.T.astype(jnp.float32)
    cotangent_local = cotangent.T
    first_gain = take_portion(ln1_gain, row_place, width_row, 0)
    first_normed, first_unit, first_inverse = norm_forward(
        residual, first_gain, take_portion(ln1_bias, row_place, width_row, 0), feature_totals
    )
    first_gathered = column_rows(first_normed.astype(jnp.bfloat16))

    def qkv_term(first_row, row_count):
        return jnp.einsum("td,sde->tse", first_gathered, w_qkv, preferred_element_type=jnp.float32)

    bias_col = take_portion(qv_bias, col_place, width_col, 1)
    bias_rows = jnp.stack([bias_col[0], jnp.zeros_like(bias_col[0]), bias_col[1]])
    qkv_sum = summed_over_row(qkv_term, seq_rows)
    qkv = (qkv_sum + bias_rows).astype(jnp.bfloat16)
    blocks = qkv.reshape(seq_count, LEN, 3, width_col)
    attn_blocks, log_totals = lax.map(attend_forward, (blocks, prefix))
    attn = attn_blocks.reshape(seq_rows, width_col)
    attn_gathered = row_rows(attn)

    def out_term(first_row, row_count):
        return jnp.dot(attn_gathered, w_out, preferred_element_type=jnp.float32)

    middle = (
        residual
        + summed_over_col(out_term, local_rows)
        + take_portion(out_bias, row_place, width_row, 0)
    )
    grad_output = cotangent_local.astype(jnp.float32)
    second_gain = take_portion(ln2_gain, row_place, width_row, 0)
    second_normed, second_unit, second_inverse = norm_forward(
        middle, second_gain, take_portion(ln2_bias, row_place, width_row, 0), feature_totals
    )
    second_gathered = column_rows(second_normed.astype(jnp.bfloat16))

    def up_term(first_row, row_count):
        return jnp.dot(second_gathered, w_fc, preferred_element_type=jnp.float32)

    hidden = summed_over_row(up_term, seq_rows) + take_portion(fc_bias, col_place, hidden_col, 0)
    active, gelu_pull = jax.vjp(gelu_tanh, hidden)
    active_gathered = row_rows(active.astype(jnp.bfloat16))

    def down_term(first_row, row_count):
        return jnp.einsum("tf,df->td", active_gathered, w_proj, preferred_element_type=jnp.float32)

    final_rows = (
        middle
        + summed_over_col(down_term, local_rows)
        + take_portion(proj_bias, row_place, width_row, 0)
    )
    output = final_rows.astype(jnp.bfloat16)
    grad_gathered = column_rows(cotangent_local)
    w_proj_grad = jnp.einsum(
        "tf,td->df", active_gathered, grad_gathered, preferred_element_type=jnp.float32
    )

    def active_term(first_row, row_count):
        return jnp.einsum("td,df->tf", grad_gathered, w_proj, preferred_element_type=jnp.float32)

    hidden_grad = gelu_pull(summed_over_row(active_term, seq_rows))[0].astype(jnp.bfloat16)
    hidden_gathered = row_rows(hidden_grad)
    w_fc_grad = jnp.einsum(
        "td,tf->df", second_gathered, hidden_gathered, preferred_element_type=jnp.float32
    )

    def second_term(first_row, row_count):
        return jnp.einsum("tf,df->td", hidden_gathered, w_fc, preferred_element_type=jnp.float32)

    second_grad = summed_over_col(second_term, local_rows)
    middle_grad = grad_output + norm_backward(
        second_grad, second_unit, second_inverse, second_gain, feature_totals
    )
    ln2_gain_part = place_portion(jnp.sum(second_grad * second_unit, axis=0), row_place, D, 0)
    ln2_bias_part = place_portion(jnp.sum(second_grad, axis=0), row_place, D, 0)
    fc_bias_part = place_portion(jnp.sum(hidden_grad.astype(jnp.float32), axis=0), col_place, FF, 0)
    proj_bias_part = place_portion(jnp.sum(grad_output, axis=0), row_place, D, 0)
    branch_grad = middle_grad.astype(jnp.bfloat16)
    branch_gathered = column_rows(branch_grad)
    w_out_grad = jnp.einsum(
        "te,td->ed", attn_gathered, branch_gathered, preferred_element_type=jnp.float32
    )

    def attn_term(first_row, row_count):
        return jnp.einsum("td,ed->te", branch_gathered, w_out, preferred_element_type=jnp.float32)

    attn_grad = summed_over_row(attn_term, seq_rows).astype(jnp.bfloat16)
    qkv_grad = lax.map(
        attend_backward, (blocks, prefix, log_totals, attn_grad.reshape(seq_count, LEN, width_col))
    )
    qkv_grad = qkv_grad.reshape(seq_rows, 3, width_col)
    qkv_gathered = row_rows(qkv_grad)
    w_qkv_grad = jnp.einsum(
        "td,tse->sde", first_gathered, qkv_gathered, preferred_element_type=jnp.float32
    )

    def first_term(first_row, row_count):
        return jnp.einsum("tse,sde->td", qkv_gathered, w_qkv, preferred_element_type=jnp.float32)

    first_grad = summed_over_col(first_term, local_rows)
    input_grad = middle_grad + norm_backward(
        first_grad, first_unit, first_inverse, first_gain, feature_totals
    )
    qkv_totals = jnp.sum(qkv_grad.astype(jnp.float32), axis=0)
    qv_part = place_portion(jnp.stack([qkv_totals[0], qkv_totals[2]]), col_place, D, 1)
    out_bias_part = place_portion(jnp.sum(branch_grad.astype(jnp.float32), axis=0), row_place, D, 0)
    ln1_gain_part = place_portion(jnp.sum(first_grad * first_unit, axis=0), row_place, D, 0)
    ln1_bias_part = place_portion(jnp.sum(first_grad, axis=0), row_place, D, 0)
    vectors = lax.psum(
        (
            ln1_gain_part,
            ln1_bias_part,
            qv_part,
            out_bias_part,
            ln2_gain_part,
            ln2_bias_part,
            fc_bias_part,
            proj_bias_part,
        ),
        ("dp", "row", "col"),
    )
    matrices = (
        lax.psum(w_qkv_grad.astype(jnp.bfloat16), "dp").astype(jnp.float32),
        lax.psum(w_out_grad.astype(jnp.bfloat16), "dp").astype(jnp.float32),
        lax.psum(w_fc_grad.astype(jnp.bfloat16), "dp").astype(jnp.float32),
        lax.psum(w_proj_grad.astype(jnp.bfloat16), "dp").astype(jnp.float32),
    )
    return (
        output.T,
        input_grad.T,
        vectors[0],
        vectors[1],
        matrices[0],
        vectors[2],
        matrices[1],
        vectors[3],
        vectors[4],
        vectors[5],
        matrices[2],
        vectors[6],
        matrices[3],
        vectors[7],
    )


MESH = pl.DeviceIdType.MESH
WIDTH = 192
HALF = 96
QUARTER = 256
LANES = 128
WQ = 3 * WIDTH
VMEM_LIMIT = 67043328
REMOTES = 208
LOCALS = 64
FACTOR = HEAD_DIM ** (-0.5)
ANY = pl.BlockSpec(memory_space=pl.ANY)
GAIN1, BIAS1, OUT_BIAS, GAIN2, BIAS2, PROJ_BIAS, Q_BIAS, V_BIAS, FC_BIAS = range(9)
V_GAIN1, V_BIAS1, V_QUERY, V_VALUE, V_OUT, V_GAIN2, V_BIAS2, V_PROJ, V_FC = range(9)
CENTER, INVERSE = range(2)


def dot(left, right, left_axis, right_axis):
    return lax.dot_general(
        left, right, (((left_axis,), (right_axis,)), ((), ())), preferred_element_type=jnp.float32
    )


def low(value):
    return value.astype(jnp.bfloat16)


def wide(value):
    return value.astype(jnp.float32)


def aligned(start, size):
    return pl.ds(pl.multiple_of(start, size), size)


def merged(value):
    return value.reshape((value.shape[0] * value.shape[1],) + value.shape[2:])


def each(count, body):
    def step(i, carry):
        body(i)
        return carry

    lax.fori_loop(0, count, step, 0)


class Links:
    def __init__(self, send_sems, recv_sems, local_sems):
        self.d, self.r, self.c = (lax.axis_index(n) for n in ("dp", "row", "col"))
        self.send_sems, self.recv_sems, self.local_sems = send_sems, recv_sems, local_sems
        self.remotes = 0
        self.locals = 0

    def across(self, k):
        if k == 0:
            return self.r
        if k == 1:
            return self.r + 1 - 2 * lax.rem(self.r, 2)
        return lax.rem(self.r + 2, 4) if k == 2 else 3 - self.r

    def plane(self, k):
        return (self.d, self.across(k), self.c)

    def height(self, k):
        return lax.rem(self.c + k, 4)

    def column(self, k):
        return (self.d, self.r, self.height(k))

    def partner(self):
        return (1 - self.d, self.r, self.c)

    def half(self, mine=True):
        place = self.d if mine else 1 - self.d
        return pl.ds(pl.multiple_of(place * HALF, 16), HALF)

    def crossing(self, row, place):
        place = place + self.d * (3 - 2 * place)
        low_bit = lax.rem(lax.rem(row, 2) + lax.rem(place, 2), 2)
        return low_bit + 2 * lax.rem(lax.div(row, 2) + lax.div(place, 2), 2)

    def greet(self):
        devices = [self.partner(), *(self.plane(k) for k in (1, 2, 3))]
        devices += [self.column(k) for k in (1, 2, 3)]
        barrier = pltpu.get_barrier_semaphore()
        for device in devices:
            pl.semaphore_signal(barrier, 1, device_id=device, device_id_type=MESH)
        self.greeted = len(devices)

    def meet(self):
        pl.semaphore_wait(pltpu.get_barrier_semaphore(), self.greeted)

    def send(self, source, target, device):
        place = self.remotes
        self.remotes += 1
        copy = pltpu.make_async_remote_copy(
            src_ref=source,
            dst_ref=target,
            send_sem=self.send_sems.at[place],
            recv_sem=self.recv_sems.at[place],
            device_id=device,
            device_id_type=MESH,
        )
        copy.start()
        return copy

    def local(self, source, target):
        place = self.locals
        self.locals += 1
        copy = pltpu.make_async_copy(source, target, self.local_sems.at[place])
        copy.start()
        return copy


class Ticket:
    def __init__(self, links, device):
        self.place = links.remotes
        links.remotes += 1
        self.links, self.device = links, device

    def __call__(self, source, target):
        return pltpu.make_async_remote_copy(
            src_ref=source,
            dst_ref=target,
            send_sem=self.links.send_sems.at[self.place],
            recv_sem=self.links.recv_sems.at[self.place],
            device_id=self.device,
            device_id_type=MESH,
        )


class Move:
    def __init__(self, links, stays, source, target, device):
        self.stays = stays
        self.ticket = Ticket(links, device)
        self.source, self.target = source, target
        place = links.locals
        links.locals += 1
        self.local_sem = links.local_sems.at[place]

        @pl.when(jnp.logical_not(stays))
        def _():
            self.ticket(source, target).start()

        @pl.when(stays)
        def _():
            pltpu.make_async_copy(source, target, self.local_sem).start()

    def wait(self):
        @pl.when(jnp.logical_not(self.stays))
        def _():
            self.ticket(self.source, self.target).wait()

        @pl.when(self.stays)
        def _():
            pltpu.make_async_copy(self.source, self.target, self.local_sem).wait()


class PlaneGather:
    def __init__(self, links, target, in_parts=False):
        self.links, self.target = links, target
        rows = target.shape[1] // 2
        self.low, self.high = pl.ds(0, rows), pl.ds(rows, rows)
        first, second = target.at[links.r, self.low], target.at[links.r, self.high]
        self.x_low = links.send(first, first, links.plane(1))
        self.y_high = links.send(second, second, links.plane(2))
        if not in_parts:
            self.rest()

    def rest(self):
        links, target = self.links, self.target
        first, second = target.at[links.r, self.low], target.at[links.r, self.high]
        self.x_high = links.send(second, second, links.plane(1))
        self.y_low = links.send(first, first, links.plane(2))

    def relay(self):
        links = self.links
        self.x_low.wait_recv()
        block = self.target.at[links.across(1), self.low]
        self.on_y = links.send(block, block, links.plane(2))
        self.y_high.wait_recv()
        block = self.target.at[links.across(2), self.high]
        self.on_x = links.send(block, block, links.plane(1))

    def finish(self):
        self.x_high.wait_recv()
        self.y_low.wait_recv()
        for copy in (self.x_low, self.y_high, self.x_high, self.y_low):
            copy.wait_send()
        self.on_y.wait()
        self.on_x.wait()


class PlaneReduce:
    def __init__(self, links, part_of, rows, over_x, over_y, relayed):
        self.links, self.part_of = links, part_of
        self.halves = (pl.ds(0, rows // 2), pl.ds(rows // 2, rows // 2))
        self.over_x, self.over_y, self.relayed = over_x, over_y, relayed
        self.copies = {}

    def part(self, k, half):
        return self.part_of(self.links.across(k)).at[self.halves[half]]

    def give(self, k):
        links = self.links
        if k == 3:
            self.copies["x3"] = links.send(self.part(3, 0), self.over_x.at[1], links.plane(1))
            self.copies["y3"] = links.send(self.part(3, 1), self.over_y.at[1], links.plane(2))
        elif k == 1:
            self.copies["x1"] = links.send(self.part(1, 0), self.over_x.at[0], links.plane(1))
        elif k == 2:
            self.copies["y2"] = links.send(self.part(2, 1), self.over_y.at[0], links.plane(2))

    def relay(self):
        links = self.links
        self.copies["x3"].wait_recv()
        add_rows(self.over_x.at[1], [self.over_x.at[1], self.part(2, 0)])
        self.copies["xy"] = links.send(self.over_x.at[1], self.relayed.at[0], links.plane(2))
        self.copies["y3"].wait_recv()
        add_rows(self.over_y.at[1], [self.over_y.at[1], self.part(1, 1)])
        self.copies["yx"] = links.send(self.over_y.at[1], self.relayed.at[1], links.plane(1))

    def finish(self):
        for name in ("x3", "y3"):
            self.copies[name].wait_send()
        for name in ("x1", "y2", "xy", "yx"):
            self.copies[name].wait()

    def total(self, lanes):
        parts = []
        for half, over in ((0, self.over_x), (1, self.over_y)):
            value = wide(self.part(0, half)[:, lanes]) + wide(over[0, :, lanes])
            parts.append(value + wide(self.relayed[half, :, lanes]))
        return jnp.concatenate(parts, axis=0)


class Line:
    def __init__(self, links, block_of):
        self.links, self.block_of = links, block_of
        c = links.c
        self.up = [Ticket(links, (links.d, links.r, lax.rem(c + 1, 4))) for _ in range(3)]
        self.down = [Ticket(links, (links.d, links.r, lax.rem(c + 3, 4))) for _ in range(3)]

    def copy(self, ticket, place):
        return ticket(self.block_of(place), self.block_of(place))

    def step(self, t):
        c = self.links.c
        if t > 0:

            @pl.when(c >= t)
            def _():
                self.copy(self.up[t - 1], c - t).wait_recv()

            @pl.when(c <= 3 - t)
            def _():
                self.copy(self.down[t - 1], c + t).wait_recv()

        if t < 3:

            @pl.when(jnp.logical_and(c >= t, c < 3))
            def _():
                self.copy(self.up[t], c - t).start()

            @pl.when(jnp.logical_and(c <= 3 - t, c > 0))
            def _():
                self.copy(self.down[t], c + t).start()

    def finish(self):
        c = self.links.c
        for t in range(3):

            @pl.when(jnp.logical_and(c >= t, c < 3))
            def _(t=t):
                self.copy(self.up[t], c - t).wait_send()

            @pl.when(jnp.logical_and(c <= 3 - t, c > 0))
            def _(t=t):
                self.copy(self.down[t], c + t).wait_send()


class WeightGather:
    def __init__(self, links, stage, moved, target, pieces=1):
        self.links, self.moved, self.target = links, moved, target
        r, c = links.r, links.c
        self.mine = links.half()
        self.goal = links.crossing(r, c)
        size = HALF // pieces
        self.local_rows = [pl.ds(i * size, size) for i in range(pieces)]
        start = links.d * HALF
        self.rows = [pl.ds(pl.multiple_of(start + i * size, 16), size) for i in range(pieces)]
        device = (links.d, r, self.goal)
        self.turns = [
            Move(links, self.goal == c, stage.at[rows], moved.at[rows], device)
            for rows in self.local_rows
        ]

    def hop(self):
        links = self.links
        device = (links.d, self.goal, links.c)
        for i, rows in enumerate(self.local_rows):
            self.turns[i].wait()
            block = self.target.at[links.r, self.rows[i]]
            self.turns[i] = Move(links, self.goal == links.r, self.moved.at[rows], block, device)

    def begin(self):
        links = self.links

        def block_of(rows):
            return lambda place: self.target.at[links.crossing(links.r, place), rows]

        self.ways = []
        for turn, rows in zip(self.turns, self.rows):
            turn.wait()
            self.ways.append(Line(links, block_of(rows)))
            self.ways[-1].step(0)

    def line(self, t):
        if t == 0:
            self.begin()
        else:
            for way in self.ways:
                way.step(t)

    def share(self):
        for way in self.ways:
            way.finish()
        block = self.target.at[:, self.mine]
        self.shared = self.links.send(block, block, self.links.partner())

    def finish(self):
        self.shared.wait()


class SquareGather:
    def __init__(self, links, target):
        self.links, self.target = links, target
        self.mine = links.half()
        self.way = Line(links, lambda place: target.at[links.r, place, self.mine])

    def line(self, t):
        self.way.step(t)

    def cross(self):
        self.way.finish()
        self.plane = PlaneGather(self.links, self.target.at[:, :, self.mine])

    def share(self):
        self.plane.finish()
        block = self.target.at[:, :, self.mine]
        self.shared = self.links.send(block, block, self.links.partner())

    def finish(self):
        self.shared.wait()


def add_rows(target, terms):
    def step(i):
        place = aligned(i * 16, 16)
        total = wide(terms[0][place, :])
        for term in terms[1:]:
            total = total + wide(term[place, :])
        target[place, :] = total.astype(target.dtype)

    each(target.shape[0] // 16, step)


def add_blocks(target, terms):
    if len(target.shape) == 2:
        add_rows(target, terms)
    else:
        each(target.shape[0], lambda i: add_blocks(target.at[i], [term.at[i] for term in terms]))


class LineReduce:
    def __init__(self, links, block_of, up, down):
        self.links, self.block_of, self.up, self.down = links, block_of, up, down
        c = links.c
        self.rise = [Ticket(links, (links.d, links.r, lax.rem(c + 1, 4))) for _ in range(3)]
        self.fall = [Ticket(links, (links.d, links.r, lax.rem(c + 3, 4))) for _ in range(3)]

    def step(self, t):
        c = self.links.c
        for i in range(t + 1):
            goal = 3 - t + i
            self.pass_on(c == i, self.rise[goal - 1], self.up.at[goal - 1], goal, i > 0)
            goal = t - i
            self.pass_on(c == 3 - i, self.fall[goal], self.down.at[goal], goal, i > 0)

    def pass_on(self, here, ticket, slot, goal, adds):
        @pl.when(here)
        def _():
            if adds:
                ticket(slot, slot).wait_recv()
                add_blocks(slot, [slot, self.block_of(goal)])
                ticket(slot, slot).start()
            else:
                ticket(self.block_of(goal), slot).start()

    def total(self, target):
        c = self.links.c
        for goal in range(4):

            @pl.when(c == goal)
            def _(goal=goal):
                terms = [self.block_of(goal)]
                if goal > 0:
                    slot = self.up.at[goal - 1]
                    self.rise[goal - 1](slot, slot).wait_recv()
                    terms.append(slot)
                if goal < 3:
                    slot = self.down.at[goal]
                    self.fall[goal](slot, slot).wait_recv()
                    terms.append(slot)
                add_blocks(target, terms)

        for i in range(3):
            rising, falling = self.up.at[i], self.down.at[i]

            @pl.when(c < i + 1)
            def _(i=i, slot=rising):
                self.rise[i](slot, slot).wait_send()

            @pl.when(c > i)
            def _(i=i, slot=falling):
                self.fall[i](slot, slot).wait_send()


class WeightReduce:
    def __init__(self, links, grad, near, sums, up, down, fin, moved, arrived, result, pieces=1):
        self.links, self.grad, self.near, self.sums = links, grad, near, sums
        self.up, self.down, self.fin = up, down, fin
        self.moved, self.arrived, self.result = moved, arrived, result
        size = HALF // pieces
        self.rows = [pl.ds(i * size, size) for i in range(pieces)]
        self.to_near = [self.send_near(i * size, size) for i in range(pieces)]

    def send_near(self, first, size):
        links = self.links
        other = pl.ds(pl.multiple_of((1 - links.d) * HALF + first, 16), size)
        rows = pl.ds(first, size)
        return links.send(self.grad.at[:, other], self.near.at[:, rows], links.partner())

    def add_near(self):
        links = self.links

        def block_of(rows):
            return lambda place: self.sums.at[links.crossing(links.r, place), rows]

        self.ways = []
        for copy, rows in zip(self.to_near, self.rows):
            copy.wait()
            first = links.d * HALF + rows.start
            mine = pl.ds(pl.multiple_of(first, 16), rows.size)
            each(
                4,
                lambda b, rows=rows, mine=mine: add_rows(
                    self.sums.at[b, rows], [self.grad.at[b, mine], self.near.at[b, rows]]
                ),
            )
            up, down = self.up.at[:, rows], self.down.at[:, rows]
            self.ways.append(LineReduce(links, block_of(rows), up, down))

    def line(self, i):
        for way in self.ways:
            way.step(i)

    def hop(self):
        links = self.links
        self.goal = links.crossing(links.r, links.c)
        device = (links.d, self.goal, links.c)
        self.turns = []
        for way, rows in zip(self.ways, self.rows):
            way.total(self.fin.at[rows])
            stays = self.goal == links.r
            self.turns.append(Move(links, stays, self.fin.at[rows], self.moved.at[rows], device))

    def back(self):
        links = self.links
        device = (links.d, links.r, self.goal)
        for i, rows in enumerate(self.rows):
            self.turns[i].wait()
            stays = self.goal == links.c
            self.turns[i] = Move(links, stays, self.moved.at[rows], self.arrived.at[rows], device)

    def share(self):
        for turn in self.turns:
            turn.wait()
        self.give(self.arrived)

    def give(self, total):
        links, mine = self.links, self.links.half()
        self.last = [
            links.send(total, self.result.at[mine], links.partner()),
            links.local(total, self.result.at[mine]),
        ]

    def finish(self):
        for copy in self.last:
            copy.wait()


class SquareReduce(WeightReduce):
    def __init__(self, links, grad, near, sums, up, down, fin, came, arrived, result):
        self.links, self.grad, self.near, self.sums = links, grad, near, sums
        self.up, self.down, self.fin = up, down, fin
        self.came, self.arrived, self.result = came, arrived, result
        self.to_near = links.send(grad.at[:, :, links.half(False)], near, links.partner())

    def add_near(self):
        mine = self.links.half()
        self.to_near.wait()
        add_blocks(self.sums, [self.grad.at[:, :, mine], self.near])
        self.ways = [
            LineReduce(self.links, lambda place: self.sums.at[:, place], self.up, self.down)
        ]

    def hop(self):
        links = self.links
        self.ways[0].total(self.fin)
        self.crossing = [
            links.send(self.fin.at[links.across(k)], self.came.at[k - 1], links.plane(k))
            for k in (3, 1, 2)
        ]

    def back(self):
        for copy in self.crossing:
            copy.wait()
        came = self.came
        add_rows(self.arrived, [self.fin.at[self.links.r], came.at[0], came.at[1], came.at[2]])

    def share(self):
        self.give(self.arrived)


def normalize(source_of, target, stats, gain, offset):
    def step(j):
        lanes = aligned(j * LANES, LANES)
        values = source_of(lanes)
        center = jnp.sum(values, axis=0, keepdims=True) / D
        square = jnp.sum(values * values, axis=0, keepdims=True) / D
        inverse = lax.rsqrt(square - center * center + epsilon)
        stats[CENTER : CENTER + 1, lanes] = center
        stats[INVERSE : INVERSE + 1, lanes] = inverse
        target[:, lanes] = low((values - center) * inverse * gain[...] + offset[...])

    each(LEN // LANES, step)


def key_span(block):
    return max(512, (block + 1) * QUARTER), block * QUARTER


def visible(block, first, last, limit_value):
    shape = (last - first, QUARTER)
    keys = lax.broadcasted_iota(jnp.int32, shape, 0) + first
    queries = lax.broadcasted_iota(jnp.int32, shape, 1) + block * QUARTER
    return (keys <= queries) | (keys < limit_value)


def masked(value, block, limit_value, fill):
    last, first = key_span(block)
    tail = jnp.where(visible(block, first, last, limit_value), value[first:], fill)
    return jnp.concatenate([value[:first], tail], axis=0) if first else tail


def head_rows(h, part):
    return pl.ds(h * HEAD_DIM + part * WIDTH, HEAD_DIM)


def attend(qkv, limit_value, attn_of, log_total, between):
    def head(h):
        for block in range(4):
            for action in between.get(h * 4 + block, ()):
                action()
            last, _ = key_span(block)
            lanes = slice(block * QUARTER, (block + 1) * QUARTER)
            queries = qkv[head_rows(h, 0), lanes] * jnp.bfloat16(FACTOR)
            scores = dot(qkv[head_rows(h, 1), :last], queries, 0, 0)
            scores = masked(scores, block, limit_value, masked_score)
            largest = jnp.max(scores, axis=0, keepdims=True)
            weights = jnp.exp(scores - largest)
            total = jnp.sum(weights, axis=0, keepdims=True)
            mixed = dot(qkv[head_rows(h, 2), :last], low(weights), 1, 0)
            attn_of(head_rows(h, 0), lanes, low(mixed * (1.0 / total)))
            log_total[pl.ds(h, 1), lanes] = largest + jnp.log(total)

    for h in range(3):
        head(h)


def attend_back(
    qkv, limit_value, attn_of, log_total, out_grad, qkv_grad, key_sum, value_sum, between
):
    def head(h):
        for block in (3, 2, 1, 0):
            for action in between.get(h * 4 + 3 - block, ()):
                action()
            last, _ = key_span(block)
            lanes = slice(block * QUARTER, (block + 1) * QUARTER)
            queries = qkv[head_rows(h, 0), lanes] * jnp.bfloat16(FACTOR)
            grads = out_grad[head_rows(h, 0), lanes]
            inner = jnp.sum(
                wide(attn_of(head_rows(h, 0), lanes)) * wide(grads), axis=0, keepdims=True
            )
            scores = dot(qkv[head_rows(h, 1), :last], queries, 0, 0)
            probs = jnp.exp(scores - log_total[pl.ds(h, 1), lanes])
            probs = masked(probs, block, limit_value, 0.0)
            weight_grad = dot(qkv[head_rows(h, 2), :last], grads, 0, 0)
            score_grad = low(probs * (weight_grad - inner))
            query_grad = dot(qkv[head_rows(h, 1), :last], score_grad, 1, 0) * FACTOR
            qkv_grad[head_rows(h, 0), lanes] = low(query_grad)
            key_grad = dot(queries, score_grad, 1, 1)
            value_grad = dot(grads, low(probs), 1, 1)
            if block == 3:
                key_sum[...] = key_grad
                value_sum[...] = value_grad
            else:
                key_sum[:, :last] += key_grad
                value_sum[:, :last] += value_grad
        qkv_grad[head_rows(h, 1), :] = low(key_sum[...])
        qkv_grad[head_rows(h, 2), :] = low(value_sum[...])

    for h in range(3):
        head(h)


def gelu_parts(u):
    slope = (2.0 / 3.141592653589793) ** 0.5
    square = u * u
    bent = jnp.tanh(slope * u * (1.0 + 0.044715 * square))
    shared = 0.5 * (1.0 + bent)
    derivative = shared + 0.5 * u * (1.0 - bent * bent) * (slope * (1.0 + 3.0 * 0.044715 * square))
    return u * shared, derivative


def block_kernel(
    limit, tok, gain1_in, bias1_in, wq_in, qv_in, wo_in, out_in, gain2_in, bias2_in,
    wf_in, fc_in, wp_in, proj_in, cot,
    out_hbm, grad_hbm, wq_hbm, wf_hbm, wp_hbm, wo_hbm, vec_hbm,
    rows1, qv, fc, wq_here, xt, gt, wqa, wfa, wpa, woa, zq, zf, zp, mq, mf, mp, pres, colb,
    fn, qkv, at, lse, st1, st2, mid, sn, act, slope, op, hg, sp,
    x2, y2, z2, x_out, y_out, z_out, x1, y1, z1, br, ap, dout, brf, dqkv, ksum, vsum,
    gf, gp, gq, near_f, near_p, near_q, sum_f, sum_p, sum_q, up_f, up_p, up_q, dn_f, dn_p, dn_q,
    fin_f, fin_p, fin_q, hop_f, hop_p, hop_q, got_f, got_p, got_q,
    sq, near_o, sum_o, up_o, dn_o, fin_o, hop_o, got_o,
    fgp, fsum, vcol, vec, vec_in, stat, stat_in, out_v, grad_v,
    send_sems, recv_sems, local_sems,
):
    links = Links(send_sems, recv_sems, local_sems)
    r, c = links.r, links.c
    mine = links.half()
    own = aligned(r * QUARTER, QUARTER)
    links.greet()
    singles = (gain1_in, bias1_in, out_in, gain2_in, bias2_in, proj_in)
    first = [links.local(wq_in.at[:, mine], wq_here), links.local(tok, xt.at[r])]
    first += [links.local(wo_in.at[mine], woa.at[r, c, mine])]
    first += [links.local(source, rows1.at[i]) for i, source in enumerate(singles)]
    first += [links.local(qv_in, qv), links.local(fc_in, fc)]
    then = [links.local(wf_in.at[mine], zf), links.local(wp_in.at[mine], zp)]
    then += [links.local(cot, gt.at[r])]
    for copy in first:
        copy.wait()
    zq[...] = jnp.concatenate([wq_here[i] for i in range(3)], axis=1)
    pres[r] = jnp.full((8, LANES), limit[0], jnp.int32)

    links.meet()

    get_q = WeightGather(links, zq, mq, wqa, 3)
    get_o = SquareGather(links, woa)
    get_o.line(0)
    tokens = PlaneGather(links, xt, in_parts=True)
    for copy in then:
        copy.wait()
    get_q.hop()
    tokens.rest()
    get_f = WeightGather(links, zf, mf, wfa)
    prefixes = [links.send(pres.at[r], pres.at[r], links.plane(k)) for k in (1, 2, 3)]
    get_q.line(0)
    get_o.line(1)

    def column(kind, place, values):
        spread = jnp.broadcast_to(values[None, :], (LANES, LANES))
        colb[kind, pl.ds(place * LANES, LANES)] = spread.T

    for place in range(D // LANES):
        part = pl.ds(place * LANES, LANES)
        for kind in range(len(singles)):
            column(kind, place, rows1[kind, part])
        column(Q_BIAS, place, qv[0, part])
        column(V_BIAS, place, qv[1, part])
        column(FC_BIAS, place, fc[pl.ds(pl.multiple_of(r * D + place * LANES, LANES), LANES)])

    tokens.relay()
    get_q.line(1)
    get_o.line(2)
    get_f.hop()
    get_q.line(2)
    get_o.line(3)
    get_p = WeightGather(links, zp, mp, wpa)
    get_q.line(3)
    get_q.share()
    get_f.line(0)
    tokens.finish()
    get_o.cross()
    grads = PlaneGather(links, gt, in_parts=True)
    get_p.hop()
    normalize(
        lambda lanes: wide(merged(xt[:, :, lanes])), fn, st1, colb.at[GAIN1], colb.at[BIAS1]
    )
    for copy in prefixes:
        copy.wait()
    get_q.finish()
    head_bias = aligned(r * WIDTH, WIDTH)

    def project(b):
        lanes = aligned(b * QUARTER, QUARTER)
        nothing = jnp.zeros((WIDTH, LANES), jnp.float32)
        bias = [colb[Q_BIAS, head_bias], nothing, colb[V_BIAS, head_bias]]
        bias = jnp.concatenate(bias, axis=0)
        value = dot(merged(wqa[...]), fn[:, lanes], 0, 0)
        qkv[:, lanes] = low(value + jnp.concatenate([bias, bias], axis=1))

    each(4, project)
    limit_value = pres[c][0:1, 0:1]

    def put_attn(rows, lanes, value):
        at[r, rows, lanes] = value

    def get_attn(rows, lanes):
        return at[r, rows, lanes]

    attns = []

    def gather_head(h):
        attns.append(PlaneGather(links, at.at[:, h * HEAD_DIM : (h + 1) * HEAD_DIM]))

    def get_o_relay():
        get_o.plane.relay()

    attend(
        qkv,
        limit_value,
        put_attn,
        lse,
        {
            0: [get_o_relay],
            1: [lambda: get_f.line(1)],
            4: [lambda: gather_head(0)],
            7: [lambda: get_f.line(2)],
            8: [lambda: gather_head(1), lambda: attns[0].relay()],
            10: [lambda: get_p.line(0)],
        },
    )
    gather_head(2)
    attns[1].relay()
    get_f.line(3)
    get_f.share()
    get_o.share()
    attns[2].relay()
    grads.rest()
    get_p.line(1)
    get_o.finish()
    for attn in attns:
        attn.finish()
    grads.relay()

    def join(b):
        rows = aligned(b * WIDTH, WIDTH)
        bias = jnp.concatenate([colb[OUT_BIAS, rows]] * 8, axis=1)
        value = dot(merged(woa[b]), merged(at[...]), 0, 0)
        mid[rows, :] = wide(xt[b]) + (value + bias)

    each(4, join)
    get_p.line(2)
    normalize(lambda lanes: mid[:, lanes], sn, st2, colb.at[GAIN2], colb.at[BIAS2])
    get_f.finish()

    def up(b):
        lanes = aligned(b * QUARTER, QUARTER)
        bias = colb[FC_BIAS]
        value = dot(merged(wfa[...]), sn[:, lanes], 0, 0) + jnp.concatenate([bias, bias], axis=1)
        value, derivative = gelu_parts(value)
        act[:, lanes] = low(value)
        slope[:, lanes] = derivative

    each(2, up)
    get_p.line(3)
    get_p.share()
    each(2, lambda b: up(b + 2))
    grads.finish()

    def proj_grads(b):
        some = aligned(b * QUARTER, QUARTER)
        value = low(dot(merged(gt[...]), act[some, :], 1, 1))
        gp[:, :, some] = value.reshape(4, WIDTH, QUARTER)

    each(3, proj_grads)
    put_p = WeightReduce(links, gp, near_p, sum_p, up_p, dn_p, fin_p, hop_p, got_p, wp_hbm)
    get_p.finish()

    seconds = PlaneReduce(
        links, lambda place: sp.at[:, aligned(place * QUARTER, QUARTER)], D, x2, y2, z2
    )
    for k in (3, 1, 2, 0):
        lanes = aligned(links.across(k) * QUARTER, QUARTER)
        value = dot(merged(wpa[...]), merged(gt[:, :, lanes]), 0, 0)
        hg[:, lanes] = low(value * slope[:, lanes])
        sp[:, lanes] = low(dot(merged(wfa[...]), hg[:, lanes], 1, 0))
        seconds.give(k)
        if k == 3:
            put_p.add_near()
            put_p.line(0)

    def fc_grads(b):
        some = aligned(b * QUARTER, QUARTER)
        value = low(dot(sn[...], hg[some, :], 1, 1))
        gf[:, :, some] = value.reshape(4, WIDTH, QUARTER)

    each(3, fc_grads)
    put_f = WeightReduce(links, gf, near_f, sum_f, up_f, dn_f, fin_f, hop_f, got_f, wf_hbm)
    seconds.relay()
    put_p.line(1)

    def down(b):
        lanes = aligned(b * QUARTER, QUARTER)
        value = low(dot(merged(wpa[...]), act[:, lanes], 1, 0))
        op[:, :, lanes] = value.reshape(4, WIDTH, QUARTER)

    each(4, down)
    outs = PlaneReduce(links, lambda place: op.at[place], WIDTH, x_out, y_out, z_out)
    put_f.add_near()
    put_f.line(0)
    lane = lax.broadcasted_iota(jnp.int32, (D, LANES), 1)
    total = jnp.zeros((D, 1), jnp.float32)
    for b in range(4):
        lanes = slice(b * QUARTER, (b + 1) * QUARTER)
        total = total + jnp.sum(wide(hg[:, lanes]), axis=1, keepdims=True)
    vcol[...] = jnp.where(lane == V_FC + r, total, 0.0)
    put_p.line(2)
    seconds.finish()
    outs.give(3)

    def back(j):
        lanes = aligned(r * QUARTER + j * LANES, LANES)
        part = aligned(j * LANES, LANES)
        given = seconds.total(part)
        inverse = st2[INVERSE : INVERSE + 1, lanes]
        unit = (mid[:, lanes] - st2[CENTER : CENTER + 1, lanes]) * inverse
        scaled = given * colb[GAIN2]
        plain = jnp.sum(scaled, axis=0, keepdims=True) / D
        cross = jnp.sum(scaled * unit, axis=0, keepdims=True) / D
        above = wide(merged(gt[:, :, lanes]))
        branch = low(above + inverse * (scaled - plain - unit * cross))
        br[:, :, part] = branch.reshape(4, WIDTH, LANES)
        value = jnp.where(lane == V_GAIN2, jnp.sum(given * unit, axis=1, keepdims=True), 0.0)
        value = jnp.where(lane == V_BIAS2, jnp.sum(given, axis=1, keepdims=True), value)
        value = jnp.where(lane == V_OUT, jnp.sum(wide(branch), axis=1, keepdims=True), value)
        value = jnp.where(lane == V_PROJ, jnp.sum(above, axis=1, keepdims=True), value)
        vcol[...] = vcol[...] + value

    for j in range(2):
        back(j)
    value = dot(merged(woa[0]), br[0], 1, 0)
    for b in range(1, 4):
        value = value + dot(merged(woa[b]), br[b], 1, 0)
    ap[...] = low(value).reshape(4, WIDTH, QUARTER)
    turns = [
        links.send(ap.at[links.across(k)], dout.at[:, own], links.plane(k)) for k in (3, 1, 2)
    ]
    turns.append(links.local(ap.at[r], dout.at[:, own]))
    def square_grads(b):
        value = low(dot(merged(at[:, :, own]), br[b], 1, 1))
        sq[b] = value.reshape(4, WIDTH, WIDTH)

    each(4, square_grads)
    put_o = SquareReduce(links, sq, near_o, sum_o, up_o, dn_o, fin_o, hop_o, got_o, wo_hbm)
    put_f.line(1)
    put_o.add_near()
    put_p.hop()
    for copy in turns:
        copy.wait()
    outs.give(1)
    outs.give(2)
    swaps = [
        links.send(br.at[links.across(k)], brf.at[:, own], links.plane(k)) for k in (3, 1, 2)
    ]
    swaps.append(links.local(br.at[r], brf.at[:, own]))
    attend_back(
        qkv, limit_value, get_attn, lse, dout, dqkv, ksum, vsum,
        {
            0: [lambda: put_o.line(0)],
            2: [lambda: put_f.line(2)],
            4: [put_p.back, outs.relay],
            9: [put_f.hop, put_p.share],
            11: [lambda: put_o.line(1)],
        },
    )
    for some in (slice(0, 256), slice(256, 512), slice(512, WQ)):
        value = low(dot(fn[...], dqkv[some, :], 1, 1))
        gq[:, :, some] = value.reshape(4, WIDTH, some.stop - some.start)
    put_q = WeightReduce(links, gq, near_q, sum_q, up_q, dn_q, fin_q, hop_q, got_q, wq_hbm, 3)

    stat[...] = jnp.zeros_like(stat)
    firsts = PlaneReduce(links, lambda place: fgp.at[place], WIDTH, x1, y1, z1)
    for k in (3, 1, 2, 0):
        b = links.across(k)
        rows = aligned(b * WIDTH, WIDTH)

        fsum[...] = jnp.zeros_like(fsum)

        def first_part(j, b=b, rows=rows):
            lanes = aligned(j * QUARTER, QUARTER)
            value = dot(wqa[b], dqkv[:, lanes], 1, 0)
            fgp[b, :, lanes] = low(value)
            gain = colb[GAIN1, rows]
            for i in range(2):
                half = aligned(j * QUARTER + i * LANES, LANES)
                piece = value[:, i * LANES : (i + 1) * LANES]
                unit = wide(xt[b, :, half]) - st1[CENTER : CENTER + 1, half]
                weighted = piece * (unit * st1[INVERSE : INVERSE + 1, half])
                stat[0:1, half] += jnp.sum(piece * gain, axis=0, keepdims=True)
                stat[1:2, half] += jnp.sum(weighted * gain, axis=0, keepdims=True)
                fsum[0] += weighted
                fsum[1] += piece

        each(4, first_part)
        firsts.give(k)
        spot = lane[:WIDTH]
        add = jnp.where(spot == V_GAIN1, jnp.sum(fsum[0], axis=1, keepdims=True), 0.0)
        add = jnp.where(spot == V_BIAS1, jnp.sum(fsum[1], axis=1, keepdims=True), add)
        vcol[rows, :] = vcol[rows, :] + add
        if k == 3:
            put_q.add_near()
            put_q.line(0)
        elif k == 1:
            put_f.back()
            put_o.line(2)
        elif k == 2:
            put_q.line(1)
            firsts.relay()
    stat_sends = [links.send(stat, stat_in.at[k - 1], links.plane(k)) for k in (1, 2, 3)]
    put_q.line(2)
    put_o.hop()
    rows = aligned(r * WIDTH, WIDTH)
    spot = lane[:WIDTH]
    query = jnp.zeros((WIDTH, 1), jnp.float32)
    value = jnp.zeros((WIDTH, 1), jnp.float32)
    for b in range(4):
        lanes = slice(b * QUARTER, (b + 1) * QUARTER)
        query = query + jnp.sum(wide(dqkv[:WIDTH, lanes]), axis=1, keepdims=True)
        value = value + jnp.sum(wide(dqkv[2 * WIDTH :, lanes]), axis=1, keepdims=True)
    add = jnp.where(spot == V_QUERY, query, jnp.where(spot == V_VALUE, value, 0.0))
    vcol[rows, :] = vcol[rows, :] + add
    vec[0] = vcol[...].T[:16]
    vec_near = links.send(vec.at[0], vec_in.at[0], links.partner())
    put_f.share()
    put_q.hop()
    vec_near.wait()
    vec[1] = vec[0] + vec_in[0]
    vec_plane = [links.send(vec.at[1], vec_in.at[k], links.plane(k)) for k in (1, 2, 3)]
    put_o.back()
    put_o.share()
    put_q.back()
    for copy in vec_plane:
        copy.wait()
    vec[2] = vec[1] + vec_in[1] + vec_in[2] + vec_in[3]
    vec_high = [links.send(vec.at[2], vec_in.at[3 + k], links.column(k)) for k in (1, 2, 3)]
    outs.finish()

    def last_out(j):
        lanes = aligned(j * LANES, LANES)
        value = mid[rows, lanes] + colb[PROJ_BIAS, rows] + outs.total(lanes)
        out_v[:, lanes] = low(value)

    each(LEN // LANES, last_out)
    ends = [links.local(out_v, out_hbm)]
    for copy in swaps + stat_sends:
        copy.wait()
    firsts.finish()
    stat[...] = stat[...] + stat_in[0] + stat_in[1] + stat_in[2]

    def last_grad(j):
        lanes = aligned(j * LANES, LANES)
        inverse = st1[INVERSE : INVERSE + 1, lanes]
        unit = (wide(xt[r, :, lanes]) - st1[CENTER : CENTER + 1, lanes]) * inverse
        value = firsts.total(lanes) * colb[GAIN1, rows] - stat[0:1, lanes] / D
        grad_v[:, lanes] = wide(brf[:, lanes]) + inverse * (value - unit * (stat[1:2, lanes] / D))

    each(LEN // LANES, last_grad)
    ends.append(links.local(grad_v, grad_hbm))
    put_q.share()
    for copy in vec_high:
        copy.wait()
    vec[3] = vec[2] + vec_in[4] + vec_in[5] + vec_in[6]
    ends.append(links.local(vec.at[3], vec_hbm))
    for copy in ends:
        copy.wait()
    for put in (put_f, put_p, put_o, put_q):
        put.finish()


def run_block(*arguments):
    narrow, full = jnp.bfloat16, jnp.float32
    vmem = pltpu.VMEM
    sequence, tall = (4, WIDTH, LEN), (D, LEN)

    def thirds(lead=()):
        return [vmem(lead + (HALF, width), narrow) for width in (D, D, WQ)]

    def plane_sums(rows, lanes):
        return [vmem((2, rows // 2, lanes), narrow) for _ in range(3)]

    scratch = [
        vmem((6, D), full), vmem((2, D), full), vmem((FF,), full), vmem((3, HALF, WIDTH), narrow),
        vmem(sequence, narrow), vmem(sequence, narrow),
        vmem((4, WIDTH, WQ), narrow), vmem((4, WIDTH, D), narrow), vmem((4, WIDTH, D), narrow),
        vmem((4, 4, WIDTH, WIDTH), narrow),
        vmem((HALF, WQ), narrow), vmem((HALF, D), narrow), vmem((HALF, D), narrow),
        vmem((HALF, WQ), narrow), vmem((HALF, D), narrow), vmem((HALF, D), narrow),
        vmem((4, 8, LANES), jnp.int32), vmem((9, D, LANES), full),
        vmem(tall, narrow), vmem((WQ, LEN), narrow), vmem(sequence, narrow),
        vmem((8, LEN), full), vmem((8, LEN), full), vmem((8, LEN), full),
        vmem(tall, full), vmem(tall, narrow), vmem(tall, narrow), vmem(tall, full),
        vmem(sequence, narrow), vmem(tall, narrow), vmem(tall, narrow),
        *plane_sums(D, QUARTER), *plane_sums(WIDTH, LEN), *plane_sums(WIDTH, LEN),
        vmem((4, WIDTH, QUARTER), narrow), vmem((4, WIDTH, QUARTER), narrow),
        vmem((WIDTH, LEN), narrow), vmem((WIDTH, LEN), narrow), vmem((WQ, LEN), narrow),
        vmem((HEAD_DIM, LEN), full), vmem((HEAD_DIM, LEN), full),
        vmem((4, WIDTH, D), narrow), vmem((4, WIDTH, D), narrow), vmem((4, WIDTH, WQ), narrow),
        *thirds((4,)), *thirds((4,)), *thirds((3,)), *thirds((3,)), *thirds(), *thirds(), *thirds(),
        vmem((4, 4, WIDTH, WIDTH), narrow), vmem((4, 4, HALF, WIDTH), narrow),
        vmem((4, 4, HALF, WIDTH), narrow), vmem((3, 4, HALF, WIDTH), narrow),
        vmem((3, 4, HALF, WIDTH), narrow), vmem((4, HALF, WIDTH), narrow),
        vmem((3, HALF, WIDTH), narrow), vmem((HALF, WIDTH), narrow),
        vmem(sequence, narrow), vmem((2, WIDTH, LANES), full), vmem((D, LANES), full),
        vmem((4, 16, D), full), vmem((7, 16, D), full), vmem((8, LEN), full), vmem((3, 8, LEN), full),
        vmem((WIDTH, LEN), narrow), vmem((WIDTH, LEN), full),
        pltpu.SemaphoreType.DMA((REMOTES,)), pltpu.SemaphoreType.DMA((REMOTES,)),
        pltpu.SemaphoreType.DMA((LOCALS,)),
    ]
    results = [
        ((WIDTH, LEN), narrow), ((WIDTH, LEN), full), ((WIDTH, WQ), narrow), ((WIDTH, D), narrow),
        ((WIDTH, D), narrow), ((WIDTH, WIDTH), narrow), ((16, D), full),
    ]
    return pl.pallas_call(
        block_kernel,
        out_shape=[jax.ShapeDtypeStruct(*result) for result in results],
        in_specs=[pl.BlockSpec(memory_space=pltpu.SMEM)] + [ANY] * (len(arguments) - 1),
        out_specs=[ANY] * len(results),
        scratch_shapes=scratch,
        compiler_params=pltpu.CompilerParams(
            collective_id=0, has_side_effects=True, vmem_limit_bytes=VMEM_LIMIT
        ),
        name="block",
    )(*arguments)


def finish_kernel(
    out, grad, wq, wf, wp, wo, vec,
    out_done, grad_done, gain1, bias1, wq_done, qv, wo_done, out_bias, gain2, bias2,
    wf_done, fc, wp_done, proj,
):
    out_done[...] = out[...]
    grad_done[...] = grad[...]
    for i in range(3):
        wq_done[i] = wide(wq[:, i * WIDTH : (i + 1) * WIDTH])
    wo_done[...] = wide(wo[...])
    wf_done[...] = wide(wf[...])
    wp_done[...] = wide(wp[...])
    singles = ((gain1, V_GAIN1), (bias1, V_BIAS1), (out_bias, V_OUT), (gain2, V_GAIN2))
    for target, row in singles + ((bias2, V_BIAS2), (proj, V_PROJ)):
        target[...] = vec[row]
    qv[...] = vec[V_QUERY : V_VALUE + 1]
    for i in range(4):
        fc[pl.ds(i * D, D)] = vec[V_FC + i]


def plane_device(
    tokens, prefix, ln1_gain, ln1_bias, w_qkv, qv_bias, w_out, out_bias,
    ln2_gain, ln2_bias, w_fc, fc_bias, w_proj, proj_bias, cotangent,
):
    pieces = run_block(
        prefix, tokens, ln1_gain, ln1_bias, w_qkv, qv_bias, w_out, out_bias,
        ln2_gain, ln2_bias, w_fc, fc_bias, w_proj, proj_bias, cotangent,
    )
    wide_results = [
        (WIDTH, LEN), (D,), (D,), (3, WIDTH, WIDTH), (2, D), (WIDTH, WIDTH), (D,), (D,), (D,),
        (WIDTH, D), (FF,), (WIDTH, D), (D,),
    ]
    results = [jax.ShapeDtypeStruct((WIDTH, LEN), jnp.bfloat16)]
    results += [jax.ShapeDtypeStruct(dims, jnp.float32) for dims in wide_results]
    return pl.pallas_call(
        finish_kernel,
        out_shape=results,
        in_specs=[pl.BlockSpec(memory_space=pltpu.VMEM)] * len(pieces),
        out_specs=[pl.BlockSpec(memory_space=pltpu.VMEM)] * len(results),
        name="results",
    )(*pieces)


def solution(mesh):
    on_device = plane_device if dict(mesh.shape) == {"dp": 2, "row": 4, "col": 4} else general_device
    placed = (
        P("row", ("dp", "col")),
        P(("dp", "row")),
        P(),
        P(),
        P(None, "row", "col"),
        P(),
        P("col", "row"),
        P(),
        P(),
        P(),
        P("row", "col"),
        P(),
        P("row", "col"),
        P(),
        P("row", ("dp", "col")),
    )
    return jax.shard_map(
        on_device,
        mesh=mesh,
        in_specs=placed,
        out_specs=(
            P("row", ("dp", "col")),
            P("row", ("dp", "col")),
            P(),
            P(),
            P(None, "row", "col"),
            P(),
            P("col", "row"),
            P(),
            P(),
            P(),
            P("row", "col"),
            P(),
            P("row", "col"),
            P(),
        ),
        check_vma=False,
    )
```

```python
import functools

import jax
import jax.numpy as jnp
from jax import lax
from jax.experimental import pallas as pl
from jax.experimental.pallas import tpu as pltpu
from jax.sharding import PartitionSpec as P

D = 768
FF = 3072
HEAD_DIM = 64
LEN = 1024


epsilon = 1e-05
masked_score = -1e30


def feature_totals(values):
    return lax.psum(values, "row")


def column_rows(values):
    return lax.all_gather(values, "col", axis=0, tiled=True)


def row_rows(values):
    return lax.all_gather(values, "row", axis=0, tiled=True)


def summed_over_row(term_fn, row_count):
    return lax.psum_scatter(
        term_fn(jnp.int32(0), row_count * lax.axis_size("row")),
        "row",
        scatter_dimension=0,
        tiled=True,
    )


def summed_over_col(term_fn, row_count):
    return lax.psum_scatter(
        term_fn(jnp.int32(0), row_count * lax.axis_size("col")),
        "col",
        scatter_dimension=0,
        tiled=True,
    )


def take_portion(complete, position, portion_size, along):
    return lax.dynamic_slice_in_dim(complete, position * portion_size, portion_size, along)


def place_portion(portion, position, full_size, along):
    zeroed_shape = portion.shape[:along] + (full_size,) + portion.shape[along + 1 :]
    zeroed = jnp.zeros(zeroed_shape, jnp.float32)
    return lax.dynamic_update_slice_in_dim(zeroed, portion, position * portion.shape[along], along)


def gelu_tanh(values):
    return jax.nn.gelu(values, approximate=True)


def norm_forward(values, norm_gain, norm_offset, totals_fn):
    plain_sum, square_sum = totals_fn((jnp.sum(values, axis=1), jnp.sum(values * values, axis=1)))
    center = (plain_sum / D)[:, None]
    inverse = lax.rsqrt(square_sum[:, None] / D - center * center + epsilon)
    unit_rows = (values - center) * inverse
    return (unit_rows * norm_gain + norm_offset, unit_rows, inverse)


def norm_backward(grad_rows, unit_rows, inverse, norm_gain, totals_fn):
    scaled = grad_rows * norm_gain
    plain_sum, cross_sum = totals_fn((jnp.sum(scaled, axis=1), jnp.sum(scaled * unit_rows, axis=1)))
    return inverse * (scaled - (plain_sum / D)[:, None] - unit_rows * (cross_sum / D)[:, None])


def split_heads(flat_rows):
    return flat_rows.reshape(LEN, flat_rows.shape[1] // HEAD_DIM, HEAD_DIM)


def scores_of(queries, keys_block, limit_value):
    raw_scores = jnp.einsum("qhe,khe->hqk", queries, keys_block, preferred_element_type=jnp.float32)
    raw_scores = raw_scores * HEAD_DIM ** (-0.5)
    places = jnp.arange(LEN, dtype=jnp.int32)
    visible = (places[None, :] <= places[:, None]) | (places[None, :] < limit_value)
    return jnp.where(visible[None], raw_scores, masked_score)


def attend_forward(packed):
    block_rows, limit_value = packed
    queries = split_heads(block_rows[:, 0])
    keys_block = split_heads(block_rows[:, 1])
    values_block = split_heads(block_rows[:, 2])
    scores = scores_of(queries, keys_block, limit_value)
    largest = jnp.max(scores, axis=-1, keepdims=True)
    weights = jnp.exp(scores - largest)
    row_totals = jnp.sum(weights, axis=-1, keepdims=True)
    probs = (weights / row_totals).astype(jnp.bfloat16)
    mixed = jnp.einsum("hqk,khe->qhe", probs, values_block, preferred_element_type=jnp.float32)
    return (mixed.reshape(LEN, -1).astype(jnp.bfloat16), (largest + jnp.log(row_totals))[..., 0])


def attend_backward(packed):
    block_rows, limit_value, log_total, out_grad = packed
    queries = split_heads(block_rows[:, 0])
    keys_block = split_heads(block_rows[:, 1])
    values_block = split_heads(block_rows[:, 2])
    scores = scores_of(queries, keys_block, limit_value)
    probs = jnp.exp(scores - log_total[..., None])
    probs_low = probs.astype(jnp.bfloat16)
    grad_heads = split_heads(out_grad)
    weight_grad = jnp.einsum(
        "qhe,khe->hqk", grad_heads, values_block, preferred_element_type=jnp.float32
    )
    row_inner = jnp.sum(probs * weight_grad, axis=-1, keepdims=True)
    score_grad = (probs * (weight_grad - row_inner)).astype(jnp.bfloat16)
    query_grad = jnp.einsum(
        "hqk,khe->qhe", score_grad, keys_block, preferred_element_type=jnp.float32
    )
    key_grad = jnp.einsum("hqk,qhe->khe", score_grad, queries, preferred_element_type=jnp.float32)
    value_grad = jnp.einsum(
        "hqk,qhe->khe", probs_low, grad_heads, preferred_element_type=jnp.float32
    )
    score_factor = HEAD_DIM ** (-0.5)
    stacked = jnp.stack(
        [
            (query_grad * score_factor).reshape(LEN, -1),
            (key_grad * score_factor).reshape(LEN, -1),
            value_grad.reshape(LEN, -1),
        ],
        axis=1,
    )
    return stacked.astype(jnp.bfloat16)


def general_device(
    tokens,
    prefix,
    ln1_gain,
    ln1_bias,
    w_qkv,
    qv_bias,
    w_out,
    out_bias,
    ln2_gain,
    ln2_bias,
    w_fc,
    fc_bias,
    w_proj,
    proj_bias,
    cotangent,
):
    row_place = lax.axis_index("row")
    col_place = lax.axis_index("col")
    row_devices = lax.axis_size("row")
    col_devices = lax.axis_size("col")
    width_row, local_rows = tokens.shape
    width_col = w_qkv.shape[2]
    hidden_col = w_fc.shape[1]
    seq_rows = local_rows * col_devices // row_devices
    seq_count = seq_rows // LEN
    residual = tokens.T.astype(jnp.float32)
    cotangent_local = cotangent.T
    first_gain = take_portion(ln1_gain, row_place, width_row, 0)
    first_normed, first_unit, first_inverse = norm_forward(
        residual, first_gain, take_portion(ln1_bias, row_place, width_row, 0), feature_totals
    )
    first_gathered = column_rows(first_normed.astype(jnp.bfloat16))

    def qkv_term(first_row, row_count):
        return jnp.einsum("td,sde->tse", first_gathered, w_qkv, preferred_element_type=jnp.float32)

    bias_col = take_portion(qv_bias, col_place, width_col, 1)
    bias_rows = jnp.stack([bias_col[0], jnp.zeros_like(bias_col[0]), bias_col[1]])
    qkv_sum = summed_over_row(qkv_term, seq_rows)
    qkv = (qkv_sum + bias_rows).astype(jnp.bfloat16)
    blocks = qkv.reshape(seq_count, LEN, 3, width_col)
    attn_blocks, log_totals = lax.map(attend_forward, (blocks, prefix))
    attn = attn_blocks.reshape(seq_rows, width_col)
    attn_gathered = row_rows(attn)

    def out_term(first_row, row_count):
        return jnp.dot(attn_gathered, w_out, preferred_element_type=jnp.float32)

    middle = (
        residual
        + summed_over_col(out_term, local_rows)
        + take_portion(out_bias, row_place, width_row, 0)
    )
    grad_output = cotangent_local.astype(jnp.float32)
    second_gain = take_portion(ln2_gain, row_place, width_row, 0)
    second_normed, second_unit, second_inverse = norm_forward(
        middle, second_gain, take_portion(ln2_bias, row_place, width_row, 0), feature_totals
    )
    second_gathered = column_rows(second_normed.astype(jnp.bfloat16))

    def up_term(first_row, row_count):
        return jnp.dot(second_gathered, w_fc, preferred_element_type=jnp.float32)

    hidden = summed_over_row(up_term, seq_rows) + take_portion(fc_bias, col_place, hidden_col, 0)
    active, gelu_pull = jax.vjp(gelu_tanh, hidden)
    active_gathered = row_rows(active.astype(jnp.bfloat16))

    def down_term(first_row, row_count):
        return jnp.einsum("tf,df->td", active_gathered, w_proj, preferred_element_type=jnp.float32)

    final_rows = (
        middle
        + summed_over_col(down_term, local_rows)
        + take_portion(proj_bias, row_place, width_row, 0)
    )
    output = final_rows.astype(jnp.bfloat16)
    grad_gathered = column_rows(cotangent_local)
    w_proj_grad = jnp.einsum(
        "tf,td->df", active_gathered, grad_gathered, preferred_element_type=jnp.float32
    )

    def active_term(first_row, row_count):
        return jnp.einsum("td,df->tf", grad_gathered, w_proj, preferred_element_type=jnp.float32)

    hidden_grad = gelu_pull(summed_over_row(active_term, seq_rows))[0].astype(jnp.bfloat16)
    hidden_gathered = row_rows(hidden_grad)
    w_fc_grad = jnp.einsum(
        "td,tf->df", second_gathered, hidden_gathered, preferred_element_type=jnp.float32
    )

    def second_term(first_row, row_count):
        return jnp.einsum("tf,df->td", hidden_gathered, w_fc, preferred_element_type=jnp.float32)

    second_grad = summed_over_col(second_term, local_rows)
    middle_grad = grad_output + norm_backward(
        second_grad, second_unit, second_inverse, second_gain, feature_totals
    )
    ln2_gain_part = place_portion(jnp.sum(second_grad * second_unit, axis=0), row_place, D, 0)
    ln2_bias_part = place_portion(jnp.sum(second_grad, axis=0), row_place, D, 0)
    fc_bias_part = place_portion(jnp.sum(hidden_grad.astype(jnp.float32), axis=0), col_place, FF, 0)
    proj_bias_part = place_portion(jnp.sum(grad_output, axis=0), row_place, D, 0)
    branch_grad = middle_grad.astype(jnp.bfloat16)
    branch_gathered = column_rows(branch_grad)
    w_out_grad = jnp.einsum(
        "te,td->ed", attn_gathered, branch_gathered, preferred_element_type=jnp.float32
    )

    def attn_term(first_row, row_count):
        return jnp.einsum("td,ed->te", branch_gathered, w_out, preferred_element_type=jnp.float32)

    attn_grad = summed_over_row(attn_term, seq_rows).astype(jnp.bfloat16)
    qkv_grad = lax.map(
        attend_backward, (blocks, prefix, log_totals, attn_grad.reshape(seq_count, LEN, width_col))
    )
    qkv_grad = qkv_grad.reshape(seq_rows, 3, width_col)
    qkv_gathered = row_rows(qkv_grad)
    w_qkv_grad = jnp.einsum(
        "td,tse->sde", first_gathered, qkv_gathered, preferred_element_type=jnp.float32
    )

    def first_term(first_row, row_count):
        return jnp.einsum("tse,sde->td", qkv_gathered, w_qkv, preferred_element_type=jnp.float32)

    first_grad = summed_over_col(first_term, local_rows)
    input_grad = middle_grad + norm_backward(
        first_grad, first_unit, first_inverse, first_gain, feature_totals
    )
    qkv_totals = jnp.sum(qkv_grad.astype(jnp.float32), axis=0)
    qv_part = place_portion(jnp.stack([qkv_totals[0], qkv_totals[2]]), col_place, D, 1)
    out_bias_part = place_portion(jnp.sum(branch_grad.astype(jnp.float32), axis=0), row_place, D, 0)
    ln1_gain_part = place_portion(jnp.sum(first_grad * first_unit, axis=0), row_place, D, 0)
    ln1_bias_part = place_portion(jnp.sum(first_grad, axis=0), row_place, D, 0)
    vectors = lax.psum(
        (
            ln1_gain_part,
            ln1_bias_part,
            qv_part,
            out_bias_part,
            ln2_gain_part,
            ln2_bias_part,
            fc_bias_part,
            proj_bias_part,
        ),
        ("dp", "row", "col"),
    )
    matrices = (
        lax.psum(w_qkv_grad.astype(jnp.bfloat16), "dp").astype(jnp.float32),
        lax.psum(w_out_grad.astype(jnp.bfloat16), "dp").astype(jnp.float32),
        lax.psum(w_fc_grad.astype(jnp.bfloat16), "dp").astype(jnp.float32),
        lax.psum(w_proj_grad.astype(jnp.bfloat16), "dp").astype(jnp.float32),
    )
    return (
        output.T,
        input_grad.T,
        vectors[0],
        vectors[1],
        matrices[0],
        vectors[2],
        matrices[1],
        vectors[3],
        vectors[4],
        vectors[5],
        matrices[2],
        vectors[6],
        matrices[3],
        vectors[7],
    )


MESH = pl.DeviceIdType.MESH
WIDTH = 192
HALF = 96
QUARTER = 256
LANES = 128
WQ = 3 * WIDTH
VMEM_LIMIT = 67043328
REMOTES = 208
LOCALS = 64
FACTOR = HEAD_DIM ** (-0.5)
ANY = pl.BlockSpec(memory_space=pl.ANY)
GAIN1, BIAS1, OUT_BIAS, GAIN2, BIAS2, PROJ_BIAS, Q_BIAS, V_BIAS, FC_BIAS = range(9)
V_GAIN1, V_BIAS1, V_QUERY, V_VALUE, V_OUT, V_GAIN2, V_BIAS2, V_PROJ, V_FC = range(9)
CENTER, INVERSE = range(2)


def dot(left, right, left_axis, right_axis):
    return lax.dot_general(
        left, right, (((left_axis,), (right_axis,)), ((), ())), preferred_element_type=jnp.float32
    )


def low(value):
    return value.astype(jnp.bfloat16)


def wide(value):
    return value.astype(jnp.float32)


def aligned(start, size):
    return pl.ds(pl.multiple_of(start, size), size)


def merged(value):
    return value.reshape((value.shape[0] * value.shape[1],) + value.shape[2:])


def each(count, body):
    def step(i, carry):
        body(i)
        return carry

    lax.fori_loop(0, count, step, 0)


class Links:
    def __init__(self, send_sems, recv_sems, local_sems):
        self.d, self.r, self.c = (lax.axis_index(n) for n in ("dp", "row", "col"))
        self.send_sems, self.recv_sems, self.local_sems = send_sems, recv_sems, local_sems
        self.remotes = 0
        self.locals = 0

    def across(self, k):
        if k == 0:
            return self.r
        if k == 1:
            return self.r + 1 - 2 * lax.rem(self.r, 2)
        return lax.rem(self.r + 2, 4) if k == 2 else 3 - self.r

    def plane(self, k):
        return (self.d, self.across(k), self.c)

    def height(self, k):
        return lax.rem(self.c + k, 4)

    def column(self, k):
        return (self.d, self.r, self.height(k))

    def partner(self):
        return (1 - self.d, self.r, self.c)

    def half(self, mine=True):
        place = self.d if mine else 1 - self.d
        return pl.ds(pl.multiple_of(place * HALF, 16), HALF)

    def crossing(self, row, place):
        place = place + self.d * (3 - 2 * place)
        low_bit = lax.rem(lax.rem(row, 2) + lax.rem(place, 2), 2)
        return low_bit + 2 * lax.rem(lax.div(row, 2) + lax.div(place, 2), 2)

    def greet(self):
        devices = [self.partner(), *(self.plane(k) for k in (1, 2, 3))]
        devices += [self.column(k) for k in (1, 2, 3)]
        barrier = pltpu.get_barrier_semaphore()
        for device in devices:
            pl.semaphore_signal(barrier, 1, device_id=device, device_id_type=MESH)
        self.greeted = len(devices)
        to, since = self.routed(), self.routed_back()

        @pl.when(jnp.logical_not(self.stays()))
        def _():
            for device in (to, since):
                pl.semaphore_signal(barrier, 1, device_id=device, device_id_type=MESH)

    def meet(self):
        count = jnp.where(self.stays(), self.greeted, self.greeted + 2)
        pl.semaphore_wait(pltpu.get_barrier_semaphore(), count)

    def routed(self):
        return (self.d, self.c, self.crossing(self.r, self.c))

    def routed_back(self):
        return (self.d, self.crossing(self.r, self.c), self.r)

    def stays(self):
        return jnp.logical_and(self.r == self.c, self.crossing(self.r, self.c) == self.c)

    def send(self, source, target, device):
        place = self.remotes
        self.remotes += 1
        copy = pltpu.make_async_remote_copy(
            src_ref=source,
            dst_ref=target,
            send_sem=self.send_sems.at[place],
            recv_sem=self.recv_sems.at[place],
            device_id=device,
            device_id_type=MESH,
        )
        copy.start()
        return copy

    def local(self, source, target):
        place = self.locals
        self.locals += 1
        copy = pltpu.make_async_copy(source, target, self.local_sems.at[place])
        copy.start()
        return copy


class Ticket:
    def __init__(self, links, device):
        self.place = links.remotes
        links.remotes += 1
        self.links, self.device = links, device

    def __call__(self, source, target):
        return pltpu.make_async_remote_copy(
            src_ref=source,
            dst_ref=target,
            send_sem=self.links.send_sems.at[self.place],
            recv_sem=self.links.recv_sems.at[self.place],
            device_id=self.device,
            device_id_type=MESH,
        )


class Move:
    def __init__(self, links, stays, source, target, device):
        self.stays = stays
        self.ticket = Ticket(links, device)
        self.source, self.target = source, target
        place = links.locals
        links.locals += 1
        self.local_sem = links.local_sems.at[place]

        @pl.when(jnp.logical_not(stays))
        def _():
            self.ticket(source, target).start()

        @pl.when(stays)
        def _():
            pltpu.make_async_copy(source, target, self.local_sem).start()

    def wait(self):
        @pl.when(jnp.logical_not(self.stays))
        def _():
            self.ticket(self.source, self.target).wait()

        @pl.when(self.stays)
        def _():
            pltpu.make_async_copy(self.source, self.target, self.local_sem).wait()


class PlaneGather:
    def __init__(self, links, target, in_parts=False):
        self.links, self.target = links, target
        rows = target.shape[1] // 2
        self.low, self.high = pl.ds(0, rows), pl.ds(rows, rows)
        first, second = target.at[links.r, self.low], target.at[links.r, self.high]
        self.x_low = links.send(first, first, links.plane(1))
        self.y_high = links.send(second, second, links.plane(2))
        if not in_parts:
            self.rest()

    def rest(self):
        links, target = self.links, self.target
        first, second = target.at[links.r, self.low], target.at[links.r, self.high]
        self.x_high = links.send(second, second, links.plane(1))
        self.y_low = links.send(first, first, links.plane(2))

    def relay(self):
        links = self.links
        self.x_low.wait_recv()
        block = self.target.at[links.across(1), self.low]
        self.on_y = links.send(block, block, links.plane(2))
        self.y_high.wait_recv()
        block = self.target.at[links.across(2), self.high]
        self.on_x = links.send(block, block, links.plane(1))

    def finish(self):
        self.x_high.wait_recv()
        self.y_low.wait_recv()
        for copy in (self.x_low, self.y_high, self.x_high, self.y_low):
            copy.wait_send()
        self.on_y.wait()
        self.on_x.wait()


class PlaneReduce:
    def __init__(self, links, part_of, rows, over_x, over_y, relayed):
        self.links, self.part_of = links, part_of
        self.halves = (pl.ds(0, rows // 2), pl.ds(rows // 2, rows // 2))
        self.over_x, self.over_y, self.relayed = over_x, over_y, relayed
        self.copies = {}

    def part(self, k, half):
        return self.part_of(self.links.across(k)).at[self.halves[half]]

    def give(self, k):
        links = self.links
        if k == 3:
            self.copies["x3"] = links.send(self.part(3, 0), self.over_x.at[1], links.plane(1))
            self.copies["y3"] = links.send(self.part(3, 1), self.over_y.at[1], links.plane(2))
        elif k == 1:
            self.copies["x1"] = links.send(self.part(1, 0), self.over_x.at[0], links.plane(1))
        elif k == 2:
            self.copies["y2"] = links.send(self.part(2, 1), self.over_y.at[0], links.plane(2))

    def relay(self):
        links = self.links
        self.copies["x3"].wait_recv()
        add_rows(self.over_x.at[1], [self.over_x.at[1], self.part(2, 0)])
        self.copies["xy"] = links.send(self.over_x.at[1], self.relayed.at[0], links.plane(2))
        self.copies["y3"].wait_recv()
        add_rows(self.over_y.at[1], [self.over_y.at[1], self.part(1, 1)])
        self.copies["yx"] = links.send(self.over_y.at[1], self.relayed.at[1], links.plane(1))

    def finish(self):
        for name in ("x3", "y3"):
            self.copies[name].wait_send()
        for name in ("x1", "y2", "xy", "yx"):
            self.copies[name].wait()

    def total(self, lanes):
        parts = []
        for half, over in ((0, self.over_x), (1, self.over_y)):
            value = wide(self.part(0, half)[:, lanes]) + wide(over[0, :, lanes])
            parts.append(value + wide(self.relayed[half, :, lanes]))
        return jnp.concatenate(parts, axis=0)


class Line:
    def __init__(self, links, block_of):
        self.links, self.block_of = links, block_of
        c = links.c
        self.up = [Ticket(links, (links.d, links.r, lax.rem(c + 1, 4))) for _ in range(3)]
        self.down = [Ticket(links, (links.d, links.r, lax.rem(c + 3, 4))) for _ in range(3)]

    def copy(self, ticket, place):
        return ticket(self.block_of(place), self.block_of(place))

    def step(self, t):
        c = self.links.c
        if t > 0:

            @pl.when(c >= t)
            def _():
                self.copy(self.up[t - 1], c - t).wait_recv()

            @pl.when(c <= 3 - t)
            def _():
                self.copy(self.down[t - 1], c + t).wait_recv()

        if t < 3:

            @pl.when(jnp.logical_and(c >= t, c < 3))
            def _():
                self.copy(self.up[t], c - t).start()

            @pl.when(jnp.logical_and(c <= 3 - t, c > 0))
            def _():
                self.copy(self.down[t], c + t).start()

    def finish(self):
        c = self.links.c
        for t in range(3):

            @pl.when(jnp.logical_and(c >= t, c < 3))
            def _(t=t):
                self.copy(self.up[t], c - t).wait_send()

            @pl.when(jnp.logical_and(c <= 3 - t, c > 0))
            def _(t=t):
                self.copy(self.down[t], c + t).wait_send()


class WeightGather:
    def __init__(self, links, stage, moved, target, pieces=1):
        self.links, self.moved, self.target = links, moved, target
        r, c = links.r, links.c
        self.mine = links.half()
        self.goal = links.crossing(r, c)
        size = HALF // pieces
        self.local_rows = [pl.ds(i * size, size) for i in range(pieces)]
        start = links.d * HALF
        self.rows = [pl.ds(pl.multiple_of(start + i * size, 16), size) for i in range(pieces)]
        device = (links.d, r, self.goal)
        self.turns = [
            Move(links, self.goal == c, stage.at[rows], moved.at[rows], device)
            for rows in self.local_rows
        ]

    def hop(self):
        links = self.links
        device = (links.d, self.goal, links.c)
        for i, rows in enumerate(self.local_rows):
            self.turns[i].wait()
            block = self.target.at[links.r, self.rows[i]]
            self.turns[i] = Move(links, self.goal == links.r, self.moved.at[rows], block, device)

    def begin(self):
        links = self.links

        def block_of(rows):
            return lambda place: self.target.at[links.crossing(links.r, place), rows]

        self.ways = []
        for turn, rows in zip(self.turns, self.rows):
            turn.wait()
            self.ways.append(Line(links, block_of(rows)))
            self.ways[-1].step(0)

    def line(self, t):
        if t == 0:
            self.begin()
        else:
            for way in self.ways:
                way.step(t)

    def share(self):
        for way in self.ways:
            way.finish()
        block = self.target.at[:, self.mine]
        self.shared = self.links.send(block, block, self.links.partner())

    def finish(self):
        self.shared.wait()


class RoutedGather(WeightGather):
    def __init__(self, links, stage, target, pieces=1):
        self.links, self.target = links, target
        self.mine = links.half()
        size = HALF // pieces
        start = links.d * HALF
        self.rows = [pl.ds(pl.multiple_of(start + i * size, 16), size) for i in range(pieces)]
        self.turns = [
            Move(
                links,
                links.stays(),
                stage.at[pl.ds(i * size, size)],
                target.at[links.r, rows],
                links.routed(),
            )
            for i, rows in enumerate(self.rows)
        ]


class SquareGather:
    def __init__(self, links, target):
        self.links, self.target = links, target
        self.mine = links.half()
        self.way = Line(links, lambda place: target.at[links.r, place, self.mine])

    def line(self, t):
        self.way.step(t)

    def cross(self):
        self.way.finish()
        self.plane = PlaneGather(self.links, self.target.at[:, :, self.mine])

    def share(self):
        self.plane.finish()
        block = self.target.at[:, :, self.mine]
        self.shared = self.links.send(block, block, self.links.partner())

    def finish(self):
        self.shared.wait()


def add_rows(target, terms):
    if len(terms) == 2:
        target[...] = terms[0][...] + terms[1][...]
        return

    def step(i):
        place = aligned(i * 16, 16)
        total = wide(terms[0][place, :])
        for term in terms[1:]:
            total = total + wide(term[place, :])
        target[place, :] = total.astype(target.dtype)

    each(target.shape[0] // 16, step)


def add_blocks(target, terms):
    if len(target.shape) == 2:
        add_rows(target, terms)
    else:
        each(target.shape[0], lambda i: add_blocks(target.at[i], [term.at[i] for term in terms]))


class LineReduce:
    def __init__(self, links, block_of, up, down):
        self.links, self.block_of, self.up, self.down = links, block_of, up, down
        c = links.c
        self.rise = [Ticket(links, (links.d, links.r, lax.rem(c + 1, 4))) for _ in range(3)]
        self.fall = [Ticket(links, (links.d, links.r, lax.rem(c + 3, 4))) for _ in range(3)]

    def step(self, t):
        c = self.links.c
        for i in range(t + 1):
            goal = 3 - t + i
            self.pass_on(c == i, self.rise[goal - 1], self.up.at[goal - 1], goal, i > 0)
            goal = t - i
            self.pass_on(c == 3 - i, self.fall[goal], self.down.at[goal], goal, i > 0)

    def pass_on(self, here, ticket, slot, goal, adds):
        @pl.when(here)
        def _():
            if adds:
                ticket(slot, slot).wait_recv()
                add_blocks(slot, [slot, self.block_of(goal)])
                ticket(slot, slot).start()
            else:
                ticket(self.block_of(goal), slot).start()

    def total(self, target):
        c = self.links.c
        for goal in range(4):

            @pl.when(c == goal)
            def _(goal=goal):
                terms = [self.block_of(goal)]
                if goal > 0:
                    slot = self.up.at[goal - 1]
                    self.rise[goal - 1](slot, slot).wait_recv()
                    terms.append(slot)
                if goal < 3:
                    slot = self.down.at[goal]
                    self.fall[goal](slot, slot).wait_recv()
                    terms.append(slot)
                add_blocks(target, terms)

        for i in range(3):
            rising, falling = self.up.at[i], self.down.at[i]

            @pl.when(c < i + 1)
            def _(i=i, slot=rising):
                self.rise[i](slot, slot).wait_send()

            @pl.when(c > i)
            def _(i=i, slot=falling):
                self.fall[i](slot, slot).wait_send()


class WeightReduce:
    def __init__(self, links, grad, near, sums, up, down, fin, moved, arrived, result, pieces=1):
        self.links, self.grad, self.near, self.sums = links, grad, near, sums
        self.up, self.down, self.fin = up, down, fin
        self.moved, self.arrived, self.result = moved, arrived, result
        size = HALF // pieces
        self.rows = [pl.ds(i * size, size) for i in range(pieces)]
        self.to_near = [self.send_near(i * size, size) for i in range(pieces)]

    def send_near(self, first, size):
        links = self.links
        other = pl.ds(pl.multiple_of((1 - links.d) * HALF + first, 16), size)
        rows = pl.ds(first, size)
        return links.send(self.grad.at[:, other], self.near.at[:, rows], links.partner())

    def add_near(self):
        links = self.links

        def block_of(rows):
            return lambda place: self.sums.at[links.crossing(links.r, place), rows]

        self.ways = []
        for copy, rows in zip(self.to_near, self.rows):
            copy.wait()
            first = links.d * HALF + rows.start
            mine = pl.ds(pl.multiple_of(first, 16), rows.size)
            each(
                4,
                lambda b, rows=rows, mine=mine: add_rows(
                    self.sums.at[b, rows], [self.grad.at[b, mine], self.near.at[b, rows]]
                ),
            )
            up, down = self.up.at[:, rows], self.down.at[:, rows]
            self.ways.append(LineReduce(links, block_of(rows), up, down))

    def line(self, i):
        for way in self.ways:
            way.step(i)

    def hop(self):
        links = self.links
        self.goal = links.crossing(links.r, links.c)
        device = (links.d, self.goal, links.c)
        self.turns = []
        for way, rows in zip(self.ways, self.rows):
            way.total(self.fin.at[rows])
            stays = self.goal == links.r
            self.turns.append(Move(links, stays, self.fin.at[rows], self.moved.at[rows], device))

    def back(self):
        links = self.links
        device = (links.d, links.r, self.goal)
        for i, rows in enumerate(self.rows):
            self.turns[i].wait()
            stays = self.goal == links.c
            self.turns[i] = Move(links, stays, self.moved.at[rows], self.arrived.at[rows], device)

    def share(self):
        for turn in self.turns:
            turn.wait()
        self.give(self.arrived)

    def give(self, total):
        links, mine = self.links, self.links.half()
        self.last = [
            links.send(total, self.result.at[mine], links.partner()),
            links.local(total, self.result.at[mine]),
        ]

    def finish(self):
        for copy in self.last:
            copy.wait()


class SquareReduce(WeightReduce):
    def __init__(self, links, grad, near, sums, up, down, fin, came, arrived, result):
        self.links, self.grad, self.near, self.sums = links, grad, near, sums
        self.up, self.down, self.fin = up, down, fin
        self.came, self.arrived, self.result = came, arrived, result
        self.to_near = links.send(grad.at[:, :, links.half(False)], near, links.partner())

    def add_near(self):
        mine = self.links.half()
        self.to_near.wait()
        add_blocks(self.sums, [self.grad.at[:, :, mine], self.near])
        self.ways = [
            LineReduce(self.links, lambda place: self.sums.at[:, place], self.up, self.down)
        ]

    def hop(self):
        links = self.links
        self.ways[0].total(self.fin)
        self.crossing = [
            links.send(self.fin.at[links.across(k)], self.came.at[k - 1], links.plane(k))
            for k in (3, 1, 2)
        ]

    def back(self):
        for copy in self.crossing:
            copy.wait()
        came = self.came
        add_rows(self.arrived, [self.fin.at[self.links.r], came.at[0], came.at[1], came.at[2]])

    def share(self):
        self.give(self.arrived)


def normalize(source_of, target, stats, gain, offset):
    def step(j):
        lanes = aligned(j * LANES, LANES)
        values = source_of(lanes)
        center = jnp.sum(values, axis=0, keepdims=True) / D
        square = jnp.sum(values * values, axis=0, keepdims=True) / D
        inverse = lax.rsqrt(square - center * center + epsilon)
        stats[CENTER : CENTER + 1, lanes] = center
        stats[INVERSE : INVERSE + 1, lanes] = inverse
        target[:, lanes] = low((values - center) * inverse * gain[...] + offset[...])

    each(LEN // LANES, step)


def key_span(block):
    return max(512, (block + 1) * QUARTER), block * QUARTER


def visible(block, first, last, limit_value):
    shape = (last - first, QUARTER)
    keys = lax.broadcasted_iota(jnp.int32, shape, 0) + first
    queries = lax.broadcasted_iota(jnp.int32, shape, 1) + block * QUARTER
    return (keys <= queries) | (keys < limit_value)


def masked(value, block, limit_value, fill):
    last, first = key_span(block)
    tail = jnp.where(visible(block, first, last, limit_value), value[first:], fill)
    return jnp.concatenate([value[:first], tail], axis=0) if first else tail


def head_rows(h, part):
    return pl.ds(h * HEAD_DIM + part * WIDTH, HEAD_DIM)


def attend(qkv, limit_value, attn_of, log_total, between):
    def head(h):
        for block in range(4):
            for action in between.get(h * 4 + block, ()):
                action()
            last, _ = key_span(block)
            lanes = slice(block * QUARTER, (block + 1) * QUARTER)
            queries = qkv[head_rows(h, 0), lanes] * jnp.bfloat16(FACTOR)
            scores = dot(qkv[head_rows(h, 1), :last], queries, 0, 0)
            scores = masked(scores, block, limit_value, masked_score)
            largest = jnp.max(scores, axis=0, keepdims=True)
            weights = jnp.exp(scores - largest)
            total = jnp.sum(weights, axis=0, keepdims=True)
            mixed = dot(qkv[head_rows(h, 2), :last], low(weights), 1, 0)
            attn_of(head_rows(h, 0), lanes, low(mixed * (1.0 / total)))
            log_total[pl.ds(h, 1), lanes] = largest + jnp.log(total)

    for h in range(3):
        head(h)


def attend_back(
    qkv, limit_value, attn_of, log_total, out_grad, qkv_grad, key_sum, value_sum, between
):
    def head(h):
        for block in (3, 2, 1, 0):
            for action in between.get(h * 4 + 3 - block, ()):
                action()
            last, _ = key_span(block)
            lanes = slice(block * QUARTER, (block + 1) * QUARTER)
            queries = qkv[head_rows(h, 0), lanes] * jnp.bfloat16(FACTOR)
            grads = out_grad[head_rows(h, 0), lanes]
            inner = jnp.sum(
                wide(attn_of(head_rows(h, 0), lanes)) * wide(grads), axis=0, keepdims=True
            )
            scores = dot(qkv[head_rows(h, 1), :last], queries, 0, 0)
            probs = jnp.exp(scores - log_total[pl.ds(h, 1), lanes])
            probs = masked(probs, block, limit_value, 0.0)
            weight_grad = dot(qkv[head_rows(h, 2), :last], grads, 0, 0)
            score_grad = low(probs * (weight_grad - inner))
            query_grad = dot(qkv[head_rows(h, 1), :last], score_grad, 1, 0) * FACTOR
            qkv_grad[head_rows(h, 0), lanes] = low(query_grad)
            key_grad = dot(queries, score_grad, 1, 1)
            value_grad = dot(grads, low(probs), 1, 1)
            if block == 3:
                key_sum[...] = key_grad
                value_sum[...] = value_grad
            else:
                key_sum[:, :last] += key_grad
                value_sum[:, :last] += value_grad
        qkv_grad[head_rows(h, 1), :] = low(key_sum[...])
        qkv_grad[head_rows(h, 2), :] = low(value_sum[...])

    for h in range(3):
        head(h)


def gelu_parts(u):
    slope = (2.0 / 3.141592653589793) ** 0.5
    square = u * u
    bent = jnp.tanh(slope * u * (1.0 + 0.044715 * square))
    shared = 0.5 * (1.0 + bent)
    derivative = shared + 0.5 * u * (1.0 - bent * bent) * (slope * (1.0 + 3.0 * 0.044715 * square))
    return u * shared, derivative


def block_kernel(
    limit, tok, gain1_in, bias1_in, wq_in, qv_in, wo_in, out_in, gain2_in, bias2_in,
    wf_in, fc_in, wp_in, proj_in, cot,
    out_hbm, grad_hbm, wq_hbm, wf_hbm, wp_hbm, wo_hbm, vec_hbm,
    rows1, qv, fc, wq_here, xt, gt, wqa, wfa, wpa, woa, zq, zf, zp, mf, mp, pres, colb,
    fn, qkv, at, lse, st1, st2, mid, sn, act, slope, op, hg, sp,
    x2, y2, z2, x_out, y_out, z_out, x1, y1, z1, br, ap, dout, brf, dqkv, ksum, vsum,
    gf, gp, gq, near_f, near_p, near_q, sum_f, sum_p, sum_q, up_f, up_p, up_q, dn_f, dn_p, dn_q,
    fin_f, fin_p, fin_q, hop_f, hop_p, hop_q, got_f, got_p, got_q,
    sq, near_o, sum_o, up_o, dn_o, fin_o, hop_o, got_o,
    fgp, fsum, vcol, vec, vec_in, stat, stat_in, out_v, grad_v,
    send_sems, recv_sems, local_sems,
):
    links = Links(send_sems, recv_sems, local_sems)
    r, c = links.r, links.c
    mine = links.half()
    own = aligned(r * QUARTER, QUARTER)
    links.greet()
    singles = (gain1_in, bias1_in, out_in, gain2_in, bias2_in, proj_in)
    first = [links.local(wq_in.at[:, mine], wq_here), links.local(tok, xt.at[r])]
    first += [links.local(wo_in.at[mine], woa.at[r, c, mine])]
    first += [links.local(source, rows1.at[i]) for i, source in enumerate(singles)]
    first += [links.local(qv_in, qv), links.local(fc_in, fc)]
    then = [links.local(wf_in.at[mine], zf), links.local(wp_in.at[mine], zp)]
    then += [links.local(cot, gt.at[r])]
    for copy in first:
        copy.wait()
    zq[...] = jnp.concatenate([wq_here[i] for i in range(3)], axis=1)
    pres[r] = jnp.full((8, LANES), limit[0], jnp.int32)

    links.meet()

    get_q = RoutedGather(links, zq, wqa, 3)
    get_o = SquareGather(links, woa)
    get_o.line(0)
    tokens = PlaneGather(links, xt, in_parts=True)
    for copy in then:
        copy.wait()
    prefixes = [links.send(pres.at[r], pres.at[r], links.plane(k)) for k in (1, 2, 3)]
    get_q.line(0)
    tokens.rest()
    get_f = WeightGather(links, zf, mf, wfa)
    get_o.line(1)

    def column(kind, place, values):
        spread = jnp.broadcast_to(values[None, :], (LANES, LANES))
        colb[kind, pl.ds(place * LANES, LANES)] = spread.T

    for place in range(D // LANES):
        part = pl.ds(place * LANES, LANES)
        for kind in range(len(singles)):
            column(kind, place, rows1[kind, part])
        column(Q_BIAS, place, qv[0, part])
        column(V_BIAS, place, qv[1, part])
        column(FC_BIAS, place, fc[pl.ds(pl.multiple_of(r * D + place * LANES, LANES), LANES)])

    tokens.relay()
    get_q.line(1)
    get_o.line(2)
    get_f.hop()
    get_q.line(2)
    get_o.line(3)
    get_p = WeightGather(links, zp, mp, wpa)
    get_q.line(3)
    get_q.share()
    get_f.line(0)
    tokens.finish()
    get_o.cross()
    grads = PlaneGather(links, gt, in_parts=True)
    get_p.hop()
    normalize(
        lambda lanes: wide(merged(xt[:, :, lanes])), fn, st1, colb.at[GAIN1], colb.at[BIAS1]
    )
    for copy in prefixes:
        copy.wait()
    get_q.finish()
    head_bias = aligned(r * WIDTH, WIDTH)

    def project(b):
        lanes = aligned(b * QUARTER, QUARTER)
        nothing = jnp.zeros((WIDTH, LANES), jnp.float32)
        bias = [colb[Q_BIAS, head_bias], nothing, colb[V_BIAS, head_bias]]
        bias = jnp.concatenate(bias, axis=0)
        value = dot(merged(wqa[...]), fn[:, lanes], 0, 0)
        qkv[:, lanes] = low(value + jnp.concatenate([bias, bias], axis=1))

    each(4, project)
    limit_value = pres[c][0:1, 0:1]

    def put_attn(rows, lanes, value):
        at[r, rows, lanes] = value

    def get_attn(rows, lanes):
        return at[r, rows, lanes]

    attns = []

    def gather_head(h):
        attns.append(PlaneGather(links, at.at[:, h * HEAD_DIM : (h + 1) * HEAD_DIM]))

    def get_o_relay():
        get_o.plane.relay()

    attend(
        qkv,
        limit_value,
        put_attn,
        lse,
        {
            0: [get_o_relay],
            1: [lambda: get_f.line(1)],
            4: [lambda: gather_head(0)],
            7: [lambda: get_f.line(2)],
            8: [lambda: gather_head(1), lambda: attns[0].relay()],
            10: [lambda: get_p.line(0)],
        },
    )
    gather_head(2)
    attns[1].relay()
    get_f.line(3)
    get_f.share()
    get_o.share()
    attns[2].relay()
    grads.rest()
    get_p.line(1)
    get_o.finish()
    for attn in attns:
        attn.finish()
    grads.relay()

    def join(b):
        rows = aligned(b * WIDTH, WIDTH)
        bias = jnp.concatenate([colb[OUT_BIAS, rows]] * 8, axis=1)
        value = dot(merged(woa[b]), merged(at[...]), 0, 0)
        mid[rows, :] = wide(xt[b]) + (value + bias)

    each(4, join)
    get_p.line(2)
    normalize(lambda lanes: mid[:, lanes], sn, st2, colb.at[GAIN2], colb.at[BIAS2])
    get_f.finish()

    def up(b):
        lanes = aligned(b * QUARTER, QUARTER)
        bias = colb[FC_BIAS]
        value = dot(merged(wfa[...]), sn[:, lanes], 0, 0) + jnp.concatenate([bias, bias], axis=1)
        value, derivative = gelu_parts(value)
        act[:, lanes] = low(value)
        slope[:, lanes] = derivative

    each(2, up)
    get_p.line(3)
    get_p.share()
    each(2, lambda b: up(b + 2))
    grads.finish()

    def proj_grads(b):
        some = aligned(b * QUARTER, QUARTER)
        value = low(dot(merged(gt[...]), act[some, :], 1, 1))
        gp[:, :, some] = value.reshape(4, WIDTH, QUARTER)

    each(3, proj_grads)
    put_p = WeightReduce(links, gp, near_p, sum_p, up_p, dn_p, fin_p, hop_p, got_p, wp_hbm)
    get_p.finish()

    seconds = PlaneReduce(
        links, lambda place: sp.at[:, aligned(place * QUARTER, QUARTER)], D, x2, y2, z2
    )
    for k in (3, 1, 2, 0):
        lanes = aligned(links.across(k) * QUARTER, QUARTER)
        value = dot(merged(wpa[...]), merged(gt[:, :, lanes]), 0, 0)
        hg[:, lanes] = low(value * slope[:, lanes])
        sp[:, lanes] = low(dot(merged(wfa[...]), hg[:, lanes], 1, 0))
        seconds.give(k)
        if k == 2:
            put_p.add_near()
            put_p.line(0)

    def fc_grads(b):
        some = aligned(b * QUARTER, QUARTER)
        value = low(dot(sn[...], hg[some, :], 1, 1))
        gf[:, :, some] = value.reshape(4, WIDTH, QUARTER)

    each(3, fc_grads)
    put_f = WeightReduce(links, gf, near_f, sum_f, up_f, dn_f, fin_f, hop_f, got_f, wf_hbm)
    seconds.relay()
    put_p.line(1)

    def down(b):
        lanes = aligned(b * QUARTER, QUARTER)
        value = low(dot(merged(wpa[...]), act[:, lanes], 1, 0))
        op[:, :, lanes] = value.reshape(4, WIDTH, QUARTER)

    each(4, down)
    outs = PlaneReduce(links, lambda place: op.at[place], WIDTH, x_out, y_out, z_out)
    put_f.add_near()
    put_f.line(0)
    lane = lax.broadcasted_iota(jnp.int32, (D, LANES), 1)
    total = jnp.zeros((D, 1), jnp.float32)
    for b in range(4):
        lanes = slice(b * QUARTER, (b + 1) * QUARTER)
        total = total + jnp.sum(wide(hg[:, lanes]), axis=1, keepdims=True)
    vcol[...] = jnp.where(lane == V_FC + r, total, 0.0)
    put_p.line(2)
    seconds.finish()
    outs.give(3)

    def back(j):
        lanes = aligned(r * QUARTER + j * LANES, LANES)
        part = aligned(j * LANES, LANES)
        given = seconds.total(part)
        inverse = st2[INVERSE : INVERSE + 1, lanes]
        unit = (mid[:, lanes] - st2[CENTER : CENTER + 1, lanes]) * inverse
        scaled = given * colb[GAIN2]
        plain = jnp.sum(scaled, axis=0, keepdims=True) / D
        cross = jnp.sum(scaled * unit, axis=0, keepdims=True) / D
        above = wide(merged(gt[:, :, lanes]))
        branch = low(above + inverse * (scaled - plain - unit * cross))
        br[:, :, part] = branch.reshape(4, WIDTH, LANES)
        value = jnp.where(lane == V_GAIN2, jnp.sum(given * unit, axis=1, keepdims=True), 0.0)
        value = jnp.where(lane == V_BIAS2, jnp.sum(given, axis=1, keepdims=True), value)
        value = jnp.where(lane == V_OUT, jnp.sum(wide(branch), axis=1, keepdims=True), value)
        value = jnp.where(lane == V_PROJ, jnp.sum(above, axis=1, keepdims=True), value)
        vcol[...] = vcol[...] + value

    for j in range(2):
        back(j)
    value = dot(merged(woa[0]), br[0], 1, 0)
    for b in range(1, 4):
        value = value + dot(merged(woa[b]), br[b], 1, 0)
    ap[...] = low(value).reshape(4, WIDTH, QUARTER)
    turns = [
        links.send(ap.at[links.across(k)], dout.at[:, own], links.plane(k)) for k in (3, 1, 2)
    ]
    turns.append(links.local(ap.at[r], dout.at[:, own]))
    def square_grads(b):
        value = low(dot(merged(at[:, :, own]), br[b], 1, 1))
        sq[b] = value.reshape(4, WIDTH, WIDTH)

    each(4, square_grads)
    put_o = SquareReduce(links, sq, near_o, sum_o, up_o, dn_o, fin_o, hop_o, got_o, wo_hbm)
    put_f.line(1)
    put_o.add_near()
    put_p.hop()
    for copy in turns:
        copy.wait()
    outs.give(1)
    outs.give(2)
    swaps = [
        links.send(br.at[links.across(k)], brf.at[:, own], links.plane(k)) for k in (3, 1, 2)
    ]
    swaps.append(links.local(br.at[r], brf.at[:, own]))
    attend_back(
        qkv, limit_value, get_attn, lse, dout, dqkv, ksum, vsum,
        {
            0: [lambda: put_o.line(0)],
            2: [lambda: put_f.line(2)],
            4: [put_p.back, outs.relay],
            9: [put_f.hop, put_p.share],
            11: [lambda: put_o.line(1)],
        },
    )
    for some in (slice(0, 256), slice(256, 512), slice(512, WQ)):
        value = low(dot(fn[...], dqkv[some, :], 1, 1))
        gq[:, :, some] = value.reshape(4, WIDTH, some.stop - some.start)
    put_q = WeightReduce(links, gq, near_q, sum_q, up_q, dn_q, fin_q, hop_q, got_q, wq_hbm, 3)

    stat[...] = jnp.zeros_like(stat)
    firsts = PlaneReduce(links, lambda place: fgp.at[place], WIDTH, x1, y1, z1)
    for k in (3, 1, 2, 0):
        b = links.across(k)
        rows = aligned(b * WIDTH, WIDTH)

        fsum[...] = jnp.zeros_like(fsum)

        def first_part(j, b=b, rows=rows):
            lanes = aligned(j * QUARTER, QUARTER)
            value = dot(wqa[b], dqkv[:, lanes], 1, 0)
            fgp[b, :, lanes] = low(value)
            gain = colb[GAIN1, rows]
            for i in range(2):
                half = aligned(j * QUARTER + i * LANES, LANES)
                piece = value[:, i * LANES : (i + 1) * LANES]
                unit = wide(xt[b, :, half]) - st1[CENTER : CENTER + 1, half]
                weighted = piece * (unit * st1[INVERSE : INVERSE + 1, half])
                stat[0:1, half] += jnp.sum(piece * gain, axis=0, keepdims=True)
                stat[1:2, half] += jnp.sum(weighted * gain, axis=0, keepdims=True)
                fsum[0] += weighted
                fsum[1] += piece

        each(4, first_part)
        firsts.give(k)
        spot = lane[:WIDTH]
        add = jnp.where(spot == V_GAIN1, jnp.sum(fsum[0], axis=1, keepdims=True), 0.0)
        add = jnp.where(spot == V_BIAS1, jnp.sum(fsum[1], axis=1, keepdims=True), add)
        vcol[rows, :] = vcol[rows, :] + add
        if k == 3:
            put_q.add_near()
            put_q.line(0)
            put_f.back()
    stat_sends = [links.send(stat, stat_in.at[k - 1], links.plane(k)) for k in (1, 2, 3)]
    put_q.line(1)
    firsts.relay()
    put_o.line(2)
    put_f.share()
    rows = aligned(r * WIDTH, WIDTH)
    spot = lane[:WIDTH]
    query = jnp.zeros((WIDTH, 1), jnp.float32)
    value = jnp.zeros((WIDTH, 1), jnp.float32)
    for b in range(4):
        lanes = slice(b * QUARTER, (b + 1) * QUARTER)
        query = query + jnp.sum(wide(dqkv[:WIDTH, lanes]), axis=1, keepdims=True)
        value = value + jnp.sum(wide(dqkv[2 * WIDTH :, lanes]), axis=1, keepdims=True)
    add = jnp.where(spot == V_QUERY, query, jnp.where(spot == V_VALUE, value, 0.0))
    vcol[rows, :] = vcol[rows, :] + add
    vec[0] = vcol[...].T[:16]
    vec_near = links.send(vec.at[0], vec_in.at[0], links.partner())
    put_q.line(2)
    vec_near.wait()
    vec[1] = vec[0] + vec_in[0]
    vec_plane = [links.send(vec.at[1], vec_in.at[k], links.plane(k)) for k in (1, 2, 3)]
    put_o.hop()
    put_q.hop()
    put_o.back()
    put_o.share()
    put_q.back()
    for copy in vec_plane:
        copy.wait()
    vec[2] = vec[1] + vec_in[1] + vec_in[2] + vec_in[3]
    vec_high = [links.send(vec.at[2], vec_in.at[3 + k], links.column(k)) for k in (1, 2, 3)]
    outs.finish()

    def last_out(j):
        lanes = aligned(j * LANES, LANES)
        value = mid[rows, lanes] + colb[PROJ_BIAS, rows] + outs.total(lanes)
        out_v[:, lanes] = low(value)

    each(LEN // LANES, last_out)
    ends = [links.local(out_v, out_hbm)]
    for copy in swaps + stat_sends:
        copy.wait()
    firsts.finish()
    stat[...] = stat[...] + stat_in[0] + stat_in[1] + stat_in[2]

    def last_grad(j):
        lanes = aligned(j * LANES, LANES)
        inverse = st1[INVERSE : INVERSE + 1, lanes]
        unit = (wide(xt[r, :, lanes]) - st1[CENTER : CENTER + 1, lanes]) * inverse
        value = firsts.total(lanes) * colb[GAIN1, rows] - stat[0:1, lanes] / D
        grad_v[:, lanes] = wide(brf[:, lanes]) + inverse * (value - unit * (stat[1:2, lanes] / D))

    each(LEN // LANES, last_grad)
    ends.append(links.local(grad_v, grad_hbm))
    put_q.share()
    for copy in vec_high:
        copy.wait()
    vec[3] = vec[2] + vec_in[4] + vec_in[5] + vec_in[6]
    ends.append(links.local(vec.at[3], vec_hbm))
    for copy in ends:
        copy.wait()
    for put in (put_f, put_p, put_o, put_q):
        put.finish()


def run_block(*arguments):
    narrow, full = jnp.bfloat16, jnp.float32
    vmem = pltpu.VMEM
    sequence, tall = (4, WIDTH, LEN), (D, LEN)

    def thirds(lead=()):
        return [vmem(lead + (HALF, width), narrow) for width in (D, D, WQ)]

    def plane_sums(rows, lanes):
        return [vmem((2, rows // 2, lanes), narrow) for _ in range(3)]

    scratch = [
        vmem((6, D), full), vmem((2, D), full), vmem((FF,), full), vmem((3, HALF, WIDTH), narrow),
        vmem(sequence, narrow), vmem(sequence, narrow),
        vmem((4, WIDTH, WQ), narrow), vmem((4, WIDTH, D), narrow), vmem((4, WIDTH, D), narrow),
        vmem((4, 4, WIDTH, WIDTH), narrow),
        vmem((HALF, WQ), narrow), vmem((HALF, D), narrow), vmem((HALF, D), narrow),
        vmem((HALF, D), narrow), vmem((HALF, D), narrow),
        vmem((4, 8, LANES), jnp.int32), vmem((9, D, LANES), full),
        vmem(tall, narrow), vmem((WQ, LEN), narrow), vmem(sequence, narrow),
        vmem((8, LEN), full), vmem((8, LEN), full), vmem((8, LEN), full),
        vmem(tall, full), vmem(tall, narrow), vmem(tall, narrow), vmem(tall, full),
        vmem(sequence, narrow), vmem(tall, narrow), vmem(tall, narrow),
        *plane_sums(D, QUARTER), *plane_sums(WIDTH, LEN), *plane_sums(WIDTH, LEN),
        vmem((4, WIDTH, QUARTER), narrow), vmem((4, WIDTH, QUARTER), narrow),
        vmem((WIDTH, LEN), narrow), vmem((WIDTH, LEN), narrow), vmem((WQ, LEN), narrow),
        vmem((HEAD_DIM, LEN), full), vmem((HEAD_DIM, LEN), full),
        vmem((4, WIDTH, D), narrow), vmem((4, WIDTH, D), narrow), vmem((4, WIDTH, WQ), narrow),
        *thirds((4,)), *thirds((4,)), *thirds((3,)), *thirds((3,)), *thirds(), *thirds(), *thirds(),
        vmem((4, 4, WIDTH, WIDTH), narrow), vmem((4, 4, HALF, WIDTH), narrow),
        vmem((4, 4, HALF, WIDTH), narrow), vmem((3, 4, HALF, WIDTH), narrow),
        vmem((3, 4, HALF, WIDTH), narrow), vmem((4, HALF, WIDTH), narrow),
        vmem((3, HALF, WIDTH), narrow), vmem((HALF, WIDTH), narrow),
        vmem(sequence, narrow), vmem((2, WIDTH, LANES), full), vmem((D, LANES), full),
        vmem((4, 16, D), full), vmem((7, 16, D), full), vmem((8, LEN), full), vmem((3, 8, LEN), full),
        vmem((WIDTH, LEN), narrow), vmem((WIDTH, LEN), full),
        pltpu.SemaphoreType.DMA((REMOTES,)), pltpu.SemaphoreType.DMA((REMOTES,)),
        pltpu.SemaphoreType.DMA((LOCALS,)),
    ]
    results = [
        ((WIDTH, LEN), narrow), ((WIDTH, LEN), full), ((WIDTH, WQ), narrow), ((WIDTH, D), narrow),
        ((WIDTH, D), narrow), ((WIDTH, WIDTH), narrow), ((16, D), full),
    ]
    return pl.pallas_call(
        block_kernel,
        out_shape=[jax.ShapeDtypeStruct(*result) for result in results],
        in_specs=[pl.BlockSpec(memory_space=pltpu.SMEM)] + [ANY] * (len(arguments) - 1),
        out_specs=[ANY] * len(results),
        scratch_shapes=scratch,
        compiler_params=pltpu.CompilerParams(
            collective_id=0, has_side_effects=True, vmem_limit_bytes=VMEM_LIMIT
        ),
        name="block",
    )(*arguments)


def finish_kernel(
    out, grad, wq, wf, wp, wo, vec,
    out_done, grad_done, gain1, bias1, wq_done, qv, wo_done, out_bias, gain2, bias2,
    wf_done, fc, wp_done, proj,
):
    out_done[...] = out[...]
    grad_done[...] = grad[...]
    for i in range(3):
        wq_done[i] = wide(wq[:, i * WIDTH : (i + 1) * WIDTH])
    wo_done[...] = wide(wo[...])
    wf_done[...] = wide(wf[...])
    wp_done[...] = wide(wp[...])
    singles = ((gain1, V_GAIN1), (bias1, V_BIAS1), (out_bias, V_OUT), (gain2, V_GAIN2))
    for target, row in singles + ((bias2, V_BIAS2), (proj, V_PROJ)):
        target[...] = vec[row]
    qv[...] = vec[V_QUERY : V_VALUE + 1]
    for i in range(4):
        fc[pl.ds(i * D, D)] = vec[V_FC + i]


def plane_device(
    tokens, prefix, ln1_gain, ln1_bias, w_qkv, qv_bias, w_out, out_bias,
    ln2_gain, ln2_bias, w_fc, fc_bias, w_proj, proj_bias, cotangent,
):
    pieces = run_block(
        prefix, tokens, ln1_gain, ln1_bias, w_qkv, qv_bias, w_out, out_bias,
        ln2_gain, ln2_bias, w_fc, fc_bias, w_proj, proj_bias, cotangent,
    )
    wide_results = [
        (WIDTH, LEN), (D,), (D,), (3, WIDTH, WIDTH), (2, D), (WIDTH, WIDTH), (D,), (D,), (D,),
        (WIDTH, D), (FF,), (WIDTH, D), (D,),
    ]
    results = [jax.ShapeDtypeStruct((WIDTH, LEN), jnp.bfloat16)]
    results += [jax.ShapeDtypeStruct(dims, jnp.float32) for dims in wide_results]
    return pl.pallas_call(
        finish_kernel,
        out_shape=results,
        in_specs=[pl.BlockSpec(memory_space=pltpu.VMEM)] * len(pieces),
        out_specs=[pl.BlockSpec(memory_space=pltpu.VMEM)] * len(results),
        name="results",
    )(*pieces)


def solution(mesh):
    on_device = plane_device if dict(mesh.shape) == {"dp": 2, "row": 4, "col": 4} else general_device
    placed = (
        P("row", ("dp", "col")),
        P(("dp", "row")),
        P(),
        P(),
        P(None, "row", "col"),
        P(),
        P("col", "row"),
        P(),
        P(),
        P(),
        P("row", "col"),
        P(),
        P("row", "col"),
        P(),
        P("row", ("dp", "col")),
    )
    return jax.shard_map(
        on_device,
        mesh=mesh,
        in_specs=placed,
        out_specs=(
            P("row", ("dp", "col")),
            P("row", ("dp", "col")),
            P(),
            P(),
            P(None, "row", "col"),
            P(),
            P("col", "row"),
            P(),
            P(),
            P(),
            P("row", "col"),
            P(),
            P("row", "col"),
            P(),
        ),
        check_vma=False,
    )
```

```python
import functools

import jax
import jax.numpy as jnp
from jax import lax
from jax.experimental import pallas as pl
from jax.experimental.pallas import tpu as pltpu
from jax.sharding import PartitionSpec as P

D = 768
FF = 3072
HEAD_DIM = 64
LEN = 1024


epsilon = 1e-05
masked_score = -1e30


def feature_totals(values):
    return lax.psum(values, "row")


def column_rows(values):
    return lax.all_gather(values, "col", axis=0, tiled=True)


def row_rows(values):
    return lax.all_gather(values, "row", axis=0, tiled=True)


def summed_over_row(term_fn, row_count):
    return lax.psum_scatter(
        term_fn(jnp.int32(0), row_count * lax.axis_size("row")),
        "row",
        scatter_dimension=0,
        tiled=True,
    )


def summed_over_col(term_fn, row_count):
    return lax.psum_scatter(
        term_fn(jnp.int32(0), row_count * lax.axis_size("col")),
        "col",
        scatter_dimension=0,
        tiled=True,
    )


def take_portion(complete, position, portion_size, along):
    return lax.dynamic_slice_in_dim(complete, position * portion_size, portion_size, along)


def place_portion(portion, position, full_size, along):
    zeroed_shape = portion.shape[:along] + (full_size,) + portion.shape[along + 1 :]
    zeroed = jnp.zeros(zeroed_shape, jnp.float32)
    return lax.dynamic_update_slice_in_dim(zeroed, portion, position * portion.shape[along], along)


def gelu_tanh(values):
    return jax.nn.gelu(values, approximate=True)


def norm_forward(values, norm_gain, norm_offset, totals_fn):
    plain_sum, square_sum = totals_fn((jnp.sum(values, axis=1), jnp.sum(values * values, axis=1)))
    center = (plain_sum / D)[:, None]
    inverse = lax.rsqrt(square_sum[:, None] / D - center * center + epsilon)
    unit_rows = (values - center) * inverse
    return (unit_rows * norm_gain + norm_offset, unit_rows, inverse)


def norm_backward(grad_rows, unit_rows, inverse, norm_gain, totals_fn):
    scaled = grad_rows * norm_gain
    plain_sum, cross_sum = totals_fn((jnp.sum(scaled, axis=1), jnp.sum(scaled * unit_rows, axis=1)))
    return inverse * (scaled - (plain_sum / D)[:, None] - unit_rows * (cross_sum / D)[:, None])


def split_heads(flat_rows):
    return flat_rows.reshape(LEN, flat_rows.shape[1] // HEAD_DIM, HEAD_DIM)


def scores_of(queries, keys_block, limit_value):
    raw_scores = jnp.einsum("qhe,khe->hqk", queries, keys_block, preferred_element_type=jnp.float32)
    raw_scores = raw_scores * HEAD_DIM ** (-0.5)
    places = jnp.arange(LEN, dtype=jnp.int32)
    visible = (places[None, :] <= places[:, None]) | (places[None, :] < limit_value)
    return jnp.where(visible[None], raw_scores, masked_score)


def attend_forward(packed):
    block_rows, limit_value = packed
    queries = split_heads(block_rows[:, 0])
    keys_block = split_heads(block_rows[:, 1])
    values_block = split_heads(block_rows[:, 2])
    scores = scores_of(queries, keys_block, limit_value)
    largest = jnp.max(scores, axis=-1, keepdims=True)
    weights = jnp.exp(scores - largest)
    row_totals = jnp.sum(weights, axis=-1, keepdims=True)
    probs = (weights / row_totals).astype(jnp.bfloat16)
    mixed = jnp.einsum("hqk,khe->qhe", probs, values_block, preferred_element_type=jnp.float32)
    return (mixed.reshape(LEN, -1).astype(jnp.bfloat16), (largest + jnp.log(row_totals))[..., 0])


def attend_backward(packed):
    block_rows, limit_value, log_total, out_grad = packed
    queries = split_heads(block_rows[:, 0])
    keys_block = split_heads(block_rows[:, 1])
    values_block = split_heads(block_rows[:, 2])
    scores = scores_of(queries, keys_block, limit_value)
    probs = jnp.exp(scores - log_total[..., None])
    probs_low = probs.astype(jnp.bfloat16)
    grad_heads = split_heads(out_grad)
    weight_grad = jnp.einsum(
        "qhe,khe->hqk", grad_heads, values_block, preferred_element_type=jnp.float32
    )
    row_inner = jnp.sum(probs * weight_grad, axis=-1, keepdims=True)
    score_grad = (probs * (weight_grad - row_inner)).astype(jnp.bfloat16)
    query_grad = jnp.einsum(
        "hqk,khe->qhe", score_grad, keys_block, preferred_element_type=jnp.float32
    )
    key_grad = jnp.einsum("hqk,qhe->khe", score_grad, queries, preferred_element_type=jnp.float32)
    value_grad = jnp.einsum(
        "hqk,qhe->khe", probs_low, grad_heads, preferred_element_type=jnp.float32
    )
    score_factor = HEAD_DIM ** (-0.5)
    stacked = jnp.stack(
        [
            (query_grad * score_factor).reshape(LEN, -1),
            (key_grad * score_factor).reshape(LEN, -1),
            value_grad.reshape(LEN, -1),
        ],
        axis=1,
    )
    return stacked.astype(jnp.bfloat16)


def general_device(
    tokens,
    prefix,
    ln1_gain,
    ln1_bias,
    w_qkv,
    qv_bias,
    w_out,
    out_bias,
    ln2_gain,
    ln2_bias,
    w_fc,
    fc_bias,
    w_proj,
    proj_bias,
    cotangent,
):
    row_place = lax.axis_index("row")
    col_place = lax.axis_index("col")
    row_devices = lax.axis_size("row")
    col_devices = lax.axis_size("col")
    width_row, local_rows = tokens.shape
    width_col = w_qkv.shape[2]
    hidden_col = w_fc.shape[1]
    seq_rows = local_rows * col_devices // row_devices
    seq_count = seq_rows // LEN
    residual = tokens.T.astype(jnp.float32)
    cotangent_local = cotangent.T
    first_gain = take_portion(ln1_gain, row_place, width_row, 0)
    first_normed, first_unit, first_inverse = norm_forward(
        residual, first_gain, take_portion(ln1_bias, row_place, width_row, 0), feature_totals
    )
    first_gathered = column_rows(first_normed.astype(jnp.bfloat16))

    def qkv_term(first_row, row_count):
        return jnp.einsum("td,sde->tse", first_gathered, w_qkv, preferred_element_type=jnp.float32)

    bias_col = take_portion(qv_bias, col_place, width_col, 1)
    bias_rows = jnp.stack([bias_col[0], jnp.zeros_like(bias_col[0]), bias_col[1]])
    qkv_sum = summed_over_row(qkv_term, seq_rows)
    qkv = (qkv_sum + bias_rows).astype(jnp.bfloat16)
    blocks = qkv.reshape(seq_count, LEN, 3, width_col)
    attn_blocks, log_totals = lax.map(attend_forward, (blocks, prefix))
    attn = attn_blocks.reshape(seq_rows, width_col)
    attn_gathered = row_rows(attn)

    def out_term(first_row, row_count):
        return jnp.dot(attn_gathered, w_out, preferred_element_type=jnp.float32)

    middle = (
        residual
        + summed_over_col(out_term, local_rows)
        + take_portion(out_bias, row_place, width_row, 0)
    )
    grad_output = cotangent_local.astype(jnp.float32)
    second_gain = take_portion(ln2_gain, row_place, width_row, 0)
    second_normed, second_unit, second_inverse = norm_forward(
        middle, second_gain, take_portion(ln2_bias, row_place, width_row, 0), feature_totals
    )
    second_gathered = column_rows(second_normed.astype(jnp.bfloat16))

    def up_term(first_row, row_count):
        return jnp.dot(second_gathered, w_fc, preferred_element_type=jnp.float32)

    hidden = summed_over_row(up_term, seq_rows) + take_portion(fc_bias, col_place, hidden_col, 0)
    active, gelu_pull = jax.vjp(gelu_tanh, hidden)
    active_gathered = row_rows(active.astype(jnp.bfloat16))

    def down_term(first_row, row_count):
        return jnp.einsum("tf,df->td", active_gathered, w_proj, preferred_element_type=jnp.float32)

    final_rows = (
        middle
        + summed_over_col(down_term, local_rows)
        + take_portion(proj_bias, row_place, width_row, 0)
    )
    output = final_rows.astype(jnp.bfloat16)
    grad_gathered = column_rows(cotangent_local)
    w_proj_grad = jnp.einsum(
        "tf,td->df", active_gathered, grad_gathered, preferred_element_type=jnp.float32
    )

    def active_term(first_row, row_count):
        return jnp.einsum("td,df->tf", grad_gathered, w_proj, preferred_element_type=jnp.float32)

    hidden_grad = gelu_pull(summed_over_row(active_term, seq_rows))[0].astype(jnp.bfloat16)
    hidden_gathered = row_rows(hidden_grad)
    w_fc_grad = jnp.einsum(
        "td,tf->df", second_gathered, hidden_gathered, preferred_element_type=jnp.float32
    )

    def second_term(first_row, row_count):
        return jnp.einsum("tf,df->td", hidden_gathered, w_fc, preferred_element_type=jnp.float32)

    second_grad = summed_over_col(second_term, local_rows)
    middle_grad = grad_output + norm_backward(
        second_grad, second_unit, second_inverse, second_gain, feature_totals
    )
    ln2_gain_part = place_portion(jnp.sum(second_grad * second_unit, axis=0), row_place, D, 0)
    ln2_bias_part = place_portion(jnp.sum(second_grad, axis=0), row_place, D, 0)
    fc_bias_part = place_portion(jnp.sum(hidden_grad.astype(jnp.float32), axis=0), col_place, FF, 0)
    proj_bias_part = place_portion(jnp.sum(grad_output, axis=0), row_place, D, 0)
    branch_grad = middle_grad.astype(jnp.bfloat16)
    branch_gathered = column_rows(branch_grad)
    w_out_grad = jnp.einsum(
        "te,td->ed", attn_gathered, branch_gathered, preferred_element_type=jnp.float32
    )

    def attn_term(first_row, row_count):
        return jnp.einsum("td,ed->te", branch_gathered, w_out, preferred_element_type=jnp.float32)

    attn_grad = summed_over_row(attn_term, seq_rows).astype(jnp.bfloat16)
    qkv_grad = lax.map(
        attend_backward, (blocks, prefix, log_totals, attn_grad.reshape(seq_count, LEN, width_col))
    )
    qkv_grad = qkv_grad.reshape(seq_rows, 3, width_col)
    qkv_gathered = row_rows(qkv_grad)
    w_qkv_grad = jnp.einsum(
        "td,tse->sde", first_gathered, qkv_gathered, preferred_element_type=jnp.float32
    )

    def first_term(first_row, row_count):
        return jnp.einsum("tse,sde->td", qkv_gathered, w_qkv, preferred_element_type=jnp.float32)

    first_grad = summed_over_col(first_term, local_rows)
    input_grad = middle_grad + norm_backward(
        first_grad, first_unit, first_inverse, first_gain, feature_totals
    )
    qkv_totals = jnp.sum(qkv_grad.astype(jnp.float32), axis=0)
    qv_part = place_portion(jnp.stack([qkv_totals[0], qkv_totals[2]]), col_place, D, 1)
    out_bias_part = place_portion(jnp.sum(branch_grad.astype(jnp.float32), axis=0), row_place, D, 0)
    ln1_gain_part = place_portion(jnp.sum(first_grad * first_unit, axis=0), row_place, D, 0)
    ln1_bias_part = place_portion(jnp.sum(first_grad, axis=0), row_place, D, 0)
    vectors = lax.psum(
        (
            ln1_gain_part,
            ln1_bias_part,
            qv_part,
            out_bias_part,
            ln2_gain_part,
            ln2_bias_part,
            fc_bias_part,
            proj_bias_part,
        ),
        ("dp", "row", "col"),
    )
    matrices = (
        lax.psum(w_qkv_grad.astype(jnp.bfloat16), "dp").astype(jnp.float32),
        lax.psum(w_out_grad.astype(jnp.bfloat16), "dp").astype(jnp.float32),
        lax.psum(w_fc_grad.astype(jnp.bfloat16), "dp").astype(jnp.float32),
        lax.psum(w_proj_grad.astype(jnp.bfloat16), "dp").astype(jnp.float32),
    )
    return (
        output.T,
        input_grad.T,
        vectors[0],
        vectors[1],
        matrices[0],
        vectors[2],
        matrices[1],
        vectors[3],
        vectors[4],
        vectors[5],
        matrices[2],
        vectors[6],
        matrices[3],
        vectors[7],
    )


MESH = pl.DeviceIdType.MESH
WIDTH = 192
HALF = 96
QUARTER = 256
LANES = 128
WQ = 3 * WIDTH
VMEM_LIMIT = 67043328
REMOTES = 208
LOCALS = 64
FACTOR = HEAD_DIM ** (-0.5)
ANY = pl.BlockSpec(memory_space=pl.ANY)
GAIN1, BIAS1, OUT_BIAS, GAIN2, BIAS2, PROJ_BIAS, Q_BIAS, V_BIAS, FC_BIAS = range(9)
V_GAIN1, V_BIAS1, V_QUERY, V_VALUE, V_OUT, V_GAIN2, V_BIAS2, V_PROJ, V_FC = range(9)
CENTER, INVERSE = range(2)


def dot(left, right, left_axis, right_axis):
    return lax.dot_general(
        left, right, (((left_axis,), (right_axis,)), ((), ())), preferred_element_type=jnp.float32
    )


def low(value):
    return value.astype(jnp.bfloat16)


def wide(value):
    return value.astype(jnp.float32)


def aligned(start, size):
    return pl.ds(pl.multiple_of(start, size), size)


def merged(value):
    return value.reshape((value.shape[0] * value.shape[1],) + value.shape[2:])


def each(count, body):
    def step(i, carry):
        body(i)
        return carry

    lax.fori_loop(0, count, step, 0)


class Links:
    def __init__(self, send_sems, recv_sems, local_sems):
        self.d, self.r, self.c = (lax.axis_index(n) for n in ("dp", "row", "col"))
        self.send_sems, self.recv_sems, self.local_sems = send_sems, recv_sems, local_sems
        self.remotes = 0
        self.locals = 0

    def across(self, k):
        if k == 0:
            return self.r
        if k == 1:
            return self.r + 1 - 2 * lax.rem(self.r, 2)
        return lax.rem(self.r + 2, 4) if k == 2 else 3 - self.r

    def plane(self, k):
        return (self.d, self.across(k), self.c)

    def height(self, k):
        return lax.rem(self.c + k, 4)

    def column(self, k):
        return (self.d, self.r, self.height(k))

    def partner(self):
        return (1 - self.d, self.r, self.c)

    def half(self, mine=True):
        place = self.d if mine else 1 - self.d
        return pl.ds(pl.multiple_of(place * HALF, 16), HALF)

    def crossing(self, row, place):
        place = place + self.d * (3 - 2 * place)
        low_bit = lax.rem(lax.rem(row, 2) + lax.rem(place, 2), 2)
        return low_bit + 2 * lax.rem(lax.div(row, 2) + lax.div(place, 2), 2)

    def greet(self):
        devices = [self.partner(), *(self.plane(k) for k in (1, 2, 3))]
        devices += [self.column(k) for k in (1, 2, 3)]
        barrier = pltpu.get_barrier_semaphore()
        for device in devices:
            pl.semaphore_signal(barrier, 1, device_id=device, device_id_type=MESH)
        self.greeted = len(devices)
        to, since = self.routed(), self.routed_back()

        @pl.when(jnp.logical_not(self.stays()))
        def _():
            for device in (to, since):
                pl.semaphore_signal(barrier, 1, device_id=device, device_id_type=MESH)

    def meet(self):
        count = jnp.where(self.stays(), self.greeted, self.greeted + 2)
        pl.semaphore_wait(pltpu.get_barrier_semaphore(), count)

    def routed(self):
        return (self.d, self.c, self.crossing(self.r, self.c))

    def routed_back(self):
        return (self.d, self.crossing(self.r, self.c), self.r)

    def stays(self):
        return jnp.logical_and(self.r == self.c, self.crossing(self.r, self.c) == self.c)

    def send(self, source, target, device):
        place = self.remotes
        self.remotes += 1
        copy = pltpu.make_async_remote_copy(
            src_ref=source,
            dst_ref=target,
            send_sem=self.send_sems.at[place],
            recv_sem=self.recv_sems.at[place],
            device_id=device,
            device_id_type=MESH,
        )
        copy.start()
        return copy

    def local(self, source, target):
        place = self.locals
        self.locals += 1
        copy = pltpu.make_async_copy(source, target, self.local_sems.at[place])
        copy.start()
        return copy


class Ticket:
    def __init__(self, links, device):
        self.place = links.remotes
        links.remotes += 1
        self.links, self.device = links, device

    def __call__(self, source, target):
        return pltpu.make_async_remote_copy(
            src_ref=source,
            dst_ref=target,
            send_sem=self.links.send_sems.at[self.place],
            recv_sem=self.links.recv_sems.at[self.place],
            device_id=self.device,
            device_id_type=MESH,
        )


class Move:
    def __init__(self, links, stays, source, target, device):
        self.stays = stays
        self.ticket = Ticket(links, device)
        self.source, self.target = source, target
        place = links.locals
        links.locals += 1
        self.local_sem = links.local_sems.at[place]

        @pl.when(jnp.logical_not(stays))
        def _():
            self.ticket(source, target).start()

        @pl.when(stays)
        def _():
            pltpu.make_async_copy(source, target, self.local_sem).start()

    def wait(self):
        @pl.when(jnp.logical_not(self.stays))
        def _():
            self.ticket(self.source, self.target).wait()

        @pl.when(self.stays)
        def _():
            pltpu.make_async_copy(self.source, self.target, self.local_sem).wait()


class PlaneGather:
    def __init__(self, links, target, in_parts=False):
        self.links, self.target = links, target
        rows = target.shape[1] // 2
        self.low, self.high = pl.ds(0, rows), pl.ds(rows, rows)
        first, second = target.at[links.r, self.low], target.at[links.r, self.high]
        self.x_low = links.send(first, first, links.plane(1))
        self.y_high = links.send(second, second, links.plane(2))
        if not in_parts:
            self.rest()

    def rest(self):
        links, target = self.links, self.target
        first, second = target.at[links.r, self.low], target.at[links.r, self.high]
        self.x_high = links.send(second, second, links.plane(1))
        self.y_low = links.send(first, first, links.plane(2))

    def relay(self):
        links = self.links
        self.x_low.wait_recv()
        block = self.target.at[links.across(1), self.low]
        self.on_y = links.send(block, block, links.plane(2))
        self.y_high.wait_recv()
        block = self.target.at[links.across(2), self.high]
        self.on_x = links.send(block, block, links.plane(1))

    def finish(self):
        self.x_high.wait_recv()
        self.y_low.wait_recv()
        for copy in (self.x_low, self.y_high, self.x_high, self.y_low):
            copy.wait_send()
        self.on_y.wait()
        self.on_x.wait()


class PlaneReduce:
    def __init__(self, links, part_of, rows, over_x, over_y, relayed):
        self.links, self.part_of = links, part_of
        self.halves = (pl.ds(0, rows // 2), pl.ds(rows // 2, rows // 2))
        self.over_x, self.over_y, self.relayed = over_x, over_y, relayed
        self.copies = {}

    def part(self, k, half):
        return self.part_of(self.links.across(k)).at[self.halves[half]]

    def give(self, k):
        links = self.links
        if k == 3:
            self.copies["x3"] = links.send(self.part(3, 0), self.over_x.at[1], links.plane(1))
            self.copies["y3"] = links.send(self.part(3, 1), self.over_y.at[1], links.plane(2))
        elif k == 1:
            self.copies["x1"] = links.send(self.part(1, 0), self.over_x.at[0], links.plane(1))
        elif k == 2:
            self.copies["y2"] = links.send(self.part(2, 1), self.over_y.at[0], links.plane(2))

    def relay(self):
        links = self.links
        self.copies["x3"].wait_recv()
        add_rows(self.over_x.at[1], [self.over_x.at[1], self.part(2, 0)])
        self.copies["xy"] = links.send(self.over_x.at[1], self.relayed.at[0], links.plane(2))
        self.copies["y3"].wait_recv()
        add_rows(self.over_y.at[1], [self.over_y.at[1], self.part(1, 1)])
        self.copies["yx"] = links.send(self.over_y.at[1], self.relayed.at[1], links.plane(1))

    def finish(self):
        for name in ("x3", "y3"):
            self.copies[name].wait_send()
        for name in ("x1", "y2", "xy", "yx"):
            self.copies[name].wait()

    def total(self, lanes):
        parts = []
        for half, over in ((0, self.over_x), (1, self.over_y)):
            value = wide(self.part(0, half)[:, lanes]) + wide(over[0, :, lanes])
            parts.append(value + wide(self.relayed[half, :, lanes]))
        return jnp.concatenate(parts, axis=0)


class Line:
    def __init__(self, links, block_of):
        self.links, self.block_of = links, block_of
        c = links.c
        self.up = [Ticket(links, (links.d, links.r, lax.rem(c + 1, 4))) for _ in range(3)]
        self.down = [Ticket(links, (links.d, links.r, lax.rem(c + 3, 4))) for _ in range(3)]

    def copy(self, ticket, place):
        return ticket(self.block_of(place), self.block_of(place))

    def step(self, t):
        c = self.links.c
        if t > 0:

            @pl.when(c >= t)
            def _():
                self.copy(self.up[t - 1], c - t).wait_recv()

            @pl.when(c <= 3 - t)
            def _():
                self.copy(self.down[t - 1], c + t).wait_recv()

        if t < 3:

            @pl.when(jnp.logical_and(c >= t, c < 3))
            def _():
                self.copy(self.up[t], c - t).start()

            @pl.when(jnp.logical_and(c <= 3 - t, c > 0))
            def _():
                self.copy(self.down[t], c + t).start()

    def finish(self):
        c = self.links.c
        for t in range(3):

            @pl.when(jnp.logical_and(c >= t, c < 3))
            def _(t=t):
                self.copy(self.up[t], c - t).wait_send()

            @pl.when(jnp.logical_and(c <= 3 - t, c > 0))
            def _(t=t):
                self.copy(self.down[t], c + t).wait_send()


class WeightGather:
    def __init__(self, links, stage, moved, target, pieces=1):
        self.links, self.moved, self.target = links, moved, target
        r, c = links.r, links.c
        self.mine = links.half()
        self.goal = links.crossing(r, c)
        size = HALF // pieces
        self.local_rows = [pl.ds(i * size, size) for i in range(pieces)]
        start = links.d * HALF
        self.rows = [pl.ds(pl.multiple_of(start + i * size, 16), size) for i in range(pieces)]
        device = (links.d, r, self.goal)
        self.turns = [
            Move(links, self.goal == c, stage.at[rows], moved.at[rows], device)
            for rows in self.local_rows
        ]

    def hop(self):
        links = self.links
        device = (links.d, self.goal, links.c)
        for i, rows in enumerate(self.local_rows):
            self.turns[i].wait()
            block = self.target.at[links.r, self.rows[i]]
            self.turns[i] = Move(links, self.goal == links.r, self.moved.at[rows], block, device)

    def begin(self):
        links = self.links

        def block_of(rows):
            return lambda place: self.target.at[links.crossing(links.r, place), rows]

        self.ways = []
        for turn, rows in zip(self.turns, self.rows):
            turn.wait()
            self.ways.append(Line(links, block_of(rows)))
            self.ways[-1].step(0)

    def line(self, t):
        if t == 0:
            self.begin()
        else:
            for way in self.ways:
                way.step(t)

    def share(self):
        for way in self.ways:
            way.finish()
        block = self.target.at[:, self.mine]
        self.shared = self.links.send(block, block, self.links.partner())

    def finish(self):
        self.shared.wait()


class RoutedGather(WeightGather):
    def __init__(self, links, stage, target, pieces=1):
        self.links, self.target = links, target
        self.mine = links.half()
        size = HALF // pieces
        start = links.d * HALF
        self.rows = [pl.ds(pl.multiple_of(start + i * size, 16), size) for i in range(pieces)]
        self.turns = [
            Move(
                links,
                links.stays(),
                stage.at[pl.ds(i * size, size)],
                target.at[links.r, rows],
                links.routed(),
            )
            for i, rows in enumerate(self.rows)
        ]


class SquareGather:
    def __init__(self, links, target):
        self.links, self.target = links, target
        self.mine = links.half()
        self.way = Line(links, lambda place: target.at[links.r, place, self.mine])

    def line(self, t):
        self.way.step(t)

    def cross(self):
        self.way.finish()
        self.plane = PlaneGather(self.links, self.target.at[:, :, self.mine])

    def share(self):
        self.plane.finish()
        block = self.target.at[:, :, self.mine]
        self.shared = self.links.send(block, block, self.links.partner())

    def finish(self):
        self.shared.wait()


def add_rows(target, terms):
    if len(terms) == 2:
        target[...] = terms[0][...] + terms[1][...]
        return

    def step(i):
        place = aligned(i * 16, 16)
        total = wide(terms[0][place, :])
        for term in terms[1:]:
            total = total + wide(term[place, :])
        target[place, :] = total.astype(target.dtype)

    each(target.shape[0] // 16, step)


def add_blocks(target, terms):
    if len(target.shape) == 2:
        add_rows(target, terms)
    else:
        each(target.shape[0], lambda i: add_blocks(target.at[i], [term.at[i] for term in terms]))


class LineReduce:
    def __init__(self, links, block_of, up, down):
        self.links, self.block_of, self.up, self.down = links, block_of, up, down
        c = links.c
        self.rise = [Ticket(links, (links.d, links.r, lax.rem(c + 1, 4))) for _ in range(3)]
        self.fall = [Ticket(links, (links.d, links.r, lax.rem(c + 3, 4))) for _ in range(3)]

    def step(self, t):
        c = self.links.c
        for i in range(t + 1):
            goal = 3 - t + i
            self.pass_on(c == i, self.rise[goal - 1], self.up.at[goal - 1], goal, i > 0)
            goal = t - i
            self.pass_on(c == 3 - i, self.fall[goal], self.down.at[goal], goal, i > 0)

    def pass_on(self, here, ticket, slot, goal, adds):
        @pl.when(here)
        def _():
            if adds:
                ticket(slot, slot).wait_recv()
                add_blocks(slot, [slot, self.block_of(goal)])
                ticket(slot, slot).start()
            else:
                ticket(self.block_of(goal), slot).start()

    def total(self, target):
        c = self.links.c
        for goal in range(4):

            @pl.when(c == goal)
            def _(goal=goal):
                terms = [self.block_of(goal)]
                if goal > 0:
                    slot = self.up.at[goal - 1]
                    self.rise[goal - 1](slot, slot).wait_recv()
                    terms.append(slot)
                if goal < 3:
                    slot = self.down.at[goal]
                    self.fall[goal](slot, slot).wait_recv()
                    terms.append(slot)
                add_blocks(target, terms)

        for i in range(3):
            rising, falling = self.up.at[i], self.down.at[i]

            @pl.when(c < i + 1)
            def _(i=i, slot=rising):
                self.rise[i](slot, slot).wait_send()

            @pl.when(c > i)
            def _(i=i, slot=falling):
                self.fall[i](slot, slot).wait_send()


class WeightReduce:
    def __init__(self, links, grad, near, sums, up, down, fin, moved, arrived, result, pieces=1):
        self.links, self.grad, self.near, self.sums = links, grad, near, sums
        self.up, self.down, self.fin = up, down, fin
        self.moved, self.arrived, self.result = moved, arrived, result
        size = HALF // pieces
        self.rows = [pl.ds(i * size, size) for i in range(pieces)]
        self.to_near = [self.send_near(i * size, size) for i in range(pieces)]

    def send_near(self, first, size):
        links = self.links
        other = pl.ds(pl.multiple_of((1 - links.d) * HALF + first, 16), size)
        rows = pl.ds(first, size)
        return links.send(self.grad.at[:, other], self.near.at[:, rows], links.partner())

    def add_near(self):
        links = self.links

        def block_of(rows):
            return lambda place: self.sums.at[links.crossing(links.r, place), rows]

        self.ways = []
        for copy, rows in zip(self.to_near, self.rows):
            copy.wait()
            first = links.d * HALF + rows.start
            mine = pl.ds(pl.multiple_of(first, 16), rows.size)
            each(
                4,
                lambda b, rows=rows, mine=mine: add_rows(
                    self.sums.at[b, rows], [self.grad.at[b, mine], self.near.at[b, rows]]
                ),
            )
            up, down = self.up.at[:, rows], self.down.at[:, rows]
            self.ways.append(LineReduce(links, block_of(rows), up, down))

    def line(self, i):
        for way in self.ways:
            way.step(i)

    def hop(self):
        links = self.links
        self.goal = links.crossing(links.r, links.c)
        device = (links.d, self.goal, links.c)
        self.turns = []
        for way, rows in zip(self.ways, self.rows):
            way.total(self.fin.at[rows])
            stays = self.goal == links.r
            self.turns.append(Move(links, stays, self.fin.at[rows], self.moved.at[rows], device))

    def back(self):
        links = self.links
        device = (links.d, links.r, self.goal)
        for i, rows in enumerate(self.rows):
            self.turns[i].wait()
            stays = self.goal == links.c
            self.turns[i] = Move(links, stays, self.moved.at[rows], self.arrived.at[rows], device)

    def share(self):
        for turn in self.turns:
            turn.wait()
        self.give(self.arrived)

    def give(self, total):
        links, mine = self.links, self.links.half()
        self.last = [
            links.send(total, self.result.at[mine], links.partner()),
            links.local(total, self.result.at[mine]),
        ]

    def finish(self):
        for copy in self.last:
            copy.wait()


class SquareReduce(WeightReduce):
    def __init__(self, links, grad, near, sums, up, down, fin, came, arrived, result):
        self.links, self.grad, self.near, self.sums = links, grad, near, sums
        self.up, self.down, self.fin = up, down, fin
        self.came, self.arrived, self.result = came, arrived, result
        self.to_near = links.send(grad.at[:, :, links.half(False)], near, links.partner())

    def add_near(self):
        mine = self.links.half()
        self.to_near.wait()
        add_blocks(self.sums, [self.grad.at[:, :, mine], self.near])
        self.ways = [
            LineReduce(self.links, lambda place: self.sums.at[:, place], self.up, self.down)
        ]

    def hop(self):
        links = self.links
        self.ways[0].total(self.fin)
        self.crossing = [
            links.send(self.fin.at[links.across(k)], self.came.at[k - 1], links.plane(k))
            for k in (3, 1, 2)
        ]

    def back(self):
        for copy in self.crossing:
            copy.wait()
        came = self.came
        add_rows(self.arrived, [self.fin.at[self.links.r], came.at[0], came.at[1], came.at[2]])

    def share(self):
        self.give(self.arrived)


def normalize(source_of, target, stats, gain, offset):
    def step(j):
        lanes = aligned(j * LANES, LANES)
        values = source_of(lanes)
        center = jnp.sum(values, axis=0, keepdims=True) / D
        square = jnp.sum(values * values, axis=0, keepdims=True) / D
        inverse = lax.rsqrt(square - center * center + epsilon)
        stats[CENTER : CENTER + 1, lanes] = center
        stats[INVERSE : INVERSE + 1, lanes] = inverse
        target[:, lanes] = low((values - center) * inverse * gain[...] + offset[...])

    each(LEN // LANES, step)


def key_span(block):
    return max(512, (block + 1) * QUARTER), block * QUARTER


def visible(block, first, last, limit_value):
    shape = (last - first, QUARTER)
    keys = lax.broadcasted_iota(jnp.int32, shape, 0) + first
    queries = lax.broadcasted_iota(jnp.int32, shape, 1) + block * QUARTER
    return (keys <= queries) | (keys < limit_value)


def masked(value, block, limit_value, fill):
    last, first = key_span(block)
    tail = jnp.where(visible(block, first, last, limit_value), value[first:], fill)
    return jnp.concatenate([value[:first], tail], axis=0) if first else tail


def head_rows(h, part):
    return pl.ds(h * HEAD_DIM + part * WIDTH, HEAD_DIM)


def attend(qkv, limit_value, attn_of, log_total, between):
    def head(h):
        for block in range(4):
            for action in between.get(h * 4 + block, ()):
                action()
            last, _ = key_span(block)
            lanes = slice(block * QUARTER, (block + 1) * QUARTER)
            queries = qkv[head_rows(h, 0), lanes] * jnp.bfloat16(FACTOR)
            scores = dot(qkv[head_rows(h, 1), :last], queries, 0, 0)
            scores = masked(scores, block, limit_value, masked_score)
            largest = jnp.max(scores, axis=0, keepdims=True)
            weights = jnp.exp(scores - largest)
            total = jnp.sum(weights, axis=0, keepdims=True)
            mixed = dot(qkv[head_rows(h, 2), :last], low(weights), 1, 0)
            attn_of(head_rows(h, 0), lanes, low(mixed * (1.0 / total)))
            log_total[pl.ds(h, 1), lanes] = largest + jnp.log(total)

    for h in range(3):
        head(h)


def attend_back(
    qkv, limit_value, attn_of, log_total, out_grad, qkv_grad, key_sum, value_sum, between
):
    def head(h):
        for block in (3, 2, 1, 0):
            for action in between.get(h * 4 + 3 - block, ()):
                action()
            last, _ = key_span(block)
            lanes = slice(block * QUARTER, (block + 1) * QUARTER)
            queries = qkv[head_rows(h, 0), lanes] * jnp.bfloat16(FACTOR)
            grads = out_grad[head_rows(h, 0), lanes]
            inner = jnp.sum(
                wide(attn_of(head_rows(h, 0), lanes)) * wide(grads), axis=0, keepdims=True
            )
            scores = dot(qkv[head_rows(h, 1), :last], queries, 0, 0)
            probs = jnp.exp(scores - log_total[pl.ds(h, 1), lanes])
            probs = masked(probs, block, limit_value, 0.0)
            weight_grad = dot(qkv[head_rows(h, 2), :last], grads, 0, 0)
            score_grad = low(probs * (weight_grad - inner))
            query_grad = dot(qkv[head_rows(h, 1), :last], score_grad, 1, 0) * FACTOR
            qkv_grad[head_rows(h, 0), lanes] = low(query_grad)
            key_grad = dot(queries, score_grad, 1, 1)
            value_grad = dot(grads, low(probs), 1, 1)
            if block == 3:
                key_sum[...] = key_grad
                value_sum[...] = value_grad
            else:
                key_sum[:, :last] += key_grad
                value_sum[:, :last] += value_grad
        qkv_grad[head_rows(h, 1), :] = low(key_sum[...])
        qkv_grad[head_rows(h, 2), :] = low(value_sum[...])

    for h in range(3):
        head(h)


def gelu_parts(u):
    slope = (2.0 / 3.141592653589793) ** 0.5
    square = u * u
    bent = jnp.tanh(slope * u * (1.0 + 0.044715 * square))
    shared = 0.5 * (1.0 + bent)
    derivative = shared + 0.5 * u * (1.0 - bent * bent) * (slope * (1.0 + 3.0 * 0.044715 * square))
    return u * shared, derivative


def block_kernel(
    limit, tok, gain1_in, bias1_in, wq_in, qv_in, wo_in, out_in, gain2_in, bias2_in,
    wf_in, fc_in, wp_in, proj_in, cot,
    out_hbm, grad_hbm, wq_hbm, wf_hbm, wp_hbm, wo_hbm, vec_hbm,
    rows1, qv, fc, wq_here, xt, gt, wqa, wfa, wpa, woa, zq, zf, zp, mf, mp, pres, colb,
    fn, qkv, at, lse, st1, st2, mid, sn, act, slope, op, hg, sp,
    x2, y2, z2, x_out, y_out, z_out, x1, y1, z1, br, ap, dout, brf, dqkv, ksum, vsum,
    gf, gp, gq, near_f, near_p, near_q, sum_f, sum_p, sum_q, up_f, up_p, up_q, dn_f, dn_p, dn_q,
    fin_f, fin_p, fin_q, hop_f, hop_p, hop_q, got_f, got_p, got_q,
    sq, near_o, sum_o, up_o, dn_o, fin_o, hop_o, got_o,
    fgp, fsum, vcol, vec, vec_in, stat, stat_in, out_v, grad_v,
    send_sems, recv_sems, local_sems,
):
    links = Links(send_sems, recv_sems, local_sems)
    r, c = links.r, links.c
    mine = links.half()
    own = aligned(r * QUARTER, QUARTER)
    links.greet()
    singles = (gain1_in, bias1_in, out_in, gain2_in, bias2_in, proj_in)
    first = [links.local(wq_in.at[:, mine], wq_here), links.local(tok, xt.at[r])]
    first += [links.local(wo_in.at[mine], woa.at[r, c, mine])]
    first += [links.local(source, rows1.at[i]) for i, source in enumerate(singles)]
    first += [links.local(qv_in, qv), links.local(fc_in, fc)]
    then = [links.local(wf_in.at[mine], zf), links.local(wp_in.at[mine], zp)]
    then += [links.local(cot, gt.at[r])]
    for copy in first:
        copy.wait()
    zq[...] = jnp.concatenate([wq_here[i] for i in range(3)], axis=1)
    pres[r] = jnp.full((8, LANES), limit[0], jnp.int32)

    links.meet()

    get_q = RoutedGather(links, zq, wqa, 2)
    get_o = SquareGather(links, woa)
    get_o.line(0)
    tokens = PlaneGather(links, xt, in_parts=True)
    for copy in then:
        copy.wait()
    prefixes = [links.send(pres.at[r], pres.at[r], links.plane(k)) for k in (1, 2, 3)]
    get_q.line(0)
    tokens.rest()
    get_f = WeightGather(links, zf, mf, wfa)
    get_o.line(1)

    def column(kind, place, values):
        spread = jnp.broadcast_to(values[None, :], (LANES, LANES))
        colb[kind, pl.ds(place * LANES, LANES)] = spread.T

    for place in range(D // LANES):
        part = pl.ds(place * LANES, LANES)
        for kind in range(len(singles)):
            column(kind, place, rows1[kind, part])
        column(Q_BIAS, place, qv[0, part])
        column(V_BIAS, place, qv[1, part])
        column(FC_BIAS, place, fc[pl.ds(pl.multiple_of(r * D + place * LANES, LANES), LANES)])

    tokens.relay()
    get_q.line(1)
    get_o.line(2)
    get_f.hop()
    get_q.line(2)
    get_o.line(3)
    get_p = WeightGather(links, zp, mp, wpa)
    get_q.line(3)
    get_q.share()
    get_f.line(0)
    tokens.finish()
    get_o.cross()
    grads = PlaneGather(links, gt, in_parts=True)
    get_p.hop()
    normalize(
        lambda lanes: wide(merged(xt[:, :, lanes])), fn, st1, colb.at[GAIN1], colb.at[BIAS1]
    )
    for copy in prefixes:
        copy.wait()
    get_q.finish()
    head_bias = aligned(r * WIDTH, WIDTH)

    def project(b):
        lanes = aligned(b * QUARTER, QUARTER)
        nothing = jnp.zeros((WIDTH, LANES), jnp.float32)
        bias = [colb[Q_BIAS, head_bias], nothing, colb[V_BIAS, head_bias]]
        bias = jnp.concatenate(bias, axis=0)
        value = dot(merged(wqa[...]), fn[:, lanes], 0, 0)
        qkv[:, lanes] = low(value + jnp.concatenate([bias, bias], axis=1))

    each(4, project)
    limit_value = pres[c][0:1, 0:1]

    def put_attn(rows, lanes, value):
        at[r, rows, lanes] = value

    def get_attn(rows, lanes):
        return at[r, rows, lanes]

    attns = []

    def gather_head(h):
        attns.append(PlaneGather(links, at.at[:, h * HEAD_DIM : (h + 1) * HEAD_DIM]))

    def get_o_relay():
        get_o.plane.relay()

    attend(
        qkv,
        limit_value,
        put_attn,
        lse,
        {
            0: [get_o_relay],
            1: [lambda: get_f.line(1)],
            4: [lambda: gather_head(0)],
            7: [lambda: get_f.line(2)],
            8: [lambda: gather_head(1), lambda: attns[0].relay()],
            10: [lambda: get_p.line(0)],
        },
    )
    gather_head(2)
    attns[1].relay()
    get_f.line(3)
    get_f.share()
    get_o.share()
    attns[2].relay()
    grads.rest()
    get_p.line(1)
    get_o.finish()
    for attn in attns:
        attn.finish()
    grads.relay()

    def join(b):
        rows = aligned(b * WIDTH, WIDTH)
        bias = jnp.concatenate([colb[OUT_BIAS, rows]] * 8, axis=1)
        value = dot(merged(woa[b]), merged(at[...]), 0, 0)
        mid[rows, :] = wide(xt[b]) + (value + bias)

    each(4, join)
    get_p.line(2)
    normalize(lambda lanes: mid[:, lanes], sn, st2, colb.at[GAIN2], colb.at[BIAS2])
    get_f.finish()

    def up(b):
        lanes = aligned(b * QUARTER, QUARTER)
        bias = colb[FC_BIAS]
        value = dot(merged(wfa[...]), sn[:, lanes], 0, 0) + jnp.concatenate([bias, bias], axis=1)
        value, derivative = gelu_parts(value)
        act[:, lanes] = low(value)
        slope[:, lanes] = derivative

    each(2, up)
    get_p.line(3)
    get_p.share()
    each(2, lambda b: up(b + 2))
    grads.finish()

    def proj_grads(b):
        some = aligned(b * QUARTER, QUARTER)
        value = low(dot(merged(gt[...]), act[some, :], 1, 1))
        gp[:, :, some] = value.reshape(4, WIDTH, QUARTER)

    each(3, proj_grads)
    put_p = WeightReduce(links, gp, near_p, sum_p, up_p, dn_p, fin_p, hop_p, got_p, wp_hbm)
    get_p.finish()

    seconds = PlaneReduce(
        links, lambda place: sp.at[:, aligned(place * QUARTER, QUARTER)], D, x2, y2, z2
    )
    for k in (3, 1, 2, 0):
        lanes = aligned(links.across(k) * QUARTER, QUARTER)
        value = dot(merged(wpa[...]), merged(gt[:, :, lanes]), 0, 0)
        hg[:, lanes] = low(value * slope[:, lanes])
        sp[:, lanes] = low(dot(merged(wfa[...]), hg[:, lanes], 1, 0))
        seconds.give(k)
        if k == 2:
            put_p.add_near()
            put_p.line(0)

    def fc_grads(b):
        some = aligned(b * QUARTER, QUARTER)
        value = low(dot(sn[...], hg[some, :], 1, 1))
        gf[:, :, some] = value.reshape(4, WIDTH, QUARTER)

    each(3, fc_grads)
    put_f = WeightReduce(links, gf, near_f, sum_f, up_f, dn_f, fin_f, hop_f, got_f, wf_hbm)
    seconds.relay()
    put_p.line(1)

    def down(b):
        lanes = aligned(b * QUARTER, QUARTER)
        value = low(dot(merged(wpa[...]), act[:, lanes], 1, 0))
        op[:, :, lanes] = value.reshape(4, WIDTH, QUARTER)

    each(4, down)
    outs = PlaneReduce(links, lambda place: op.at[place], WIDTH, x_out, y_out, z_out)
    put_f.add_near()
    put_f.line(0)
    lane = lax.broadcasted_iota(jnp.int32, (D, LANES), 1)
    total = jnp.zeros((D, 1), jnp.float32)
    for b in range(4):
        lanes = slice(b * QUARTER, (b + 1) * QUARTER)
        total = total + jnp.sum(wide(hg[:, lanes]), axis=1, keepdims=True)
    vcol[...] = jnp.where(lane == V_FC + r, total, 0.0)
    put_p.line(2)
    seconds.finish()
    outs.give(3)

    def back(j):
        lanes = aligned(r * QUARTER + j * LANES, LANES)
        part = aligned(j * LANES, LANES)
        given = seconds.total(part)
        inverse = st2[INVERSE : INVERSE + 1, lanes]
        unit = (mid[:, lanes] - st2[CENTER : CENTER + 1, lanes]) * inverse
        scaled = given * colb[GAIN2]
        plain = jnp.sum(scaled, axis=0, keepdims=True) / D
        cross = jnp.sum(scaled * unit, axis=0, keepdims=True) / D
        above = wide(merged(gt[:, :, lanes]))
        branch = low(above + inverse * (scaled - plain - unit * cross))
        br[:, :, part] = branch.reshape(4, WIDTH, LANES)
        value = jnp.where(lane == V_GAIN2, jnp.sum(given * unit, axis=1, keepdims=True), 0.0)
        value = jnp.where(lane == V_BIAS2, jnp.sum(given, axis=1, keepdims=True), value)
        value = jnp.where(lane == V_OUT, jnp.sum(wide(branch), axis=1, keepdims=True), value)
        value = jnp.where(lane == V_PROJ, jnp.sum(above, axis=1, keepdims=True), value)
        vcol[...] = vcol[...] + value

    for j in range(2):
        back(j)
    value = dot(merged(woa[0]), br[0], 1, 0)
    for b in range(1, 4):
        value = value + dot(merged(woa[b]), br[b], 1, 0)
    ap[...] = low(value).reshape(4, WIDTH, QUARTER)
    turns = [
        links.send(ap.at[links.across(k)], dout.at[:, own], links.plane(k)) for k in (3, 1, 2)
    ]
    turns.append(links.local(ap.at[r], dout.at[:, own]))
    def square_grads(b):
        value = low(dot(merged(at[:, :, own]), br[b], 1, 1))
        sq[b] = value.reshape(4, WIDTH, WIDTH)

    each(4, square_grads)
    put_o = SquareReduce(links, sq, near_o, sum_o, up_o, dn_o, fin_o, hop_o, got_o, wo_hbm)
    put_f.line(1)
    put_o.add_near()
    put_p.hop()
    for copy in turns:
        copy.wait()
    outs.give(1)
    outs.give(2)
    swaps = [
        links.send(br.at[links.across(k)], brf.at[:, own], links.plane(k)) for k in (3, 1, 2)
    ]
    swaps.append(links.local(br.at[r], brf.at[:, own]))
    attend_back(
        qkv, limit_value, get_attn, lse, dout, dqkv, ksum, vsum,
        {
            0: [lambda: put_o.line(0)],
            2: [lambda: put_f.line(2)],
            4: [put_p.back, outs.relay],
            9: [put_f.hop, put_p.share],
            11: [lambda: put_o.line(1)],
        },
    )
    for some in (slice(0, 256), slice(256, 512), slice(512, WQ)):
        value = low(dot(fn[...], dqkv[some, :], 1, 1))
        gq[:, :, some] = value.reshape(4, WIDTH, some.stop - some.start)
    put_q = WeightReduce(links, gq, near_q, sum_q, up_q, dn_q, fin_q, hop_q, got_q, wq_hbm, 3)

    stat[...] = jnp.zeros_like(stat)
    firsts = PlaneReduce(links, lambda place: fgp.at[place], WIDTH, x1, y1, z1)
    for k in (3, 1, 2, 0):
        b = links.across(k)
        rows = aligned(b * WIDTH, WIDTH)

        fsum[...] = jnp.zeros_like(fsum)

        def first_part(j, b=b, rows=rows):
            lanes = aligned(j * QUARTER, QUARTER)
            value = dot(wqa[b], dqkv[:, lanes], 1, 0)
            fgp[b, :, lanes] = low(value)
            gain = colb[GAIN1, rows]
            for i in range(2):
                half = aligned(j * QUARTER + i * LANES, LANES)
                piece = value[:, i * LANES : (i + 1) * LANES]
                unit = wide(xt[b, :, half]) - st1[CENTER : CENTER + 1, half]
                weighted = piece * (unit * st1[INVERSE : INVERSE + 1, half])
                stat[0:1, half] += jnp.sum(piece * gain, axis=0, keepdims=True)
                stat[1:2, half] += jnp.sum(weighted * gain, axis=0, keepdims=True)
                fsum[0] += weighted
                fsum[1] += piece

        each(4, first_part)
        firsts.give(k)
        spot = lane[:WIDTH]
        add = jnp.where(spot == V_GAIN1, jnp.sum(fsum[0], axis=1, keepdims=True), 0.0)
        add = jnp.where(spot == V_BIAS1, jnp.sum(fsum[1], axis=1, keepdims=True), add)
        vcol[rows, :] = vcol[rows, :] + add
        if k == 3:
            put_q.add_near()
            put_q.line(0)
            put_f.back()
    stat_sends = [links.send(stat, stat_in.at[k - 1], links.plane(k)) for k in (1, 2, 3)]
    put_q.line(1)
    firsts.relay()
    put_o.line(2)
    put_f.share()
    rows = aligned(r * WIDTH, WIDTH)
    spot = lane[:WIDTH]
    query = jnp.zeros((WIDTH, 1), jnp.float32)
    value = jnp.zeros((WIDTH, 1), jnp.float32)
    for b in range(4):
        lanes = slice(b * QUARTER, (b + 1) * QUARTER)
        query = query + jnp.sum(wide(dqkv[:WIDTH, lanes]), axis=1, keepdims=True)
        value = value + jnp.sum(wide(dqkv[2 * WIDTH :, lanes]), axis=1, keepdims=True)
    add = jnp.where(spot == V_QUERY, query, jnp.where(spot == V_VALUE, value, 0.0))
    vcol[rows, :] = vcol[rows, :] + add
    vec[0] = vcol[...].T[:16]
    vec_near = links.send(vec.at[0], vec_in.at[0], links.partner())
    put_q.line(2)
    vec_near.wait()
    vec[1] = vec[0] + vec_in[0]
    vec_plane = [links.send(vec.at[1], vec_in.at[k], links.plane(k)) for k in (1, 2, 3)]
    put_o.hop()
    put_q.hop()
    put_o.back()
    put_o.share()
    put_q.back()
    for copy in vec_plane:
        copy.wait()
    vec[2] = vec[1] + vec_in[1] + vec_in[2] + vec_in[3]
    vec_high = [links.send(vec.at[2], vec_in.at[3 + k], links.column(k)) for k in (1, 2, 3)]
    outs.finish()

    def last_out(j):
        lanes = aligned(j * LANES, LANES)
        value = mid[rows, lanes] + colb[PROJ_BIAS, rows] + outs.total(lanes)
        out_v[:, lanes] = low(value)

    each(LEN // LANES, last_out)
    ends = [links.local(out_v, out_hbm)]
    for copy in swaps + stat_sends:
        copy.wait()
    firsts.finish()
    stat[...] = stat[...] + stat_in[0] + stat_in[1] + stat_in[2]

    def last_grad(j):
        lanes = aligned(j * LANES, LANES)
        inverse = st1[INVERSE : INVERSE + 1, lanes]
        unit = (wide(xt[r, :, lanes]) - st1[CENTER : CENTER + 1, lanes]) * inverse
        value = firsts.total(lanes) * colb[GAIN1, rows] - stat[0:1, lanes] / D
        grad_v[:, lanes] = wide(brf[:, lanes]) + inverse * (value - unit * (stat[1:2, lanes] / D))

    each(LEN // LANES, last_grad)
    ends.append(links.local(grad_v, grad_hbm))
    put_q.share()
    for copy in vec_high:
        copy.wait()
    vec[3] = vec[2] + vec_in[4] + vec_in[5] + vec_in[6]
    ends.append(links.local(vec.at[3], vec_hbm))
    for copy in ends:
        copy.wait()
    for put in (put_f, put_p, put_o, put_q):
        put.finish()


def run_block(*arguments):
    narrow, full = jnp.bfloat16, jnp.float32
    vmem = pltpu.VMEM
    sequence, tall = (4, WIDTH, LEN), (D, LEN)

    def thirds(lead=()):
        return [vmem(lead + (HALF, width), narrow) for width in (D, D, WQ)]

    def plane_sums(rows, lanes):
        return [vmem((2, rows // 2, lanes), narrow) for _ in range(3)]

    scratch = [
        vmem((6, D), full), vmem((2, D), full), vmem((FF,), full), vmem((3, HALF, WIDTH), narrow),
        vmem(sequence, narrow), vmem(sequence, narrow),
        vmem((4, WIDTH, WQ), narrow), vmem((4, WIDTH, D), narrow), vmem((4, WIDTH, D), narrow),
        vmem((4, 4, WIDTH, WIDTH), narrow),
        vmem((HALF, WQ), narrow), vmem((HALF, D), narrow), vmem((HALF, D), narrow),
        vmem((HALF, D), narrow), vmem((HALF, D), narrow),
        vmem((4, 8, LANES), jnp.int32), vmem((9, D, LANES), full),
        vmem(tall, narrow), vmem((WQ, LEN), narrow), vmem(sequence, narrow),
        vmem((8, LEN), full), vmem((8, LEN), full), vmem((8, LEN), full),
        vmem(tall, full), vmem(tall, narrow), vmem(tall, narrow), vmem(tall, full),
        vmem(sequence, narrow), vmem(tall, narrow), vmem(tall, narrow),
        *plane_sums(D, QUARTER), *plane_sums(WIDTH, LEN), *plane_sums(WIDTH, LEN),
        vmem((4, WIDTH, QUARTER), narrow), vmem((4, WIDTH, QUARTER), narrow),
        vmem((WIDTH, LEN), narrow), vmem((WIDTH, LEN), narrow), vmem((WQ, LEN), narrow),
        vmem((HEAD_DIM, LEN), full), vmem((HEAD_DIM, LEN), full),
        vmem((4, WIDTH, D), narrow), vmem((4, WIDTH, D), narrow), vmem((4, WIDTH, WQ), narrow),
        *thirds((4,)), *thirds((4,)), *thirds((3,)), *thirds((3,)), *thirds(), *thirds(), *thirds(),
        vmem((4, 4, WIDTH, WIDTH), narrow), vmem((4, 4, HALF, WIDTH), narrow),
        vmem((4, 4, HALF, WIDTH), narrow), vmem((3, 4, HALF, WIDTH), narrow),
        vmem((3, 4, HALF, WIDTH), narrow), vmem((4, HALF, WIDTH), narrow),
        vmem((3, HALF, WIDTH), narrow), vmem((HALF, WIDTH), narrow),
        vmem(sequence, narrow), vmem((2, WIDTH, LANES), full), vmem((D, LANES), full),
        vmem((4, 16, D), full), vmem((7, 16, D), full), vmem((8, LEN), full), vmem((3, 8, LEN), full),
        vmem((WIDTH, LEN), narrow), vmem((WIDTH, LEN), full),
        pltpu.SemaphoreType.DMA((REMOTES,)), pltpu.SemaphoreType.DMA((REMOTES,)),
        pltpu.SemaphoreType.DMA((LOCALS,)),
    ]
    results = [
        ((WIDTH, LEN), narrow), ((WIDTH, LEN), full), ((WIDTH, WQ), narrow), ((WIDTH, D), narrow),
        ((WIDTH, D), narrow), ((WIDTH, WIDTH), narrow), ((16, D), full),
    ]
    return pl.pallas_call(
        block_kernel,
        out_shape=[jax.ShapeDtypeStruct(*result) for result in results],
        in_specs=[pl.BlockSpec(memory_space=pltpu.SMEM)] + [ANY] * (len(arguments) - 1),
        out_specs=[ANY] * len(results),
        scratch_shapes=scratch,
        compiler_params=pltpu.CompilerParams(
            collective_id=0, has_side_effects=True, vmem_limit_bytes=VMEM_LIMIT
        ),
        name="block",
    )(*arguments)


def finish_kernel(
    out, grad, wq, wf, wp, wo, vec,
    out_done, grad_done, gain1, bias1, wq_done, qv, wo_done, out_bias, gain2, bias2,
    wf_done, fc, wp_done, proj,
):
    out_done[...] = out[...]
    grad_done[...] = grad[...]
    for i in range(3):
        wq_done[i] = wide(wq[:, i * WIDTH : (i + 1) * WIDTH])
    wo_done[...] = wide(wo[...])
    wf_done[...] = wide(wf[...])
    wp_done[...] = wide(wp[...])
    singles = ((gain1, V_GAIN1), (bias1, V_BIAS1), (out_bias, V_OUT), (gain2, V_GAIN2))
    for target, row in singles + ((bias2, V_BIAS2), (proj, V_PROJ)):
        target[...] = vec[row]
    qv[...] = vec[V_QUERY : V_VALUE + 1]
    for i in range(4):
        fc[pl.ds(i * D, D)] = vec[V_FC + i]


def plane_device(
    tokens, prefix, ln1_gain, ln1_bias, w_qkv, qv_bias, w_out, out_bias,
    ln2_gain, ln2_bias, w_fc, fc_bias, w_proj, proj_bias, cotangent,
):
    pieces = run_block(
        prefix, tokens, ln1_gain, ln1_bias, w_qkv, qv_bias, w_out, out_bias,
        ln2_gain, ln2_bias, w_fc, fc_bias, w_proj, proj_bias, cotangent,
    )
    wide_results = [
        (WIDTH, LEN), (D,), (D,), (3, WIDTH, WIDTH), (2, D), (WIDTH, WIDTH), (D,), (D,), (D,),
        (WIDTH, D), (FF,), (WIDTH, D), (D,),
    ]
    results = [jax.ShapeDtypeStruct((WIDTH, LEN), jnp.bfloat16)]
    results += [jax.ShapeDtypeStruct(dims, jnp.float32) for dims in wide_results]
    return pl.pallas_call(
        finish_kernel,
        out_shape=results,
        in_specs=[pl.BlockSpec(memory_space=pltpu.VMEM)] * len(pieces),
        out_specs=[pl.BlockSpec(memory_space=pltpu.VMEM)] * len(results),
        name="results",
    )(*pieces)


def solution(mesh):
    on_device = plane_device if dict(mesh.shape) == {"dp": 2, "row": 4, "col": 4} else general_device
    placed = (
        P("row", ("dp", "col")),
        P(("dp", "row")),
        P(),
        P(),
        P(None, "row", "col"),
        P(),
        P("col", "row"),
        P(),
        P(),
        P(),
        P("row", "col"),
        P(),
        P("row", "col"),
        P(),
        P("row", ("dp", "col")),
    )
    return jax.shard_map(
        on_device,
        mesh=mesh,
        in_specs=placed,
        out_specs=(
            P("row", ("dp", "col")),
            P("row", ("dp", "col")),
            P(),
            P(),
            P(None, "row", "col"),
            P(),
            P("col", "row"),
            P(),
            P(),
            P(),
            P("row", "col"),
            P(),
            P("row", "col"),
            P(),
        ),
        check_vma=False,
    )
```
